32 devices in a mesh: dp: 2 (over x), sp: 4 (over y, core), ctx: 4 (over z).
Axes of the slice: x: 2, y: 2, z: 4, core: 2. Of those that a mesh axis runs over, the one named last changes fastest.
Arguments:
- tokens: bfloat16 [2, 2048, 768], P('dp', ('sp', 'ctx')), may hold values from -6 to 6
- cotangent: bfloat16 [2, 2048, 768], P('dp', ('sp', 'ctx')), may hold values from -6 to 6
- lengths: int32 [2], P('dp'), may hold values from 512 to 2048, as said below
- kept_keys: int32 [2, 4, 512, 12, 64], P('dp', None, 'ctx', 'sp'), may hold values from 0 to 1983, as said below
- first_gain: bfloat16 [768], P('dp'), may hold values from 0.5 to 1.5
- qkv_weight: bfloat16 [768, 2304], P('dp'), may hold values from -0.21875 to 0.21875
- score_weight: bfloat16 [768, 12], P('dp'), may hold values from -0.4375 to 0.4375
- out_weight: bfloat16 [768, 768], P('dp'), may hold values from -1.25 to 1.25
- second_gain: bfloat16 [768], P('dp'), may hold values from 0.5 to 1.5
- fc_weight: bfloat16 [768, 3072], P('dp'), may hold values from -0.21875 to 0.21875
- proj_weight: bfloat16 [3072, 768], P('dp'), may hold values from -0.15625 to 0.15625
Outputs:
- output: bfloat16 [2, 2048, 768], P('dp', ('sp', 'ctx'))
- input_grad: bfloat16 [2, 2048, 768], P('dp', ('sp', 'ctx'))
- first_gain_grad: float32 [768], P('dp')
- qkv_grad: float32 [768, 2304], P('dp')
- score_grad: float32 [768, 12], P('dp')
- out_grad: float32 [768, 768], P('dp')
- second_gain_grad: float32 [768], P('dp')
- fc_grad: float32 [768, 3072], P('dp')
- proj_grad: float32 [3072, 768], P('dp')
The draws below stay inside these ranges and needn't reach their ends.
Inputs may be any that keep to these rules, and one draw needn't show every extreme that they name: `lengths`: the valid tokens of a slot stand at its start; in every draw some slot is full. `kept_keys`: an entry for the query at position t names a key position of the same slot at most t - 64; where t < 64 the entries are 0 and unused. Positions may repeat.
All inputs are finite; a program needn't handle non-finite values.
Results may differ from the reference program's by a relative error of at most 0.02.
Values may be sent and summed in bfloat16 or wider, within the bound.
No kernel may reach another device: no remote copies, remote signals or barrier semaphores. Data moves between devices by JAX's collectives and lax.ppermute only.
A program may use at most 256 MiB of HBM per device.

```python
import jax
import jax.numpy as jnp
from jax import lax

D = 768
H = 12
HD = 64
FF = 3072
KSEL = 64
WIN = 64
SLOT = 2048
SLOTS = 2
N_SP = 4


def draw_lengths(key, part):
    spread = jax.random.randint(jax.random.fold_in(key, 11), (SLOTS,), SLOT // 4, SLOT + 1)
    order = jax.random.permutation(jax.random.fold_in(key, 12), SLOTS)
    return jnp.where(order == 0, SLOT, spread).astype(jnp.int32)


def draw_kept_keys(key, part):
    segment = SLOT // N_SP
    position = jnp.arange(N_SP, dtype=jnp.int32)[:, None] * segment + jnp.arange(segment, dtype=jnp.int32)[None, :]
    upper = jnp.maximum(position - WIN + 1, 1)
    shape = (SLOTS, N_SP, segment, H, KSEL)
    picks = jax.random.randint(jax.random.fold_in(key, 13), shape, 0, upper[None, :, :, None, None])
    return jnp.where(position[None, :, :, None, None] >= WIN, picks, 0).astype(jnp.int32)


def block_levels(key, extent, pieces, smallest, top_value):
    def one(axis_at, blocks):
        draws = jax.random.uniform(jax.random.fold_in(jax.random.fold_in(key, 6), axis_at), (blocks,), jnp.float32, smallest / len(pieces), top_value / len(pieces))
        return jnp.repeat(jnp.exp(draws), extent[axis_at] // blocks).reshape((-1,) + (1,) * (len(extent) - axis_at - 1))

    factor_of = one(*pieces[0])
    for cut in pieces[1:]:
        factor_of = factor_of * one(*cut)
    return factor_of


def scatter_about(stream_key, shape, scale, limit, cuts=(), kind=jnp.bfloat16):
    drawn = jax.random.normal(stream_key, shape, jnp.float32) * scale
    if len(cuts) > 0:
        drawn = block_levels(stream_key, shape, cuts, -0.22, 0.18) * drawn
    return jnp.clip(drawn, min=-limit, max=limit).astype(kind)


def setup_inputs(seed: int = 0) -> dict:
    key_of = jax.random.split(jax.random.key(seed), 12)
    return {
        "tokens": scatter_about(key_of[0], (SLOTS, SLOT, D), 1.0, 6.0, ((0, 2), (1, 16))),
        "cotangent": scatter_about(key_of[1], (SLOTS, SLOT, D), 1.0, 6.0, ((0, 2), (1, 16))),
        "lengths": draw_lengths(jax.random.fold_in(key_of[11], 71), 0),
        "kept_keys": draw_kept_keys(jax.random.fold_in(key_of[11], 71), 0),
        "first_gain": jnp.clip(1.0 + 0.1 * jax.random.normal(key_of[4], (D,), jnp.float32), 0.5, 1.5).astype(jnp.bfloat16),
        "qkv_weight": scatter_about(key_of[5], (D, 3 * D), D ** -0.5, 0.21875, ((0, 2),)),
        "score_weight": scatter_about(key_of[6], (D, H), (D // 4) ** -0.5, 0.4375, ((0, 2),)),
        "out_weight": scatter_about(key_of[7], (D, D), (D // 32) ** -0.5, 1.25, ((0, 2),)),
        "second_gain": jnp.clip(1.0 + 0.1 * jax.random.normal(key_of[8], (D,), jnp.float32), 0.5, 1.5).astype(jnp.bfloat16),
        "fc_weight": scatter_about(key_of[9], (D, FF), D ** -0.5, 0.21875, ((0, 2),)),
        "proj_weight": scatter_about(key_of[10], (FF, D), (FF // 2) ** -0.5, 0.15625, ((0, 2),)),
    }


HIGHEST = lax.Precision.HIGHEST
EPSILON = 1e-05

@jax.custom_vjp
def low(v):
    return lax.optimization_barrier(v.astype(jnp.bfloat16)).astype(jnp.float32)

@jax.custom_vjp
def low_back(v):
    return v

def low_keep(v):
    return (low(v), None)

def low_pass(kept, grad):
    return (grad,)

def back_keep(v):
    return (v, None)

def back_low(kept, grad):
    return (low(grad),)
low.defvjp(low_keep, low_pass)
low_back.defvjp(back_keep, back_low)

def product(left, right):
    return jnp.dot(left, right, precision=HIGHEST)

def layer_norm(values, gain):
    mean_value = lax.optimization_barrier(jnp.mean(values, axis=-1, keepdims=True))
    centred = values - mean_value
    variance = lax.optimization_barrier(jnp.mean(centred * centred, axis=-1, keepdims=True))
    return centred * lax.rsqrt(variance + EPSILON) * gain

def attend_block(query, picked, start, keys_pad, values_pad, gates_pad):
    row_count = query.shape[0]
    head_count = query.shape[1]
    score_scale = HD ** (-0.5)
    span_len = row_count + WIN
    key_slab = lax.dynamic_slice_in_dim(keys_pad, start, span_len, 0)
    value_slab = lax.dynamic_slice_in_dim(values_pad, start, span_len, 0)
    gate_slab = lax.dynamic_slice_in_dim(gates_pad, start, span_len, 0)
    head_ids = jnp.arange(head_count, dtype=jnp.int32)[None, :, None]
    rows_at = picked + WIN
    key_pick = keys_pad[rows_at, head_ids]
    value_pick = values_pad[rows_at, head_ids]
    near_scores = jnp.einsum('rhd,jhd->rhj', query, key_slab, precision=HIGHEST) * score_scale + jnp.transpose(gate_slab)[None]
    far_scores = jnp.einsum('rhd,rhmd->rhm', query, key_pick, precision=HIGHEST) * score_scale + gates_pad[rows_at, head_ids]
    row_ids = jnp.arange(row_count, dtype=jnp.int32)[:, None, None]
    col_ids = jnp.arange(span_len, dtype=jnp.int32)[None, None, :]
    near_ok = (col_ids > row_ids) & (col_ids <= row_ids + WIN) & (col_ids + start >= WIN)
    near_ok = jnp.broadcast_to(near_ok, near_scores.shape)
    far_ok = jnp.broadcast_to(start + row_ids >= WIN, far_scores.shape)
    scores = low_back(jnp.concatenate([near_scores, far_scores], axis=-1))
    allowed = jnp.concatenate([near_ok, far_ok], axis=-1)
    masked = jnp.where(allowed, scores, -1e+30)
    largest = lax.optimization_barrier(jnp.max(masked, axis=-1, keepdims=True))
    expo = jnp.exp(masked - largest)
    prob = expo / lax.optimization_barrier(jnp.sum(expo, axis=-1, keepdims=True))
    weights = low(prob)
    near_out = jnp.einsum('rhj,jhd->rhd', weights[..., :span_len], value_slab, precision=HIGHEST)
    far_out = jnp.einsum('rhm,rhmd->rhd', weights[..., span_len:], value_pick, precision=HIGHEST)
    return near_out + far_out

def slot_forward(params, inputs, length, picked_all):
    first_gain, qkv_weight, score_weight, out_weight, second_gain, fc_weight, proj_weight = params
    norm_one = low(layer_norm(inputs, first_gain))
    qkv_rows = low_back(low(product(norm_one, qkv_weight)))
    key_score = low_back(low(product(norm_one, score_weight)))
    gate = -jnp.log1p(jnp.exp(-key_score))
    triple = qkv_rows.reshape(SLOT, H, 3, HD)
    query = triple[:, :, 0]
    keys_pad = jnp.pad(triple[:, :, 1], ((WIN, 0), (0, 0), (0, 0)))
    values_pad = jnp.pad(triple[:, :, 2], ((WIN, 0), (0, 0), (0, 0)))
    gates_pad = jnp.pad(gate, ((WIN, 0), (0, 0)))
    block_rows = min(512, SLOT)
    block_count = SLOT // block_rows
    query_blocks = query.reshape(block_count, block_rows, H, HD)
    picked_blocks = picked_all.reshape(block_count, block_rows, H, KSEL)
    starts = jnp.arange(block_count, dtype=jnp.int32) * block_rows

    def one_block(item):
        return attend_block(item[0], item[1], item[2], keys_pad, values_pad, gates_pad)
    outs = lax.map(jax.checkpoint(one_block), (query_blocks, picked_blocks, starts))
    attended = low_back(low(outs.reshape(SLOT, D)))
    branch = low_back(product(attended, out_weight))
    mixed = inputs + branch
    norm_two = low(layer_norm(mixed, second_gain))
    hidden_pre = low_back(product(norm_two, fc_weight))
    active = low(jax.nn.gelu(hidden_pre, approximate=True))
    result = mixed + product(active, proj_weight)
    is_valid = jnp.arange(SLOT, dtype=jnp.int32) < length
    return jnp.where(is_valid[:, None], result, 0.0)

def reference(tokens, cotangent, lengths, kept_keys, first_gain, qkv_weight, score_weight, out_weight, second_gain, fc_weight, proj_weight):
    params = tuple((item.astype(jnp.float32) for item in (first_gain, qkv_weight, score_weight, out_weight, second_gain, fc_weight, proj_weight)))
    picked_slots = kept_keys.reshape(SLOTS, SLOT, H, KSEL)

    def one_slot(totals, item):
        slot_tokens, slot_cot, length, picked = item

        def forward(weights, inputs):
            return slot_forward(weights, inputs, length, picked)
        result, pull = jax.vjp(forward, params, slot_tokens.astype(jnp.float32))
        grad_params, grad_inputs = pull(slot_cot.astype(jnp.float32))
        totals = tuple((left + right for left, right in zip(totals, grad_params)))
        return (totals, (result.astype(jnp.bfloat16), grad_inputs.astype(jnp.bfloat16)))
    start_totals = tuple((jnp.zeros_like(item) for item in params))
    totals, (outputs, input_grads) = lax.scan(one_slot, start_totals, (tokens, cotangent, lengths, picked_slots))
    return (outputs, input_grads, totals[0], totals[1], totals[2], totals[3], totals[4], totals[5], totals[6])
```

```python
import functools

import jax
import jax.numpy as jnp
from jax import lax
from jax.experimental import pallas as pl
from jax.experimental.pallas import tpu as pltpu
from jax.sharding import PartitionSpec as P

H = 12
HD = 64
WIN = 64
LANES = 128
SLOT = 2048


EPSILON = 1e-05


def layer_norm(values, gain):
    mean_value = jnp.mean(values, axis=-1, keepdims=True)
    centred = values - mean_value
    variance = jnp.mean(centred * centred, axis=-1, keepdims=True)
    return centred * lax.rsqrt(variance + EPSILON) * gain


def tanh_gelu(values):
    return jax.nn.gelu(values, approximate=True)


def contract_rows(left, right):
    return lax.dot_general(
        left, right, (((0,), (0,)), ((), ())), preferred_element_type=jnp.float32
    )


def contract_cols(left, right):
    return lax.dot_general(
        left, right, (((1,), (1,)), ((), ())), preferred_element_type=jnp.float32
    )


NT = (((1,), (1,)), ((), ()))


def attend_body(tiles, base, idx_ref, q_ref, kv_ref, gate_ref, out_ref, prob_ref, score_ref, pair_ref):
    rows = q_ref.shape[0]
    span = tiles * LANES
    f32, bf16 = jnp.float32, jnp.bfloat16
    score_ref[:, :span] = (
        lax.dot_general(q_ref[...], kv_ref[:span, :], NT, preferred_element_type=f32) * HD ** (-0.5)
        + gate_ref[0, :, :span]
    )
    kept = idx_ref[0, 0]
    pair_ref[...] = jnp.concatenate([kept, kept], axis=1)
    wide = 8 * HD
    sub = lax.broadcasted_iota(jnp.int32, (8, wide), 0)
    lane = lax.broadcasted_iota(jnp.int32, (8, wide), 1)
    own = (lane // HD) == sub
    subf = sub.astype(f32)
    ahead = lax.broadcasted_iota(jnp.int32, (8, LANES), 0) - lax.broadcasted_iota(jnp.int32, (8, LANES), 1)
    near_from = max(0, tiles - 5)

    def eight(start):
        four = pair_ref[pl.ds(start, 8), :]
        index = jnp.concatenate([four] * 4, axis=1)
        pos = base + start + sub
        high = jnp.where(own & (pos >= WIN), index >> 7, -2).astype(f32)
        low = jnp.sum(jnp.where(own, (index & 127).astype(f32), 0.0), axis=0, keepdims=True) - subf
        high_pair = jnp.concatenate([high, high - 1.0], axis=0).astype(bf16)
        low_pair = jnp.concatenate([low, low - 8.0], axis=0).astype(bf16)
        one, zero = jnp.ones((), bf16), jnp.zeros((), bf16)
        left = jnp.concatenate(
            [jnp.where(high_pair == jnp.array(2 * p, bf16), one, zero) for p in range(tiles // 2)], axis=0
        )
        right = jnp.concatenate(
            [jnp.where(low_pair == jnp.array(16 * p, bf16), one, zero) for p in range(8)], axis=0
        )
        count = lax.dot_general(left, right, NT, preferred_element_type=f32)
        gap = ahead + (base + start)
        masked, counts = [], []
        largest = None
        for tile in range(tiles):
            number = count[8 * tile : 8 * tile + 8, :]
            if tile >= near_from:
                far = gap - tile * LANES
                number = number + jnp.where((far >= 0) & (far < WIN), 1.0, 0.0)
            value = jnp.where(number > 0.0, score_ref[pl.ds(start, 8), tile * LANES : (tile + 1) * LANES], -1e30)
            counts.append(number)
            masked.append(value)
            largest = value if largest is None else jnp.maximum(largest, value)
        top = jnp.max(largest, axis=1, keepdims=True)
        total = None
        expos = []
        for number, value in zip(counts, masked):
            expo = jnp.exp(value - top) * number
            expos.append(expo)
            total = expo if total is None else total + expo
        inverse = 1.0 / jnp.sum(total, axis=1, keepdims=True)
        return [expo * inverse for expo in expos]

    def step(index, carry):
        start = pl.multiple_of(index * 16, 16)
        first, second = eight(start), eight(start + 8)
        for tile in range(tiles):
            prob_ref[0, 0, pl.ds(start, 16), tile * LANES : (tile + 1) * LANES] = jnp.concatenate(
                [first[tile], second[tile]], axis=0
            ).astype(bf16)
        return carry

    lax.fori_loop(0, rows // 16, step, 0)
    both = jnp.dot(prob_ref[0, 0, :, :span], kv_ref[:span, :], preferred_element_type=f32)
    out_ref[0] = both[:, HD:].astype(bf16)


def attend_kernel(parts, chunk, base_ref, *refs):
    part = pl.program_id(1)
    base = base_ref[0] + part * chunk
    for at in range(parts):
        pl.when(part == at)(
            functools.partial(attend_body, (at + 1) * chunk // LANES, base, *refs)
        )


def attend(base, kept, query, pairs, gates):
    heads, parts, block, keep = kept.shape
    slot = pairs.shape[0]
    chunk = slot // parts
    grid_spec = pltpu.PrefetchScalarGridSpec(
        num_scalar_prefetch=1,
        grid=(heads, parts),
        in_specs=[
            pl.BlockSpec((1, 1, block, keep), lambda h, r, b: (h, r, 0, 0)),
            pl.BlockSpec((block, LANES), lambda h, r, b: (r, h)),
            pl.BlockSpec((slot, LANES), lambda h, r, b: (0, h)),
            pl.BlockSpec((1, 1, slot), lambda h, r, b: (h, 0, 0)),
        ],
        out_specs=[
            pl.BlockSpec((1, block, HD), lambda h, r, b: (h, r, 0)),
            pl.BlockSpec((1, 1, block, slot), lambda h, r, b: (h, r, 0, 0)),
        ],
        scratch_shapes=[pltpu.VMEM((block, slot), jnp.float32), pltpu.VMEM((block, 2 * keep), jnp.int32)],
    )
    return pl.pallas_call(
        functools.partial(attend_kernel, parts, chunk),
        grid_spec=grid_spec,
        out_shape=[
            jax.ShapeDtypeStruct((heads, parts * block, HD), jnp.bfloat16),
            jax.ShapeDtypeStruct((heads, parts, block, slot), jnp.bfloat16),
        ],
        name="attend",
    )(base, kept, query, pairs, gates)


def attend_back_body(first, tiles, chunk, q_ref, grad_ref, kv_ref, prob_ref, dq_ref, dkv_ref, gate_ref, raw_ref):
    f32, bf16 = jnp.float32, jnp.bfloat16
    rows = q_ref.shape[0]
    steps = tiles * LANES // chunk
    if first:
        dkv_ref[...] = jnp.zeros_like(dkv_ref)
        gate_ref[...] = jnp.zeros_like(gate_ref)
    dot_sum = None
    for at in range(steps):
        cols = slice(at * chunk, (at + 1) * chunk)
        raw = lax.dot_general(grad_ref[...], kv_ref[cols, :], NT, preferred_element_type=f32)
        raw_ref[:, cols] = raw
        part = jnp.sum(raw * prob_ref[0, 0, :, cols].astype(f32), axis=1, keepdims=True)
        dot_sum = part if dot_sum is None else dot_sum + part
    lane = lax.broadcasted_iota(jnp.int32, (rows, LANES), 1)
    scaled = jnp.where(lane == HD, 1.0, q_ref[...].astype(f32) * HD ** (-0.5))
    query_t = jnp.transpose(scaled)[: HD + 16].astype(bf16)
    grad_t = jnp.transpose(grad_ref[...].astype(f32))[HD:].astype(bf16)
    dq = None
    for at in range(steps):
        cols = slice(at * chunk, (at + 1) * chunk)
        prob = prob_ref[0, 0, :, cols]
        grad_score = (prob.astype(f32) * (raw_ref[:, cols] - dot_sum)).astype(bf16)
        piece = jnp.dot(grad_score, kv_ref[cols, :], preferred_element_type=f32)
        dq = piece if dq is None else dq + piece
        keys = jnp.dot(query_t, grad_score, preferred_element_type=f32)
        dkv_ref[0, :HD, cols] += keys[:HD]
        gate_ref[0, :, cols] += keys[HD : HD + 8]
        dkv_ref[0, HD:, cols] += jnp.dot(grad_t, prob, preferred_element_type=f32)
    dq_ref[0] = (dq[:, :HD] * HD ** (-0.5)).astype(dq_ref.dtype)


def attend_back_kernel(parts, chunk, *refs):
    part = pl.program_id(1)
    for at in range(parts):
        pl.when(part == at)(
            functools.partial(attend_back_body, at == 0, (at + 1) * chunk // LANES, chunk, *refs)
        )


def attend_back(query, grad, pairs, prob):
    heads, parts, block, slot = prob.shape
    chunk = slot // parts
    return pl.pallas_call(
        functools.partial(attend_back_kernel, parts, chunk),
        grid=(heads, parts),
        in_specs=[
            pl.BlockSpec((block, LANES), lambda h, r: (r, h)),
            pl.BlockSpec((block, LANES), lambda h, r: (r, h)),
            pl.BlockSpec((slot, LANES), lambda h, r: (0, h)),
            pl.BlockSpec((1, 1, block, slot), lambda h, r: (h, r, 0, 0)),
        ],
        out_specs=[
            pl.BlockSpec((1, block, HD), lambda h, r: (h, r, 0)),
            pl.BlockSpec((1, LANES, slot), lambda h, r: (h, 0, 0)),
            pl.BlockSpec((1, 8, slot), lambda h, r: (h, 0, 0)),
        ],
        out_shape=[
            jax.ShapeDtypeStruct((heads, parts * block, HD), jnp.float32),
            jax.ShapeDtypeStruct((heads, LANES, slot), jnp.float32),
            jax.ShapeDtypeStruct((heads, 8, slot), jnp.float32),
        ],
        scratch_shapes=[pltpu.VMEM((block, slot), jnp.float32)],
        name="attend_back",
    )(query, grad, pairs, prob)


def per_device(
    tokens,
    cotangent,
    lengths,
    kept_keys,
    first_gain,
    qkv_weight,
    score_weight,
    out_weight,
    second_gain,
    fc_weight,
    proj_weight,
):
    gathered = (
        lax.all_gather(first_gain, "dp", axis=0, tiled=True),
        lax.all_gather(qkv_weight, "dp", axis=0, tiled=True),
        lax.all_gather(score_weight, "dp", axis=0, tiled=True),
        lax.all_gather(out_weight, "dp", axis=0, tiled=True),
        lax.all_gather(second_gain, "dp", axis=0, tiled=True),
        lax.all_gather(fc_weight, "dp", axis=0, tiled=True),
        lax.all_gather(proj_weight, "dp", axis=0, tiled=True),
    )
    gain_one, qkv_full, score_full, out_full, gain_two, fc_full, proj_full = gathered
    gain_one = gain_one.astype(jnp.float32)
    gain_two = gain_two.astype(jnp.float32)
    seg_count = lax.axis_size("sp")
    ctx_count = lax.axis_size("ctx")
    local_rows = tokens.shape[1]
    heads_here = H // seg_count
    segment = SLOT // seg_count
    ctx_at = lax.axis_index("ctx")
    positions = (lax.axis_index("sp") * ctx_count + ctx_at) * local_rows + jnp.arange(
        local_rows, dtype=jnp.int32
    )
    is_valid = positions < lengths[0]
    inputs = tokens[0].astype(jnp.float32)
    norm_one = layer_norm(inputs, gain_one).astype(jnp.bfloat16)
    qkv_rows = jnp.dot(norm_one, qkv_full, preferred_element_type=jnp.float32).astype(jnp.bfloat16)
    key_score = jnp.dot(norm_one, score_full, preferred_element_type=jnp.float32).astype(
        jnp.bfloat16
    )
    head_qkv, head_score = (
        lax.all_to_all(qkv_rows, "sp", split_axis=1, concat_axis=0, tiled=True),
        lax.all_to_all(key_score, "sp", split_axis=1, concat_axis=0, tiled=True),
    )
    triple = head_qkv.reshape(seg_count, local_rows, heads_here, 3 * HD)
    queries = triple[..., :HD]
    pairs = triple[..., HD:].reshape(seg_count, local_rows, heads_here * 2 * HD)
    local_scores = head_score.reshape(seg_count, local_rows, heads_here)
    all_pairs, all_scores = (
        lax.all_gather(pairs, "ctx", axis=1, tiled=True),
        lax.all_gather(local_scores, "ctx", axis=1, tiled=True),
    )
    pairs_full = all_pairs.reshape(SLOT, heads_here * 2 * HD)
    raw_scores = all_scores.reshape(SLOT, heads_here).astype(jnp.float32)
    gates_full = -jnp.log1p(jnp.exp(-raw_scores)).T[:, None]
    kept = jnp.transpose(kept_keys[0], (2, 0, 1, 3))
    query_rows = seg_count * local_rows
    query_wide = jnp.pad(queries, ((0, 0), (0, 0), (0, 0), (0, HD))).reshape(
        query_rows, heads_here * LANES
    )
    base = (ctx_at * local_rows).astype(jnp.int32)[None]
    head_outs, prob = attend(base, kept, query_wide, pairs_full, gates_full)
    attended_heads = jnp.transpose(head_outs, (1, 0, 2))
    attended = lax.all_to_all(
        attended_heads.reshape(seg_count * local_rows, heads_here * HD),
        "sp",
        split_axis=0,
        concat_axis=1,
        tiled=True,
    )
    mixed = inputs + jnp.dot(attended, out_full, preferred_element_type=jnp.float32)
    norm_two = layer_norm(mixed, gain_two).astype(jnp.bfloat16)
    hidden_pre = jnp.dot(norm_two, fc_full, preferred_element_type=jnp.float32)
    active = tanh_gelu(hidden_pre).astype(jnp.bfloat16)
    result = jnp.where(
        is_valid[:, None],
        mixed + jnp.dot(active, proj_full, preferred_element_type=jnp.float32),
        0.0,
    )
    output = result.astype(jnp.bfloat16)[None]
    grad_out = jnp.where(is_valid[:, None], cotangent[0], jnp.zeros_like(cotangent[0]))
    proj_grad = contract_rows(active, grad_out)
    grad_active = contract_cols(grad_out, proj_full)
    _, gelu_pull = jax.vjp(tanh_gelu, hidden_pre)
    grad_pre = gelu_pull(grad_active)[0].astype(jnp.bfloat16)
    fc_grad = contract_rows(norm_two, grad_pre)
    grad_norm_two = contract_cols(grad_pre, fc_full)
    _, second_pull = jax.vjp(layer_norm, mixed, gain_two)
    grad_mixed_norm, second_gain_grad = second_pull(grad_norm_two)
    grad_mixed = grad_out.astype(jnp.float32) + grad_mixed_norm
    grad_branch = grad_mixed.astype(jnp.bfloat16)
    out_grad = contract_rows(attended, grad_branch)
    grad_attended = contract_cols(grad_branch, out_full).astype(jnp.bfloat16)
    head_grad = lax.all_to_all(grad_attended, "sp", split_axis=1, concat_axis=0, tiled=True)
    grad_wide = jnp.pad(
        head_grad.reshape(query_rows, heads_here, HD), ((0, 0), (0, 0), (HD, 0))
    ).reshape(query_rows, heads_here * LANES)
    query_grads, pair_grads, gate_grads = attend_back(query_wide, grad_wide, pairs_full, prob)
    grad_queries = jnp.transpose(query_grads, (1, 0, 2)).reshape(
        seg_count, local_rows, heads_here, HD
    )
    pair_grad = jnp.transpose(pair_grads, (2, 0, 1)).reshape(
        seg_count, segment, heads_here * 2 * HD
    )
    gate_total = gate_grads[:, 0].T.reshape(seg_count, segment, heads_here)
    pair_mine, gate_mine = (
        lax.psum_scatter(pair_grad, "ctx", scatter_dimension=1, tiled=True),
        lax.psum_scatter(gate_total, "ctx", scatter_dimension=1, tiled=True),
    )
    score_here = local_scores.astype(jnp.float32)
    grad_key_score = (gate_mine * jax.nn.sigmoid(-score_here)).astype(jnp.bfloat16)
    grad_triple = jnp.concatenate(
        [grad_queries, pair_mine.reshape(seg_count, local_rows, heads_here, 2 * HD)], axis=-1
    )
    grad_triple = grad_triple.astype(jnp.bfloat16).reshape(
        seg_count * local_rows, heads_here * 3 * HD
    )
    grad_qkv, grad_score = (
        lax.all_to_all(grad_triple, "sp", split_axis=0, concat_axis=1, tiled=True),
        lax.all_to_all(
            grad_key_score.reshape(seg_count * local_rows, heads_here),
            "sp",
            split_axis=0,
            concat_axis=1,
            tiled=True,
        ),
    )
    qkv_grad = contract_rows(norm_one, grad_qkv)
    score_grad = contract_rows(norm_one, grad_score)
    grad_norm_one = contract_cols(grad_qkv, qkv_full) + contract_cols(grad_score, score_full)
    _, first_pull = jax.vjp(layer_norm, inputs, gain_one)
    grad_input_norm, first_gain_grad = first_pull(grad_norm_one)
    input_grad = (grad_mixed + grad_input_norm).astype(jnp.bfloat16)[None]
    shards = (
        lax.psum_scatter(
            first_gain_grad.astype(jnp.bfloat16), "dp", scatter_dimension=0, tiled=True
        ).astype(jnp.float32),
        lax.psum_scatter(
            qkv_grad.astype(jnp.bfloat16), "dp", scatter_dimension=0, tiled=True
        ).astype(jnp.float32),
        lax.psum_scatter(
            score_grad.astype(jnp.bfloat16), "dp", scatter_dimension=0, tiled=True
        ).astype(jnp.float32),
        lax.psum_scatter(
            out_grad.astype(jnp.bfloat16), "dp", scatter_dimension=0, tiled=True
        ).astype(jnp.float32),
        lax.psum_scatter(
            second_gain_grad.astype(jnp.bfloat16), "dp", scatter_dimension=0, tiled=True
        ).astype(jnp.float32),
        lax.psum_scatter(
            fc_grad.astype(jnp.bfloat16), "dp", scatter_dimension=0, tiled=True
        ).astype(jnp.float32),
        lax.psum_scatter(
            proj_grad.astype(jnp.bfloat16), "dp", scatter_dimension=0, tiled=True
        ).astype(jnp.float32),
    )
    reduced = (
        lax.psum(shards[0].astype(jnp.bfloat16), ("sp", "ctx")).astype(jnp.float32),
        lax.psum(shards[1].astype(jnp.bfloat16), ("sp", "ctx")).astype(jnp.float32),
        lax.psum(shards[2].astype(jnp.bfloat16), ("sp", "ctx")).astype(jnp.float32),
        lax.psum(shards[3].astype(jnp.bfloat16), ("sp", "ctx")).astype(jnp.float32),
        lax.psum(shards[4].astype(jnp.bfloat16), ("sp", "ctx")).astype(jnp.float32),
        lax.psum(shards[5].astype(jnp.bfloat16), ("sp", "ctx")).astype(jnp.float32),
        lax.psum(shards[6].astype(jnp.bfloat16), ("sp", "ctx")).astype(jnp.float32),
    )
    return (
        output,
        input_grad,
        reduced[0],
        reduced[1],
        reduced[2],
        reduced[3],
        reduced[4],
        reduced[5],
        reduced[6],
    )


def solution(mesh):
    placed = (
        P("dp", ("sp", "ctx"), None),
        P("dp", ("sp", "ctx"), None),
        P("dp"),
        P("dp", None, "ctx", "sp", None),
        P("dp"),
        P("dp", None),
        P("dp", None),
        P("dp", None),
        P("dp"),
        P("dp", None),
        P("dp", None),
    )
    return jax.shard_map(
        per_device,
        mesh=mesh,
        in_specs=placed,
        out_specs=(
            P("dp", ("sp", "ctx"), None),
            P("dp", ("sp", "ctx"), None),
            P("dp"),
            P("dp", None),
            P("dp", None),
            P("dp", None),
            P("dp"),
            P("dp", None),
            P("dp", None),
        ),
        check_vma=False,
    )
```

```python
import functools

import jax
import jax.numpy as jnp
from jax import lax
from jax.experimental import pallas as pl
from jax.experimental.pallas import tpu as pltpu
from jax.sharding import PartitionSpec as P

H = 12
HD = 64
WIN = 64
LANES = 128
SLOT = 2048


EPSILON = 1e-05


def layer_norm(values, gain):
    mean_value = jnp.mean(values, axis=-1, keepdims=True)
    centred = values - mean_value
    variance = jnp.mean(centred * centred, axis=-1, keepdims=True)
    return centred * lax.rsqrt(variance + EPSILON) * gain


def tanh_gelu(values):
    return jax.nn.gelu(values, approximate=True)


def contract_rows(left, right):
    return lax.dot_general(
        left, right, (((0,), (0,)), ((), ())), preferred_element_type=jnp.float32
    )


def contract_cols(left, right):
    return lax.dot_general(
        left, right, (((1,), (1,)), ((), ())), preferred_element_type=jnp.float32
    )


NT = (((1,), (1,)), ((), ()))


PAD_ROWS = 16


def slot_order(src_ref, kv_ref):
    count, height, _ = src_ref.shape
    for tile in range(kv_ref.shape[0] // LANES):
        part, at = divmod(tile, count)
        kv_ref[tile * LANES : (tile + 1) * LANES, :] = src_ref[at, part * LANES : (part + 1) * LANES, :]


def slot_gates(src_ref, gate_ref):
    count, height, _ = src_ref.shape
    for at in range(count):
        scores = src_ref[at, height - PAD_ROWS :, :].astype(jnp.float32)
        gates = -jnp.log1p(jnp.exp(-scores))
        for part in range(gate_ref.shape[1] // LANES // count):
            tile = part * count + at
            gate_ref[:, tile * LANES : (tile + 1) * LANES] = jnp.broadcast_to(gates[part : part + 1, :], (8, LANES))


def attend_body(first, tiles, base, idx_ref, q_ref, src_ref, out_ref, prob_ref, score_ref, pair_ref, kv_ref, gate_ref):
    rows = q_ref.shape[0]
    if first:
        slot_order(src_ref, kv_ref)
        slot_gates(src_ref, gate_ref)
    span = tiles * LANES
    f32, bf16 = jnp.float32, jnp.bfloat16
    score_ref[:, :span] = (
        lax.dot_general(q_ref[...], kv_ref[:span, :], NT, preferred_element_type=f32) * HD ** (-0.5)
        + gate_ref[0:1, :span]
    )
    kept = idx_ref[0, 0]
    pair_ref[...] = jnp.concatenate([kept, kept], axis=1)
    wide = 8 * HD
    sub = lax.broadcasted_iota(jnp.int32, (8, wide), 0)
    lane = lax.broadcasted_iota(jnp.int32, (8, wide), 1)
    own = (lane // HD) == sub
    subf = sub.astype(f32)
    ahead = lax.broadcasted_iota(jnp.int32, (8, LANES), 0) - lax.broadcasted_iota(jnp.int32, (8, LANES), 1)
    near_from = max(0, tiles - 5)

    def eight(start):
        four = pair_ref[pl.ds(start, 8), :]
        index = jnp.concatenate([four] * 4, axis=1)
        pos = base + start + sub
        high = jnp.where(own & (pos >= WIN), index >> 7, -2).astype(f32)
        low = jnp.sum(jnp.where(own, (index & 127).astype(f32), 0.0), axis=0, keepdims=True) - subf
        high_pair = jnp.concatenate([high, high - 1.0], axis=0).astype(bf16)
        low_pair = jnp.concatenate([low, low - 8.0], axis=0).astype(bf16)
        one, zero = jnp.ones((), bf16), jnp.zeros((), bf16)
        left = jnp.concatenate(
            [jnp.where(high_pair == jnp.array(2 * p, bf16), one, zero) for p in range(tiles // 2)], axis=0
        )
        right = jnp.concatenate(
            [jnp.where(low_pair == jnp.array(16 * p, bf16), one, zero) for p in range(8)], axis=0
        )
        count = lax.dot_general(left, right, NT, preferred_element_type=f32)
        gap = ahead + (base + start)
        masked, counts = [], []
        largest = None
        for tile in range(tiles):
            number = count[8 * tile : 8 * tile + 8, :]
            if tile >= near_from:
                far = gap - tile * LANES
                number = number + jnp.where((far >= 0) & (far < WIN), 1.0, 0.0)
            value = jnp.where(number > 0.0, score_ref[pl.ds(start, 8), tile * LANES : (tile + 1) * LANES], -1e30)
            counts.append(number)
            masked.append(value)
            largest = value if largest is None else jnp.maximum(largest, value)
        top = jnp.max(largest, axis=1, keepdims=True)
        total = None
        expos = []
        for number, value in zip(counts, masked):
            expo = jnp.exp(value - top) * number
            expos.append(expo)
            total = expo if total is None else total + expo
        inverse = 1.0 / jnp.sum(total, axis=1, keepdims=True)
        return [expo * inverse for expo in expos]

    def step(index, carry):
        start = pl.multiple_of(index * 16, 16)
        first, second = eight(start), eight(start + 8)
        for tile in range(tiles):
            prob_ref[0, 0, pl.ds(start, 16), tile * LANES : (tile + 1) * LANES] = jnp.concatenate(
                [first[tile], second[tile]], axis=0
            ).astype(bf16)
        return carry

    lax.fori_loop(0, rows // 16, step, 0)
    both = jnp.dot(prob_ref[0, 0, :, :span], kv_ref[:span, :], preferred_element_type=f32)
    out_ref[0] = both[:, HD:].astype(bf16)


def attend_kernel(parts, chunk, base_ref, *refs):
    part = pl.program_id(1)
    base = base_ref[0] + part * chunk
    for at in range(parts):
        pl.when(part == at)(
            functools.partial(attend_body, at == 0, (at + 1) * chunk // LANES, base, *refs)
        )


def attend(base, kept, query, pairs):
    heads, parts, block, keep = kept.shape
    count, height, _ = pairs.shape
    slot = count * (height - PAD_ROWS)
    chunk = slot // parts
    grid_spec = pltpu.PrefetchScalarGridSpec(
        num_scalar_prefetch=1,
        grid=(heads, parts),
        in_specs=[
            pl.BlockSpec((1, 1, block, keep), lambda h, r, b: (h, r, 0, 0)),
            pl.BlockSpec((block, LANES), lambda h, r, b: (r, h)),
            pl.BlockSpec((count, height, LANES), lambda h, r, b: (0, 0, h)),
        ],
        out_specs=[
            pl.BlockSpec((1, block, HD), lambda h, r, b: (h, r, 0)),
            pl.BlockSpec((1, 1, block, slot), lambda h, r, b: (h, r, 0, 0)),
        ],
        scratch_shapes=[
            pltpu.VMEM((block, slot), jnp.float32),
            pltpu.VMEM((block, 2 * keep), jnp.int32),
            pltpu.VMEM((slot, LANES), jnp.bfloat16),
            pltpu.VMEM((8, slot), jnp.float32),
        ],
    )
    return pl.pallas_call(
        functools.partial(attend_kernel, parts, chunk),
        grid_spec=grid_spec,
        out_shape=[
            jax.ShapeDtypeStruct((heads, parts * block, HD), jnp.bfloat16),
            jax.ShapeDtypeStruct((heads, parts, block, slot), jnp.bfloat16),
        ],
        name="attend",
    )(base, kept, query, pairs)


def attend_back_body(first, last, tiles, chunk, q_ref, grad_ref, src_ref, prob_ref, dq_ref, out_ref, raw_ref, kv_ref, dkv_ref, gate_ref):
    f32, bf16 = jnp.float32, jnp.bfloat16
    rows = q_ref.shape[0]
    steps = tiles * LANES // chunk
    if first:
        slot_order(src_ref, kv_ref)
        dkv_ref[...] = jnp.zeros_like(dkv_ref)
        gate_ref[...] = jnp.zeros_like(gate_ref)
    dot_sum = None
    for at in range(steps):
        cols = slice(at * chunk, (at + 1) * chunk)
        raw = lax.dot_general(grad_ref[...], kv_ref[cols, :], NT, preferred_element_type=f32)
        raw_ref[:, cols] = raw
        part = jnp.sum(raw * prob_ref[0, 0, :, cols].astype(f32), axis=1, keepdims=True)
        dot_sum = part if dot_sum is None else dot_sum + part
    lane = lax.broadcasted_iota(jnp.int32, (rows, LANES), 1)
    scaled = jnp.where(lane == HD, 1.0, q_ref[...].astype(f32) * HD ** (-0.5))
    query_t = jnp.transpose(scaled)[: HD + 16].astype(bf16)
    grad_t = jnp.transpose(grad_ref[...].astype(f32))[HD:].astype(bf16)
    dq = None
    for at in range(steps):
        cols = slice(at * chunk, (at + 1) * chunk)
        prob = prob_ref[0, 0, :, cols]
        grad_score = (prob.astype(f32) * (raw_ref[:, cols] - dot_sum)).astype(bf16)
        piece = jnp.dot(grad_score, kv_ref[cols, :], preferred_element_type=f32)
        dq = piece if dq is None else dq + piece
        keys = jnp.dot(query_t, grad_score, preferred_element_type=f32)
        dkv_ref[:HD, cols] += keys[:HD]
        gate_ref[:, cols] += keys[HD : HD + 8]
        dkv_ref[HD:, cols] += jnp.dot(grad_t, prob, preferred_element_type=f32)
    dq_ref[...] = (dq * HD ** (-0.5)).astype(dq_ref.dtype)
    if last:
        count, height, _ = out_ref.shape
        parts = (height - PAD_ROWS) // LANES
        for at in range(count):
            rows_of = []
            for part in range(parts):
                cols = slice((part * count + at) * LANES, (part * count + at + 1) * LANES)
                out_ref[at, part * LANES : (part + 1) * LANES, :] = jnp.transpose(dkv_ref[:, cols]).astype(bf16)
                rows_of.append(gate_ref[0:1, cols])
            rows_of.append(jnp.zeros((PAD_ROWS - parts, LANES), f32))
            out_ref[at, height - PAD_ROWS :, :] = jnp.concatenate(rows_of, axis=0).astype(bf16)


def attend_back_kernel(parts, chunk, *refs):
    part = pl.program_id(1)
    for at in range(parts):
        pl.when(part == at)(
            functools.partial(attend_back_body, at == 0, at == parts - 1, (at + 1) * chunk // LANES, chunk, *refs)
        )


def attend_back(query, grad, pairs, prob):
    heads, parts, block, slot = prob.shape
    count, height, width = pairs.shape
    chunk = slot // parts
    return pl.pallas_call(
        functools.partial(attend_back_kernel, parts, chunk),
        grid=(heads, parts),
        in_specs=[
            pl.BlockSpec((block, LANES), lambda h, r: (r, h)),
            pl.BlockSpec((block, LANES), lambda h, r: (r, h)),
            pl.BlockSpec((count, height, LANES), lambda h, r: (0, 0, h)),
            pl.BlockSpec((1, 1, block, slot), lambda h, r: (h, r, 0, 0)),
        ],
        out_specs=[
            pl.BlockSpec((block, LANES), lambda h, r: (r, h)),
            pl.BlockSpec((count, height, LANES), lambda h, r: (0, 0, h)),
        ],
        out_shape=[
            jax.ShapeDtypeStruct((parts * block, heads * LANES), jnp.bfloat16),
            jax.ShapeDtypeStruct((count, height, width), jnp.bfloat16),
        ],
        scratch_shapes=[
            pltpu.VMEM((block, slot), jnp.float32),
            pltpu.VMEM((slot, LANES), jnp.bfloat16),
            pltpu.VMEM((LANES, slot), jnp.float32),
            pltpu.VMEM((8, slot), jnp.float32),
        ],
        name="attend_back",
    )(query, grad, pairs, prob)


def dp_gather(mine):
    if lax.axis_size("dp") != 2:
        return lax.all_gather(mine, "dp", axis=0, tiled=True)
    other = lax.ppermute(mine, "dp", [(0, 1), (1, 0)])
    return jnp.where(
        lax.axis_index("dp") == 0, jnp.concatenate([mine, other]), jnp.concatenate([other, mine])
    )


def dp_scatter(parts):
    if lax.axis_size("dp") != 2:
        return lax.psum_scatter(parts, "dp", scatter_dimension=0, tiled=False)
    at = lax.axis_index("dp")
    mine = lax.dynamic_index_in_dim(parts, at, 0, keepdims=False)
    sent = lax.dynamic_index_in_dim(parts, 1 - at, 0, keepdims=False)
    other = lax.ppermute(sent, "dp", [(0, 1), (1, 0)])
    return (mine.astype(jnp.float32) + other.astype(jnp.float32)).astype(parts.dtype)


def per_device(
    tokens,
    cotangent,
    lengths,
    kept_keys,
    first_gain,
    qkv_weight,
    score_weight,
    out_weight,
    second_gain,
    fc_weight,
    proj_weight,
):
    f32, bf16 = jnp.float32, jnp.bfloat16
    dp_count = lax.axis_size("dp")
    seg_count = lax.axis_size("sp")
    ctx_count = lax.axis_size("ctx")
    dp_at = lax.axis_index("dp")
    sp_at = lax.axis_index("sp")
    ctx_at = lax.axis_index("ctx")
    rows = tokens.shape[1]
    width = tokens.shape[2]
    group_rows = seg_count * rows
    heads = H // seg_count
    head_cols = heads * 3 * HD
    hidden = fc_weight.shape[1]
    hidden_part = hidden // (dp_count * seg_count)
    piece = width // (dp_count * ctx_count)

    own_in = jnp.concatenate(
        [
            lax.dynamic_slice_in_dim(qkv_weight, sp_at * head_cols, head_cols, 1),
            lax.dynamic_slice_in_dim(score_weight, sp_at * heads, heads, 1),
            first_gain[:, None],
            second_gain[:, None],
        ],
        axis=1,
    )
    all_in = dp_gather(own_in)
    tokens_group = lax.all_gather(tokens[0], "sp", axis=0, tiled=True)
    in_weight = all_in[:, : head_cols + heads]
    gain_one = all_in[:, head_cols + heads].astype(f32)
    gain_two = all_in[:, head_cols + heads + 1].astype(f32)

    out_own = out_weight
    fc_own = lax.dynamic_index_in_dim(
        fc_weight.reshape(width // dp_count, dp_count, seg_count, hidden_part), sp_at, 2, keepdims=False
    ).reshape(width // dp_count, dp_count * hidden_part)
    proj_own = lax.dynamic_slice_in_dim(proj_weight, sp_at * hidden_part, hidden_part, 0)
    all_in, out_own, fc_own, proj_own = lax.optimization_barrier((all_in, out_own, fc_own, proj_own))

    inputs = tokens[0].astype(f32)
    inputs_group = tokens_group.astype(f32)
    norm_one = layer_norm(inputs_group, gain_one).astype(bf16)
    qkv_rows = jnp.dot(norm_one, in_weight[:, :head_cols], preferred_element_type=f32).astype(bf16)
    key_score = lax.dot_general(
        in_weight[:, head_cols:], norm_one, (((0,), (1,)), ((), ())), preferred_element_type=f32
    ).astype(bf16)
    triple = qkv_rows.reshape(group_rows, heads, 3 * HD)
    score_rows = jnp.transpose(key_score.reshape(heads, seg_count, rows), (1, 0, 2)).reshape(
        seg_count, heads * rows
    )
    pairs_own = jnp.concatenate(
        [
            triple[..., HD:].reshape(group_rows, heads * 2 * HD),
            jnp.pad(score_rows, ((0, PAD_ROWS - seg_count), (0, 0))),
        ],
        axis=0,
    )
    pairs = lax.all_gather(pairs_own, "ctx", axis=0, tiled=False)
    query_wide = jnp.pad(triple[..., :HD], ((0, 0), (0, 0), (0, HD))).reshape(group_rows, heads * LANES)
    kept = jnp.transpose(kept_keys[0], (2, 0, 1, 3))
    base = (ctx_at * rows).astype(jnp.int32)[None]
    head_outs, prob = attend(base, kept, query_wide, pairs)
    attended = jnp.transpose(head_outs, (1, 0, 2)).reshape(group_rows, heads * HD)

    out_all = dp_gather(out_own)
    out_part = lax.dynamic_slice_in_dim(out_all, sp_at * heads * HD, heads * HD, 0)
    fc_part = dp_gather(fc_own)
    proj_part = dp_gather(proj_own)
    cot_group = lax.all_gather(cotangent[0], "sp", axis=0, tiled=True)
    group_at = jnp.arange(group_rows, dtype=jnp.int32)
    group_positions = (group_at // rows) * (ctx_count * rows) + ctx_at * rows + group_at % rows
    grad_out_group = jnp.where((group_positions < lengths[0])[:, None], cot_group, jnp.zeros_like(cot_group))
    positions = (sp_at * ctx_count + ctx_at) * rows + jnp.arange(rows, dtype=jnp.int32)
    is_valid = (positions < lengths[0])[:, None]

    branch = jnp.dot(attended, out_part, preferred_element_type=f32).astype(bf16)
    mixed = inputs + lax.psum_scatter(branch, "sp", scatter_dimension=0, tiled=True).astype(f32)
    norm_two_own = layer_norm(mixed, gain_two).astype(bf16)
    norm_two = lax.all_gather(norm_two_own, "sp", axis=0, tiled=True)
    hidden_pre = jnp.dot(norm_two, fc_part, preferred_element_type=f32)
    active = tanh_gelu(hidden_pre).astype(bf16)
    grad_active = contract_cols(grad_out_group, proj_part)
    _, gelu_pull = jax.vjp(tanh_gelu, hidden_pre)
    grad_pre = gelu_pull(grad_active)[0].astype(bf16)
    grad_norm_two = lax.psum_scatter(
        contract_cols(grad_pre, fc_part).astype(bf16), "sp", scatter_dimension=0, tiled=True
    ).astype(f32)
    _, second_pull = jax.vjp(layer_norm, mixed, gain_two)
    grad_mixed_norm, second_gain_grad = second_pull(grad_norm_two)
    grad_out = jnp.where(is_valid, cotangent[0], jnp.zeros_like(cotangent[0])).astype(f32)
    grad_mixed = grad_out + grad_mixed_norm
    grad_branch = lax.all_gather(grad_mixed.astype(bf16), "sp", axis=0, tiled=True)

    out_wide = jnp.pad(out_part.reshape(heads, HD, width), ((0, 0), (HD, 0), (0, 0))).reshape(heads * LANES, width)
    grad_wide = contract_cols(grad_branch, out_wide).astype(bf16)
    query_grads, pair_grads = attend_back(query_wide, grad_wide, pairs, prob)
    pair_mine = lax.psum_scatter(pair_grads, "ctx", scatter_dimension=0, tiled=False)

    expanded = lax.psum_scatter(
        jnp.dot(active, proj_part, preferred_element_type=f32).astype(bf16), "sp", scatter_dimension=0, tiled=True
    ).astype(f32)
    output = jnp.where(is_valid, mixed + expanded, 0.0).astype(bf16)[None]

    big = jnp.concatenate(
        [
            contract_rows(norm_two, grad_pre).astype(bf16).reshape(dp_count, ctx_count, piece, width),
            contract_rows(active, grad_out_group).astype(bf16).reshape(dp_count, ctx_count, -1, width),
            contract_rows(attended, grad_branch).astype(bf16).reshape(dp_count, ctx_count, -1, width),
        ],
        axis=2,
    )
    big_own = lax.psum_scatter(dp_scatter(big), "ctx", scatter_dimension=0, tiled=False)
    proj_piece = hidden // (seg_count * dp_count * ctx_count)
    both = piece + proj_piece
    out_piece = heads * HD // (dp_count * ctx_count)
    out_rows = dp_gather(big_own[both:])
    big_all = lax.all_gather(jnp.concatenate([big_own[:both], out_rows], axis=0), ("sp", "ctx"), axis=0, tiled=False)
    big_all = big_all.reshape(seg_count, ctx_count, both + dp_count * out_piece, width)
    fc_grad = jnp.transpose(
        big_all[:, :, :piece].reshape(seg_count, ctx_count, piece, dp_count, hidden_part), (1, 2, 3, 0, 4)
    ).reshape(width // dp_count, hidden).astype(f32)
    proj_grad = big_all[:, :, piece:both].reshape(hidden // dp_count, width).astype(f32)
    out_grad = jnp.transpose(
        big_all[:, :, both:].reshape(seg_count, ctx_count, dp_count, out_piece, width), (0, 2, 1, 3, 4)
    ).reshape(width, width)
    out_grad = lax.dynamic_slice_in_dim(out_grad, dp_at * (width // dp_count), width // dp_count, 0).astype(f32)

    grad_triple = jnp.concatenate(
        [
            query_grads.reshape(group_rows, heads, LANES)[..., :HD],
            pair_mine[:group_rows].reshape(group_rows, heads, 2 * HD),
        ],
        axis=-1,
    ).reshape(group_rows, head_cols)
    gate_rows = jnp.transpose(
        pair_mine[group_rows : group_rows + seg_count].reshape(seg_count, heads, rows), (1, 0, 2)
    ).reshape(heads, group_rows)
    grad_score = (gate_rows.astype(f32) * jax.nn.sigmoid(-key_score.astype(f32))).astype(bf16)
    grad_norm_part = contract_cols(grad_triple, in_weight[:, :head_cols]) + lax.dot_general(
        grad_score, in_weight[:, head_cols:], (((0,), (1,)), ((), ())), preferred_element_type=f32
    )
    grad_norm_one = lax.psum_scatter(grad_norm_part.astype(bf16), "sp", scatter_dimension=0, tiled=True).astype(f32)
    _, first_pull = jax.vjp(layer_norm, inputs, gain_one)
    grad_input_norm, first_gain_grad = first_pull(grad_norm_one)
    input_grad = (grad_mixed + grad_input_norm).astype(bf16)[None]

    small = jnp.concatenate(
        [
            contract_rows(norm_one, grad_triple).astype(bf16),
            lax.dot_general(norm_one, grad_score, (((0,), (1,)), ((), ())), preferred_element_type=f32).astype(bf16),
            first_gain_grad.astype(bf16)[:, None],
            second_gain_grad.astype(bf16)[:, None],
        ],
        axis=1,
    ).reshape(dp_count, ctx_count, piece, head_cols + heads + 2)
    small_own = lax.psum_scatter(dp_scatter(small), "ctx", scatter_dimension=0, tiled=False)
    small_all = lax.all_gather(small_own, ("sp", "ctx"), axis=0, tiled=False).reshape(
        seg_count, ctx_count * piece, head_cols + heads + 2
    )
    qkv_grad = jnp.transpose(small_all[:, :, :head_cols], (1, 0, 2)).reshape(-1, seg_count * head_cols).astype(f32)
    score_grad = jnp.transpose(small_all[:, :, head_cols : head_cols + heads], (1, 0, 2)).reshape(-1, H).astype(f32)
    gains = jnp.sum(small_all[:, :, head_cols + heads :].astype(f32), axis=0)
    return (output, input_grad, gains[:, 0], qkv_grad, score_grad, out_grad, gains[:, 1], fc_grad, proj_grad)


def solution(mesh):
    placed = (
        P("dp", ("sp", "ctx"), None),
        P("dp", ("sp", "ctx"), None),
        P("dp"),
        P("dp", None, "ctx", "sp", None),
        P("dp"),
        P("dp", None),
        P("dp", None),
        P("dp", None),
        P("dp"),
        P("dp", None),
        P("dp", None),
    )
    return jax.shard_map(
        per_device,
        mesh=mesh,
        in_specs=placed,
        out_specs=(
            P("dp", ("sp", "ctx"), None),
            P("dp", ("sp", "ctx"), None),
            P("dp"),
            P("dp", None),
            P("dp", None),
            P("dp", None),
            P("dp"),
            P("dp", None),
            P("dp", None),
        ),
        check_vma=False,
    )
```

```python
import functools

import jax
import jax.numpy as jnp
from jax import lax
from jax.experimental import pallas as pl
from jax.experimental.pallas import tpu as pltpu
from jax.sharding import PartitionSpec as P

H = 12
HD = 64
WIN = 64
LANES = 128
SLOT = 2048


EPSILON = 1e-05


def layer_norm(values, gain):
    mean_value = jnp.mean(values, axis=-1, keepdims=True)
    centred = values - mean_value
    variance = jnp.mean(centred * centred, axis=-1, keepdims=True)
    return centred * lax.rsqrt(variance + EPSILON) * gain


def tanh_gelu(values):
    return jax.nn.gelu(values, approximate=True)


def contract_rows(left, right):
    return lax.dot_general(
        left, right, (((0,), (0,)), ((), ())), preferred_element_type=jnp.float32
    )


def contract_cols(left, right):
    return lax.dot_general(
        left, right, (((1,), (1,)), ((), ())), preferred_element_type=jnp.float32
    )


NT = (((1,), (1,)), ((), ()))


PAD_ROWS = 16


def slot_order(src_ref, kv_ref):
    count, height, _ = src_ref.shape
    for tile in range(kv_ref.shape[0] // LANES):
        part, at = divmod(tile, count)
        kv_ref[tile * LANES : (tile + 1) * LANES, :] = src_ref[at, part * LANES : (part + 1) * LANES, :]


def slot_gates(src_ref, gate_ref):
    count, height, _ = src_ref.shape
    for at in range(count):
        scores = src_ref[at, height - PAD_ROWS :, :].astype(jnp.float32)
        gates = -jnp.log1p(jnp.exp(-scores))
        for part in range(gate_ref.shape[1] // LANES // count):
            tile = part * count + at
            gate_ref[:, tile * LANES : (tile + 1) * LANES] = jnp.broadcast_to(gates[part : part + 1, :], (8, LANES))


def attend_body(first, tiles, base, idx_ref, q_ref, src_ref, out_ref, prob_ref, score_ref, pair_ref, kv_ref, gate_ref):
    rows = q_ref.shape[0]
    if first:
        slot_order(src_ref, kv_ref)
        slot_gates(src_ref, gate_ref)
    span = tiles * LANES
    f32, bf16 = jnp.float32, jnp.bfloat16
    score_ref[:, :span] = (
        lax.dot_general(q_ref[...], kv_ref[:span, :], NT, preferred_element_type=f32) * HD ** (-0.5)
        + gate_ref[0:1, :span]
    )
    kept = idx_ref[0, 0]
    pair_ref[...] = jnp.concatenate([kept, kept], axis=1)
    wide = 8 * HD
    sub = lax.broadcasted_iota(jnp.int32, (8, wide), 0)
    lane = lax.broadcasted_iota(jnp.int32, (8, wide), 1)
    own = (lane // HD) == sub
    subf = sub.astype(f32)
    ahead = lax.broadcasted_iota(jnp.int32, (8, LANES), 0) - lax.broadcasted_iota(jnp.int32, (8, LANES), 1)
    near_from = max(0, tiles - 5)

    def eight(start):
        four = pair_ref[pl.ds(start, 8), :]
        index = jnp.concatenate([four] * 4, axis=1)
        pos = base + start + sub
        high = jnp.where(own & (pos >= WIN), index >> 7, -2).astype(f32)
        low = jnp.sum(jnp.where(own, (index & 127).astype(f32), 0.0), axis=0, keepdims=True) - subf
        high_pair = jnp.concatenate([high, high - 1.0], axis=0).astype(bf16)
        low_pair = jnp.concatenate([low, low - 8.0], axis=0).astype(bf16)
        one, zero = jnp.ones((), bf16), jnp.zeros((), bf16)
        left = jnp.concatenate(
            [jnp.where(high_pair == jnp.array(2 * p, bf16), one, zero) for p in range(tiles // 2)], axis=0
        )
        right = jnp.concatenate(
            [jnp.where(low_pair == jnp.array(16 * p, bf16), one, zero) for p in range(8)], axis=0
        )
        count = lax.dot_general(left, right, NT, preferred_element_type=f32)
        gap = ahead + (base + start)
        masked, counts = [], []
        largest = None
        for tile in range(tiles):
            number = count[8 * tile : 8 * tile + 8, :]
            if tile >= near_from:
                far = gap - tile * LANES
                number = number + jnp.where((far >= 0) & (far < WIN), 1.0, 0.0)
            value = jnp.where(number > 0.0, score_ref[pl.ds(start, 8), tile * LANES : (tile + 1) * LANES], -1e30)
            counts.append(number)
            masked.append(value)
            largest = value if largest is None else jnp.maximum(largest, value)
        top = jnp.max(largest, axis=1, keepdims=True)
        total = None
        expos = []
        for number, value in zip(counts, masked):
            expo = jnp.exp(value - top) * number
            expos.append(expo)
            total = expo if total is None else total + expo
        inverse = 1.0 / jnp.sum(total, axis=1, keepdims=True)
        return [expo * inverse for expo in expos]

    def step(index, carry):
        start = pl.multiple_of(index * 16, 16)
        first, second = eight(start), eight(start + 8)
        for tile in range(tiles):
            prob_ref[0, 0, pl.ds(start, 16), tile * LANES : (tile + 1) * LANES] = jnp.concatenate(
                [first[tile], second[tile]], axis=0
            ).astype(bf16)
        return carry

    lax.fori_loop(0, rows // 16, step, 0)
    both = jnp.dot(prob_ref[0, 0, :, :span], kv_ref[:span, :], preferred_element_type=f32)
    out_ref[0] = both[:, HD:].astype(bf16)


def attend_kernel(parts, chunk, base_ref, *refs):
    part = pl.program_id(1)
    base = base_ref[0] + part * chunk
    for at in range(parts):
        pl.when(part == at)(
            functools.partial(attend_body, at == 0, (at + 1) * chunk // LANES, base, *refs)
        )


def attend(base, kept, query, pairs):
    heads, parts, block, keep = kept.shape
    count, height, _ = pairs.shape
    slot = count * (height - PAD_ROWS)
    chunk = slot // parts
    grid_spec = pltpu.PrefetchScalarGridSpec(
        num_scalar_prefetch=1,
        grid=(heads, parts),
        in_specs=[
            pl.BlockSpec((1, 1, block, keep), lambda h, r, b: (h, r, 0, 0)),
            pl.BlockSpec((block, LANES), lambda h, r, b: (r, h)),
            pl.BlockSpec((count, height, LANES), lambda h, r, b: (0, 0, h)),
        ],
        out_specs=[
            pl.BlockSpec((1, block, HD), lambda h, r, b: (h, r, 0)),
            pl.BlockSpec((1, 1, block, slot), lambda h, r, b: (h, r, 0, 0)),
        ],
        scratch_shapes=[
            pltpu.VMEM((block, slot), jnp.float32),
            pltpu.VMEM((block, 2 * keep), jnp.int32),
            pltpu.VMEM((slot, LANES), jnp.bfloat16),
            pltpu.VMEM((8, slot), jnp.float32),
        ],
    )
    return pl.pallas_call(
        functools.partial(attend_kernel, parts, chunk),
        grid_spec=grid_spec,
        out_shape=[
            jax.ShapeDtypeStruct((heads, parts * block, HD), jnp.bfloat16),
            jax.ShapeDtypeStruct((heads, parts, block, slot), jnp.bfloat16),
        ],
        name="attend",
    )(base, kept, query, pairs)


def attend_back_body(first, last, tiles, chunk, q_ref, grad_ref, src_ref, prob_ref, dq_ref, out_ref, raw_ref, kv_ref, dkv_ref, gate_ref):
    f32, bf16 = jnp.float32, jnp.bfloat16
    rows = q_ref.shape[0]
    steps = tiles * LANES // chunk
    if first:
        slot_order(src_ref, kv_ref)
        dkv_ref[...] = jnp.zeros_like(dkv_ref)
        gate_ref[...] = jnp.zeros_like(gate_ref)
    dot_sum = None
    for at in range(steps):
        cols = slice(at * chunk, (at + 1) * chunk)
        raw = lax.dot_general(grad_ref[...], kv_ref[cols, :], NT, preferred_element_type=f32)
        raw_ref[:, cols] = raw
        part = jnp.sum(raw * prob_ref[0, 0, :, cols].astype(f32), axis=1, keepdims=True)
        dot_sum = part if dot_sum is None else dot_sum + part
    lane = lax.broadcasted_iota(jnp.int32, (rows, LANES), 1)
    scaled = jnp.where(lane == HD, 1.0, q_ref[...].astype(f32) * HD ** (-0.5))
    query_t = jnp.transpose(scaled)[: HD + 16].astype(bf16)
    grad_t = jnp.transpose(grad_ref[...].astype(f32))[HD:].astype(bf16)
    dq = None
    for at in range(steps):
        cols = slice(at * chunk, (at + 1) * chunk)
        prob = prob_ref[0, 0, :, cols]
        grad_score = (prob.astype(f32) * (raw_ref[:, cols] - dot_sum)).astype(bf16)
        piece = jnp.dot(grad_score, kv_ref[cols, :], preferred_element_type=f32)
        dq = piece if dq is None else dq + piece
        keys = jnp.dot(query_t, grad_score, preferred_element_type=f32)
        dkv_ref[:HD, cols] += keys[:HD]
        gate_ref[:, cols] += keys[HD : HD + 8]
        dkv_ref[HD:, cols] += jnp.dot(grad_t, prob, preferred_element_type=f32)
    dq_ref[...] = (dq * HD ** (-0.5)).astype(dq_ref.dtype)
    if last:
        count, height, _ = out_ref.shape
        parts = (height - PAD_ROWS) // LANES
        for at in range(count):
            rows_of = []
            for part in range(parts):
                cols = slice((part * count + at) * LANES, (part * count + at + 1) * LANES)
                out_ref[at, part * LANES : (part + 1) * LANES, :] = jnp.transpose(dkv_ref[:, cols]).astype(bf16)
                rows_of.append(gate_ref[0:1, cols])
            rows_of.append(jnp.zeros((PAD_ROWS - parts, LANES), f32))
            out_ref[at, height - PAD_ROWS :, :] = jnp.concatenate(rows_of, axis=0).astype(bf16)


def attend_back_kernel(parts, chunk, *refs):
    part = pl.program_id(1)
    for at in range(parts):
        pl.when(part == at)(
            functools.partial(attend_back_body, at == 0, at == parts - 1, (at + 1) * chunk // LANES, chunk, *refs)
        )


def attend_back(query, grad, pairs, prob):
    heads, parts, block, slot = prob.shape
    count, height, width = pairs.shape
    chunk = slot // parts
    return pl.pallas_call(
        functools.partial(attend_back_kernel, parts, chunk),
        grid=(heads, parts),
        in_specs=[
            pl.BlockSpec((block, LANES), lambda h, r: (r, h)),
            pl.BlockSpec((block, LANES), lambda h, r: (r, h)),
            pl.BlockSpec((count, height, LANES), lambda h, r: (0, 0, h)),
            pl.BlockSpec((1, 1, block, slot), lambda h, r: (h, r, 0, 0)),
        ],
        out_specs=[
            pl.BlockSpec((block, LANES), lambda h, r: (r, h)),
            pl.BlockSpec((count, height, LANES), lambda h, r: (0, 0, h)),
        ],
        out_shape=[
            jax.ShapeDtypeStruct((parts * block, heads * LANES), jnp.bfloat16),
            jax.ShapeDtypeStruct((count, height, width), jnp.bfloat16),
        ],
        scratch_shapes=[
            pltpu.VMEM((block, slot), jnp.float32),
            pltpu.VMEM((slot, LANES), jnp.bfloat16),
            pltpu.VMEM((LANES, slot), jnp.float32),
            pltpu.VMEM((8, slot), jnp.float32),
        ],
        name="attend_back",
    )(query, grad, pairs, prob)


def dp_gather(mine):
    if lax.axis_size("dp") != 2:
        return lax.all_gather(mine, "dp", axis=0, tiled=True)
    other = lax.ppermute(mine, "dp", [(0, 1), (1, 0)])
    return jnp.where(
        lax.axis_index("dp") == 0, jnp.concatenate([mine, other]), jnp.concatenate([other, mine])
    )


def dp_scatter(parts):
    if lax.axis_size("dp") != 2:
        return lax.psum_scatter(parts, "dp", scatter_dimension=0, tiled=False)
    at = lax.axis_index("dp")
    mine = lax.dynamic_index_in_dim(parts, at, 0, keepdims=False)
    sent = lax.dynamic_index_in_dim(parts, 1 - at, 0, keepdims=False)
    other = lax.ppermute(sent, "dp", [(0, 1), (1, 0)])
    return (mine.astype(jnp.float32) + other.astype(jnp.float32)).astype(parts.dtype)


def exchange_sum(parts, axis):
    came = lax.all_to_all(parts, axis, split_axis=0, concat_axis=0, tiled=True)
    return jnp.sum(came.astype(jnp.float32), axis=0)


def per_device(
    tokens,
    cotangent,
    lengths,
    kept_keys,
    first_gain,
    qkv_weight,
    score_weight,
    out_weight,
    second_gain,
    fc_weight,
    proj_weight,
):
    f32, bf16 = jnp.float32, jnp.bfloat16
    dp_count = lax.axis_size("dp")
    seg_count = lax.axis_size("sp")
    ctx_count = lax.axis_size("ctx")
    dp_at = lax.axis_index("dp")
    sp_at = lax.axis_index("sp")
    ctx_at = lax.axis_index("ctx")
    rows = tokens.shape[1]
    width = tokens.shape[2]
    group_rows = seg_count * rows
    heads = H // seg_count
    head_cols = heads * 3 * HD
    hidden = fc_weight.shape[1]
    hidden_part = hidden // (dp_count * seg_count)
    piece = width // (dp_count * ctx_count)

    own_in = jnp.concatenate(
        [
            lax.dynamic_slice_in_dim(qkv_weight, sp_at * head_cols, head_cols, 1),
            lax.dynamic_slice_in_dim(score_weight, sp_at * heads, heads, 1),
            first_gain[:, None],
            second_gain[:, None],
        ],
        axis=1,
    )
    all_in = dp_gather(own_in)
    tokens_group = lax.all_gather(tokens[0], "sp", axis=0, tiled=True)
    in_weight = all_in[:, : head_cols + heads]
    gain_one = all_in[:, head_cols + heads].astype(f32)
    gain_two = all_in[:, head_cols + heads + 1].astype(f32)

    out_own = out_weight
    fc_own = lax.dynamic_index_in_dim(
        fc_weight.reshape(width // dp_count, dp_count, seg_count, hidden_part), sp_at, 2, keepdims=False
    ).reshape(width // dp_count, dp_count * hidden_part)
    proj_own = lax.dynamic_slice_in_dim(proj_weight, sp_at * hidden_part, hidden_part, 0)
    all_in, out_own, fc_own, proj_own = lax.optimization_barrier((all_in, out_own, fc_own, proj_own))

    inputs = tokens[0].astype(f32)
    inputs_group = tokens_group.astype(f32)
    norm_one = layer_norm(inputs_group, gain_one).astype(bf16)
    qkv_rows = jnp.dot(norm_one, in_weight[:, :head_cols], preferred_element_type=f32).astype(bf16)
    key_score = lax.dot_general(
        in_weight[:, head_cols:], norm_one, (((0,), (1,)), ((), ())), preferred_element_type=f32
    ).astype(bf16)
    triple = qkv_rows.reshape(group_rows, heads, 3 * HD)
    score_rows = jnp.transpose(key_score.reshape(heads, seg_count, rows), (1, 0, 2)).reshape(
        seg_count, heads * rows
    )
    pairs_own = jnp.concatenate(
        [
            triple[..., HD:].reshape(group_rows, heads * 2 * HD),
            jnp.pad(score_rows, ((0, PAD_ROWS - seg_count), (0, 0))),
        ],
        axis=0,
    )
    pairs = lax.all_gather(pairs_own, "ctx", axis=0, tiled=False)
    query_wide = jnp.pad(triple[..., :HD], ((0, 0), (0, 0), (0, HD))).reshape(group_rows, heads * LANES)
    kept = jnp.transpose(kept_keys[0], (2, 0, 1, 3))
    base = (ctx_at * rows).astype(jnp.int32)[None]
    head_outs, prob = attend(base, kept, query_wide, pairs)
    attended = jnp.transpose(head_outs, (1, 0, 2)).reshape(group_rows, heads * HD)

    out_all = dp_gather(out_own)
    out_part = lax.dynamic_slice_in_dim(out_all, sp_at * heads * HD, heads * HD, 0)
    fc_part = dp_gather(fc_own)
    proj_part = dp_gather(proj_own)
    cot_group = lax.all_gather(cotangent[0], "sp", axis=0, tiled=True)
    group_at = jnp.arange(group_rows, dtype=jnp.int32)
    group_positions = (group_at // rows) * (ctx_count * rows) + ctx_at * rows + group_at % rows
    grad_out_group = jnp.where((group_positions < lengths[0])[:, None], cot_group, jnp.zeros_like(cot_group))
    positions = (sp_at * ctx_count + ctx_at) * rows + jnp.arange(rows, dtype=jnp.int32)
    is_valid = (positions < lengths[0])[:, None]

    branch = jnp.dot(attended, out_part, preferred_element_type=f32).astype(bf16)
    mixed = inputs + exchange_sum(branch.reshape(seg_count, rows, width), "sp")
    norm_two_own = layer_norm(mixed, gain_two).astype(bf16)
    norm_two = lax.all_gather(norm_two_own, "sp", axis=0, tiled=True)
    hidden_pre = jnp.dot(norm_two, fc_part, preferred_element_type=f32)
    active = tanh_gelu(hidden_pre).astype(bf16)
    grad_active = contract_cols(grad_out_group, proj_part)
    _, gelu_pull = jax.vjp(tanh_gelu, hidden_pre)
    grad_pre = gelu_pull(grad_active)[0].astype(bf16)
    fc_parts = jnp.transpose(
        contract_rows(norm_two, grad_pre).astype(bf16).reshape(dp_count, ctx_count, piece, width), (1, 0, 2, 3)
    )
    proj_parts = contract_rows(active, grad_out_group).astype(bf16).reshape(dp_count, ctx_count, -1, width)
    grad_norm_parts, fc_parts, proj_parts = lax.optimization_barrier(
        (contract_cols(grad_pre, fc_part).astype(bf16), fc_parts, proj_parts)
    )
    fc_ctx = lax.psum_scatter(fc_parts, "ctx", scatter_dimension=0, tiled=False)
    proj_dp = dp_scatter(proj_parts)
    grad_norm_two = exchange_sum(grad_norm_parts.reshape(seg_count, rows, width), "sp")
    _, second_pull = jax.vjp(layer_norm, mixed, gain_two)
    grad_mixed_norm, second_gain_grad = second_pull(grad_norm_two)
    grad_out = jnp.where(is_valid, cotangent[0], jnp.zeros_like(cotangent[0])).astype(f32)
    grad_mixed = grad_out + grad_mixed_norm
    grad_branch = lax.all_gather(grad_mixed.astype(bf16), "sp", axis=0, tiled=True)

    out_wide = jnp.pad(out_part.reshape(heads, HD, width), ((0, 0), (HD, 0), (0, 0))).reshape(heads * LANES, width)
    grad_wide = contract_cols(grad_branch, out_wide).astype(bf16)
    grad_wide, proj_dp = lax.optimization_barrier((grad_wide, proj_dp))
    proj_own = lax.psum_scatter(proj_dp, "ctx", scatter_dimension=0, tiled=False)
    query_grads, pair_grads = attend_back(query_wide, grad_wide, pairs, prob)
    pair_mine = lax.psum_scatter(pair_grads, "ctx", scatter_dimension=0, tiled=False)

    fc_ctx, active_late, attended_late, _ = lax.optimization_barrier((fc_ctx, active, attended, query_grads))
    fc_own = dp_scatter(fc_ctx)
    out_dp = dp_scatter(
        contract_rows(attended_late, grad_branch).astype(bf16).reshape(dp_count, ctx_count, -1, width)
    )
    out_rows = dp_gather(exchange_sum(out_dp, "ctx").astype(bf16))
    expanded = exchange_sum(
        jnp.dot(active_late, proj_part, preferred_element_type=f32).astype(bf16).reshape(seg_count, rows, width), "sp"
    )
    output = jnp.where(is_valid, mixed + expanded, 0.0).astype(bf16)[None]
    proj_piece = hidden // (seg_count * dp_count * ctx_count)
    both = piece + proj_piece
    out_piece = heads * HD // (dp_count * ctx_count)
    big_all = lax.all_gather(
        jnp.concatenate([fc_own, proj_own, out_rows], axis=0), ("sp", "ctx"), axis=0, tiled=False
    ).reshape(seg_count, ctx_count, both + dp_count * out_piece, width)
    fc_grad = jnp.transpose(
        big_all[:, :, :piece].reshape(seg_count, ctx_count, piece, dp_count, hidden_part), (1, 2, 3, 0, 4)
    ).reshape(width // dp_count, hidden).astype(f32)
    proj_grad = big_all[:, :, piece:both].reshape(hidden // dp_count, width).astype(f32)
    out_grad = jnp.transpose(
        big_all[:, :, both:].reshape(seg_count, ctx_count, dp_count, out_piece, width), (0, 2, 1, 3, 4)
    ).reshape(width, width)
    out_grad = lax.dynamic_slice_in_dim(out_grad, dp_at * (width // dp_count), width // dp_count, 0).astype(f32)

    grad_triple = jnp.concatenate(
        [
            query_grads.reshape(group_rows, heads, LANES)[..., :HD],
            pair_mine[:group_rows].reshape(group_rows, heads, 2 * HD),
        ],
        axis=-1,
    ).reshape(group_rows, head_cols)
    gate_rows = jnp.transpose(
        pair_mine[group_rows : group_rows + seg_count].reshape(seg_count, heads, rows), (1, 0, 2)
    ).reshape(heads, group_rows)
    grad_score = (gate_rows.astype(f32) * jax.nn.sigmoid(-key_score.astype(f32))).astype(bf16)
    grad_norm_part = contract_cols(grad_triple, in_weight[:, :head_cols]) + lax.dot_general(
        grad_score, in_weight[:, head_cols:], (((0,), (1,)), ((), ())), preferred_element_type=f32
    )
    _, gain_pull = jax.vjp(lambda gain: layer_norm(inputs_group, gain), gain_one)
    first_gain_grad = gain_pull(grad_norm_part)[0]
    grad_norm_one = exchange_sum(grad_norm_part.astype(bf16).reshape(seg_count, rows, width), "sp")
    _, first_pull = jax.vjp(lambda values: layer_norm(values, gain_one), inputs)
    grad_input_norm = first_pull(grad_norm_one)[0]
    input_grad = (grad_mixed + grad_input_norm).astype(bf16)[None]

    small = jnp.concatenate(
        [
            contract_rows(norm_one, grad_triple).astype(bf16),
            lax.dot_general(norm_one, grad_score, (((0,), (1,)), ((), ())), preferred_element_type=f32).astype(bf16),
            first_gain_grad.astype(bf16)[:, None],
            second_gain_grad.astype(bf16)[:, None],
        ],
        axis=1,
    ).reshape(dp_count, ctx_count, piece, head_cols + heads + 2)
    small_own = exchange_sum(dp_scatter(small), "ctx").astype(bf16)
    small_all = lax.all_gather(small_own, ("sp", "ctx"), axis=0, tiled=False).reshape(
        seg_count, ctx_count * piece, head_cols + heads + 2
    )
    qkv_grad = jnp.transpose(small_all[:, :, :head_cols], (1, 0, 2)).reshape(-1, seg_count * head_cols).astype(f32)
    score_grad = jnp.transpose(small_all[:, :, head_cols : head_cols + heads], (1, 0, 2)).reshape(-1, H).astype(f32)
    gains = jnp.sum(small_all[:, :, head_cols + heads :].astype(f32), axis=0)
    return (output, input_grad, gains[:, 0], qkv_grad, score_grad, out_grad, gains[:, 1], fc_grad, proj_grad)


def solution(mesh):
    placed = (
        P("dp", ("sp", "ctx"), None),
        P("dp", ("sp", "ctx"), None),
        P("dp"),
        P("dp", None, "ctx", "sp", None),
        P("dp"),
        P("dp", None),
        P("dp", None),
        P("dp", None),
        P("dp"),
        P("dp", None),
        P("dp", None),
    )
    return jax.shard_map(
        per_device,
        mesh=mesh,
        in_specs=placed,
        out_specs=(
            P("dp", ("sp", "ctx"), None),
            P("dp", ("sp", "ctx"), None),
            P("dp"),
            P("dp", None),
            P("dp", None),
            P("dp", None),
            P("dp"),
            P("dp", None),
            P("dp", None),
        ),
        check_vma=False,
    )
```

```python
import functools

import jax
import jax.numpy as jnp
from jax import lax
from jax.experimental import pallas as pl
from jax.experimental.pallas import tpu as pltpu
from jax.sharding import PartitionSpec as P

H = 12
HD = 64
WIN = 64
LANES = 128
SLOT = 2048


EPSILON = 1e-05


def layer_norm(values, gain):
    mean_value = jnp.mean(values, axis=-1, keepdims=True)
    centred = values - mean_value
    variance = jnp.mean(centred * centred, axis=-1, keepdims=True)
    return centred * lax.rsqrt(variance + EPSILON) * gain


def tanh_gelu(values):
    return jax.nn.gelu(values, approximate=True)


def contract_rows(left, right):
    return lax.dot_general(
        left, right, (((0,), (0,)), ((), ())), preferred_element_type=jnp.float32
    )


def contract_cols(left, right):
    return lax.dot_general(
        left, right, (((1,), (1,)), ((), ())), preferred_element_type=jnp.float32
    )


NT = (((1,), (1,)), ((), ()))


PAD_ROWS = 16


def slot_order(src_ref, kv_ref):
    count, height, _ = src_ref.shape
    for tile in range(kv_ref.shape[0] // LANES):
        part, at = divmod(tile, count)
        kv_ref[tile * LANES : (tile + 1) * LANES, :] = src_ref[at, part * LANES : (part + 1) * LANES, :]


def slot_gates(src_ref, gate_ref):
    count, height, _ = src_ref.shape
    for at in range(count):
        scores = src_ref[at, height - PAD_ROWS :, :].astype(jnp.float32)
        gates = -jnp.log1p(jnp.exp(-scores))
        for part in range(gate_ref.shape[1] // LANES // count):
            tile = part * count + at
            gate_ref[:, tile * LANES : (tile + 1) * LANES] = jnp.broadcast_to(gates[part : part + 1, :], (8, LANES))


def attend_body(first, tiles, base, idx_ref, q_ref, src_ref, out_ref, prob_ref, score_ref, pair_ref, kv_ref, gate_ref):
    rows = q_ref.shape[0]
    if first:
        slot_order(src_ref, kv_ref)
        slot_gates(src_ref, gate_ref)
    span = tiles * LANES
    f32, bf16 = jnp.float32, jnp.bfloat16
    score_ref[:, :span] = (
        lax.dot_general(q_ref[...], kv_ref[:span, :], NT, preferred_element_type=f32) * HD ** (-0.5)
        + gate_ref[0:1, :span]
    )
    kept = idx_ref[0, 0]
    pair_ref[...] = jnp.concatenate([kept, kept], axis=1)
    wide = 8 * HD
    sub = lax.broadcasted_iota(jnp.int32, (8, wide), 0)
    lane = lax.broadcasted_iota(jnp.int32, (8, wide), 1)
    own = (lane // HD) == sub
    subf = sub.astype(f32)
    ahead = lax.broadcasted_iota(jnp.int32, (8, LANES), 0) - lax.broadcasted_iota(jnp.int32, (8, LANES), 1)
    near_from = max(0, tiles - 5)

    def eight(start):
        four = pair_ref[pl.ds(start, 8), :]
        index = jnp.concatenate([four] * 4, axis=1)
        pos = base + start + sub
        high = jnp.where(own & (pos >= WIN), index >> 7, -2).astype(f32)
        low = jnp.sum(jnp.where(own, (index & 127).astype(f32), 0.0), axis=0, keepdims=True) - subf
        high_pair = jnp.concatenate([high, high - 1.0], axis=0).astype(bf16)
        low_pair = jnp.concatenate([low, low - 8.0], axis=0).astype(bf16)
        one, zero = jnp.ones((), bf16), jnp.zeros((), bf16)
        left = jnp.concatenate(
            [jnp.where(high_pair == jnp.array(2 * p, bf16), one, zero) for p in range(tiles // 2)], axis=0
        )
        right = jnp.concatenate(
            [jnp.where(low_pair == jnp.array(16 * p, bf16), one, zero) for p in range(8)], axis=0
        )
        count = lax.dot_general(left, right, NT, preferred_element_type=f32)
        gap = ahead + (base + start)
        masked, counts = [], []
        largest = None
        for tile in range(tiles):
            number = count[8 * tile : 8 * tile + 8, :]
            if tile >= near_from:
                far = gap - tile * LANES
                number = number + jnp.where((far >= 0) & (far < WIN), 1.0, 0.0)
            value = jnp.where(number > 0.0, score_ref[pl.ds(start, 8), tile * LANES : (tile + 1) * LANES], -1e30)
            counts.append(number)
            masked.append(value)
            largest = value if largest is None else jnp.maximum(largest, value)
        top = jnp.max(largest, axis=1, keepdims=True)
        total = None
        expos = []
        for number, value in zip(counts, masked):
            expo = jnp.exp(value - top) * number
            expos.append(expo)
            total = expo if total is None else total + expo
        inverse = 1.0 / jnp.sum(total, axis=1, keepdims=True)
        return [expo * inverse for expo in expos]

    def step(index, carry):
        start = pl.multiple_of(index * 16, 16)
        first, second = eight(start), eight(start + 8)
        for tile in range(tiles):
            prob_ref[0, 0, pl.ds(start, 16), tile * LANES : (tile + 1) * LANES] = jnp.concatenate(
                [first[tile], second[tile]], axis=0
            ).astype(bf16)
        return carry

    lax.fori_loop(0, rows // 16, step, 0)
    both = jnp.dot(prob_ref[0, 0, :, :span], kv_ref[:span, :], preferred_element_type=f32)
    out_ref[0] = both[:, HD:].astype(bf16)


def attend_kernel(parts, chunk, base_ref, *refs):
    part = pl.program_id(1)
    base = base_ref[0] + part * chunk
    for at in range(parts):
        pl.when(part == at)(
            functools.partial(attend_body, at == 0, (at + 1) * chunk // LANES, base, *refs)
        )


def attend(base, kept, query, pairs):
    heads, parts, block, keep = kept.shape
    count, height, _ = pairs.shape
    slot = count * (height - PAD_ROWS)
    chunk = slot // parts
    grid_spec = pltpu.PrefetchScalarGridSpec(
        num_scalar_prefetch=1,
        grid=(heads, parts),
        in_specs=[
            pl.BlockSpec((1, 1, block, keep), lambda h, r, b: (h, r, 0, 0)),
            pl.BlockSpec((block, LANES), lambda h, r, b: (r, h)),
            pl.BlockSpec((count, height, LANES), lambda h, r, b: (0, 0, h)),
        ],
        out_specs=[
            pl.BlockSpec((1, block, HD), lambda h, r, b: (h, r, 0)),
            pl.BlockSpec((1, 1, block, slot), lambda h, r, b: (h, r, 0, 0)),
        ],
        scratch_shapes=[
            pltpu.VMEM((block, slot), jnp.float32),
            pltpu.VMEM((block, 2 * keep), jnp.int32),
            pltpu.VMEM((slot, LANES), jnp.bfloat16),
            pltpu.VMEM((8, slot), jnp.float32),
        ],
    )
    return pl.pallas_call(
        functools.partial(attend_kernel, parts, chunk),
        grid_spec=grid_spec,
        out_shape=[
            jax.ShapeDtypeStruct((heads, parts * block, HD), jnp.bfloat16),
            jax.ShapeDtypeStruct((heads, parts, block, slot), jnp.bfloat16),
        ],
        name="attend",
    )(base, kept, query, pairs)


def attend_back_body(first, last, tiles, chunk, q_ref, grad_ref, src_ref, prob_ref, dq_ref, out_ref, raw_ref, kv_ref, dkv_ref, gate_ref):
    f32, bf16 = jnp.float32, jnp.bfloat16
    rows = q_ref.shape[0]
    steps = tiles * LANES // chunk
    if first:
        slot_order(src_ref, kv_ref)
        dkv_ref[...] = jnp.zeros_like(dkv_ref)
        gate_ref[...] = jnp.zeros_like(gate_ref)
    dot_sum = None
    for at in range(steps):
        cols = slice(at * chunk, (at + 1) * chunk)
        raw = lax.dot_general(grad_ref[...], kv_ref[cols, :], NT, preferred_element_type=f32)
        raw_ref[:, cols] = raw
        part = jnp.sum(raw * prob_ref[0, 0, :, cols].astype(f32), axis=1, keepdims=True)
        dot_sum = part if dot_sum is None else dot_sum + part
    lane = lax.broadcasted_iota(jnp.int32, (rows, LANES), 1)
    scaled = jnp.where(lane == HD, 1.0, q_ref[...].astype(f32) * HD ** (-0.5))
    query_t = jnp.transpose(scaled)[: HD + 16].astype(bf16)
    grad_t = jnp.transpose(grad_ref[...].astype(f32))[HD:].astype(bf16)
    dq = None
    for at in range(steps):
        cols = slice(at * chunk, (at + 1) * chunk)
        prob = prob_ref[0, 0, :, cols]
        grad_score = (prob.astype(f32) * (raw_ref[:, cols] - dot_sum)).astype(bf16)
        piece = jnp.dot(grad_score, kv_ref[cols, :], preferred_element_type=f32)
        dq = piece if dq is None else dq + piece
        keys = jnp.dot(query_t, grad_score, preferred_element_type=f32)
        dkv_ref[:HD, cols] += keys[:HD]
        gate_ref[:, cols] += keys[HD : HD + 8]
        dkv_ref[HD:, cols] += jnp.dot(grad_t, prob, preferred_element_type=f32)
    dq_ref[...] = (dq * HD ** (-0.5)).astype(dq_ref.dtype)
    if last:
        count, height, _ = out_ref.shape
        parts = (height - PAD_ROWS) // LANES
        for at in range(count):
            rows_of = []
            for part in range(parts):
                cols = slice((part * count + at) * LANES, (part * count + at + 1) * LANES)
                out_ref[at, part * LANES : (part + 1) * LANES, :] = jnp.transpose(dkv_ref[:, cols]).astype(bf16)
                rows_of.append(gate_ref[0:1, cols])
            rows_of.append(jnp.zeros((PAD_ROWS - parts, LANES), f32))
            out_ref[at, height - PAD_ROWS :, :] = jnp.concatenate(rows_of, axis=0).astype(bf16)


def attend_back_kernel(parts, chunk, *refs):
    part = pl.program_id(1)
    for at in range(parts):
        pl.when(part == at)(
            functools.partial(attend_back_body, at == 0, at == parts - 1, (at + 1) * chunk // LANES, chunk, *refs)
        )


def attend_back(query, grad, pairs, prob):
    heads, parts, block, slot = prob.shape
    count, height, width = pairs.shape
    chunk = slot // parts
    return pl.pallas_call(
        functools.partial(attend_back_kernel, parts, chunk),
        grid=(heads, parts),
        in_specs=[
            pl.BlockSpec((block, LANES), lambda h, r: (r, h)),
            pl.BlockSpec((block, LANES), lambda h, r: (r, h)),
            pl.BlockSpec((count, height, LANES), lambda h, r: (0, 0, h)),
            pl.BlockSpec((1, 1, block, slot), lambda h, r: (h, r, 0, 0)),
        ],
        out_specs=[
            pl.BlockSpec((block, LANES), lambda h, r: (r, h)),
            pl.BlockSpec((count, height, LANES), lambda h, r: (0, 0, h)),
        ],
        out_shape=[
            jax.ShapeDtypeStruct((parts * block, heads * LANES), jnp.bfloat16),
            jax.ShapeDtypeStruct((count, height, width), jnp.bfloat16),
        ],
        scratch_shapes=[
            pltpu.VMEM((block, slot), jnp.float32),
            pltpu.VMEM((slot, LANES), jnp.bfloat16),
            pltpu.VMEM((LANES, slot), jnp.float32),
            pltpu.VMEM((8, slot), jnp.float32),
        ],
        name="attend_back",
    )(query, grad, pairs, prob)


def dp_gather(mine):
    if lax.axis_size("dp") != 2:
        return lax.all_gather(mine, "dp", axis=0, tiled=True)
    other = lax.ppermute(mine, "dp", [(0, 1), (1, 0)])
    return jnp.where(
        lax.axis_index("dp") == 0, jnp.concatenate([mine, other]), jnp.concatenate([other, mine])
    )


def dp_scatter(parts):
    if lax.axis_size("dp") != 2:
        return lax.psum_scatter(parts, "dp", scatter_dimension=0, tiled=False)
    at = lax.axis_index("dp")
    mine = lax.dynamic_index_in_dim(parts, at, 0, keepdims=False)
    sent = lax.dynamic_index_in_dim(parts, 1 - at, 0, keepdims=False)
    other = lax.ppermute(sent, "dp", [(0, 1), (1, 0)])
    return (mine.astype(jnp.float32) + other.astype(jnp.float32)).astype(parts.dtype)


def group_rows_of(mine, group, count):
    height = mine.shape[0]
    if lax.axis_size("dp") != 2 or height % count != 0:
        whole = lax.all_gather(mine, "dp", axis=0, tiled=True)
        return lax.dynamic_slice_in_dim(whole, group * count, count, 0)
    near = lax.dynamic_slice_in_dim(mine, group * count % height, count, 0)
    far = lax.ppermute(near, "dp", [(0, 1), (1, 0)])
    return jnp.where(lax.axis_index("dp") == group * count // height, near, far)


def dp_sum(mine):
    if lax.axis_size("dp") != 2:
        return lax.psum(mine, "dp")
    other = lax.ppermute(mine, "dp", [(0, 1), (1, 0)])
    return (mine.astype(jnp.float32) + other.astype(jnp.float32)).astype(mine.dtype)


def exchange_sum(parts, axis):
    came = lax.all_to_all(parts, axis, split_axis=0, concat_axis=0, tiled=True)
    return jnp.sum(came.astype(jnp.float32), axis=0)


def per_device(
    tokens,
    cotangent,
    lengths,
    kept_keys,
    first_gain,
    qkv_weight,
    score_weight,
    out_weight,
    second_gain,
    fc_weight,
    proj_weight,
):
    f32, bf16 = jnp.float32, jnp.bfloat16
    dp_count = lax.axis_size("dp")
    seg_count = lax.axis_size("sp")
    ctx_count = lax.axis_size("ctx")
    dp_at = lax.axis_index("dp")
    sp_at = lax.axis_index("sp")
    ctx_at = lax.axis_index("ctx")
    rows = tokens.shape[1]
    width = tokens.shape[2]
    group_rows = seg_count * rows
    heads = H // seg_count
    head_cols = heads * 3 * HD
    hidden = fc_weight.shape[1]
    hidden_part = hidden // (dp_count * seg_count)
    piece = width // (dp_count * ctx_count)

    own_in = jnp.concatenate(
        [
            lax.dynamic_slice_in_dim(qkv_weight, sp_at * head_cols, head_cols, 1),
            lax.dynamic_slice_in_dim(score_weight, sp_at * heads, heads, 1),
            first_gain[:, None],
            second_gain[:, None],
        ],
        axis=1,
    )
    all_in = dp_gather(own_in)
    tokens_group = lax.all_gather(tokens[0], "sp", axis=0, tiled=True)
    in_weight = all_in[:, : head_cols + heads]
    gain_one = all_in[:, head_cols + heads].astype(f32)
    gain_two = all_in[:, head_cols + heads + 1].astype(f32)

    fc_own = jnp.concatenate(
        [
            lax.dynamic_slice_in_dim(fc_weight, (at * seg_count + sp_at) * hidden_part, hidden_part, 1)
            for at in range(dp_count)
        ],
        axis=1,
    )
    proj_own = lax.dynamic_slice_in_dim(proj_weight, sp_at * hidden_part, hidden_part, 0)
    all_in, out_own, fc_own, proj_own = lax.optimization_barrier((all_in, out_weight, fc_own, proj_own))
    out_part = group_rows_of(out_own, sp_at, heads * HD)
    fc_part = dp_gather(fc_own)
    proj_part = dp_gather(proj_own)

    inputs = tokens[0].astype(f32)
    inputs_group = tokens_group.astype(f32)
    norm_one = layer_norm(inputs_group, gain_one).astype(bf16)
    qkv_rows = jnp.dot(norm_one, in_weight[:, :head_cols], preferred_element_type=f32).astype(bf16)
    key_score = lax.dot_general(
        in_weight[:, head_cols:], norm_one, (((0,), (1,)), ((), ())), preferred_element_type=f32
    ).astype(bf16)
    triple = qkv_rows.reshape(group_rows, heads, 3 * HD)
    score_rows = jnp.transpose(key_score.reshape(heads, seg_count, rows), (1, 0, 2)).reshape(
        seg_count, heads * rows
    )
    pairs_own = jnp.concatenate(
        [
            triple[..., HD:].reshape(group_rows, heads * 2 * HD),
            jnp.pad(score_rows, ((0, PAD_ROWS - seg_count), (0, 0))),
        ],
        axis=0,
    )
    cot_own, pairs_own = lax.optimization_barrier((cotangent[0], pairs_own))
    cot_group = lax.all_gather(cot_own, "sp", axis=0, tiled=True)
    pairs = lax.all_gather(pairs_own, "ctx", axis=0, tiled=False)
    query_wide = jnp.pad(triple[..., :HD], ((0, 0), (0, 0), (0, HD))).reshape(group_rows, heads * LANES)
    kept = jnp.transpose(kept_keys[0], (2, 0, 1, 3))
    base = (ctx_at * rows).astype(jnp.int32)[None]
    query_wide, cot_group, out_part, fc_part, proj_part = lax.optimization_barrier(
        (query_wide, cot_group, out_part, fc_part, proj_part)
    )
    head_outs, prob = attend(base, kept, query_wide, pairs)
    attended = jnp.transpose(head_outs, (1, 0, 2)).reshape(group_rows, heads * HD)

    group_at = jnp.arange(group_rows, dtype=jnp.int32)
    group_positions = (group_at // rows) * (ctx_count * rows) + ctx_at * rows + group_at % rows
    grad_out_group = jnp.where((group_positions < lengths[0])[:, None], cot_group, jnp.zeros_like(cot_group))
    positions = (sp_at * ctx_count + ctx_at) * rows + jnp.arange(rows, dtype=jnp.int32)
    is_valid = (positions < lengths[0])[:, None]

    branch = jnp.dot(attended, out_part, preferred_element_type=f32).astype(bf16)
    mixed = inputs + exchange_sum(branch.reshape(seg_count, rows, width), "sp")
    norm_two_own = layer_norm(mixed, gain_two).astype(bf16)
    norm_two = lax.all_gather(norm_two_own, "sp", axis=0, tiled=True)
    hidden_pre = jnp.dot(norm_two, fc_part, preferred_element_type=f32)
    active = tanh_gelu(hidden_pre).astype(bf16)
    grad_active = contract_cols(grad_out_group, proj_part)
    _, gelu_pull = jax.vjp(tanh_gelu, hidden_pre)
    grad_pre = gelu_pull(grad_active)[0].astype(bf16)
    fc_parts = contract_rows(norm_two, grad_pre).astype(bf16).reshape(dp_count, ctx_count, piece, width)
    proj_parts = contract_rows(active, grad_out_group).astype(bf16).reshape(dp_count, ctx_count, -1, width)
    grad_norm_parts, fc_parts, proj_parts = lax.optimization_barrier(
        (contract_cols(grad_pre, fc_part).astype(bf16), fc_parts, proj_parts)
    )
    fc_dp = dp_scatter(fc_parts)
    proj_dp = dp_scatter(proj_parts)
    grad_norm_two = exchange_sum(grad_norm_parts.reshape(seg_count, rows, width), "sp")
    _, second_pull = jax.vjp(layer_norm, mixed, gain_two)
    grad_mixed_norm, second_gain_grad = second_pull(grad_norm_two)
    grad_out = jnp.where(is_valid, cotangent[0], jnp.zeros_like(cotangent[0])).astype(f32)
    grad_mixed = grad_out + grad_mixed_norm
    grad_branch = lax.all_gather(grad_mixed.astype(bf16), "sp", axis=0, tiled=True)

    out_wide = jnp.pad(out_part.reshape(heads, HD, width), ((0, 0), (HD, 0), (0, 0))).reshape(heads * LANES, width)
    grad_wide = contract_cols(grad_branch, out_wide).astype(bf16)
    out_sum = dp_sum(contract_rows(attended, grad_branch).astype(bf16))
    grad_wide, fc_dp = lax.optimization_barrier((grad_wide, fc_dp))
    fc_own = exchange_sum(fc_dp, "ctx").astype(bf16)
    query_grads, pair_grads = attend_back(query_wide, grad_wide, pairs, prob)
    pair_mine = lax.psum_scatter(pair_grads, "ctx", scatter_dimension=0, tiled=False)
    proj_own = exchange_sum(proj_dp, "ctx").astype(bf16)
    out_own = exchange_sum(out_sum.reshape(ctx_count, -1, width), "ctx").astype(bf16)

    active_late, _ = lax.optimization_barrier((active, query_grads))
    expanded = exchange_sum(
        jnp.dot(active_late, proj_part, preferred_element_type=f32).astype(bf16).reshape(seg_count, rows, width), "sp"
    )
    output = jnp.where(is_valid, mixed + expanded, 0.0).astype(bf16)[None]
    big = jnp.concatenate([fc_own, proj_own, out_own], axis=0)
    pair_mine, big, output = lax.optimization_barrier((pair_mine, big, output))
    big_all = lax.all_gather(big, ("sp", "ctx"), axis=0, tiled=False).reshape(seg_count, ctx_count, -1, width)
    proj_piece = hidden // (seg_count * dp_count * ctx_count)
    both = piece + proj_piece

    grad_triple = jnp.concatenate(
        [
            query_grads.reshape(group_rows, heads, LANES)[..., :HD],
            pair_mine[:group_rows].reshape(group_rows, heads, 2 * HD),
        ],
        axis=-1,
    ).reshape(group_rows, head_cols)
    gate_rows = jnp.transpose(
        pair_mine[group_rows : group_rows + seg_count].reshape(seg_count, heads, rows), (1, 0, 2)
    ).reshape(heads, group_rows)
    grad_score = (gate_rows.astype(f32) * jax.nn.sigmoid(-key_score.astype(f32))).astype(bf16)
    grad_norm_part = contract_cols(grad_triple, in_weight[:, :head_cols]) + lax.dot_general(
        grad_score, in_weight[:, head_cols:], (((0,), (1,)), ((), ())), preferred_element_type=f32
    )
    _, gain_pull = jax.vjp(lambda gain: layer_norm(inputs_group, gain), gain_one)
    first_gain_grad = gain_pull(grad_norm_part)[0]
    grad_norm_one = exchange_sum(grad_norm_part.astype(bf16).reshape(seg_count, rows, width), "sp")
    _, first_pull = jax.vjp(lambda values: layer_norm(values, gain_one), inputs)
    grad_input_norm = first_pull(grad_norm_one)[0]
    input_grad = (grad_mixed + grad_input_norm).astype(bf16)[None]

    small = jnp.concatenate(
        [
            contract_rows(norm_one, grad_triple).astype(bf16),
            lax.dot_general(norm_one, grad_score, (((0,), (1,)), ((), ())), preferred_element_type=f32).astype(bf16),
            first_gain_grad.astype(bf16)[:, None],
            second_gain_grad.astype(bf16)[:, None],
        ],
        axis=1,
    ).reshape(dp_count, ctx_count, piece, head_cols + heads + 2)
    small_own = exchange_sum(dp_scatter(small), "ctx").astype(bf16)
    small_own, big_all = lax.optimization_barrier((small_own, big_all))
    small_all = lax.all_gather(small_own, ("sp", "ctx"), axis=0, tiled=False).reshape(
        seg_count, ctx_count * piece, head_cols + heads + 2
    )
    groups = range(seg_count)
    fc_grad = jnp.concatenate(
        [
            big_all[at, :, :piece, part * hidden_part : (part + 1) * hidden_part].reshape(-1, hidden_part)
            for part in range(dp_count)
            for at in groups
        ],
        axis=1,
    ).astype(f32)
    proj_grad = big_all[:, :, piece:both].reshape(hidden // dp_count, width).astype(f32)
    out_grad = lax.dynamic_slice_in_dim(
        big_all[:, :, both:].reshape(width, width), dp_at * (width // dp_count), width // dp_count, 0
    ).astype(f32)
    qkv_grad = jnp.concatenate([small_all[at, :, :head_cols] for at in groups], axis=1).astype(f32)
    score_grad = jnp.concatenate([small_all[at, :, head_cols : head_cols + heads] for at in groups], axis=1).astype(f32)
    gains = jnp.sum(small_all[:, :, head_cols + heads :].astype(f32), axis=0)
    return (output, input_grad, gains[:, 0], qkv_grad, score_grad, out_grad, gains[:, 1], fc_grad, proj_grad)


def solution(mesh):
    placed = (
        P("dp", ("sp", "ctx"), None),
        P("dp", ("sp", "ctx"), None),
        P("dp"),
        P("dp", None, "ctx", "sp", None),
        P("dp"),
        P("dp", None),
        P("dp", None),
        P("dp", None),
        P("dp"),
        P("dp", None),
        P("dp", None),
    )
    return jax.shard_map(
        per_device,
        mesh=mesh,
        in_specs=placed,
        out_specs=(
            P("dp", ("sp", "ctx"), None),
            P("dp", ("sp", "ctx"), None),
            P("dp"),
            P("dp", None),
            P("dp", None),
            P("dp", None),
            P("dp"),
            P("dp", None),
            P("dp", None),
        ),
        check_vma=False,
    )
```

```python
import functools

import jax
import jax.numpy as jnp
from jax import lax
from jax.experimental import pallas as pl
from jax.experimental.pallas import tpu as pltpu
from jax.sharding import PartitionSpec as P

H = 12
HD = 64
WIN = 64
LANES = 128
SLOT = 2048


EPSILON = 1e-05


def layer_norm(values, gain):
    mean_value = jnp.mean(values, axis=-1, keepdims=True)
    centred = values - mean_value
    variance = jnp.mean(centred * centred, axis=-1, keepdims=True)
    return centred * lax.rsqrt(variance + EPSILON) * gain


def tanh_gelu(values):
    return jax.nn.gelu(values, approximate=True)


def contract_rows(left, right):
    return lax.dot_general(
        left, right, (((0,), (0,)), ((), ())), preferred_element_type=jnp.float32
    )


def contract_cols(left, right):
    return lax.dot_general(
        left, right, (((1,), (1,)), ((), ())), preferred_element_type=jnp.float32
    )


NT = (((1,), (1,)), ((), ()))


PAD_ROWS = 16


def slot_order(src_ref, kv_ref):
    count, height, _ = src_ref.shape
    for tile in range(kv_ref.shape[0] // LANES):
        part, at = divmod(tile, count)
        kv_ref[tile * LANES : (tile + 1) * LANES, :] = src_ref[at, part * LANES : (part + 1) * LANES, :]


def slot_gates(src_ref, gate_ref):
    count, height, _ = src_ref.shape
    for at in range(count):
        scores = src_ref[at, height - PAD_ROWS :, :].astype(jnp.float32)
        gates = -jnp.log1p(jnp.exp(-scores))
        for part in range(gate_ref.shape[1] // LANES // count):
            tile = part * count + at
            gate_ref[:, tile * LANES : (tile + 1) * LANES] = jnp.broadcast_to(gates[part : part + 1, :], (8, LANES))


def attend_body(first, tiles, base, idx_ref, q_ref, src_ref, out_ref, prob_ref, score_ref, pair_ref, kv_ref, gate_ref):
    rows = q_ref.shape[0]
    if first:
        slot_order(src_ref, kv_ref)
        slot_gates(src_ref, gate_ref)
    span = tiles * LANES
    f32, bf16 = jnp.float32, jnp.bfloat16
    score_ref[:, :span] = (
        lax.dot_general(q_ref[...], kv_ref[:span, :], NT, preferred_element_type=f32) * HD ** (-0.5)
        + gate_ref[0:1, :span]
    )
    kept = idx_ref[0, 0]
    pair_ref[...] = jnp.concatenate([kept, kept], axis=1)
    wide = 8 * HD
    sub = lax.broadcasted_iota(jnp.int32, (8, wide), 0)
    lane = lax.broadcasted_iota(jnp.int32, (8, wide), 1)
    own = (lane // HD) == sub
    subf = sub.astype(f32)
    ahead = lax.broadcasted_iota(jnp.int32, (8, LANES), 0) - lax.broadcasted_iota(jnp.int32, (8, LANES), 1)
    near_from = max(0, tiles - 5)

    def eight(start):
        four = pair_ref[pl.ds(start, 8), :]
        index = jnp.concatenate([four] * 4, axis=1)
        pos = base + start + sub
        high = jnp.where(own & (pos >= WIN), index >> 7, -2).astype(f32)
        low = jnp.sum(jnp.where(own, (index & 127).astype(f32), 0.0), axis=0, keepdims=True) - subf
        high_pair = jnp.concatenate([high, high - 1.0], axis=0).astype(bf16)
        low_pair = jnp.concatenate([low, low - 8.0], axis=0).astype(bf16)
        one, zero = jnp.ones((), bf16), jnp.zeros((), bf16)
        left = jnp.concatenate(
            [jnp.where(high_pair == jnp.array(2 * p, bf16), one, zero) for p in range(tiles // 2)], axis=0
        )
        right = jnp.concatenate(
            [jnp.where(low_pair == jnp.array(16 * p, bf16), one, zero) for p in range(8)], axis=0
        )
        count = lax.dot_general(left, right, NT, preferred_element_type=f32)
        gap = ahead + (base + start)
        masked, counts = [], []
        largest = None
        for tile in range(tiles):
            number = count[8 * tile : 8 * tile + 8, :]
            if tile >= near_from:
                far = gap - tile * LANES
                number = number + jnp.where((far >= 0) & (far < WIN), 1.0, 0.0)
            value = jnp.where(number > 0.0, score_ref[pl.ds(start, 8), tile * LANES : (tile + 1) * LANES], -1e30)
            counts.append(number)
            masked.append(value)
            largest = value if largest is None else jnp.maximum(largest, value)
        top = jnp.max(largest, axis=1, keepdims=True)
        total = None
        expos = []
        for number, value in zip(counts, masked):
            expo = jnp.exp(value - top) * number
            expos.append(expo)
            total = expo if total is None else total + expo
        inverse = 1.0 / jnp.sum(total, axis=1, keepdims=True)
        return [expo * inverse for expo in expos]

    def step(index, carry):
        start = pl.multiple_of(index * 16, 16)
        first, second = eight(start), eight(start + 8)
        for tile in range(tiles):
            prob_ref[0, 0, pl.ds(start, 16), tile * LANES : (tile + 1) * LANES] = jnp.concatenate(
                [first[tile], second[tile]], axis=0
            ).astype(bf16)
        return carry

    lax.fori_loop(0, rows // 16, step, 0)
    both = jnp.dot(prob_ref[0, 0, :, :span], kv_ref[:span, :], preferred_element_type=f32)
    out_ref[0] = both[:, HD:].astype(bf16)


def attend_kernel(parts, chunk, base_ref, *refs):
    part = pl.program_id(0)
    base = base_ref[0] + part * chunk
    for at in range(parts):
        pl.when(part == at)(
            functools.partial(attend_body, at == 0, (at + 1) * chunk // LANES, base, *refs)
        )


def attend(head, base, kept, query, pairs):
    _, parts, block, keep = kept.shape
    count, height, _ = pairs.shape
    slot = count * (height - PAD_ROWS)
    chunk = slot // parts
    grid_spec = pltpu.PrefetchScalarGridSpec(
        num_scalar_prefetch=1,
        grid=(parts,),
        in_specs=[
            pl.BlockSpec((1, 1, block, keep), lambda r, b: (head, r, 0, 0)),
            pl.BlockSpec((block, LANES), lambda r, b: (r, head)),
            pl.BlockSpec((count, height, LANES), lambda r, b: (0, 0, 0)),
        ],
        out_specs=[
            pl.BlockSpec((1, block, HD), lambda r, b: (0, r, 0)),
            pl.BlockSpec((1, 1, block, slot), lambda r, b: (0, r, 0, 0)),
        ],
        scratch_shapes=[
            pltpu.VMEM((block, slot), jnp.float32),
            pltpu.VMEM((block, 2 * keep), jnp.int32),
            pltpu.VMEM((slot, LANES), jnp.bfloat16),
            pltpu.VMEM((8, slot), jnp.float32),
        ],
    )
    return pl.pallas_call(
        functools.partial(attend_kernel, parts, chunk),
        grid_spec=grid_spec,
        out_shape=[
            jax.ShapeDtypeStruct((1, parts * block, HD), jnp.bfloat16),
            jax.ShapeDtypeStruct((1, parts, block, slot), jnp.bfloat16),
        ],
        name="attend",
    )(base, kept, query, pairs)


def attend_back_body(first, last, tiles, chunk, q_ref, grad_ref, src_ref, prob_ref, dq_ref, out_ref, gates_ref, raw_ref, kv_ref, dkv_ref, gate_ref):
    f32, bf16 = jnp.float32, jnp.bfloat16
    rows = q_ref.shape[0]
    steps = tiles * LANES // chunk
    if first:
        slot_order(src_ref, kv_ref)
        dkv_ref[...] = jnp.zeros_like(dkv_ref)
        gate_ref[...] = jnp.zeros_like(gate_ref)
    dot_sum = None
    for at in range(steps):
        cols = slice(at * chunk, (at + 1) * chunk)
        raw = lax.dot_general(grad_ref[...], kv_ref[cols, :], NT, preferred_element_type=f32)
        raw_ref[:, cols] = raw
        part = jnp.sum(raw * prob_ref[0, 0, :, cols].astype(f32), axis=1, keepdims=True)
        dot_sum = part if dot_sum is None else dot_sum + part
    lane = lax.broadcasted_iota(jnp.int32, (rows, LANES), 1)
    scaled = jnp.where(lane == HD, 1.0, q_ref[...].astype(f32) * HD ** (-0.5))
    query_t = jnp.transpose(scaled)[: HD + 16].astype(bf16)
    grad_t = jnp.transpose(grad_ref[...].astype(f32))[HD:].astype(bf16)
    dq = None
    for at in range(steps):
        cols = slice(at * chunk, (at + 1) * chunk)
        prob = prob_ref[0, 0, :, cols]
        grad_score = (prob.astype(f32) * (raw_ref[:, cols] - dot_sum)).astype(bf16)
        piece = jnp.dot(grad_score, kv_ref[cols, :], preferred_element_type=f32)
        dq = piece if dq is None else dq + piece
        keys = jnp.dot(query_t, grad_score, preferred_element_type=f32)
        dkv_ref[:HD, cols] += keys[:HD]
        gate_ref[:, cols] += keys[HD : HD + 8]
        dkv_ref[HD:, cols] += jnp.dot(grad_t, prob, preferred_element_type=f32)
    dq_ref[...] = (dq * HD ** (-0.5)).astype(dq_ref.dtype)
    if last:
        count, height, _ = out_ref.shape
        parts = height // LANES
        for at in range(count):
            rows_of = []
            for part in range(parts):
                cols = slice((part * count + at) * LANES, (part * count + at + 1) * LANES)
                out_ref[at, part * LANES : (part + 1) * LANES, :] = jnp.transpose(dkv_ref[:, cols]).astype(bf16)
                rows_of.append(gate_ref[0:1, cols])
            rows_of.append(jnp.zeros((PAD_ROWS - parts, LANES), f32))
            gates_ref[at] = jnp.concatenate(rows_of, axis=0).astype(bf16)


def attend_back_kernel(parts, chunk, *refs):
    part = pl.program_id(0)
    for at in range(parts):
        pl.when(part == at)(
            functools.partial(attend_back_body, at == 0, at == parts - 1, (at + 1) * chunk // LANES, chunk, *refs)
        )


def attend_back(head, query, grad, pairs, prob):
    _, parts, block, slot = prob.shape
    count, height, _ = pairs.shape
    chunk = slot // parts
    return pl.pallas_call(
        functools.partial(attend_back_kernel, parts, chunk),
        grid=(parts,),
        in_specs=[
            pl.BlockSpec((block, LANES), lambda r: (r, head)),
            pl.BlockSpec((block, LANES), lambda r: (r, head)),
            pl.BlockSpec((count, height, LANES), lambda r: (0, 0, 0)),
            pl.BlockSpec((1, 1, block, slot), lambda r: (0, r, 0, 0)),
        ],
        out_specs=[
            pl.BlockSpec((block, LANES), lambda r: (r, 0)),
            pl.BlockSpec((count, height - PAD_ROWS, LANES), lambda r: (0, 0, 0)),
            pl.BlockSpec((count, PAD_ROWS, LANES), lambda r: (0, 0, 0)),
        ],
        out_shape=[
            jax.ShapeDtypeStruct((parts * block, LANES), jnp.bfloat16),
            jax.ShapeDtypeStruct((count, height - PAD_ROWS, LANES), jnp.bfloat16),
            jax.ShapeDtypeStruct((count, PAD_ROWS, LANES), jnp.bfloat16),
        ],
        scratch_shapes=[
            pltpu.VMEM((block, slot), jnp.float32),
            pltpu.VMEM((slot, LANES), jnp.bfloat16),
            pltpu.VMEM((LANES, slot), jnp.float32),
            pltpu.VMEM((8, slot), jnp.float32),
        ],
        name="attend_back",
    )(query, grad, pairs, prob)


def unpack_kernel(groups, heads, small_ref, qkv_ref, score_ref):
    keys = heads * 2 * HD
    for at in range(groups):
        values = small_ref[at].astype(jnp.float32)
        for head in range(heads):
            start = (at * heads + head) * 3 * HD
            qkv_ref[:, start : start + HD] = values[:, keys + head * HD : keys + (head + 1) * HD]
            qkv_ref[:, start + HD : start + 3 * HD] = values[:, head * 2 * HD : (head + 1) * 2 * HD]
        score_ref[:, at * heads : (at + 1) * heads] = values[:, keys + heads * HD : keys + heads * HD + heads]


def unpack(small, heads):
    groups, rows, width = small.shape
    block = 96 if rows % 96 == 0 else rows
    return pl.pallas_call(
        functools.partial(unpack_kernel, groups, heads),
        grid=(rows // block,),
        in_specs=[pl.BlockSpec((groups, block, width), lambda r: (0, r, 0))],
        out_specs=[
            pl.BlockSpec((block, groups * heads * 3 * HD), lambda r: (r, 0)),
            pl.BlockSpec((block, groups * heads), lambda r: (r, 0)),
        ],
        out_shape=[
            jax.ShapeDtypeStruct((rows, groups * heads * 3 * HD), jnp.float32),
            jax.ShapeDtypeStruct((rows, groups * heads), jnp.float32),
        ],
        name="unpack",
    )(small)


def ctx_gather(mine):
    copies = jnp.broadcast_to(mine[None], (lax.axis_size("ctx"),) + mine.shape)
    return lax.all_to_all(copies, "ctx", split_axis=0, concat_axis=0, tiled=True)


def arrange_kernel(heads, rows, qkv_ref, score_ref, gains_ref, out_ref):
    f32 = jnp.float32
    values = qkv_ref[...].astype(f32)
    keys = heads * 2 * HD
    width = out_ref.shape[1]
    pieces = [values[:, (3 * head + 1) * HD : (3 * head + 3) * HD] for head in range(heads)]
    pieces += [values[:, 3 * head * HD : (3 * head + 1) * HD] for head in range(heads)]
    pieces += [score_ref[...].astype(f32), jnp.zeros((rows, width - heads * 3 * HD - heads), f32)]
    out_ref[:rows, :] = jnp.concatenate(pieces, axis=1).astype(out_ref.dtype)
    out_ref[rows:, :] = jnp.concatenate(
        [gains_ref[...].astype(f32), jnp.zeros((gains_ref.shape[0], width - rows), f32)], axis=1
    ).astype(out_ref.dtype)


def arrange(qkv, score, gains, width):
    rows, heads = score.shape
    return pl.pallas_call(
        functools.partial(arrange_kernel, heads, rows),
        out_shape=jax.ShapeDtypeStruct((rows + PAD_ROWS, width), qkv.dtype),
        name="arrange",
    )(qkv, score, gains)


def dp_send(mine):
    if lax.axis_size("dp") != 2:
        return lax.all_gather(mine, "dp", axis=0, tiled=True)
    return lax.ppermute(mine, "dp", [(0, 1), (1, 0)])


def dp_join(mine, came):
    if lax.axis_size("dp") != 2:
        return came
    return jnp.where(
        lax.axis_index("dp") == 0, jnp.concatenate([mine, came]), jnp.concatenate([came, mine])
    )


def dp_scatter(parts):
    if lax.axis_size("dp") != 2:
        return lax.psum_scatter(parts, "dp", scatter_dimension=0, tiled=False)
    at = lax.axis_index("dp")
    mine = lax.dynamic_index_in_dim(parts, at, 0, keepdims=False)
    sent = lax.dynamic_index_in_dim(parts, 1 - at, 0, keepdims=False)
    other = lax.ppermute(sent, "dp", [(0, 1), (1, 0)])
    return (mine.astype(jnp.float32) + other.astype(jnp.float32)).astype(parts.dtype)


def group_rows_of(mine, group, count):
    height = mine.shape[0]
    if lax.axis_size("dp") != 2 or height % count != 0:
        whole = lax.all_gather(mine, "dp", axis=0, tiled=True)
        return lax.dynamic_slice_in_dim(whole, group * count, count, 0)
    near = lax.dynamic_slice_in_dim(mine, group * count % height, count, 0)
    far = lax.ppermute(near, "dp", [(0, 1), (1, 0)])
    return jnp.where(lax.axis_index("dp") == group * count // height, near, far)


def dp_sum(mine):
    if lax.axis_size("dp") != 2:
        return lax.psum(mine, "dp")
    other = lax.ppermute(mine, "dp", [(0, 1), (1, 0)])
    return (mine.astype(jnp.float32) + other.astype(jnp.float32)).astype(mine.dtype)


def exchange_sum(parts, axis):
    came = lax.all_to_all(parts, axis, split_axis=0, concat_axis=0, tiled=True)
    return jnp.sum(came.astype(jnp.float32), axis=0)


def per_device(
    tokens,
    cotangent,
    lengths,
    kept_keys,
    first_gain,
    qkv_weight,
    score_weight,
    out_weight,
    second_gain,
    fc_weight,
    proj_weight,
):
    f32, bf16 = jnp.float32, jnp.bfloat16
    dp_count = lax.axis_size("dp")
    seg_count = lax.axis_size("sp")
    ctx_count = lax.axis_size("ctx")
    dp_at = lax.axis_index("dp")
    sp_at = lax.axis_index("sp")
    ctx_at = lax.axis_index("ctx")
    rows = tokens.shape[1]
    width = tokens.shape[2]
    group_rows = seg_count * rows
    heads = H // seg_count
    head_cols = heads * 3 * HD
    hidden = fc_weight.shape[1]
    hidden_part = hidden // (dp_count * seg_count)
    piece = width // (dp_count * ctx_count)

    keys = heads * 2 * HD
    wide = -(-(head_cols + heads + 2) // LANES) * LANES
    weight_rows = width // dp_count
    own_in = arrange(
        lax.dynamic_slice_in_dim(qkv_weight, sp_at * head_cols, head_cols, 1),
        lax.dynamic_slice_in_dim(score_weight, sp_at * heads, heads, 1),
        jnp.pad(jnp.stack([first_gain, second_gain]), ((0, PAD_ROWS - 2), (0, 0))),
        wide,
    )
    if dp_count == 2:
        other_in = lax.ppermute(own_in, "dp", [(0, 1), (1, 0)])
        parts_in = [
            jnp.where(dp_at == at, own_in, other_in) for at in range(dp_count)
        ]
    else:
        parts_in = list(lax.all_gather(own_in, "dp", axis=0, tiled=False))
    tokens_group = lax.all_gather(tokens[0], "sp", axis=0, tiled=True)
    all_in = jnp.concatenate([part[:weight_rows] for part in parts_in])
    gain_one = jnp.concatenate([part[weight_rows, :weight_rows] for part in parts_in]).astype(f32)
    gain_two = jnp.concatenate([part[weight_rows + 1, :weight_rows] for part in parts_in]).astype(f32)

    fc_own = jnp.concatenate(
        [
            lax.dynamic_slice_in_dim(fc_weight, (at * seg_count + sp_at) * hidden_part, hidden_part, 1)
            for at in range(dp_count)
        ],
        axis=1,
    )
    proj_own = lax.dynamic_slice_in_dim(proj_weight, sp_at * hidden_part, hidden_part, 0)
    all_in, out_own, fc_own, proj_own = lax.optimization_barrier((all_in, out_weight, fc_own, proj_own))
    out_part = group_rows_of(out_own, sp_at, heads * HD)
    fc_came = dp_send(fc_own)
    proj_came = dp_send(proj_own)

    inputs = tokens[0].astype(f32)
    inputs_group = tokens_group.astype(f32)
    norm_one = layer_norm(inputs_group, gain_one).astype(bf16)
    qkv_rows = jnp.dot(norm_one, all_in, preferred_element_type=f32).astype(bf16)
    score_weight_part = all_in[:, head_cols : head_cols + heads]
    key_score = lax.dot_general(
        score_weight_part, norm_one, (((0,), (1,)), ((), ())), preferred_element_type=f32
    ).astype(bf16)
    score_rows = jnp.transpose(key_score.reshape(heads, seg_count, rows), (1, 0, 2)).reshape(
        seg_count, heads * rows
    )
    padded = jnp.pad(score_rows, ((0, PAD_ROWS - seg_count), (0, 0)))
    pairs_own = [
        jnp.concatenate([qkv_rows[:, head * 2 * HD : (head + 1) * 2 * HD], padded[:, head * rows : (head + 1) * rows]], axis=0)
        for head in range(heads)
    ]
    query_wide = jnp.pad(
        qkv_rows[:, keys:head_cols].reshape(group_rows, heads, HD), ((0, 0), (0, 0), (0, HD))
    ).reshape(group_rows, heads * LANES)
    kept = jnp.transpose(kept_keys[0], (2, 0, 1, 3))
    base = (ctx_at * rows).astype(jnp.int32)[None]
    cot_own, pairs_own[0] = lax.optimization_barrier((cotangent[0], pairs_own[0]))
    cot_group = lax.all_gather(cot_own, "sp", axis=0, tiled=True)
    norm_own = lax.dynamic_slice_in_dim(norm_one, sp_at * rows, rows, 0)
    pairs, attended, probs = [], [], []
    for head in range(heads):
        here = ctx_gather(pairs_own[head])
        if head == 0:
            here, cot_group = lax.optimization_barrier((here, cot_group))
        else:
            here, attended[-1] = lax.optimization_barrier((here, attended[-1]))
        if head + 1 < heads:
            here, pairs_own[head + 1] = lax.optimization_barrier((here, pairs_own[head + 1]))
        else:
            here, norm_own, fc_came, proj_came = lax.optimization_barrier((here, norm_own, fc_came, proj_came))
        pairs.append(here)
        head_out, prob = attend(head, base, kept, query_wide, pairs[head])
        attended.append(head_out[0])
        probs.append(prob)
    norm_slot = lax.all_gather(norm_own, ("ctx", "sp"), axis=0, tiled=True)
    attended = jnp.concatenate(attended, axis=1)
    fc_part = dp_join(fc_own, fc_came)
    proj_part = dp_join(proj_own, proj_came)

    group_at = jnp.arange(group_rows, dtype=jnp.int32)
    group_positions = (group_at // rows) * (ctx_count * rows) + ctx_at * rows + group_at % rows
    grad_out_group = jnp.where((group_positions < lengths[0])[:, None], cot_group, jnp.zeros_like(cot_group))
    positions = (sp_at * ctx_count + ctx_at) * rows + jnp.arange(rows, dtype=jnp.int32)
    is_valid = (positions < lengths[0])[:, None]

    branch = jnp.dot(attended, out_part, preferred_element_type=f32).astype(bf16)
    mixed = inputs + exchange_sum(branch.reshape(seg_count, rows, width), "sp")
    norm_two_own = layer_norm(mixed, gain_two).astype(bf16)
    norm_two = lax.all_gather(norm_two_own, "sp", axis=0, tiled=True)
    hidden_pre = jnp.dot(norm_two, fc_part, preferred_element_type=f32)
    active = tanh_gelu(hidden_pre).astype(bf16)
    grad_active = contract_cols(grad_out_group, proj_part)
    _, gelu_pull = jax.vjp(tanh_gelu, hidden_pre)
    grad_pre = gelu_pull(grad_active)[0].astype(bf16)
    fc_parts = contract_rows(norm_two, grad_pre).astype(bf16).reshape(dp_count, ctx_count, piece, width)
    proj_parts = contract_rows(active, grad_out_group).astype(bf16).reshape(dp_count, ctx_count, -1, width)
    grad_pre, fc_parts, proj_parts = lax.optimization_barrier((grad_pre, fc_parts, proj_parts))
    fc_dp = dp_scatter(fc_parts)
    proj_dp = dp_scatter(proj_parts)
    grad_norm_parts = contract_cols(grad_pre, fc_part).astype(bf16)
    grad_norm_two = exchange_sum(grad_norm_parts.reshape(seg_count, rows, width), "sp")
    _, second_pull = jax.vjp(layer_norm, mixed, gain_two)
    grad_mixed_norm, second_gain_grad = second_pull(grad_norm_two)
    grad_out = jnp.where(is_valid, cotangent[0], jnp.zeros_like(cotangent[0])).astype(f32)
    grad_mixed = grad_out + grad_mixed_norm
    grad_branch = lax.all_gather(grad_mixed.astype(bf16), "sp", axis=0, tiled=True)

    out_wide = jnp.pad(out_part.reshape(heads, HD, width), ((0, 0), (HD, 0), (0, 0))).reshape(heads * LANES, width)
    grad_wide = contract_cols(grad_branch, out_wide).astype(bf16)
    out_mine = contract_rows(attended, grad_branch).astype(bf16)
    grad_wide, fc_dp, out_mine = lax.optimization_barrier((grad_wide, fc_dp, out_mine))
    out_sum = dp_sum(out_mine)
    fc_came = lax.all_to_all(fc_dp, "ctx", split_axis=0, concat_axis=0, tiled=True)
    query_grads, pair_grads, gate_grads = [], [], []
    for head in range(heads):
        grads = attend_back(head, query_wide, grad_wide, pairs[head], probs[head])
        query_grads.append(grads[0])
        pair_grads.append(grads[1])
        gate_grads.append(grads[2])
    query_grads, pair_grads, gate_grads, fc_came, proj_dp, out_sum = lax.optimization_barrier(
        (query_grads, pair_grads, gate_grads, fc_came, proj_dp, out_sum)
    )
    late = jnp.concatenate([proj_dp, out_sum.reshape(ctx_count, -1, width)], axis=1)
    late_came = lax.all_to_all(late, "ctx", split_axis=0, concat_axis=0, tiled=True)

    query_all = jnp.concatenate([grad[:, :HD] for grad in query_grads], axis=1)
    tail_cols = wide - keys
    score_slot = jnp.stack([pair[:, group_rows : group_rows + seg_count] for pair in pairs])
    gates_slot = jnp.stack([gates[:, :seg_count] for gates in gate_grads])
    grad_score_slot = (
        gates_slot.astype(f32) * jax.nn.sigmoid(-score_slot.astype(f32))
    ).astype(bf16).reshape(heads, ctx_count * group_rows)
    scores_at = heads * HD
    pieces = [contract_rows(norm_slot, grad.reshape(-1, LANES)) for grad in pair_grads]
    tail = contract_rows(norm_one, jnp.pad(query_all, ((0, 0), (0, tail_cols - scores_at)))) + lax.dot_general(
        norm_slot,
        jnp.pad(grad_score_slot, ((scores_at, tail_cols - scores_at - heads), (0, 0))),
        (((0,), (1,)), ((), ())),
        preferred_element_type=f32,
    )
    first_gain_grad = jnp.sum(tail * all_in[:, keys:].astype(f32), axis=1)
    for head in range(heads):
        first_gain_grad += jnp.sum(
            pieces[head] * all_in[:, head * 2 * HD : (head + 1) * 2 * HD].astype(f32), axis=1
        )
    first_gain_grad = first_gain_grad / gain_one
    lane = jnp.arange(tail_cols)[None, :]
    tail = jnp.where(lane == scores_at + heads, first_gain_grad[:, None], tail)
    tail = jnp.where(lane == scores_at + heads + 1, second_gain_grad[:, None], tail)
    small = jnp.concatenate([part.astype(bf16) for part in pieces + [tail]], axis=1).reshape(
        dp_count, ctx_count, piece, wide
    )
    small_dp, late_came = lax.optimization_barrier((dp_scatter(small), late_came))
    small_came = lax.all_to_all(small_dp, "ctx", split_axis=0, concat_axis=0, tiled=True)

    def total(came):
        return jnp.sum(came.astype(f32), axis=0).astype(bf16)

    big = jnp.concatenate([total(fc_came), total(late_came)], axis=0)
    big_all = lax.all_gather(big, ("sp", "ctx"), axis=0, tiled=False).reshape(seg_count, ctx_count, -1, width)
    proj_piece = hidden // (seg_count * dp_count * ctx_count)
    both = piece + proj_piece
    small_own = total(small_came)
    small_own, pair_grads, gate_grads, active_late = lax.optimization_barrier(
        (small_own, pair_grads, gate_grads, active)
    )
    pair_mine = exchange_sum(jnp.concatenate(pair_grads, axis=2), "ctx").astype(bf16)
    gate_mine = exchange_sum(jnp.concatenate([gates[:, :seg_count] for gates in gate_grads], axis=2), "ctx")
    expanded = exchange_sum(
        jnp.dot(active_late, proj_part, preferred_element_type=f32).astype(bf16).reshape(seg_count, rows, width), "sp"
    )
    output = jnp.where(is_valid, mixed + expanded, 0.0).astype(bf16)[None]
    gate_rows = jnp.transpose(gate_mine.reshape(seg_count, heads, rows), (1, 0, 2)).reshape(heads, group_rows)
    grad_score = (gate_rows * jax.nn.sigmoid(-key_score.astype(f32))).astype(bf16)
    grad_norm_part = (
        contract_cols(pair_mine, all_in[:, :keys])
        + contract_cols(query_all, all_in[:, keys:head_cols])
        + lax.dot_general(grad_score, score_weight_part, (((0,), (1,)), ((), ())), preferred_element_type=f32)
    )
    grad_norm_one = exchange_sum(grad_norm_part.astype(bf16).reshape(seg_count, rows, width), "sp")
    _, first_pull = jax.vjp(lambda values: layer_norm(values, gain_one), inputs)
    grad_input_norm = first_pull(grad_norm_one)[0]
    input_grad = (grad_mixed + grad_input_norm).astype(bf16)[None]

    small_own, big_all = lax.optimization_barrier((small_own, big_all))
    small_all = lax.all_gather(small_own, ("sp", "ctx"), axis=0, tiled=False).reshape(
        seg_count, ctx_count * piece, wide
    )
    groups = range(seg_count)
    fc_grad = jnp.concatenate(
        [
            big_all[at, :, :piece, part * hidden_part : (part + 1) * hidden_part].reshape(-1, hidden_part)
            for part in range(dp_count)
            for at in groups
        ],
        axis=1,
    ).astype(f32)
    proj_grad = big_all[:, :, piece:both].reshape(hidden // dp_count, width).astype(f32)
    out_grad = lax.dynamic_slice_in_dim(
        big_all[:, :, both:].reshape(width, width), dp_at * (width // dp_count), width // dp_count, 0
    ).astype(f32)
    qkv_grad, score_grad = unpack(small_all, heads)
    gains = jnp.sum(small_all[:, :, head_cols + heads : head_cols + heads + 2].astype(f32), axis=0)
    return (output, input_grad, gains[:, 0], qkv_grad, score_grad, out_grad, gains[:, 1], fc_grad, proj_grad)


def solution(mesh):
    placed = (
        P("dp", ("sp", "ctx"), None),
        P("dp", ("sp", "ctx"), None),
        P("dp"),
        P("dp", None, "ctx", "sp", None),
        P("dp"),
        P("dp", None),
        P("dp", None),
        P("dp", None),
        P("dp"),
        P("dp", None),
        P("dp", None),
    )
    return jax.shard_map(
        per_device,
        mesh=mesh,
        in_specs=placed,
        out_specs=(
            P("dp", ("sp", "ctx"), None),
            P("dp", ("sp", "ctx"), None),
            P("dp"),
            P("dp", None),
            P("dp", None),
            P("dp", None),
            P("dp"),
            P("dp", None),
            P("dp", None),
        ),
        check_vma=False,
    )
```

```python
import functools

import jax
import jax.numpy as jnp
from jax import lax
from jax.experimental import pallas as pl
from jax.experimental.pallas import tpu as pltpu
from jax.sharding import PartitionSpec as P

H = 12
HD = 64
WIN = 64
LANES = 128
SLOT = 2048


EPSILON = 1e-05


def layer_norm(values, gain):
    mean_value = jnp.mean(values, axis=-1, keepdims=True)
    centred = values - mean_value
    variance = jnp.mean(centred * centred, axis=-1, keepdims=True)
    return centred * lax.rsqrt(variance + EPSILON) * gain


def tanh_gelu(values):
    return jax.nn.gelu(values, approximate=True)


def contract_rows(left, right):
    return lax.dot_general(
        left, right, (((0,), (0,)), ((), ())), preferred_element_type=jnp.float32
    )


def contract_cols(left, right):
    return lax.dot_general(
        left, right, (((1,), (1,)), ((), ())), preferred_element_type=jnp.float32
    )


NT = (((1,), (1,)), ((), ()))


PAD_ROWS = 16


def slot_order(src_ref, kv_ref):
    count, height, _ = src_ref.shape
    for tile in range(kv_ref.shape[0] // LANES):
        part, at = divmod(tile, count)
        kv_ref[tile * LANES : (tile + 1) * LANES, :] = src_ref[at, part * LANES : (part + 1) * LANES, :]


def slot_gates(src_ref, gate_ref):
    count, height, _ = src_ref.shape
    for at in range(count):
        scores = src_ref[at, height - PAD_ROWS :, :].astype(jnp.float32)
        gates = -jnp.log1p(jnp.exp(-scores))
        for part in range(gate_ref.shape[1] // LANES // count):
            tile = part * count + at
            gate_ref[:, tile * LANES : (tile + 1) * LANES] = jnp.broadcast_to(gates[part : part + 1, :], (8, LANES))


def attend_body(first, tiles, base, idx_ref, q_ref, src_ref, out_ref, prob_ref, score_ref, pair_ref, kv_ref, gate_ref):
    rows = q_ref.shape[0]
    if first:
        slot_order(src_ref, kv_ref)
        slot_gates(src_ref, gate_ref)
    span = tiles * LANES
    f32, bf16 = jnp.float32, jnp.bfloat16
    score_ref[:, :span] = (
        lax.dot_general(q_ref[...], kv_ref[:span, :], NT, preferred_element_type=f32) * HD ** (-0.5)
        + gate_ref[0:1, :span]
    )
    kept = idx_ref[0, 0]
    pair_ref[...] = jnp.concatenate([kept, kept], axis=1)
    wide = 8 * HD
    sub = lax.broadcasted_iota(jnp.int32, (8, wide), 0)
    lane = lax.broadcasted_iota(jnp.int32, (8, wide), 1)
    own = (lane // HD) == sub
    subf = sub.astype(f32)
    ahead = lax.broadcasted_iota(jnp.int32, (8, LANES), 0) - lax.broadcasted_iota(jnp.int32, (8, LANES), 1)
    near_from = max(0, tiles - 5)

    def eight(start):
        four = pair_ref[pl.ds(start, 8), :]
        index = jnp.concatenate([four] * 4, axis=1)
        pos = base + start + sub
        high = jnp.where(own & (pos >= WIN), index >> 7, -2).astype(f32)
        low = jnp.sum(jnp.where(own, (index & 127).astype(f32), 0.0), axis=0, keepdims=True) - subf
        high_pair = jnp.concatenate([high, high - 1.0], axis=0).astype(bf16)
        low_pair = jnp.concatenate([low, low - 8.0], axis=0).astype(bf16)
        one, zero = jnp.ones((), bf16), jnp.zeros((), bf16)
        left = jnp.concatenate(
            [jnp.where(high_pair == jnp.array(2 * p, bf16), one, zero) for p in range(tiles // 2)], axis=0
        )
        right = jnp.concatenate(
            [jnp.where(low_pair == jnp.array(16 * p, bf16), one, zero) for p in range(8)], axis=0
        )
        count = lax.dot_general(left, right, NT, preferred_element_type=f32)
        gap = ahead + (base + start)
        masked, counts = [], []
        largest = None
        for tile in range(tiles):
            number = count[8 * tile : 8 * tile + 8, :]
            if tile >= near_from:
                far = gap - tile * LANES
                number = number + jnp.where((far >= 0) & (far < WIN), 1.0, 0.0)
            value = jnp.where(number > 0.0, score_ref[pl.ds(start, 8), tile * LANES : (tile + 1) * LANES], -1e30)
            counts.append(number)
            masked.append(value)
            largest = value if largest is None else jnp.maximum(largest, value)
        top = jnp.max(largest, axis=1, keepdims=True)
        total = None
        expos = []
        for number, value in zip(counts, masked):
            expo = jnp.exp(value - top) * number
            expos.append(expo)
            total = expo if total is None else total + expo
        inverse = 1.0 / jnp.sum(total, axis=1, keepdims=True)
        return [expo * inverse for expo in expos]

    def step(index, carry):
        start = pl.multiple_of(index * 16, 16)
        first, second = eight(start), eight(start + 8)
        for tile in range(tiles):
            prob_ref[0, 0, pl.ds(start, 16), tile * LANES : (tile + 1) * LANES] = jnp.concatenate(
                [first[tile], second[tile]], axis=0
            ).astype(bf16)
        return carry

    lax.fori_loop(0, rows // 16, step, 0)
    both = jnp.dot(prob_ref[0, 0, :, :span], kv_ref[:span, :], preferred_element_type=f32)
    out_ref[0] = both[:, HD:].astype(bf16)


def attend_kernel(parts, chunk, base_ref, *refs):
    part = pl.program_id(1)
    base = base_ref[0] + part * chunk
    for at in range(parts):
        pl.when(part == at)(
            functools.partial(attend_body, at == 0, (at + 1) * chunk // LANES, base, *refs)
        )


def attend(base, kept, query, pairs):
    heads, parts, block, keep = kept.shape
    count, height, _ = pairs.shape
    slot = count * (height - PAD_ROWS)
    chunk = slot // parts
    grid_spec = pltpu.PrefetchScalarGridSpec(
        num_scalar_prefetch=1,
        grid=(heads, parts),
        in_specs=[
            pl.BlockSpec((1, 1, block, keep), lambda h, r, b: (h, r, 0, 0)),
            pl.BlockSpec((block, LANES), lambda h, r, b: (r, h)),
            pl.BlockSpec((count, height, LANES), lambda h, r, b: (0, 0, h)),
        ],
        out_specs=[
            pl.BlockSpec((1, block, HD), lambda h, r, b: (h, r, 0)),
            pl.BlockSpec((1, 1, block, slot), lambda h, r, b: (h, r, 0, 0)),
        ],
        scratch_shapes=[
            pltpu.VMEM((block, slot), jnp.float32),
            pltpu.VMEM((block, 2 * keep), jnp.int32),
            pltpu.VMEM((slot, LANES), jnp.bfloat16),
            pltpu.VMEM((8, slot), jnp.float32),
        ],
    )
    return pl.pallas_call(
        functools.partial(attend_kernel, parts, chunk),
        grid_spec=grid_spec,
        out_shape=[
            jax.ShapeDtypeStruct((heads, parts * block, HD), jnp.bfloat16),
            jax.ShapeDtypeStruct((heads, parts, block, slot), jnp.bfloat16),
        ],
        name="attend",
    )(base, kept, query, pairs)


def attend_back_body(first, last, tiles, chunk, q_ref, grad_ref, src_ref, prob_ref, dq_ref, out_ref, raw_ref, kv_ref, dkv_ref, gate_ref):
    f32, bf16 = jnp.float32, jnp.bfloat16
    rows = q_ref.shape[0]
    steps = tiles * LANES // chunk
    if first:
        slot_order(src_ref, kv_ref)
        dkv_ref[...] = jnp.zeros_like(dkv_ref)
        gate_ref[...] = jnp.zeros_like(gate_ref)
    dot_sum = None
    for at in range(steps):
        cols = slice(at * chunk, (at + 1) * chunk)
        raw = lax.dot_general(grad_ref[...], kv_ref[cols, :], NT, preferred_element_type=f32)
        raw_ref[:, cols] = raw
        part = jnp.sum(raw * prob_ref[0, 0, :, cols].astype(f32), axis=1, keepdims=True)
        dot_sum = part if dot_sum is None else dot_sum + part
    lane = lax.broadcasted_iota(jnp.int32, (rows, LANES), 1)
    scaled = jnp.where(lane == HD, 1.0, q_ref[...].astype(f32) * HD ** (-0.5))
    query_t = jnp.transpose(scaled)[: HD + 16].astype(bf16)
    grad_t = jnp.transpose(grad_ref[...].astype(f32))[HD:].astype(bf16)
    dq = None
    for at in range(steps):
        cols = slice(at * chunk, (at + 1) * chunk)
        prob = prob_ref[0, 0, :, cols]
        grad_score = (prob.astype(f32) * (raw_ref[:, cols] - dot_sum)).astype(bf16)
        piece = jnp.dot(grad_score, kv_ref[cols, :], preferred_element_type=f32)
        dq = piece if dq is None else dq + piece
        keys = jnp.dot(query_t, grad_score, preferred_element_type=f32)
        dkv_ref[:HD, cols] += keys[:HD]
        gate_ref[:, cols] += keys[HD : HD + 8]
        dkv_ref[HD:, cols] += jnp.dot(grad_t, prob, preferred_element_type=f32)
    dq_ref[...] = (dq * HD ** (-0.5)).astype(dq_ref.dtype)
    if last:
        count, height, _ = out_ref.shape
        parts = (height - PAD_ROWS) // LANES
        for at in range(count):
            rows_of = []
            for part in range(parts):
                cols = slice((part * count + at) * LANES, (part * count + at + 1) * LANES)
                out_ref[at, part * LANES : (part + 1) * LANES, :] = jnp.transpose(dkv_ref[:, cols]).astype(bf16)
                rows_of.append(gate_ref[0:1, cols])
            rows_of.append(jnp.zeros((PAD_ROWS - parts, LANES), f32))
            out_ref[at, height - PAD_ROWS :, :] = jnp.concatenate(rows_of, axis=0).astype(bf16)


def attend_back_kernel(parts, chunk, *refs):
    part = pl.program_id(1)
    for at in range(parts):
        pl.when(part == at)(
            functools.partial(attend_back_body, at == 0, at == parts - 1, (at + 1) * chunk // LANES, chunk, *refs)
        )


def attend_back(query, grad, pairs, prob):
    heads, parts, block, slot = prob.shape
    count, height, width = pairs.shape
    chunk = slot // parts
    return pl.pallas_call(
        functools.partial(attend_back_kernel, parts, chunk),
        grid=(heads, parts),
        in_specs=[
            pl.BlockSpec((block, LANES), lambda h, r: (r, h)),
            pl.BlockSpec((block, LANES), lambda h, r: (r, h)),
            pl.BlockSpec((count, height, LANES), lambda h, r: (0, 0, h)),
            pl.BlockSpec((1, 1, block, slot), lambda h, r: (h, r, 0, 0)),
        ],
        out_specs=[
            pl.BlockSpec((block, LANES), lambda h, r: (r, h)),
            pl.BlockSpec((count, height, LANES), lambda h, r: (0, 0, h)),
        ],
        out_shape=[
            jax.ShapeDtypeStruct((parts * block, heads * LANES), jnp.bfloat16),
            jax.ShapeDtypeStruct((count, height, width), jnp.bfloat16),
        ],
        scratch_shapes=[
            pltpu.VMEM((block, slot), jnp.float32),
            pltpu.VMEM((slot, LANES), jnp.bfloat16),
            pltpu.VMEM((LANES, slot), jnp.float32),
            pltpu.VMEM((8, slot), jnp.float32),
        ],
        name="attend_back",
    )(query, grad, pairs, prob)


def finish_kernel(heads, norm_ref, pair_ref, dq_ref, score_ref, in_ref, gain_ref, small_ref, grad_ref):
    f32, bf16 = jnp.float32, jnp.bfloat16
    group = norm_ref.shape[1]
    parts = group // LANES
    wide = in_ref.shape[1]
    gates = pair_ref[group:, :].astype(f32)
    total = jnp.concatenate(
        [
            jnp.concatenate([gates[at : at + 1, head * LANES : (head + 1) * LANES] for at in range(parts)], axis=1)
            for head in range(heads)
        ],
        axis=0,
    )
    total = total * jax.nn.sigmoid(-score_ref[...].astype(f32))
    scores = jnp.transpose(jnp.concatenate([total, jnp.zeros((LANES - heads, group), f32)], axis=0))
    rest = wide - heads * 3 * HD
    columns = jnp.concatenate(
        [pair_ref[:group, :].astype(f32)]
        + [dq_ref[:, head * LANES : head * LANES + HD].astype(f32) for head in range(heads)]
        + [scores[:, :rest]],
        axis=1,
    ).astype(bf16)
    small = jnp.dot(norm_ref[...], columns, preferred_element_type=f32)
    gain_grad = jnp.sum(small * in_ref[...].astype(f32), axis=1, keepdims=True) / gain_ref[:, 0:1]
    lane = lax.broadcasted_iota(jnp.int32, small.shape, 1)
    at = heads * 3 * HD + heads
    small = jnp.where(lane == at, gain_grad, jnp.where(lane == at + 1, gain_ref[:, 1:2], small))
    small_ref[...] = small.astype(bf16)
    grad_ref[...] = lax.dot_general(columns, in_ref[...], NT, preferred_element_type=f32).astype(bf16)


def finish(norm_t, pair, dq, score, weights, gains):
    width, group = norm_t.shape
    heads = score.shape[0]
    return pl.pallas_call(
        functools.partial(finish_kernel, heads),
        out_shape=[
            jax.ShapeDtypeStruct(weights.shape, jnp.bfloat16),
            jax.ShapeDtypeStruct((group, width), jnp.bfloat16),
        ],
        name="finish",
    )(norm_t, pair, dq, score, weights, gains)


def unpack_kernel(groups, heads, small_ref, qkv_ref, score_ref):
    keys = heads * 2 * HD
    for at in range(groups):
        values = small_ref[at].astype(jnp.float32)
        for head in range(heads):
            start = (at * heads + head) * 3 * HD
            qkv_ref[:, start : start + HD] = values[:, keys + head * HD : keys + (head + 1) * HD]
            qkv_ref[:, start + HD : start + 3 * HD] = values[:, head * 2 * HD : (head + 1) * 2 * HD]
        score_ref[:, at * heads : (at + 1) * heads] = values[:, keys + heads * HD : keys + heads * HD + heads]


def unpack(small, heads):
    groups, rows, width = small.shape
    block = 96 if rows % 96 == 0 else rows
    return pl.pallas_call(
        functools.partial(unpack_kernel, groups, heads),
        grid=(rows // block,),
        in_specs=[pl.BlockSpec((groups, block, width), lambda r: (0, r, 0))],
        out_specs=[
            pl.BlockSpec((block, groups * heads * 3 * HD), lambda r: (r, 0)),
            pl.BlockSpec((block, groups * heads), lambda r: (r, 0)),
        ],
        out_shape=[
            jax.ShapeDtypeStruct((rows, groups * heads * 3 * HD), jnp.float32),
            jax.ShapeDtypeStruct((rows, groups * heads), jnp.float32),
        ],
        name="unpack",
    )(small)


def arrange_kernel(heads, rows, qkv_ref, score_ref, gains_ref, out_ref):
    f32 = jnp.float32
    values = qkv_ref[...].astype(f32)
    keys = heads * 2 * HD
    width = out_ref.shape[1]
    pieces = [values[:, (3 * head + 1) * HD : (3 * head + 3) * HD] for head in range(heads)]
    pieces += [values[:, 3 * head * HD : (3 * head + 1) * HD] for head in range(heads)]
    pieces += [score_ref[...].astype(f32), jnp.zeros((rows, width - heads * 3 * HD - heads), f32)]
    out_ref[:rows, :] = jnp.concatenate(pieces, axis=1).astype(out_ref.dtype)
    out_ref[rows:, :] = jnp.concatenate(
        [gains_ref[...].astype(f32), jnp.zeros((gains_ref.shape[0], width - rows), f32)], axis=1
    ).astype(out_ref.dtype)


def arrange(qkv, score, gains, width):
    rows, heads = score.shape
    return pl.pallas_call(
        functools.partial(arrange_kernel, heads, rows),
        out_shape=jax.ShapeDtypeStruct((rows + PAD_ROWS, width), qkv.dtype),
        name="arrange",
    )(qkv, score, gains)


def dp_send(mine):
    if lax.axis_size("dp") != 2:
        return lax.all_gather(mine, "dp", axis=0, tiled=True)
    return lax.ppermute(mine, "dp", [(0, 1), (1, 0)])


def dp_join(mine, came):
    if lax.axis_size("dp") != 2:
        return came
    return jnp.where(
        lax.axis_index("dp") == 0, jnp.concatenate([mine, came]), jnp.concatenate([came, mine])
    )


def dp_scatter(parts):
    if lax.axis_size("dp") != 2:
        return lax.psum_scatter(parts, "dp", scatter_dimension=0, tiled=False)
    at = lax.axis_index("dp")
    mine = lax.dynamic_index_in_dim(parts, at, 0, keepdims=False)
    sent = lax.dynamic_index_in_dim(parts, 1 - at, 0, keepdims=False)
    other = lax.ppermute(sent, "dp", [(0, 1), (1, 0)])
    return (mine.astype(jnp.float32) + other.astype(jnp.float32)).astype(parts.dtype)


def group_rows_of(mine, group, count):
    height = mine.shape[0]
    if lax.axis_size("dp") != 2 or height % count != 0:
        whole = lax.all_gather(mine, "dp", axis=0, tiled=True)
        return lax.dynamic_slice_in_dim(whole, group * count, count, 0)
    near = lax.dynamic_slice_in_dim(mine, group * count % height, count, 0)
    far = lax.ppermute(near, "dp", [(0, 1), (1, 0)])
    return jnp.where(lax.axis_index("dp") == group * count // height, near, far)


def dp_sum(mine):
    if lax.axis_size("dp") != 2:
        return lax.psum(mine, "dp")
    other = lax.ppermute(mine, "dp", [(0, 1), (1, 0)])
    return (mine.astype(jnp.float32) + other.astype(jnp.float32)).astype(mine.dtype)


def exchange_sum(parts, axis):
    came = lax.all_to_all(parts, axis, split_axis=0, concat_axis=0, tiled=True)
    return jnp.sum(came.astype(jnp.float32), axis=0)


def per_device(
    tokens,
    cotangent,
    lengths,
    kept_keys,
    first_gain,
    qkv_weight,
    score_weight,
    out_weight,
    second_gain,
    fc_weight,
    proj_weight,
):
    f32, bf16 = jnp.float32, jnp.bfloat16
    dp_count = lax.axis_size("dp")
    seg_count = lax.axis_size("sp")
    ctx_count = lax.axis_size("ctx")
    dp_at = lax.axis_index("dp")
    sp_at = lax.axis_index("sp")
    ctx_at = lax.axis_index("ctx")
    rows = tokens.shape[1]
    width = tokens.shape[2]
    group_rows = seg_count * rows
    heads = H // seg_count
    head_cols = heads * 3 * HD
    hidden = fc_weight.shape[1]
    hidden_part = hidden // (dp_count * seg_count)
    piece = width // (dp_count * ctx_count)

    keys = heads * 2 * HD
    wide = -(-(head_cols + heads + 2) // LANES) * LANES
    weight_rows = width // dp_count
    own_in = arrange(
        lax.dynamic_slice_in_dim(qkv_weight, sp_at * head_cols, head_cols, 1),
        lax.dynamic_slice_in_dim(score_weight, sp_at * heads, heads, 1),
        jnp.pad(jnp.stack([first_gain, second_gain]), ((0, PAD_ROWS - 2), (0, 0))),
        wide,
    )
    if dp_count == 2:
        other_in = lax.ppermute(own_in, "dp", [(0, 1), (1, 0)])
        parts_in = [
            jnp.where(dp_at == at, own_in, other_in) for at in range(dp_count)
        ]
    else:
        parts_in = list(lax.all_gather(own_in, "dp", axis=0, tiled=False))
    tokens_group = lax.all_gather(tokens[0], "sp", axis=0, tiled=True)
    all_in = jnp.concatenate([part[:weight_rows] for part in parts_in])
    gain_one = jnp.concatenate([part[weight_rows, :weight_rows] for part in parts_in]).astype(f32)
    gain_two = jnp.concatenate([part[weight_rows + 1, :weight_rows] for part in parts_in]).astype(f32)

    fc_own = jnp.concatenate(
        [
            lax.dynamic_slice_in_dim(fc_weight, (at * seg_count + sp_at) * hidden_part, hidden_part, 1)
            for at in range(dp_count)
        ],
        axis=1,
    )
    proj_own = lax.dynamic_slice_in_dim(proj_weight, sp_at * hidden_part, hidden_part, 0)
    all_in, out_own, fc_own, proj_own = lax.optimization_barrier((all_in, out_weight, fc_own, proj_own))
    out_part = group_rows_of(out_own, sp_at, heads * HD)
    fc_came = dp_send(fc_own)
    proj_came = dp_send(proj_own)

    inputs = tokens[0].astype(f32)
    inputs_group = tokens_group.astype(f32)
    norm_one = layer_norm(inputs_group, gain_one).astype(bf16)
    qkv_rows = jnp.dot(norm_one, all_in, preferred_element_type=f32).astype(bf16)
    score_weight_part = all_in[:, head_cols : head_cols + heads]
    key_score = lax.dot_general(
        score_weight_part, norm_one, (((0,), (1,)), ((), ())), preferred_element_type=f32
    ).astype(bf16)
    score_rows = jnp.transpose(key_score.reshape(heads, seg_count, rows), (1, 0, 2)).reshape(
        seg_count, heads * rows
    )
    pairs_own = jnp.concatenate(
        [qkv_rows[:, :keys], jnp.pad(score_rows, ((0, PAD_ROWS - seg_count), (0, 0)))], axis=0
    )
    query_wide = jnp.pad(
        qkv_rows[:, keys:head_cols].reshape(group_rows, heads, HD), ((0, 0), (0, 0), (0, HD))
    ).reshape(group_rows, heads * LANES)
    kept = jnp.transpose(kept_keys[0], (2, 0, 1, 3))
    base = (ctx_at * rows).astype(jnp.int32)[None]
    cot_own, pairs_own = lax.optimization_barrier((cotangent[0], pairs_own))
    cot_group = lax.all_gather(cot_own, "sp", axis=0, tiled=True)
    pairs = lax.all_gather(pairs_own, "ctx", axis=0, tiled=False)
    query_wide, cot_group, out_part, fc_came, proj_came = lax.optimization_barrier(
        (query_wide, cot_group, out_part, fc_came, proj_came)
    )
    head_outs, prob = attend(base, kept, query_wide, pairs)
    attended = jnp.transpose(head_outs, (1, 0, 2)).reshape(group_rows, heads * HD)
    fc_part = dp_join(fc_own, fc_came)
    proj_part = dp_join(proj_own, proj_came)

    group_at = jnp.arange(group_rows, dtype=jnp.int32)
    group_positions = (group_at // rows) * (ctx_count * rows) + ctx_at * rows + group_at % rows
    grad_out_group = jnp.where((group_positions < lengths[0])[:, None], cot_group, jnp.zeros_like(cot_group))
    positions = (sp_at * ctx_count + ctx_at) * rows + jnp.arange(rows, dtype=jnp.int32)
    is_valid = (positions < lengths[0])[:, None]

    branch = jnp.dot(attended, out_part, preferred_element_type=f32).astype(bf16)
    mixed = inputs + exchange_sum(branch.reshape(seg_count, rows, width), "sp")
    norm_two_own = layer_norm(mixed, gain_two).astype(bf16)
    norm_two = lax.all_gather(norm_two_own, "sp", axis=0, tiled=True)
    hidden_pre = jnp.dot(norm_two, fc_part, preferred_element_type=f32)
    active = tanh_gelu(hidden_pre).astype(bf16)
    grad_active = contract_cols(grad_out_group, proj_part)
    _, gelu_pull = jax.vjp(tanh_gelu, hidden_pre)
    grad_pre = gelu_pull(grad_active)[0].astype(bf16)
    fc_parts = contract_rows(norm_two, grad_pre).astype(bf16).reshape(dp_count, ctx_count, piece, width)
    proj_parts = contract_rows(active, grad_out_group).astype(bf16).reshape(dp_count, ctx_count, -1, width)
    grad_pre, fc_parts, proj_parts = lax.optimization_barrier((grad_pre, fc_parts, proj_parts))
    fc_dp = dp_scatter(fc_parts)
    proj_dp = dp_scatter(proj_parts)
    grad_norm_parts = contract_cols(grad_pre, fc_part).astype(bf16)
    grad_norm_two = exchange_sum(grad_norm_parts.reshape(seg_count, rows, width), "sp")
    _, second_pull = jax.vjp(layer_norm, mixed, gain_two)
    grad_mixed_norm, second_gain_grad = second_pull(grad_norm_two)
    grad_out = jnp.where(is_valid, cotangent[0], jnp.zeros_like(cotangent[0])).astype(f32)
    grad_mixed = grad_out + grad_mixed_norm
    grad_branch = lax.all_gather(grad_mixed.astype(bf16), "sp", axis=0, tiled=True)

    out_wide = jnp.pad(out_part.reshape(heads, HD, width), ((0, 0), (HD, 0), (0, 0))).reshape(heads * LANES, width)
    grad_wide = contract_cols(grad_branch, out_wide).astype(bf16)
    out_mine = contract_rows(attended, grad_branch).astype(bf16)
    grad_wide, fc_dp, out_mine = lax.optimization_barrier((grad_wide, fc_dp, out_mine))
    out_sum = dp_sum(out_mine)
    fc_came = lax.all_to_all(fc_dp, "ctx", split_axis=0, concat_axis=0, tiled=True)
    query_grads, pair_grads = attend_back(query_wide, grad_wide, pairs, prob)
    query_grads, pair_grads, fc_came, proj_dp, out_sum = lax.optimization_barrier(
        (query_grads, pair_grads, fc_came, proj_dp, out_sum)
    )
    pair_mine = lax.psum_scatter(pair_grads, "ctx", scatter_dimension=0, tiled=False)
    late = jnp.concatenate([proj_dp, out_sum.reshape(ctx_count, -1, width)], axis=1)

    def total(came):
        return jnp.sum(came.astype(f32), axis=0).astype(bf16)

    late, active_late = lax.optimization_barrier((late, active))
    late_came = lax.all_to_all(late, "ctx", split_axis=0, concat_axis=0, tiled=True)
    expanded = exchange_sum(
        jnp.dot(active_late, proj_part, preferred_element_type=f32).astype(bf16).reshape(seg_count, rows, width), "sp"
    )
    big = jnp.concatenate([total(fc_came), total(late_came)], axis=0)
    norm_t = jnp.transpose(norm_one)
    gain_cols = jnp.stack([gain_one, second_gain_grad], axis=1)
    pair_mine, big, expanded, norm_t, gain_cols = lax.optimization_barrier(
        (pair_mine, big, expanded, norm_t, gain_cols)
    )
    output = jnp.where(is_valid, mixed + expanded, 0.0).astype(bf16)[None]
    big_all = lax.all_gather(big, ("sp", "ctx"), axis=0, tiled=False).reshape(seg_count, ctx_count, -1, width)
    proj_piece = hidden // (seg_count * dp_count * ctx_count)
    both = piece + proj_piece

    small, grad_norm_part = finish(norm_t, pair_mine, query_grads, key_score, all_in, gain_cols)
    small_own = exchange_sum(
        dp_scatter(small.reshape(dp_count, ctx_count, piece, wide)), "ctx"
    ).astype(bf16)
    small_own, big_all, grad_norm_part = lax.optimization_barrier((small_own, big_all, grad_norm_part))
    grad_norm_one = exchange_sum(grad_norm_part.reshape(seg_count, rows, width), "sp")
    _, first_pull = jax.vjp(lambda values: layer_norm(values, gain_one), inputs)
    grad_input_norm = first_pull(grad_norm_one)[0]
    input_grad = (grad_mixed + grad_input_norm).astype(bf16)[None]

    small_all = lax.all_gather(small_own, ("sp", "ctx"), axis=0, tiled=False).reshape(
        seg_count, ctx_count * piece, wide
    )
    groups = range(seg_count)
    fc_grad = jnp.concatenate(
        [
            big_all[at, :, :piece, part * hidden_part : (part + 1) * hidden_part].reshape(-1, hidden_part)
            for part in range(dp_count)
            for at in groups
        ],
        axis=1,
    ).astype(f32)
    proj_grad = big_all[:, :, piece:both].reshape(hidden // dp_count, width).astype(f32)
    out_grad = lax.dynamic_slice_in_dim(
        big_all[:, :, both:].reshape(width, width), dp_at * (width // dp_count), width // dp_count, 0
    ).astype(f32)
    qkv_grad, score_grad = unpack(small_all, heads)
    gains = jnp.sum(small_all[:, :, head_cols + heads : head_cols + heads + 2].astype(f32), axis=0)
    return (output, input_grad, gains[:, 0], qkv_grad, score_grad, out_grad, gains[:, 1], fc_grad, proj_grad)


def solution(mesh):
    placed = (
        P("dp", ("sp", "ctx"), None),
        P("dp", ("sp", "ctx"), None),
        P("dp"),
        P("dp", None, "ctx", "sp", None),
        P("dp"),
        P("dp", None),
        P("dp", None),
        P("dp", None),
        P("dp"),
        P("dp", None),
        P("dp", None),
    )
    return jax.shard_map(
        per_device,
        mesh=mesh,
        in_specs=placed,
        out_specs=(
            P("dp", ("sp", "ctx"), None),
            P("dp", ("sp", "ctx"), None),
            P("dp"),
            P("dp", None),
            P("dp", None),
            P("dp", None),
            P("dp"),
            P("dp", None),
            P("dp", None),
        ),
        check_vma=False,
    )
```

```python
import functools

import jax
import jax.numpy as jnp
from jax import lax
from jax.experimental import pallas as pl
from jax.experimental.pallas import tpu as pltpu
from jax.sharding import PartitionSpec as P

H = 12
HD = 64
WIN = 64
LANES = 128
SLOT = 2048


EPSILON = 1e-05


def layer_norm(values, gain):
    mean_value = jnp.mean(values, axis=-1, keepdims=True)
    centred = values - mean_value
    variance = jnp.mean(centred * centred, axis=-1, keepdims=True)
    return centred * lax.rsqrt(variance + EPSILON) * gain


def tanh_gelu(values):
    return jax.nn.gelu(values, approximate=True)


def contract_rows(left, right):
    return lax.dot_general(
        left, right, (((0,), (0,)), ((), ())), preferred_element_type=jnp.float32
    )


def contract_cols(left, right):
    return lax.dot_general(
        left, right, (((1,), (1,)), ((), ())), preferred_element_type=jnp.float32
    )


NT = (((1,), (1,)), ((), ()))


PAD_ROWS = 16


def slot_order(src_ref, kv_ref):
    count, height, _ = src_ref.shape
    for tile in range(kv_ref.shape[0] // LANES):
        part, at = divmod(tile, count)
        kv_ref[tile * LANES : (tile + 1) * LANES, :] = src_ref[at, part * LANES : (part + 1) * LANES, :]


def slot_gates(src_ref, gate_ref):
    count, height, _ = src_ref.shape
    for at in range(count):
        scores = src_ref[at, height - PAD_ROWS :, :].astype(jnp.float32)
        gates = -jnp.log1p(jnp.exp(-scores))
        for part in range(gate_ref.shape[1] // LANES // count):
            tile = part * count + at
            gate_ref[:, tile * LANES : (tile + 1) * LANES] = jnp.broadcast_to(gates[part : part + 1, :], (8, LANES))


def attend_body(first, tiles, base, idx_ref, q_ref, src_ref, out_ref, prob_ref, score_ref, pair_ref, kv_ref, gate_ref):
    rows = q_ref.shape[0]
    if first:
        slot_order(src_ref, kv_ref)
        slot_gates(src_ref, gate_ref)
    span = tiles * LANES
    f32, bf16 = jnp.float32, jnp.bfloat16
    score_ref[:, :span] = (
        lax.dot_general(q_ref[...], kv_ref[:span, :], NT, preferred_element_type=f32) * HD ** (-0.5)
        + gate_ref[0:1, :span]
    )
    kept = idx_ref[0, 0]
    pair_ref[...] = jnp.concatenate([kept, kept], axis=1)
    wide = 8 * HD
    sub = lax.broadcasted_iota(jnp.int32, (8, wide), 0)
    lane = lax.broadcasted_iota(jnp.int32, (8, wide), 1)
    own = (lane // HD) == sub
    subf = sub.astype(f32)
    ahead = lax.broadcasted_iota(jnp.int32, (8, LANES), 0) - lax.broadcasted_iota(jnp.int32, (8, LANES), 1)
    near_from = max(0, tiles - 5)

    def eight(start):
        four = pair_ref[pl.ds(start, 8), :]
        index = jnp.concatenate([four] * 4, axis=1)
        pos = base + start + sub
        high = jnp.where(own & (pos >= WIN), index >> 7, -2).astype(f32)
        low = jnp.sum(jnp.where(own, (index & 127).astype(f32), 0.0), axis=0, keepdims=True) - subf
        high_pair = jnp.concatenate([high, high - 1.0], axis=0).astype(bf16)
        low_pair = jnp.concatenate([low, low - 8.0], axis=0).astype(bf16)
        one, zero = jnp.ones((), bf16), jnp.zeros((), bf16)
        left = jnp.concatenate(
            [jnp.where(high_pair == jnp.array(2 * p, bf16), one, zero) for p in range(tiles // 2)], axis=0
        )
        right = jnp.concatenate(
            [jnp.where(low_pair == jnp.array(16 * p, bf16), one, zero) for p in range(8)], axis=0
        )
        count = lax.dot_general(left, right, NT, preferred_element_type=f32)
        gap = ahead + (base + start)
        masked, counts = [], []
        largest = None
        for tile in range(tiles):
            number = count[8 * tile : 8 * tile + 8, :]
            if tile >= near_from:
                far = gap - tile * LANES
                number = number + jnp.where((far >= 0) & (far < WIN), 1.0, 0.0)
            value = jnp.where(number > 0.0, score_ref[pl.ds(start, 8), tile * LANES : (tile + 1) * LANES], -1e30)
            counts.append(number)
            masked.append(value)
            largest = value if largest is None else jnp.maximum(largest, value)
        top = jnp.max(largest, axis=1, keepdims=True)
        total = None
        expos = []
        for number, value in zip(counts, masked):
            expo = jnp.exp(value - top) * number
            expos.append(expo)
            total = expo if total is None else total + expo
        inverse = 1.0 / jnp.sum(total, axis=1, keepdims=True)
        return [expo * inverse for expo in expos]

    def step(index, carry):
        start = pl.multiple_of(index * 16, 16)
        first, second = eight(start), eight(start + 8)
        for tile in range(tiles):
            prob_ref[0, 0, pl.ds(start, 16), tile * LANES : (tile + 1) * LANES] = jnp.concatenate(
                [first[tile], second[tile]], axis=0
            ).astype(bf16)
        return carry

    lax.fori_loop(0, rows // 16, step, 0)
    both = jnp.dot(prob_ref[0, 0, :, :span], kv_ref[:span, :], preferred_element_type=f32)
    out_ref[0] = jnp.transpose(both)[HD:, :].astype(bf16)


def attend_kernel(parts, chunk, base_ref, *refs):
    part = pl.program_id(1)
    base = base_ref[0] + part * chunk
    for at in range(parts):
        pl.when(part == at)(
            functools.partial(attend_body, at == 0, (at + 1) * chunk // LANES, base, *refs)
        )


def attend(base, kept, query, pairs):
    heads, parts, block, keep = kept.shape
    count, height, _ = pairs.shape
    slot = count * (height - PAD_ROWS)
    chunk = slot // parts
    grid_spec = pltpu.PrefetchScalarGridSpec(
        num_scalar_prefetch=1,
        grid=(heads, parts),
        in_specs=[
            pl.BlockSpec((1, 1, block, keep), lambda h, r, b: (h, r, 0, 0)),
            pl.BlockSpec((block, LANES), lambda h, r, b: (r, h)),
            pl.BlockSpec((count, height, LANES), lambda h, r, b: (0, 0, h)),
        ],
        out_specs=[
            pl.BlockSpec((1, HD, block), lambda h, r, b: (h, 0, r)),
            pl.BlockSpec((1, 1, block, slot), lambda h, r, b: (h, r, 0, 0)),
        ],
        scratch_shapes=[
            pltpu.VMEM((block, slot), jnp.float32),
            pltpu.VMEM((block, 2 * keep), jnp.int32),
            pltpu.VMEM((slot, LANES), jnp.bfloat16),
            pltpu.VMEM((8, slot), jnp.float32),
        ],
    )
    return pl.pallas_call(
        functools.partial(attend_kernel, parts, chunk),
        grid_spec=grid_spec,
        out_shape=[
            jax.ShapeDtypeStruct((heads, HD, parts * block), jnp.bfloat16),
            jax.ShapeDtypeStruct((heads, parts, block, slot), jnp.bfloat16),
        ],
        name="attend",
    )(base, kept, query, pairs)


def attend_back_body(first, last, tiles, chunk, q_ref, grad_ref, src_ref, prob_ref, dq_ref, out_ref, turned_ref, dq_turned_ref, gates_ref, raw_ref, kv_ref, dkv_ref, gate_ref):
    f32, bf16 = jnp.float32, jnp.bfloat16
    rows = q_ref.shape[0]
    steps = tiles * LANES // chunk
    if first:
        slot_order(src_ref, kv_ref)
        dkv_ref[...] = jnp.zeros_like(dkv_ref)
        gate_ref[...] = jnp.zeros_like(gate_ref)
    dot_sum = None
    for at in range(steps):
        cols = slice(at * chunk, (at + 1) * chunk)
        raw = lax.dot_general(grad_ref[...], kv_ref[cols, :], NT, preferred_element_type=f32)
        raw_ref[:, cols] = raw
        part = jnp.sum(raw * prob_ref[0, 0, :, cols].astype(f32), axis=1, keepdims=True)
        dot_sum = part if dot_sum is None else dot_sum + part
    lane = lax.broadcasted_iota(jnp.int32, (rows, LANES), 1)
    scaled = jnp.where(lane == HD, 1.0, q_ref[...].astype(f32) * HD ** (-0.5))
    query_t = jnp.transpose(scaled)[: HD + 16].astype(bf16)
    grad_t = jnp.transpose(grad_ref[...].astype(f32))[HD:].astype(bf16)
    dq = None
    for at in range(steps):
        cols = slice(at * chunk, (at + 1) * chunk)
        prob = prob_ref[0, 0, :, cols]
        grad_score = (prob.astype(f32) * (raw_ref[:, cols] - dot_sum)).astype(bf16)
        piece = jnp.dot(grad_score, kv_ref[cols, :], preferred_element_type=f32)
        dq = piece if dq is None else dq + piece
        keys = jnp.dot(query_t, grad_score, preferred_element_type=f32)
        dkv_ref[:HD, cols] += keys[:HD]
        gate_ref[:, cols] += keys[HD : HD + 8]
        dkv_ref[HD:, cols] += jnp.dot(grad_t, prob, preferred_element_type=f32)
    dq = dq * HD ** (-0.5)
    dq_ref[...] = dq.astype(dq_ref.dtype)
    dq_turned_ref[0] = jnp.transpose(dq)[:HD, :].astype(bf16)
    if last:
        turned_ref[0] = dkv_ref[...].astype(bf16)
        gates_ref[0] = gate_ref[...]
        count, height, _ = out_ref.shape
        parts = (height - PAD_ROWS) // LANES
        for at in range(count):
            rows_of = []
            for part in range(parts):
                cols = slice((part * count + at) * LANES, (part * count + at + 1) * LANES)
                out_ref[at, part * LANES : (part + 1) * LANES, :] = jnp.transpose(dkv_ref[:, cols]).astype(bf16)
                rows_of.append(gate_ref[0:1, cols])
            rows_of.append(jnp.zeros((PAD_ROWS - parts, LANES), f32))
            out_ref[at, height - PAD_ROWS :, :] = jnp.concatenate(rows_of, axis=0).astype(bf16)


def attend_back_kernel(parts, chunk, *refs):
    part = pl.program_id(1)
    for at in range(parts):
        pl.when(part == at)(
            functools.partial(attend_back_body, at == 0, at == parts - 1, (at + 1) * chunk // LANES, chunk, *refs)
        )


def attend_back(query, grad, pairs, prob):
    heads, parts, block, slot = prob.shape
    count, height, width = pairs.shape
    chunk = slot // parts
    return pl.pallas_call(
        functools.partial(attend_back_kernel, parts, chunk),
        grid=(heads, parts),
        in_specs=[
            pl.BlockSpec((block, LANES), lambda h, r: (r, h)),
            pl.BlockSpec((block, LANES), lambda h, r: (r, h)),
            pl.BlockSpec((count, height, LANES), lambda h, r: (0, 0, h)),
            pl.BlockSpec((1, 1, block, slot), lambda h, r: (h, r, 0, 0)),
        ],
        out_specs=[
            pl.BlockSpec((block, LANES), lambda h, r: (r, h)),
            pl.BlockSpec((count, height, LANES), lambda h, r: (0, 0, h)),
            pl.BlockSpec((1, LANES, slot), lambda h, r: (h, 0, 0)),
            pl.BlockSpec((1, HD, block), lambda h, r: (h, 0, r)),
            pl.BlockSpec((1, 8, slot), lambda h, r: (h, 0, 0)),
        ],
        out_shape=[
            jax.ShapeDtypeStruct((parts * block, heads * LANES), jnp.bfloat16),
            jax.ShapeDtypeStruct((count, height, width), jnp.bfloat16),
            jax.ShapeDtypeStruct((heads, LANES, slot), jnp.bfloat16),
            jax.ShapeDtypeStruct((heads, HD, parts * block), jnp.bfloat16),
            jax.ShapeDtypeStruct((heads, 8, slot), jnp.float32),
        ],
        scratch_shapes=[
            pltpu.VMEM((block, slot), jnp.float32),
            pltpu.VMEM((slot, LANES), jnp.bfloat16),
            pltpu.VMEM((LANES, slot), jnp.float32),
            pltpu.VMEM((8, slot), jnp.float32),
        ],
        name="attend_back",
    )(query, grad, pairs, prob)


def weight_kernel(turned_ref, dq_ref, gates_ref, score_ref, slot_ref, norm_ref, in_ref, gain_ref, out_ref):
    f32, bf16 = jnp.float32, jnp.bfloat16
    heads, _, slot = turned_ref.shape
    wide = in_ref.shape[1]
    width = slot_ref.shape[1]
    total = jnp.concatenate([gates_ref[head, 0:1, :] for head in range(heads)], axis=0)
    total = total * jax.nn.sigmoid(-score_ref[...].astype(f32))
    total = jnp.concatenate([total, jnp.zeros((PAD_ROWS - heads, slot), f32)], axis=0).astype(bf16)
    turned = [
        jnp.dot(turned_ref[...].reshape(heads * LANES, slot), slot_ref[...], preferred_element_type=f32),
        jnp.dot(dq_ref[...].reshape(heads * HD, -1), norm_ref[...], preferred_element_type=f32),
        jnp.dot(total, slot_ref[...], preferred_element_type=f32),
        jnp.zeros((wide - heads * 3 * HD - PAD_ROWS, width), f32),
    ]
    small = jnp.transpose(jnp.concatenate(turned, axis=0))
    gain_grad = jnp.sum(small * in_ref[...].astype(f32), axis=1, keepdims=True) / gain_ref[:, 0:1]
    lane = lax.broadcasted_iota(jnp.int32, small.shape, 1)
    at = heads * 3 * HD + heads
    small = jnp.where(lane == at, gain_grad, jnp.where(lane == at + 1, gain_ref[:, 1:2], small))
    out_ref[:, :wide] = small.astype(bf16)
    out_ref[:, wide:] = jnp.zeros((width, width - wide), bf16)


def weight_grad(turned, dq, gates, score, norm_slot, norm_one, weights, gains):
    width = norm_one.shape[1]
    return pl.pallas_call(
        weight_kernel,
        out_shape=jax.ShapeDtypeStruct((width, width), jnp.bfloat16),
        name="weight_grad",
    )(turned, dq, gates, score, norm_slot, norm_one, weights, gains)


def finish_kernel(heads, pair_ref, dq_ref, score_ref, in_ref, grad_ref):
    f32, bf16 = jnp.float32, jnp.bfloat16
    group = dq_ref.shape[0]
    parts = group // LANES
    wide = in_ref.shape[1]
    gates = pair_ref[group:, :].astype(f32)
    total = jnp.concatenate(
        [
            jnp.concatenate([gates[at : at + 1, head * LANES : (head + 1) * LANES] for at in range(parts)], axis=1)
            for head in range(heads)
        ],
        axis=0,
    )
    total = total * jax.nn.sigmoid(-score_ref[...].astype(f32))
    scores = jnp.transpose(jnp.concatenate([total, jnp.zeros((LANES - heads, group), f32)], axis=0))
    rest = wide - heads * 3 * HD
    columns = jnp.concatenate(
        [pair_ref[:group, :].astype(f32)]
        + [dq_ref[:, head * LANES : head * LANES + HD].astype(f32) for head in range(heads)]
        + [scores[:, :rest]],
        axis=1,
    ).astype(bf16)
    grad_ref[...] = lax.dot_general(columns, in_ref[...], NT, preferred_element_type=f32).astype(bf16)


def finish(pair, dq, score, weights):
    return pl.pallas_call(
        functools.partial(finish_kernel, score.shape[0]),
        out_shape=jax.ShapeDtypeStruct((dq.shape[0], weights.shape[0]), jnp.bfloat16),
        name="finish",
    )(pair, dq, score, weights)


def unpack_kernel(groups, heads, piece, parts, all_ref, qkv_ref, score_ref, fc_ref, proj_ref):
    f32 = jnp.float32
    keys = heads * 2 * HD
    part_cols = fc_ref.shape[1] // (groups * parts)
    for step in range(all_ref.shape[1]):
        rows = slice(step * piece, (step + 1) * piece)
        for at in range(groups):
            values = all_ref[at, step, :piece, :].astype(f32)
            for head in range(heads):
                start = (at * heads + head) * 3 * HD
                qkv_ref[rows, start : start + HD] = values[:, keys + head * HD : keys + (head + 1) * HD]
                qkv_ref[rows, start + HD : start + 3 * HD] = values[:, head * 2 * HD : (head + 1) * 2 * HD]
            score_ref[rows, at * heads : (at + 1) * heads] = values[:, keys + heads * HD : keys + heads * HD + heads]
            values = all_ref[at, step, piece : 2 * piece, :].astype(f32)
            for part in range(parts):
                start = (part * groups + at) * part_cols
                fc_ref[rows, start : start + part_cols] = values[:, part * part_cols : (part + 1) * part_cols]
            proj_ref[at, step] = all_ref[at, step, 2 * piece : 2 * piece + proj_ref.shape[2], :].astype(f32)


def unpack(gathered, heads, piece, proj_piece, parts, hidden):
    groups, count, rows, width = gathered.shape
    step = 1 if piece % 16 == 0 else count
    return pl.pallas_call(
        functools.partial(unpack_kernel, groups, heads, piece, parts),
        grid=(count // step,),
        in_specs=[pl.BlockSpec((groups, step, rows, width), lambda c: (0, c, 0, 0))],
        out_specs=[
            pl.BlockSpec((step * piece, groups * heads * 3 * HD), lambda c: (c, 0)),
            pl.BlockSpec((step * piece, groups * heads), lambda c: (c, 0)),
            pl.BlockSpec((step * piece, hidden), lambda c: (c, 0)),
            pl.BlockSpec((groups, step, proj_piece, width), lambda c: (0, c, 0, 0)),
        ],
        out_shape=[
            jax.ShapeDtypeStruct((count * piece, groups * heads * 3 * HD), jnp.float32),
            jax.ShapeDtypeStruct((count * piece, groups * heads), jnp.float32),
            jax.ShapeDtypeStruct((count * piece, hidden), jnp.float32),
            jax.ShapeDtypeStruct((groups, count, proj_piece, width), jnp.float32),
        ],
        name="unpack",
    )(gathered)


def arrange_kernel(heads, rows, qkv_ref, score_ref, gains_ref, out_ref):
    f32 = jnp.float32
    values = qkv_ref[...].astype(f32)
    keys = heads * 2 * HD
    width = out_ref.shape[1]
    pieces = [values[:, (3 * head + 1) * HD : (3 * head + 3) * HD] for head in range(heads)]
    pieces += [values[:, 3 * head * HD : (3 * head + 1) * HD] for head in range(heads)]
    pieces += [score_ref[...].astype(f32), jnp.zeros((rows, width - heads * 3 * HD - heads), f32)]
    out_ref[:rows, :] = jnp.concatenate(pieces, axis=1).astype(out_ref.dtype)
    out_ref[rows:, :] = jnp.concatenate(
        [gains_ref[...].astype(f32), jnp.zeros((gains_ref.shape[0], width - rows), f32)], axis=1
    ).astype(out_ref.dtype)


def arrange(qkv, score, gains, width):
    rows, heads = score.shape
    return pl.pallas_call(
        functools.partial(arrange_kernel, heads, rows),
        out_shape=jax.ShapeDtypeStruct((rows + PAD_ROWS, width), qkv.dtype),
        name="arrange",
    )(qkv, score, gains)


def dp_send(mine):
    if lax.axis_size("dp") != 2:
        return lax.all_gather(mine, "dp", axis=0, tiled=True)
    return lax.ppermute(mine, "dp", [(0, 1), (1, 0)])


def dp_join(mine, came):
    if lax.axis_size("dp") != 2:
        return came
    return jnp.where(
        lax.axis_index("dp") == 0, jnp.concatenate([mine, came]), jnp.concatenate([came, mine])
    )


def dp_scatter(parts):
    if lax.axis_size("dp") != 2:
        return lax.psum_scatter(parts, "dp", scatter_dimension=0, tiled=False)
    at = lax.axis_index("dp")
    mine = lax.dynamic_index_in_dim(parts, at, 0, keepdims=False)
    sent = lax.dynamic_index_in_dim(parts, 1 - at, 0, keepdims=False)
    other = lax.ppermute(sent, "dp", [(0, 1), (1, 0)])
    return (mine.astype(jnp.float32) + other.astype(jnp.float32)).astype(parts.dtype)


def group_rows_of(mine, group, count):
    height = mine.shape[0]
    if lax.axis_size("dp") != 2 or height % count != 0:
        whole = lax.all_gather(mine, "dp", axis=0, tiled=True)
        return lax.dynamic_slice_in_dim(whole, group * count, count, 0)
    near = lax.dynamic_slice_in_dim(mine, group * count % height, count, 0)
    far = lax.ppermute(near, "dp", [(0, 1), (1, 0)])
    return jnp.where(lax.axis_index("dp") == group * count // height, near, far)


def dp_sum(mine):
    if lax.axis_size("dp") != 2:
        return lax.psum(mine, "dp")
    other = lax.ppermute(mine, "dp", [(0, 1), (1, 0)])
    return (mine.astype(jnp.float32) + other.astype(jnp.float32)).astype(mine.dtype)


def exchange_sum(parts, axis):
    came = lax.all_to_all(parts, axis, split_axis=0, concat_axis=0, tiled=True)
    return jnp.sum(came.astype(jnp.float32), axis=0)


def per_device(
    tokens,
    cotangent,
    lengths,
    kept_keys,
    first_gain,
    qkv_weight,
    score_weight,
    out_weight,
    second_gain,
    fc_weight,
    proj_weight,
):
    f32, bf16 = jnp.float32, jnp.bfloat16
    dp_count = lax.axis_size("dp")
    seg_count = lax.axis_size("sp")
    ctx_count = lax.axis_size("ctx")
    dp_at = lax.axis_index("dp")
    sp_at = lax.axis_index("sp")
    ctx_at = lax.axis_index("ctx")
    rows = tokens.shape[1]
    width = tokens.shape[2]
    group_rows = seg_count * rows
    heads = H // seg_count
    head_cols = heads * 3 * HD
    hidden = fc_weight.shape[1]
    hidden_part = hidden // (dp_count * seg_count)
    piece = width // (dp_count * ctx_count)

    keys = heads * 2 * HD
    wide = -(-(head_cols + heads + 2) // LANES) * LANES
    weight_rows = width // dp_count
    own_in = arrange(
        lax.dynamic_slice_in_dim(qkv_weight, sp_at * head_cols, head_cols, 1),
        lax.dynamic_slice_in_dim(score_weight, sp_at * heads, heads, 1),
        jnp.pad(jnp.stack([first_gain, second_gain]), ((0, PAD_ROWS - 2), (0, 0))),
        wide,
    )
    if dp_count == 2:
        other_in = lax.ppermute(own_in, "dp", [(0, 1), (1, 0)])
        parts_in = [
            jnp.where(dp_at == at, own_in, other_in) for at in range(dp_count)
        ]
    else:
        parts_in = list(lax.all_gather(own_in, "dp", axis=0, tiled=False))
    tokens_group = lax.all_gather(tokens[0], "sp", axis=0, tiled=True)
    all_in = jnp.concatenate([part[:weight_rows] for part in parts_in])
    gain_one = jnp.concatenate([part[weight_rows, :weight_rows] for part in parts_in]).astype(f32)
    gain_two = jnp.concatenate([part[weight_rows + 1, :weight_rows] for part in parts_in]).astype(f32)

    fc_own = jnp.concatenate(
        [
            lax.dynamic_slice_in_dim(fc_weight, (at * seg_count + sp_at) * hidden_part, hidden_part, 1)
            for at in range(dp_count)
        ],
        axis=1,
    )
    proj_own = lax.dynamic_slice_in_dim(proj_weight, sp_at * hidden_part, hidden_part, 0)
    all_in, out_own, fc_own, proj_own = lax.optimization_barrier((all_in, out_weight, fc_own, proj_own))
    out_came = dp_send(out_own)
    fc_came = dp_send(fc_own)
    proj_came = dp_send(proj_own)

    inputs = tokens[0].astype(f32)
    inputs_group = tokens_group.astype(f32)
    norm_one = layer_norm(inputs_group, gain_one).astype(bf16)
    qkv_rows = jnp.dot(norm_one, all_in, preferred_element_type=f32).astype(bf16)
    score_weight_part = all_in[:, head_cols : head_cols + heads]
    key_score = lax.dot_general(
        score_weight_part, norm_one, (((0,), (1,)), ((), ())), preferred_element_type=f32
    ).astype(bf16)
    score_rows = jnp.transpose(key_score.reshape(heads, seg_count, rows), (1, 0, 2)).reshape(
        seg_count, heads * rows
    )
    pairs_own = jnp.concatenate(
        [qkv_rows[:, :keys], jnp.pad(score_rows, ((0, PAD_ROWS - seg_count), (0, 0)))], axis=0
    )
    query_wide = jnp.pad(
        qkv_rows[:, keys:head_cols].reshape(group_rows, heads, HD), ((0, 0), (0, 0), (0, HD))
    ).reshape(group_rows, heads * LANES)
    kept = jnp.transpose(kept_keys[0], (2, 0, 1, 3))
    base = (ctx_at * rows).astype(jnp.int32)[None]
    cot_own, pairs_own = lax.optimization_barrier((cotangent[0], pairs_own))
    cot_group = lax.all_gather(cot_own, "sp", axis=0, tiled=True)
    pairs = lax.all_gather(pairs_own, "ctx", axis=0, tiled=False)
    norm_own = lax.dynamic_slice_in_dim(norm_one, sp_at * rows, rows, 0)
    query_wide, cot_group, out_came, fc_came, proj_came, norm_own, pairs = lax.optimization_barrier(
        (query_wide, cot_group, out_came, fc_came, proj_came, norm_own, pairs)
    )
    norm_slot = lax.all_gather(norm_own, ("sp", "ctx"), axis=0, tiled=True)
    head_outs, prob = attend(base, kept, query_wide, pairs)
    head_outs, norm_slot = lax.optimization_barrier((head_outs, norm_slot))
    attended = head_outs.reshape(heads * HD, group_rows)
    attended_all = lax.all_gather(attended, "sp", axis=0, tiled=True)
    out_full = dp_join(out_own, out_came)
    out_part = lax.dynamic_slice_in_dim(out_full, sp_at * heads * HD, heads * HD, 0)
    fc_part = dp_join(fc_own, fc_came)
    proj_part = dp_join(proj_own, proj_came)

    group_at = jnp.arange(group_rows, dtype=jnp.int32)
    group_positions = (group_at // rows) * (ctx_count * rows) + ctx_at * rows + group_at % rows
    grad_out_group = jnp.where((group_positions < lengths[0])[:, None], cot_group, jnp.zeros_like(cot_group))
    positions = (sp_at * ctx_count + ctx_at) * rows + jnp.arange(rows, dtype=jnp.int32)
    is_valid = (positions < lengths[0])[:, None]

    mixed_group = inputs_group + contract_rows(attended_all, out_full)
    norm_two = layer_norm(mixed_group, gain_two).astype(bf16)
    mixed = lax.dynamic_slice_in_dim(mixed_group, sp_at * rows, rows, 0)
    hidden_pre = jnp.dot(norm_two, fc_part, preferred_element_type=f32)
    active = tanh_gelu(hidden_pre).astype(bf16)
    grad_active = contract_cols(grad_out_group, proj_part)
    _, gelu_pull = jax.vjp(tanh_gelu, hidden_pre)
    grad_pre = gelu_pull(grad_active)[0].astype(bf16)
    fc_parts = contract_rows(norm_two, grad_pre).astype(bf16).reshape(dp_count, ctx_count, piece, width)
    proj_parts = contract_rows(active, grad_out_group).astype(bf16).reshape(dp_count, ctx_count, -1, width)
    grad_pre, fc_parts, proj_parts = lax.optimization_barrier((grad_pre, fc_parts, proj_parts))
    mlp_dp = dp_scatter(jnp.concatenate([fc_parts, proj_parts], axis=2))
    grad_norm_parts = contract_cols(grad_pre, fc_part).astype(bf16)
    grad_norm_two = exchange_sum(grad_norm_parts.reshape(seg_count, rows, width), "sp")
    _, second_pull = jax.vjp(layer_norm, mixed, gain_two)
    grad_mixed_norm, second_gain_grad = second_pull(grad_norm_two)
    grad_out = jnp.where(is_valid, cotangent[0], jnp.zeros_like(cotangent[0])).astype(f32)
    grad_mixed = grad_out + grad_mixed_norm
    grad_branch = lax.all_gather(grad_mixed.astype(bf16), "sp", axis=0, tiled=True)

    out_wide = jnp.pad(out_part.reshape(heads, HD, width), ((0, 0), (HD, 0), (0, 0))).reshape(heads * LANES, width)
    grad_wide = contract_cols(grad_branch, out_wide).astype(bf16)
    out_mine = jnp.dot(attended, grad_branch, preferred_element_type=f32).astype(bf16)
    grad_wide, mlp_dp, out_mine = lax.optimization_barrier((grad_wide, mlp_dp, out_mine))
    out_sum = dp_sum(out_mine)
    mlp_came = lax.all_to_all(mlp_dp, "ctx", split_axis=0, concat_axis=0, tiled=True)
    score_slot = jnp.transpose(
        pairs[:, group_rows : group_rows + seg_count].reshape(ctx_count, seg_count, heads, rows), (2, 1, 0, 3)
    ).reshape(heads, -1)
    gain_cols = jnp.stack([gain_one, second_gain_grad], axis=1)
    grad_wide, score_slot, gain_cols = lax.optimization_barrier((grad_wide, score_slot, gain_cols))
    query_grads, pair_grads, turned, query_turned, gates = attend_back(query_wide, grad_wide, pairs, prob)
    pair_mine = lax.psum_scatter(pair_grads, "ctx", scatter_dimension=0, tiled=False)
    small = weight_grad(turned, query_turned, gates, score_slot, norm_slot, norm_one, all_in, gain_cols)
    small, mlp_came, out_sum = lax.optimization_barrier((small, mlp_came, out_sum))
    late = jnp.concatenate(
        [dp_scatter(small.reshape(dp_count, ctx_count, piece, width)), out_sum.reshape(ctx_count, -1, width)], axis=1
    )
    late_sum = exchange_sum(late, "ctx").astype(bf16)
    mlp_sum = jnp.sum(mlp_came.astype(f32), axis=0).astype(bf16)
    gradients = jnp.concatenate([late_sum[:piece], mlp_sum, late_sum[piece:]], axis=0)
    pair_mine, gradients, active_late = lax.optimization_barrier((pair_mine, gradients, active))
    gathered = lax.all_gather(gradients, ("sp", "ctx"), axis=0, tiled=False).reshape(seg_count, ctx_count, -1, width)
    proj_piece = hidden // (seg_count * dp_count * ctx_count)

    grad_norm_part = finish(pair_mine, query_grads, key_score, all_in)
    expanded = exchange_sum(
        jnp.dot(active_late, proj_part, preferred_element_type=f32).astype(bf16).reshape(seg_count, rows, width), "sp"
    )
    output = jnp.where(is_valid, mixed + expanded, 0.0).astype(bf16)[None]
    grad_norm_one = exchange_sum(grad_norm_part.reshape(seg_count, rows, width), "sp")
    _, first_pull = jax.vjp(lambda values: layer_norm(values, gain_one), inputs)
    grad_input_norm = first_pull(grad_norm_one)[0]
    input_grad = (grad_mixed + grad_input_norm).astype(bf16)[None]

    qkv_grad, score_grad, fc_grad, proj_grad = unpack(gathered, heads, piece, proj_piece, dp_count, hidden)
    proj_grad = proj_grad.reshape(-1, width)
    out_grad = lax.dynamic_slice_in_dim(
        gathered[:, :, 2 * piece + proj_piece :].reshape(width, width), dp_at * weight_rows, weight_rows, 0
    ).astype(f32)
    gains = jnp.sum(
        gathered[:, :, :piece, head_cols + heads : head_cols + heads + 2].astype(f32), axis=0
    ).reshape(weight_rows, 2)
    return (output, input_grad, gains[:, 0], qkv_grad, score_grad, out_grad, gains[:, 1], fc_grad, proj_grad)


def solution(mesh):
    placed = (
        P("dp", ("sp", "ctx"), None),
        P("dp", ("sp", "ctx"), None),
        P("dp"),
        P("dp", None, "ctx", "sp", None),
        P("dp"),
        P("dp", None),
        P("dp", None),
        P("dp", None),
        P("dp"),
        P("dp", None),
        P("dp", None),
    )
    return jax.shard_map(
        per_device,
        mesh=mesh,
        in_specs=placed,
        out_specs=(
            P("dp", ("sp", "ctx"), None),
            P("dp", ("sp", "ctx"), None),
            P("dp"),
            P("dp", None),
            P("dp", None),
            P("dp", None),
            P("dp"),
            P("dp", None),
            P("dp", None),
        ),
        check_vma=False,
    )
```

```python
import functools

import jax
import jax.numpy as jnp
from jax import lax
from jax.experimental import pallas as pl
from jax.experimental.pallas import tpu as pltpu
from jax.sharding import PartitionSpec as P

H = 12
HD = 64
WIN = 64
LANES = 128
SLOT = 2048


EPSILON = 1e-05


def layer_norm(values, gain):
    mean_value = jnp.mean(values, axis=-1, keepdims=True)
    centred = values - mean_value
    variance = jnp.mean(centred * centred, axis=-1, keepdims=True)
    return centred * lax.rsqrt(variance + EPSILON) * gain


def tanh_gelu(values):
    return jax.nn.gelu(values, approximate=True)


def contract_rows(left, right):
    return lax.dot_general(
        left, right, (((0,), (0,)), ((), ())), preferred_element_type=jnp.float32
    )


def contract_cols(left, right):
    return lax.dot_general(
        left, right, (((1,), (1,)), ((), ())), preferred_element_type=jnp.float32
    )


NT = (((1,), (1,)), ((), ()))


PAD_ROWS = 16
STEP = 128


def attend_body(first, tiles, base, idx_ref, q_ref, kv_ref, key_ref, out_ref, prob_ref, score_ref, pair_ref, gate_ref):
    rows = q_ref.shape[0]
    if first:
        gate_ref[...] = jnp.broadcast_to(-jnp.log1p(jnp.exp(-key_ref[0].astype(jnp.float32))), gate_ref.shape)
    span = tiles * LANES
    f32, bf16 = jnp.float32, jnp.bfloat16
    score_ref[:, :span] = (
        lax.dot_general(q_ref[...], kv_ref[:span, :], NT, preferred_element_type=f32) * HD ** (-0.5)
        + gate_ref[0:1, :span]
    )
    kept = idx_ref[0, 0]
    pair_ref[...] = jnp.concatenate([kept, kept], axis=1)
    wide = 8 * HD
    sub = lax.broadcasted_iota(jnp.int32, (8, wide), 0)
    lane = lax.broadcasted_iota(jnp.int32, (8, wide), 1)
    own = (lane // HD) == sub
    subf = sub.astype(f32)
    ahead = lax.broadcasted_iota(jnp.int32, (8, LANES), 0) - lax.broadcasted_iota(jnp.int32, (8, LANES), 1)
    near_from = max(0, tiles - 5)

    def eight(start):
        four = pair_ref[pl.ds(start, 8), :]
        index = jnp.concatenate([four] * 4, axis=1)
        pos = base + start + sub
        high = jnp.where(own & (pos >= WIN), index >> 7, -2).astype(f32)
        low = jnp.sum(jnp.where(own, (index & 127).astype(f32), 0.0), axis=0, keepdims=True) - subf
        high_pair = jnp.concatenate([high, high - 1.0], axis=0).astype(bf16)
        low_pair = jnp.concatenate([low, low - 8.0], axis=0).astype(bf16)
        one, zero = jnp.ones((), bf16), jnp.zeros((), bf16)
        left = jnp.concatenate(
            [jnp.where(high_pair == jnp.array(2 * p, bf16), one, zero) for p in range(tiles // 2)], axis=0
        )
        right = jnp.concatenate(
            [jnp.where(low_pair == jnp.array(16 * p, bf16), one, zero) for p in range(8)], axis=0
        )
        count = lax.dot_general(left, right, NT, preferred_element_type=f32)
        gap = ahead + (base + start)
        masked, counts = [], []
        largest = None
        for tile in range(tiles):
            number = count[8 * tile : 8 * tile + 8, :]
            if tile >= near_from:
                far = gap - tile * LANES
                number = number + jnp.where((far >= 0) & (far < WIN), 1.0, 0.0)
            value = jnp.where(number > 0.0, score_ref[pl.ds(start, 8), tile * LANES : (tile + 1) * LANES], -1e30)
            counts.append(number)
            masked.append(value)
            largest = value if largest is None else jnp.maximum(largest, value)
        top = jnp.max(largest, axis=1, keepdims=True)
        total = None
        expos = []
        for number, value in zip(counts, masked):
            expo = jnp.exp(value - top) * number
            expos.append(expo)
            total = expo if total is None else total + expo
        inverse = 1.0 / jnp.sum(total, axis=1, keepdims=True)
        return [expo * inverse for expo in expos]

    def step(index, carry):
        for at in range(0, STEP, 16):
            start = pl.multiple_of(index * STEP + at, 16)
            near, next_to = eight(start), eight(start + 8)
            for tile in range(tiles):
                prob_ref[0, 0, pl.ds(start, 16), tile * LANES : (tile + 1) * LANES] = jnp.concatenate(
                    [near[tile], next_to[tile]], axis=0
                ).astype(bf16)
        return carry

    if rows == STEP:
        step(0, 0)
    else:
        lax.fori_loop(0, rows // STEP, step, 0)
    both = jnp.dot(prob_ref[0, 0, :, :span], kv_ref[:span, :], preferred_element_type=f32)
    out_ref[0] = jnp.transpose(both)[HD:, :].astype(bf16)


def attend_kernel(parts, chunk, base_ref, *refs):
    part = pl.program_id(1)
    base = base_ref[0] + part * chunk
    for at in range(parts):
        pl.when(part == at)(
            functools.partial(attend_body, at == 0, (at + 1) * chunk // LANES, base, *refs)
        )


def attend(base, kept, query, pairs, key_score):
    heads, parts, block, keep = kept.shape
    slot = pairs.shape[0]
    chunk = slot // parts
    grid_spec = pltpu.PrefetchScalarGridSpec(
        num_scalar_prefetch=1,
        grid=(heads, parts),
        in_specs=[
            pl.BlockSpec((1, 1, block, keep), lambda h, r, b: (h, r, 0, 0)),
            pl.BlockSpec((block, LANES), lambda h, r, b: (r, h)),
            pl.BlockSpec((slot, LANES), lambda h, r, b: (0, h)),
            pl.BlockSpec((1, 1, slot), lambda h, r, b: (h, 0, 0)),
        ],
        out_specs=[
            pl.BlockSpec((1, HD, block), lambda h, r, b: (h, 0, r)),
            pl.BlockSpec((1, 1, block, slot), lambda h, r, b: (h, r, 0, 0)),
        ],
        scratch_shapes=[
            pltpu.VMEM((block, slot), jnp.float32),
            pltpu.VMEM((block, 2 * keep), jnp.int32),
            pltpu.VMEM((8, slot), jnp.float32),
        ],
    )
    return pl.pallas_call(
        functools.partial(attend_kernel, parts, chunk),
        grid_spec=grid_spec,
        out_shape=[
            jax.ShapeDtypeStruct((heads, HD, parts * block), jnp.bfloat16),
            jax.ShapeDtypeStruct((heads, parts, block, slot), jnp.bfloat16),
        ],
        name="attend",
    )(base, kept, query, pairs, key_score)


def attend_back_body(first, last, tiles, chunk, q_ref, grad_ref, kv_ref, prob_ref, dq_ref, out_ref, turned_ref, dq_turned_ref, gates_ref, raw_ref, dkv_ref, gate_ref):
    f32, bf16 = jnp.float32, jnp.bfloat16
    rows = q_ref.shape[0]
    steps = tiles * LANES // chunk
    if first:
        dkv_ref[...] = jnp.zeros_like(dkv_ref)
        gate_ref[...] = jnp.zeros_like(gate_ref)
    dot_sum = None
    for at in range(steps):
        cols = slice(at * chunk, (at + 1) * chunk)
        raw = lax.dot_general(grad_ref[...], kv_ref[cols, :], NT, preferred_element_type=f32)
        raw_ref[:, cols] = raw
        part = jnp.sum(raw * prob_ref[0, 0, :, cols].astype(f32), axis=1, keepdims=True)
        dot_sum = part if dot_sum is None else dot_sum + part
    lane = lax.broadcasted_iota(jnp.int32, (rows, LANES), 1)
    scaled = jnp.where(lane == HD, 1.0, q_ref[...].astype(f32) * HD ** (-0.5))
    query_t = jnp.transpose(scaled)[: HD + 16].astype(bf16)
    grad_t = jnp.transpose(grad_ref[...].astype(f32))[HD:].astype(bf16)
    dq = None
    for at in range(steps):
        cols = slice(at * chunk, (at + 1) * chunk)
        prob = prob_ref[0, 0, :, cols]
        grad_score = (prob.astype(f32) * (raw_ref[:, cols] - dot_sum)).astype(bf16)
        piece = jnp.dot(grad_score, kv_ref[cols, :], preferred_element_type=f32)
        dq = piece if dq is None else dq + piece
        keys = jnp.dot(query_t, grad_score, preferred_element_type=f32)
        dkv_ref[:HD, cols] += keys[:HD]
        gate_ref[:, cols] += keys[HD : HD + 8]
        dkv_ref[HD:, cols] += jnp.dot(grad_t, prob, preferred_element_type=f32)
    dq = dq * HD ** (-0.5)
    dq_ref[...] = dq.astype(dq_ref.dtype)
    dq_turned_ref[0] = jnp.transpose(dq)[:HD, :].astype(bf16)
    if last:
        turned_ref[0] = dkv_ref[...].astype(bf16)
        gates_ref[0] = gate_ref[...]
        count, height, _ = out_ref.shape
        parts = (height - PAD_ROWS) // LANES
        for at in range(count):
            rows_of = []
            for part in range(parts):
                cols = slice((part * count + at) * LANES, (part * count + at + 1) * LANES)
                out_ref[at, part * LANES : (part + 1) * LANES, :] = jnp.transpose(dkv_ref[:, cols]).astype(bf16)
                rows_of.append(gate_ref[0:1, cols])
            rows_of.append(jnp.zeros((PAD_ROWS - parts, LANES), f32))
            out_ref[at, height - PAD_ROWS :, :] = jnp.concatenate(rows_of, axis=0).astype(bf16)


def attend_back_kernel(parts, chunk, *refs):
    part = pl.program_id(1)
    for at in range(parts):
        pl.when(part == at)(
            functools.partial(attend_back_body, at == 0, at == parts - 1, (at + 1) * chunk // LANES, chunk, *refs)
        )


def attend_back(count, query, grad, pairs, prob):
    heads, parts, block, slot = prob.shape
    width = pairs.shape[1]
    height = slot // count + PAD_ROWS
    chunk = slot // parts
    return pl.pallas_call(
        functools.partial(attend_back_kernel, parts, chunk),
        grid=(heads, parts),
        in_specs=[
            pl.BlockSpec((block, LANES), lambda h, r: (r, h)),
            pl.BlockSpec((block, LANES), lambda h, r: (r, h)),
            pl.BlockSpec((slot, LANES), lambda h, r: (0, h)),
            pl.BlockSpec((1, 1, block, slot), lambda h, r: (h, r, 0, 0)),
        ],
        out_specs=[
            pl.BlockSpec((block, LANES), lambda h, r: (r, h)),
            pl.BlockSpec((count, height, LANES), lambda h, r: (0, 0, h)),
            pl.BlockSpec((1, LANES, slot), lambda h, r: (h, 0, 0)),
            pl.BlockSpec((1, HD, block), lambda h, r: (h, 0, r)),
            pl.BlockSpec((1, 8, slot), lambda h, r: (h, 0, 0)),
        ],
        out_shape=[
            jax.ShapeDtypeStruct((parts * block, heads * LANES), jnp.bfloat16),
            jax.ShapeDtypeStruct((count, height, width), jnp.bfloat16),
            jax.ShapeDtypeStruct((heads, LANES, slot), jnp.bfloat16),
            jax.ShapeDtypeStruct((heads, HD, parts * block), jnp.bfloat16),
            jax.ShapeDtypeStruct((heads, 8, slot), jnp.float32),
        ],
        scratch_shapes=[
            pltpu.VMEM((block, slot), jnp.float32),
            pltpu.VMEM((LANES, slot), jnp.float32),
            pltpu.VMEM((8, slot), jnp.float32),
        ],
        name="attend_back",
    )(query, grad, pairs, prob)


def weight_kernel(turned_ref, dq_ref, gates_ref, score_ref, slot_ref, norm_ref, in_ref, gain_ref, out_ref):
    f32, bf16 = jnp.float32, jnp.bfloat16
    heads, _, slot = turned_ref.shape
    wide = in_ref.shape[1]
    width = slot_ref.shape[1]
    total = jnp.concatenate([gates_ref[head, 0:1, :] for head in range(heads)], axis=0)
    total = total * jax.nn.sigmoid(-score_ref[...].astype(f32))
    total = jnp.concatenate([total, jnp.zeros((PAD_ROWS - heads, slot), f32)], axis=0).astype(bf16)
    turned = [
        jnp.dot(turned_ref[...].reshape(heads * LANES, slot), slot_ref[...], preferred_element_type=f32),
        jnp.dot(dq_ref[...].reshape(heads * HD, -1), norm_ref[...], preferred_element_type=f32),
        jnp.dot(total, slot_ref[...], preferred_element_type=f32),
        jnp.zeros((wide - heads * 3 * HD - PAD_ROWS, width), f32),
    ]
    small = jnp.transpose(jnp.concatenate(turned, axis=0))
    gain_grad = jnp.sum(small * in_ref[...].astype(f32), axis=1, keepdims=True) / gain_ref[:, 0:1]
    lane = lax.broadcasted_iota(jnp.int32, small.shape, 1)
    at = heads * 3 * HD + heads
    small = jnp.where(lane == at, gain_grad, jnp.where(lane == at + 1, gain_ref[:, 1:2], small))
    out_ref[:, :wide] = small.astype(bf16)
    out_ref[:, wide:] = jnp.zeros((width, width - wide), bf16)


def weight_grad(turned, dq, gates, score, norm_slot, norm_one, weights, gains):
    width = norm_one.shape[1]
    return pl.pallas_call(
        weight_kernel,
        out_shape=jax.ShapeDtypeStruct((width, width), jnp.bfloat16),
        name="weight_grad",
    )(turned, dq, gates, score, norm_slot, norm_one, weights, gains)


def finish_kernel(heads, pair_ref, dq_ref, score_ref, in_ref, grad_ref):
    f32, bf16 = jnp.float32, jnp.bfloat16
    group = dq_ref.shape[0]
    parts = group // LANES
    wide = in_ref.shape[1]
    gates = pair_ref[group:, :].astype(f32)
    total = jnp.concatenate(
        [
            jnp.concatenate([gates[at : at + 1, head * LANES : (head + 1) * LANES] for at in range(parts)], axis=1)
            for head in range(heads)
        ],
        axis=0,
    )
    total = total * jax.nn.sigmoid(-score_ref[...].astype(f32))
    scores = jnp.transpose(jnp.concatenate([total, jnp.zeros((LANES - heads, group), f32)], axis=0))
    rest = wide - heads * 3 * HD
    columns = jnp.concatenate(
        [pair_ref[:group, :].astype(f32)]
        + [dq_ref[:, head * LANES : head * LANES + HD].astype(f32) for head in range(heads)]
        + [scores[:, :rest]],
        axis=1,
    ).astype(bf16)
    grad_ref[...] = lax.dot_general(columns, in_ref[...], NT, preferred_element_type=f32).astype(bf16)


def finish(pair, dq, score, weights):
    return pl.pallas_call(
        functools.partial(finish_kernel, score.shape[0]),
        out_shape=jax.ShapeDtypeStruct((dq.shape[0], weights.shape[0]), jnp.bfloat16),
        name="finish",
    )(pair, dq, score, weights)


def unpack_kernel(groups, heads, piece, parts, all_ref, qkv_ref, score_ref, fc_ref, proj_ref):
    f32 = jnp.float32
    keys = heads * 2 * HD
    part_cols = fc_ref.shape[1] // (groups * parts)
    for step in range(all_ref.shape[1]):
        rows = slice(step * piece, (step + 1) * piece)
        for at in range(groups):
            values = all_ref[at, step, :piece, :].astype(f32)
            for head in range(heads):
                start = (at * heads + head) * 3 * HD
                qkv_ref[rows, start : start + HD] = values[:, keys + head * HD : keys + (head + 1) * HD]
                qkv_ref[rows, start + HD : start + 3 * HD] = values[:, head * 2 * HD : (head + 1) * 2 * HD]
            score_ref[rows, at * heads : (at + 1) * heads] = values[:, keys + heads * HD : keys + heads * HD + heads]
            values = all_ref[at, step, piece : 2 * piece, :].astype(f32)
            for part in range(parts):
                start = (part * groups + at) * part_cols
                fc_ref[rows, start : start + part_cols] = values[:, part * part_cols : (part + 1) * part_cols]
            proj_ref[at, step] = all_ref[at, step, 2 * piece : 2 * piece + proj_ref.shape[2], :].astype(f32)


def unpack(gathered, heads, piece, proj_piece, parts, hidden):
    groups, count, rows, width = gathered.shape
    step = 1 if piece % 16 == 0 else count
    return pl.pallas_call(
        functools.partial(unpack_kernel, groups, heads, piece, parts),
        grid=(count // step,),
        in_specs=[pl.BlockSpec((groups, step, rows, width), lambda c: (0, c, 0, 0))],
        out_specs=[
            pl.BlockSpec((step * piece, groups * heads * 3 * HD), lambda c: (c, 0)),
            pl.BlockSpec((step * piece, groups * heads), lambda c: (c, 0)),
            pl.BlockSpec((step * piece, hidden), lambda c: (c, 0)),
            pl.BlockSpec((groups, step, proj_piece, width), lambda c: (0, c, 0, 0)),
        ],
        out_shape=[
            jax.ShapeDtypeStruct((count * piece, groups * heads * 3 * HD), jnp.float32),
            jax.ShapeDtypeStruct((count * piece, groups * heads), jnp.float32),
            jax.ShapeDtypeStruct((count * piece, hidden), jnp.float32),
            jax.ShapeDtypeStruct((groups, count, proj_piece, width), jnp.float32),
        ],
        name="unpack",
    )(gathered)


def arrange_kernel(heads, rows, qkv_ref, score_ref, gains_ref, out_ref):
    f32 = jnp.float32
    values = qkv_ref[...].astype(f32)
    keys = heads * 2 * HD
    width = out_ref.shape[1]
    pieces = [values[:, (3 * head + 1) * HD : (3 * head + 3) * HD] for head in range(heads)]
    pieces += [values[:, 3 * head * HD : (3 * head + 1) * HD] for head in range(heads)]
    pieces += [score_ref[...].astype(f32), jnp.zeros((rows, width - heads * 3 * HD - heads), f32)]
    out_ref[:rows, :] = jnp.concatenate(pieces, axis=1).astype(out_ref.dtype)
    out_ref[rows:, :] = jnp.concatenate(
        [gains_ref[...].astype(f32), jnp.zeros((gains_ref.shape[0], width - rows), f32)], axis=1
    ).astype(out_ref.dtype)


def arrange(qkv, score, gains, width):
    rows, heads = score.shape
    return pl.pallas_call(
        functools.partial(arrange_kernel, heads, rows),
        out_shape=jax.ShapeDtypeStruct((rows + PAD_ROWS, width), qkv.dtype),
        name="arrange",
    )(qkv, score, gains)


def dp_send(mine):
    if lax.axis_size("dp") != 2:
        return lax.all_gather(mine, "dp", axis=0, tiled=True)
    return lax.ppermute(mine, "dp", [(0, 1), (1, 0)])


def dp_join(mine, came):
    if lax.axis_size("dp") != 2:
        return came
    return jnp.where(
        lax.axis_index("dp") == 0, jnp.concatenate([mine, came]), jnp.concatenate([came, mine])
    )


def dp_scatter(parts):
    if lax.axis_size("dp") != 2:
        return lax.psum_scatter(parts, "dp", scatter_dimension=0, tiled=False)
    at = lax.axis_index("dp")
    mine = lax.dynamic_index_in_dim(parts, at, 0, keepdims=False)
    sent = lax.dynamic_index_in_dim(parts, 1 - at, 0, keepdims=False)
    other = lax.ppermute(sent, "dp", [(0, 1), (1, 0)])
    return (mine.astype(jnp.float32) + other.astype(jnp.float32)).astype(parts.dtype)


def group_rows_of(mine, group, count):
    height = mine.shape[0]
    if lax.axis_size("dp") != 2 or height % count != 0:
        whole = lax.all_gather(mine, "dp", axis=0, tiled=True)
        return lax.dynamic_slice_in_dim(whole, group * count, count, 0)
    near = lax.dynamic_slice_in_dim(mine, group * count % height, count, 0)
    far = lax.ppermute(near, "dp", [(0, 1), (1, 0)])
    return jnp.where(lax.axis_index("dp") == group * count // height, near, far)


def dp_sum(mine):
    if lax.axis_size("dp") != 2:
        return lax.psum(mine, "dp")
    other = lax.ppermute(mine, "dp", [(0, 1), (1, 0)])
    return (mine.astype(jnp.float32) + other.astype(jnp.float32)).astype(mine.dtype)


def exchange_sum(parts, axis):
    came = lax.all_to_all(parts, axis, split_axis=0, concat_axis=0, tiled=True)
    return jnp.sum(came.astype(jnp.float32), axis=0)


def per_device(
    tokens,
    cotangent,
    lengths,
    kept_keys,
    first_gain,
    qkv_weight,
    score_weight,
    out_weight,
    second_gain,
    fc_weight,
    proj_weight,
):
    f32, bf16 = jnp.float32, jnp.bfloat16
    dp_count = lax.axis_size("dp")
    seg_count = lax.axis_size("sp")
    ctx_count = lax.axis_size("ctx")
    dp_at = lax.axis_index("dp")
    sp_at = lax.axis_index("sp")
    ctx_at = lax.axis_index("ctx")
    rows = tokens.shape[1]
    width = tokens.shape[2]
    group_rows = seg_count * rows
    heads = H // seg_count
    head_cols = heads * 3 * HD
    hidden = fc_weight.shape[1]
    hidden_part = hidden // (dp_count * seg_count)
    piece = width // (dp_count * ctx_count)

    keys = heads * 2 * HD
    wide = -(-(head_cols + heads + 2) // LANES) * LANES
    weight_rows = width // dp_count
    own_in = arrange(
        lax.dynamic_slice_in_dim(qkv_weight, sp_at * head_cols, head_cols, 1),
        lax.dynamic_slice_in_dim(score_weight, sp_at * heads, heads, 1),
        jnp.pad(jnp.stack([first_gain, second_gain]), ((0, PAD_ROWS - 2), (0, 0))),
        wide,
    )
    if dp_count == 2:
        other_in = lax.ppermute(own_in, "dp", [(0, 1), (1, 0)])
        parts_in = [
            jnp.where(dp_at == at, own_in, other_in) for at in range(dp_count)
        ]
    else:
        parts_in = list(lax.all_gather(own_in, "dp", axis=0, tiled=False))
    tokens_slot = lax.all_gather(tokens[0], ("sp", "ctx"), axis=0, tiled=True)
    all_in = jnp.concatenate([part[:weight_rows] for part in parts_in])
    gain_one = jnp.concatenate([part[weight_rows, :weight_rows] for part in parts_in]).astype(f32)
    gain_two = jnp.concatenate([part[weight_rows + 1, :weight_rows] for part in parts_in]).astype(f32)

    fc_own = jnp.concatenate(
        [
            lax.dynamic_slice_in_dim(fc_weight, (at * seg_count + sp_at) * hidden_part, hidden_part, 1)
            for at in range(dp_count)
        ],
        axis=1,
    )
    proj_own = lax.dynamic_slice_in_dim(proj_weight, sp_at * hidden_part, hidden_part, 0)
    all_in, out_own, fc_own, proj_own = lax.optimization_barrier((all_in, out_weight, fc_own, proj_own))
    out_came = dp_send(out_own)
    fc_came = dp_send(fc_own)
    proj_came = dp_send(proj_own)

    cot_group = lax.all_gather(cotangent[0], "sp", axis=0, tiled=True)
    kept = jnp.transpose(kept_keys[0], (2, 0, 1, 3))
    tokens_slot, cot_group, out_came, fc_came, kept = lax.optimization_barrier(
        (tokens_slot, cot_group, out_came, fc_came, kept)
    )

    def group_of(values):
        parts = values.reshape((seg_count, ctx_count, rows) + values.shape[1:])
        return lax.dynamic_index_in_dim(parts, ctx_at, 1, keepdims=False).reshape((group_rows,) + values.shape[1:])

    inputs = tokens[0].astype(f32)
    inputs_group = group_of(tokens_slot).astype(f32)
    norm_slot = layer_norm(tokens_slot.astype(f32), gain_one).astype(bf16)
    pairs = jnp.dot(norm_slot, all_in[:, :keys], preferred_element_type=f32).astype(bf16)
    score_slot = lax.dot_general(
        all_in[:, head_cols : head_cols + heads], norm_slot, (((0,), (1,)), ((), ())), preferred_element_type=f32
    ).astype(bf16)
    key_score = lax.dynamic_index_in_dim(
        score_slot.reshape(heads, seg_count, ctx_count, rows), ctx_at, 2, keepdims=False
    ).reshape(heads, group_rows)
    norm_one = group_of(norm_slot)
    query_weight = jnp.pad(
        all_in[:, keys:head_cols].reshape(width, heads, HD), ((0, 0), (0, 0), (0, HD))
    ).reshape(width, heads * LANES)
    query_wide = jnp.dot(norm_one, query_weight, preferred_element_type=f32).astype(bf16)
    base = (ctx_at * rows).astype(jnp.int32)[None]
    head_outs, prob = attend(base, kept, query_wide, pairs, score_slot[:, None])
    head_outs, proj_came = lax.optimization_barrier((head_outs, proj_came))
    attended = head_outs.reshape(heads * HD, group_rows)
    attended_all = lax.all_gather(attended, "sp", axis=0, tiled=True)
    out_full = dp_join(out_own, out_came)
    out_part = lax.dynamic_slice_in_dim(out_full, sp_at * heads * HD, heads * HD, 0)
    fc_part = dp_join(fc_own, fc_came)
    proj_part = dp_join(proj_own, proj_came)

    group_at = jnp.arange(group_rows, dtype=jnp.int32)
    group_positions = (group_at // rows) * (ctx_count * rows) + ctx_at * rows + group_at % rows
    grad_out_group = jnp.where((group_positions < lengths[0])[:, None], cot_group, jnp.zeros_like(cot_group))
    positions = (sp_at * ctx_count + ctx_at) * rows + jnp.arange(rows, dtype=jnp.int32)
    is_valid = (positions < lengths[0])[:, None]

    mixed_group = inputs_group + contract_rows(attended_all, out_full)
    norm_two = layer_norm(mixed_group, gain_two).astype(bf16)
    mixed = lax.dynamic_slice_in_dim(mixed_group, sp_at * rows, rows, 0)
    hidden_pre = jnp.dot(norm_two, fc_part, preferred_element_type=f32)
    active = tanh_gelu(hidden_pre).astype(bf16)
    grad_active = contract_cols(grad_out_group, proj_part)
    _, gelu_pull = jax.vjp(tanh_gelu, hidden_pre)
    grad_pre = gelu_pull(grad_active)[0].astype(bf16)
    fc_parts = contract_rows(norm_two, grad_pre).astype(bf16).reshape(dp_count, ctx_count, piece, width)
    proj_parts = contract_rows(active, grad_out_group).astype(bf16).reshape(dp_count, ctx_count, -1, width)
    grad_pre, fc_parts, proj_parts = lax.optimization_barrier((grad_pre, fc_parts, proj_parts))
    fc_came = lax.all_to_all(
        jnp.transpose(fc_parts, (1, 0, 2, 3)), "ctx", split_axis=0, concat_axis=0, tiled=True
    )
    proj_dp = dp_scatter(proj_parts)
    grad_norm_parts = contract_cols(grad_pre, fc_part).astype(bf16)
    grad_norm_two = exchange_sum(grad_norm_parts.reshape(seg_count, rows, width), "sp")
    _, second_pull = jax.vjp(layer_norm, mixed, gain_two)
    grad_mixed_norm, second_gain_grad = second_pull(grad_norm_two)
    grad_out = jnp.where(is_valid, cotangent[0], jnp.zeros_like(cotangent[0])).astype(f32)
    grad_mixed = grad_out + grad_mixed_norm
    grad_branch = lax.all_gather(grad_mixed.astype(bf16), "sp", axis=0, tiled=True)

    out_wide = jnp.pad(out_part.reshape(heads, HD, width), ((0, 0), (HD, 0), (0, 0))).reshape(heads * LANES, width)
    grad_wide = contract_cols(grad_branch, out_wide).astype(bf16)
    out_mine = jnp.dot(attended, grad_branch, preferred_element_type=f32).astype(bf16)
    grad_wide, fc_came, proj_dp, out_mine = lax.optimization_barrier((grad_wide, fc_came, proj_dp, out_mine))
    out_sum = dp_sum(out_mine)
    fc_own = dp_scatter(jnp.sum(fc_came.astype(f32), axis=0).astype(bf16))
    proj_came = lax.all_to_all(proj_dp, "ctx", split_axis=0, concat_axis=0, tiled=True)
    gain_cols = jnp.stack([gain_one, second_gain_grad], axis=1)
    grad_wide, gain_cols = lax.optimization_barrier((grad_wide, gain_cols))
    query_grads, pair_grads, turned, query_turned, gates = attend_back(
        ctx_count, query_wide, grad_wide, pairs, prob
    )
    pair_mine = lax.psum_scatter(pair_grads, "ctx", scatter_dimension=0, tiled=False)
    small = weight_grad(turned, query_turned, gates, score_slot, norm_slot, norm_one, all_in, gain_cols)
    small, fc_own, proj_came, out_sum = lax.optimization_barrier((small, fc_own, proj_came, out_sum))
    late = jnp.concatenate(
        [dp_scatter(small.reshape(dp_count, ctx_count, piece, width)), out_sum.reshape(ctx_count, -1, width)], axis=1
    )
    late_sum = exchange_sum(late, "ctx").astype(bf16)
    proj_sum = jnp.sum(proj_came.astype(f32), axis=0).astype(bf16)
    gradients = jnp.concatenate([late_sum[:piece], fc_own, proj_sum, late_sum[piece:]], axis=0)
    pair_mine, gradients, active_late = lax.optimization_barrier((pair_mine, gradients, active))
    gathered = lax.all_gather(gradients, ("sp", "ctx"), axis=0, tiled=False).reshape(seg_count, ctx_count, -1, width)
    proj_piece = hidden // (seg_count * dp_count * ctx_count)

    grad_norm_part = finish(pair_mine, query_grads, key_score, all_in)
    expanded = exchange_sum(
        jnp.dot(active_late, proj_part, preferred_element_type=f32).astype(bf16).reshape(seg_count, rows, width), "sp"
    )
    output = jnp.where(is_valid, mixed + expanded, 0.0).astype(bf16)[None]
    grad_norm_one = exchange_sum(grad_norm_part.reshape(seg_count, rows, width), "sp")
    _, first_pull = jax.vjp(lambda values: layer_norm(values, gain_one), inputs)
    grad_input_norm = first_pull(grad_norm_one)[0]
    input_grad = (grad_mixed + grad_input_norm).astype(bf16)[None]

    qkv_grad, score_grad, fc_grad, proj_grad = unpack(gathered, heads, piece, proj_piece, dp_count, hidden)
    proj_grad = proj_grad.reshape(-1, width)
    out_grad = lax.dynamic_slice_in_dim(
        gathered[:, :, 2 * piece + proj_piece :].reshape(width, width), dp_at * weight_rows, weight_rows, 0
    ).astype(f32)
    gains = jnp.sum(
        gathered[:, :, :piece, head_cols + heads : head_cols + heads + 2].astype(f32), axis=0
    ).reshape(weight_rows, 2)
    return (output, input_grad, gains[:, 0], qkv_grad, score_grad, out_grad, gains[:, 1], fc_grad, proj_grad)


def solution(mesh):
    placed = (
        P("dp", ("sp", "ctx"), None),
        P("dp", ("sp", "ctx"), None),
        P("dp"),
        P("dp", None, "ctx", "sp", None),
        P("dp"),
        P("dp", None),
        P("dp", None),
        P("dp", None),
        P("dp"),
        P("dp", None),
        P("dp", None),
    )
    return jax.shard_map(
        per_device,
        mesh=mesh,
        in_specs=placed,
        out_specs=(
            P("dp", ("sp", "ctx"), None),
            P("dp", ("sp", "ctx"), None),
            P("dp"),
            P("dp", None),
            P("dp", None),
            P("dp", None),
            P("dp"),
            P("dp", None),
            P("dp", None),
        ),
        check_vma=False,
    )
```

```python
import functools

import jax
import jax.numpy as jnp
from jax import lax
from jax.experimental import pallas as pl
from jax.experimental.pallas import tpu as pltpu
from jax.sharding import PartitionSpec as P

H = 12
HD = 64
WIN = 64
LANES = 128
SLOT = 2048


EPSILON = 1e-05


def layer_norm(values, gain):
    mean_value = jnp.mean(values, axis=-1, keepdims=True)
    centred = values - mean_value
    variance = jnp.mean(centred * centred, axis=-1, keepdims=True)
    return centred * lax.rsqrt(variance + EPSILON) * gain


def tanh_gelu(values):
    return jax.nn.gelu(values, approximate=True)


def contract_rows(left, right):
    return lax.dot_general(
        left, right, (((0,), (0,)), ((), ())), preferred_element_type=jnp.float32
    )


def contract_cols(left, right):
    return lax.dot_general(
        left, right, (((1,), (1,)), ((), ())), preferred_element_type=jnp.float32
    )


NT = (((1,), (1,)), ((), ()))


PAD_ROWS = 16
STEP = 128


def project_kernel(heads, tokens_ref, gain_ref, in_ref, norm_ref, pair_ref, query_ref, score_ref):
    f32, bf16 = jnp.float32, jnp.bfloat16
    keys = heads * 2 * HD
    norm = layer_norm(tokens_ref[...].astype(f32), gain_ref[...]).astype(bf16)
    norm_ref[...] = norm
    pair_ref[...] = jnp.dot(norm, in_ref[:, :keys], preferred_element_type=f32).astype(bf16)
    rest = jnp.dot(norm, in_ref[:, keys:], preferred_element_type=f32)
    for head in range(heads):
        query = rest[:, head * HD : (head + 1) * HD]
        query_ref[:, head * LANES : (head + 1) * LANES] = jnp.concatenate(
            [query, jnp.zeros_like(query)], axis=1
        ).astype(bf16)
    scores = jnp.transpose(rest)[heads * HD : heads * HD + heads, :].astype(bf16)
    for head in range(heads):
        score_ref[head] = scores[head : head + 1, :]


def project(heads, tokens, gain, weights):
    slot, width = tokens.shape
    block = 256
    return pl.pallas_call(
        functools.partial(project_kernel, heads),
        grid=(slot // block,),
        in_specs=[
            pl.BlockSpec((block, width), lambda r: (r, 0)),
            pl.BlockSpec((1, width), lambda r: (0, 0)),
            pl.BlockSpec(weights.shape, lambda r: (0, 0)),
        ],
        out_specs=[
            pl.BlockSpec((block, width), lambda r: (r, 0)),
            pl.BlockSpec((block, heads * LANES), lambda r: (r, 0)),
            pl.BlockSpec((block, heads * LANES), lambda r: (r, 0)),
            pl.BlockSpec((heads, 1, block), lambda r: (0, 0, r)),
        ],
        out_shape=[
            jax.ShapeDtypeStruct((slot, width), jnp.bfloat16),
            jax.ShapeDtypeStruct((slot, heads * LANES), jnp.bfloat16),
            jax.ShapeDtypeStruct((slot, heads * LANES), jnp.bfloat16),
            jax.ShapeDtypeStruct((heads, 1, slot), jnp.bfloat16),
        ],
        name="project",
    )(tokens, gain, weights)


def attend_body(first, tiles, base, idx_ref, q_ref, kv_ref, key_ref, out_ref, prob_ref, score_ref, pair_ref, gate_ref):
    rows = q_ref.shape[0]
    if first:
        gate_ref[...] = jnp.broadcast_to(-jnp.log1p(jnp.exp(-key_ref[0].astype(jnp.float32))), gate_ref.shape)
    span = tiles * LANES
    f32, bf16 = jnp.float32, jnp.bfloat16
    score_ref[:, :span] = (
        lax.dot_general(q_ref[...], kv_ref[:span, :], NT, preferred_element_type=f32) * HD ** (-0.5)
        + gate_ref[0:1, :span]
    )
    kept = idx_ref[0, 0]
    pair_ref[...] = jnp.concatenate([kept, kept], axis=1)
    wide = 8 * HD
    sub = lax.broadcasted_iota(jnp.int32, (8, wide), 0)
    lane = lax.broadcasted_iota(jnp.int32, (8, wide), 1)
    own = (lane // HD) == sub
    subf = sub.astype(f32)
    ahead = lax.broadcasted_iota(jnp.int32, (8, LANES), 0) - lax.broadcasted_iota(jnp.int32, (8, LANES), 1)
    near_from = max(0, tiles - 5)

    def eight(start):
        four = pair_ref[pl.ds(start, 8), :]
        index = jnp.concatenate([four] * 4, axis=1)
        pos = base + start + sub
        high = jnp.where(own & (pos >= WIN), index >> 7, -2).astype(f32)
        low = jnp.sum(jnp.where(own, (index & 127).astype(f32), 0.0), axis=0, keepdims=True) - subf
        high_pair = jnp.concatenate([high, high - 1.0], axis=0).astype(bf16)
        low_pair = jnp.concatenate([low, low - 8.0], axis=0).astype(bf16)
        one, zero = jnp.ones((), bf16), jnp.zeros((), bf16)
        left = jnp.concatenate(
            [jnp.where(high_pair == jnp.array(2 * p, bf16), one, zero) for p in range(tiles // 2)], axis=0
        )
        right = jnp.concatenate(
            [jnp.where(low_pair == jnp.array(16 * p, bf16), one, zero) for p in range(8)], axis=0
        )
        count = lax.dot_general(left, right, NT, preferred_element_type=f32)
        gap = ahead + (base + start)
        masked, counts = [], []
        largest = None
        for tile in range(tiles):
            number = count[8 * tile : 8 * tile + 8, :]
            if tile >= near_from:
                far = gap - tile * LANES
                number = number + jnp.where((far >= 0) & (far < WIN), 1.0, 0.0)
            value = jnp.where(number > 0.0, score_ref[pl.ds(start, 8), tile * LANES : (tile + 1) * LANES], -1e30)
            counts.append(number)
            masked.append(value)
            largest = value if largest is None else jnp.maximum(largest, value)
        top = jnp.max(largest, axis=1, keepdims=True)
        total = None
        expos = []
        for number, value in zip(counts, masked):
            expo = jnp.exp(value - top) * number
            expos.append(expo)
            total = expo if total is None else total + expo
        inverse = 1.0 / jnp.sum(total, axis=1, keepdims=True)
        return [expo * inverse for expo in expos]

    def step(index, carry):
        for at in range(0, STEP, 16):
            start = pl.multiple_of(index * STEP + at, 16)
            near, next_to = eight(start), eight(start + 8)
            for tile in range(tiles):
                prob_ref[0, 0, pl.ds(start, 16), tile * LANES : (tile + 1) * LANES] = jnp.concatenate(
                    [near[tile], next_to[tile]], axis=0
                ).astype(bf16)
        return carry

    if rows == STEP:
        step(0, 0)
    else:
        lax.fori_loop(0, rows // STEP, step, 0)
    both = jnp.dot(prob_ref[0, 0, :, :span], kv_ref[:span, :], preferred_element_type=f32)
    out_ref[0] = jnp.transpose(both)[HD:, :].astype(bf16)


def attend_kernel(parts, chunk, base_ref, *refs):
    part = pl.program_id(1)
    base = base_ref[0] + part * chunk
    for at in range(parts):
        pl.when(part == at)(
            functools.partial(attend_body, at == 0, (at + 1) * chunk // LANES, base, *refs)
        )


def attend(base, kept, query, pairs, key_score):
    heads, parts, block, keep = kept.shape
    slot = pairs.shape[0]
    chunk = slot // parts
    grid_spec = pltpu.PrefetchScalarGridSpec(
        num_scalar_prefetch=1,
        grid=(heads, parts),
        in_specs=[
            pl.BlockSpec((1, 1, block, keep), lambda h, r, b: (h, r, 0, 0)),
            pl.BlockSpec((block, LANES), lambda h, r, b: (r * (chunk // block) + b[1], h)),
            pl.BlockSpec((slot, LANES), lambda h, r, b: (0, h)),
            pl.BlockSpec((1, 1, slot), lambda h, r, b: (h, 0, 0)),
        ],
        out_specs=[
            pl.BlockSpec((1, HD, block), lambda h, r, b: (h, 0, r)),
            pl.BlockSpec((1, 1, block, slot), lambda h, r, b: (h, r, 0, 0)),
        ],
        scratch_shapes=[
            pltpu.VMEM((block, slot), jnp.float32),
            pltpu.VMEM((block, 2 * keep), jnp.int32),
            pltpu.VMEM((8, slot), jnp.float32),
        ],
    )
    return pl.pallas_call(
        functools.partial(attend_kernel, parts, chunk),
        grid_spec=grid_spec,
        out_shape=[
            jax.ShapeDtypeStruct((heads, HD, parts * block), jnp.bfloat16),
            jax.ShapeDtypeStruct((heads, parts, block, slot), jnp.bfloat16),
        ],
        name="attend",
    )(base, kept, query, pairs, key_score)


def attend_back_body(first, last, tiles, chunk, q_ref, grad_ref, kv_ref, prob_ref, dq_ref, out_ref, turned_ref, dq_turned_ref, gates_ref, raw_ref, dkv_ref, gate_ref):
    f32, bf16 = jnp.float32, jnp.bfloat16
    rows = q_ref.shape[0]
    steps = tiles * LANES // chunk
    if first:
        dkv_ref[...] = jnp.zeros_like(dkv_ref)
        gate_ref[...] = jnp.zeros_like(gate_ref)
    dot_sum = None
    for at in range(steps):
        cols = slice(at * chunk, (at + 1) * chunk)
        raw = lax.dot_general(grad_ref[...], kv_ref[cols, :], NT, preferred_element_type=f32)
        raw_ref[:, cols] = raw
        part = jnp.sum(raw * prob_ref[0, 0, :, cols].astype(f32), axis=1, keepdims=True)
        dot_sum = part if dot_sum is None else dot_sum + part
    lane = lax.broadcasted_iota(jnp.int32, (rows, LANES), 1)
    scaled = jnp.where(lane == HD, 1.0, q_ref[...].astype(f32) * HD ** (-0.5))
    query_t = jnp.transpose(scaled)[: HD + 16].astype(bf16)
    grad_t = jnp.transpose(grad_ref[...].astype(f32))[HD:].astype(bf16)
    dq = None
    for at in range(steps):
        cols = slice(at * chunk, (at + 1) * chunk)
        prob = prob_ref[0, 0, :, cols]
        grad_score = (prob.astype(f32) * (raw_ref[:, cols] - dot_sum)).astype(bf16)
        piece = jnp.dot(grad_score, kv_ref[cols, :], preferred_element_type=f32)
        dq = piece if dq is None else dq + piece
        keys = jnp.dot(query_t, grad_score, preferred_element_type=f32)
        dkv_ref[:HD, cols] += keys[:HD]
        gate_ref[:, cols] += keys[HD : HD + 8]
        dkv_ref[HD:, cols] += jnp.dot(grad_t, prob, preferred_element_type=f32)
    dq = dq * HD ** (-0.5)
    dq_ref[...] = dq.astype(dq_ref.dtype)
    dq_turned_ref[0] = jnp.transpose(dq)[:HD, :].astype(bf16)
    if last:
        turned_ref[0] = dkv_ref[...].astype(bf16)
        gates_ref[0] = gate_ref[...]
        count, height, _ = out_ref.shape
        parts = (height - PAD_ROWS) // LANES
        for at in range(count):
            rows_of = []
            for part in range(parts):
                cols = slice((part * count + at) * LANES, (part * count + at + 1) * LANES)
                out_ref[at, part * LANES : (part + 1) * LANES, :] = jnp.transpose(dkv_ref[:, cols]).astype(bf16)
                rows_of.append(gate_ref[0:1, cols])
            rows_of.append(jnp.zeros((PAD_ROWS - parts, LANES), f32))
            out_ref[at, height - PAD_ROWS :, :] = jnp.concatenate(rows_of, axis=0).astype(bf16)


def attend_back_kernel(parts, chunk, base_ref, *refs):
    part = pl.program_id(1)
    for at in range(parts):
        pl.when(part == at)(
            functools.partial(attend_back_body, at == 0, at == parts - 1, (at + 1) * chunk // LANES, chunk, *refs)
        )


def attend_back(count, base, query, grad, pairs, prob):
    heads, parts, block, slot = prob.shape
    width = pairs.shape[1]
    height = slot // count + PAD_ROWS
    chunk = slot // parts
    return pl.pallas_call(
        functools.partial(attend_back_kernel, parts, chunk),
        grid_spec=pltpu.PrefetchScalarGridSpec(
        num_scalar_prefetch=1,
        grid=(heads, parts),
        in_specs=[
            pl.BlockSpec((block, LANES), lambda h, r, b: (r * (chunk // block) + b[1], h)),
            pl.BlockSpec((block, LANES), lambda h, r, b: (r, h)),
            pl.BlockSpec((slot, LANES), lambda h, r, b: (0, h)),
            pl.BlockSpec((1, 1, block, slot), lambda h, r, b: (h, r, 0, 0)),
        ],
        out_specs=[
            pl.BlockSpec((block, LANES), lambda h, r, b: (r, h)),
            pl.BlockSpec((count, height, LANES), lambda h, r, b: (0, 0, h)),
            pl.BlockSpec((1, LANES, slot), lambda h, r, b: (h, 0, 0)),
            pl.BlockSpec((1, HD, block), lambda h, r, b: (h, 0, r)),
            pl.BlockSpec((1, 8, slot), lambda h, r, b: (h, 0, 0)),
        ],
        scratch_shapes=[
            pltpu.VMEM((block, slot), jnp.float32),
            pltpu.VMEM((LANES, slot), jnp.float32),
            pltpu.VMEM((8, slot), jnp.float32),
        ],
        ),
        out_shape=[
            jax.ShapeDtypeStruct((parts * block, heads * LANES), jnp.bfloat16),
            jax.ShapeDtypeStruct((count, height, width), jnp.bfloat16),
            jax.ShapeDtypeStruct((heads, LANES, slot), jnp.bfloat16),
            jax.ShapeDtypeStruct((heads, HD, parts * block), jnp.bfloat16),
            jax.ShapeDtypeStruct((heads, 8, slot), jnp.float32),
        ],
        name="attend_back",
    )(base, query, grad, pairs, prob)


def weight_kernel(turned_ref, dq_ref, gates_ref, score_ref, slot_ref, norm_ref, in_ref, gain_ref, out_ref):
    f32, bf16 = jnp.float32, jnp.bfloat16
    heads, _, slot = turned_ref.shape
    wide = in_ref.shape[1]
    width = slot_ref.shape[1]
    total = jnp.concatenate([gates_ref[head, 0:1, :] for head in range(heads)], axis=0)
    total = total * jax.nn.sigmoid(-score_ref[...].astype(f32))
    total = jnp.concatenate([total, jnp.zeros((PAD_ROWS - heads, slot), f32)], axis=0).astype(bf16)
    turned = [
        jnp.dot(turned_ref[...].reshape(heads * LANES, slot), slot_ref[...], preferred_element_type=f32),
        jnp.dot(dq_ref[...].reshape(heads * HD, -1), norm_ref[...], preferred_element_type=f32),
        jnp.dot(total, slot_ref[...], preferred_element_type=f32),
        jnp.zeros((wide - heads * 3 * HD - PAD_ROWS, width), f32),
    ]
    small = jnp.transpose(jnp.concatenate(turned, axis=0))
    gain_grad = jnp.sum(small * in_ref[...].astype(f32), axis=1, keepdims=True) / gain_ref[:, 0:1]
    lane = lax.broadcasted_iota(jnp.int32, small.shape, 1)
    at = heads * 3 * HD + heads
    small = jnp.where(lane == at, gain_grad, jnp.where(lane == at + 1, gain_ref[:, 1:2], small))
    out_ref[:, :wide] = small.astype(bf16)
    out_ref[:, wide:] = jnp.zeros((width, width - wide), bf16)


def weight_grad(turned, dq, gates, score, norm_slot, norm_one, weights, gains):
    width = norm_one.shape[1]
    return pl.pallas_call(
        weight_kernel,
        out_shape=jax.ShapeDtypeStruct((width, width), jnp.bfloat16),
        name="weight_grad",
    )(turned, dq, gates, score, norm_slot, norm_one, weights, gains)


def finish_kernel(heads, pair_ref, dq_ref, score_ref, in_ref, grad_ref):
    f32, bf16 = jnp.float32, jnp.bfloat16
    group = dq_ref.shape[0]
    parts = group // LANES
    wide = in_ref.shape[1]
    gates = pair_ref[group:, :].astype(f32)
    total = jnp.concatenate(
        [
            jnp.concatenate([gates[at : at + 1, head * LANES : (head + 1) * LANES] for at in range(parts)], axis=1)
            for head in range(heads)
        ],
        axis=0,
    )
    total = total * jax.nn.sigmoid(-score_ref[...].astype(f32))
    scores = jnp.transpose(jnp.concatenate([total, jnp.zeros((LANES - heads, group), f32)], axis=0))
    rest = wide - heads * 3 * HD
    columns = jnp.concatenate(
        [pair_ref[:group, :].astype(f32)]
        + [dq_ref[:, head * LANES : head * LANES + HD].astype(f32) for head in range(heads)]
        + [scores[:, :rest]],
        axis=1,
    ).astype(bf16)
    grad_ref[...] = lax.dot_general(columns, in_ref[...], NT, preferred_element_type=f32).astype(bf16)


def finish(pair, dq, score, weights):
    return pl.pallas_call(
        functools.partial(finish_kernel, score.shape[0]),
        out_shape=jax.ShapeDtypeStruct((dq.shape[0], weights.shape[0]), jnp.bfloat16),
        name="finish",
    )(pair, dq, score, weights)


def unpack_kernel(groups, heads, piece, parts, all_ref, qkv_ref, score_ref, fc_ref, proj_ref):
    f32 = jnp.float32
    keys = heads * 2 * HD
    part_cols = fc_ref.shape[1] // (groups * parts)
    for step in range(all_ref.shape[1]):
        rows = slice(step * piece, (step + 1) * piece)
        for at in range(groups):
            values = all_ref[at, step, :piece, :].astype(f32)
            for head in range(heads):
                start = (at * heads + head) * 3 * HD
                qkv_ref[rows, start : start + HD] = values[:, keys + head * HD : keys + (head + 1) * HD]
                qkv_ref[rows, start + HD : start + 3 * HD] = values[:, head * 2 * HD : (head + 1) * 2 * HD]
            score_ref[rows, at * heads : (at + 1) * heads] = values[:, keys + heads * HD : keys + heads * HD + heads]
            values = all_ref[at, step, piece : 2 * piece, :].astype(f32)
            for part in range(parts):
                start = (part * groups + at) * part_cols
                fc_ref[rows, start : start + part_cols] = values[:, part * part_cols : (part + 1) * part_cols]
            proj_ref[at, step] = all_ref[at, step, 2 * piece : 2 * piece + proj_ref.shape[2], :].astype(f32)


def unpack(gathered, heads, piece, proj_piece, parts, hidden):
    groups, count, rows, width = gathered.shape
    step = 1 if piece % 16 == 0 else count
    return pl.pallas_call(
        functools.partial(unpack_kernel, groups, heads, piece, parts),
        grid=(count // step,),
        in_specs=[pl.BlockSpec((groups, step, rows, width), lambda c: (0, c, 0, 0))],
        out_specs=[
            pl.BlockSpec((step * piece, groups * heads * 3 * HD), lambda c: (c, 0)),
            pl.BlockSpec((step * piece, groups * heads), lambda c: (c, 0)),
            pl.BlockSpec((step * piece, hidden), lambda c: (c, 0)),
            pl.BlockSpec((groups, step, proj_piece, width), lambda c: (0, c, 0, 0)),
        ],
        out_shape=[
            jax.ShapeDtypeStruct((count * piece, groups * heads * 3 * HD), jnp.float32),
            jax.ShapeDtypeStruct((count * piece, groups * heads), jnp.float32),
            jax.ShapeDtypeStruct((count * piece, hidden), jnp.float32),
            jax.ShapeDtypeStruct((groups, count, proj_piece, width), jnp.float32),
        ],
        name="unpack",
    )(gathered)


def arrange_kernel(heads, rows, qkv_ref, score_ref, gains_ref, out_ref):
    f32 = jnp.float32
    values = qkv_ref[...].astype(f32)
    keys = heads * 2 * HD
    width = out_ref.shape[1]
    pieces = [values[:, (3 * head + 1) * HD : (3 * head + 3) * HD] for head in range(heads)]
    pieces += [values[:, 3 * head * HD : (3 * head + 1) * HD] for head in range(heads)]
    pieces += [score_ref[...].astype(f32), jnp.zeros((rows, width - heads * 3 * HD - heads), f32)]
    out_ref[:rows, :] = jnp.concatenate(pieces, axis=1).astype(out_ref.dtype)
    out_ref[rows:, :] = jnp.concatenate(
        [gains_ref[...].astype(f32), jnp.zeros((gains_ref.shape[0], width - rows), f32)], axis=1
    ).astype(out_ref.dtype)


def arrange(qkv, score, gains, width):
    rows, heads = score.shape
    return pl.pallas_call(
        functools.partial(arrange_kernel, heads, rows),
        out_shape=jax.ShapeDtypeStruct((rows + PAD_ROWS, width), qkv.dtype),
        name="arrange",
    )(qkv, score, gains)


def dp_send(mine):
    if lax.axis_size("dp") != 2:
        return lax.all_gather(mine, "dp", axis=0, tiled=True)
    return lax.ppermute(mine, "dp", [(0, 1), (1, 0)])


def dp_join(mine, came):
    if lax.axis_size("dp") != 2:
        return came
    return jnp.where(
        lax.axis_index("dp") == 0, jnp.concatenate([mine, came]), jnp.concatenate([came, mine])
    )


def dp_scatter(parts):
    if lax.axis_size("dp") != 2:
        return lax.psum_scatter(parts, "dp", scatter_dimension=0, tiled=False)
    at = lax.axis_index("dp")
    mine = lax.dynamic_index_in_dim(parts, at, 0, keepdims=False)
    sent = lax.dynamic_index_in_dim(parts, 1 - at, 0, keepdims=False)
    other = lax.ppermute(sent, "dp", [(0, 1), (1, 0)])
    return (mine.astype(jnp.float32) + other.astype(jnp.float32)).astype(parts.dtype)


def group_rows_of(mine, group, count):
    height = mine.shape[0]
    if lax.axis_size("dp") != 2 or height % count != 0:
        whole = lax.all_gather(mine, "dp", axis=0, tiled=True)
        return lax.dynamic_slice_in_dim(whole, group * count, count, 0)
    near = lax.dynamic_slice_in_dim(mine, group * count % height, count, 0)
    far = lax.ppermute(near, "dp", [(0, 1), (1, 0)])
    return jnp.where(lax.axis_index("dp") == group * count // height, near, far)


def dp_sum(mine):
    if lax.axis_size("dp") != 2:
        return lax.psum(mine, "dp")
    other = lax.ppermute(mine, "dp", [(0, 1), (1, 0)])
    return (mine.astype(jnp.float32) + other.astype(jnp.float32)).astype(mine.dtype)


def exchange_sum(parts, axis):
    came = lax.all_to_all(parts, axis, split_axis=0, concat_axis=0, tiled=True)
    return jnp.sum(came.astype(jnp.float32), axis=0)


def per_device(
    tokens,
    cotangent,
    lengths,
    kept_keys,
    first_gain,
    qkv_weight,
    score_weight,
    out_weight,
    second_gain,
    fc_weight,
    proj_weight,
):
    f32, bf16 = jnp.float32, jnp.bfloat16
    dp_count = lax.axis_size("dp")
    seg_count = lax.axis_size("sp")
    ctx_count = lax.axis_size("ctx")
    dp_at = lax.axis_index("dp")
    sp_at = lax.axis_index("sp")
    ctx_at = lax.axis_index("ctx")
    rows = tokens.shape[1]
    width = tokens.shape[2]
    group_rows = seg_count * rows
    heads = H // seg_count
    head_cols = heads * 3 * HD
    hidden = fc_weight.shape[1]
    hidden_part = hidden // (dp_count * seg_count)
    piece = width // (dp_count * ctx_count)

    keys = heads * 2 * HD
    wide = -(-(head_cols + heads + 2) // LANES) * LANES
    weight_rows = width // dp_count
    own_in = arrange(
        lax.dynamic_slice_in_dim(qkv_weight, sp_at * head_cols, head_cols, 1),
        lax.dynamic_slice_in_dim(score_weight, sp_at * heads, heads, 1),
        jnp.pad(jnp.stack([first_gain, second_gain]), ((0, PAD_ROWS - 2), (0, 0))),
        wide,
    )
    if dp_count == 2:
        other_in = lax.ppermute(own_in, "dp", [(0, 1), (1, 0)])
        parts_in = [
            jnp.where(dp_at == at, own_in, other_in) for at in range(dp_count)
        ]
    else:
        parts_in = list(lax.all_gather(own_in, "dp", axis=0, tiled=False))
    tokens_slot = lax.all_gather(tokens[0], ("sp", "ctx"), axis=0, tiled=True)
    all_in = jnp.concatenate([part[:weight_rows] for part in parts_in])
    gain_one = jnp.concatenate([part[weight_rows, :weight_rows] for part in parts_in]).astype(f32)
    gain_two = jnp.concatenate([part[weight_rows + 1, :weight_rows] for part in parts_in]).astype(f32)

    fc_own = jnp.concatenate(
        [
            lax.dynamic_slice_in_dim(fc_weight, (at * seg_count + sp_at) * hidden_part, hidden_part, 1)
            for at in range(dp_count)
        ],
        axis=1,
    )
    proj_own = lax.dynamic_slice_in_dim(proj_weight, sp_at * hidden_part, hidden_part, 0)
    all_in, out_own, fc_own, proj_own = lax.optimization_barrier((all_in, out_weight, fc_own, proj_own))
    out_came = dp_send(out_own)
    fc_came = dp_send(fc_own)
    proj_came = dp_send(proj_own)

    cot_group = lax.all_gather(cotangent[0], "sp", axis=0, tiled=True)
    kept = jnp.transpose(kept_keys[0], (2, 0, 1, 3))
    out_full = dp_join(out_own, out_came)
    fc_part = dp_join(fc_own, fc_came)
    tokens_slot, cot_group, out_full, fc_part, kept = lax.optimization_barrier(
        (tokens_slot, cot_group, out_full, fc_part, kept)
    )

    def group_of(values):
        parts = values.reshape((seg_count, ctx_count, rows) + values.shape[1:])
        return lax.dynamic_index_in_dim(parts, ctx_at, 1, keepdims=False).reshape((group_rows,) + values.shape[1:])

    inputs = tokens[0].astype(f32)
    inputs_group = group_of(tokens_slot).astype(f32)
    norm_slot, pairs, query_slot, score_slot = project(heads, tokens_slot, gain_one[None], all_in)
    key_score = lax.dynamic_index_in_dim(
        score_slot.reshape(heads, seg_count, ctx_count, rows), ctx_at, 2, keepdims=False
    ).reshape(heads, group_rows)
    norm_one = group_of(norm_slot)
    base = jnp.stack([ctx_at * rows, ctx_at]).astype(jnp.int32)
    head_outs, prob = attend(base, kept, query_slot, pairs, score_slot)
    head_outs, proj_came = lax.optimization_barrier((head_outs, proj_came))
    attended = head_outs.reshape(heads * HD, group_rows)
    attended_all = lax.all_gather(attended, "sp", axis=0, tiled=True)
    out_part = lax.dynamic_slice_in_dim(out_full, sp_at * heads * HD, heads * HD, 0)
    proj_part = dp_join(proj_own, proj_came)

    group_at = jnp.arange(group_rows, dtype=jnp.int32)
    group_positions = (group_at // rows) * (ctx_count * rows) + ctx_at * rows + group_at % rows
    grad_out_group = jnp.where((group_positions < lengths[0])[:, None], cot_group, jnp.zeros_like(cot_group))
    positions = (sp_at * ctx_count + ctx_at) * rows + jnp.arange(rows, dtype=jnp.int32)
    is_valid = (positions < lengths[0])[:, None]

    mixed_group = inputs_group + contract_rows(attended_all, out_full)
    norm_two = layer_norm(mixed_group, gain_two).astype(bf16)
    mixed = lax.dynamic_slice_in_dim(mixed_group, sp_at * rows, rows, 0)
    hidden_pre = jnp.dot(norm_two, fc_part, preferred_element_type=f32)
    active = tanh_gelu(hidden_pre).astype(bf16)
    grad_active = contract_cols(grad_out_group, proj_part)
    _, gelu_pull = jax.vjp(tanh_gelu, hidden_pre)
    grad_pre = gelu_pull(grad_active)[0].astype(bf16)
    fc_parts = contract_rows(norm_two, grad_pre).astype(bf16).reshape(dp_count, ctx_count, piece, width)
    proj_parts = contract_rows(active, grad_out_group).astype(bf16).reshape(dp_count, ctx_count, -1, width)
    grad_pre, fc_parts, proj_parts = lax.optimization_barrier((grad_pre, fc_parts, proj_parts))
    mlp_parts = jnp.transpose(jnp.concatenate([fc_parts, proj_parts], axis=2), (1, 0, 2, 3))
    mlp_ctx = lax.psum_scatter(
        mlp_parts.reshape(ctx_count, -1, width), "ctx", scatter_dimension=0, tiled=False
    ).reshape(dp_count, -1, width)
    grad_norm_parts = contract_cols(grad_pre, fc_part).astype(bf16)
    grad_norm_two = exchange_sum(grad_norm_parts.reshape(seg_count, rows, width), "sp")
    _, second_pull = jax.vjp(layer_norm, mixed, gain_two)
    grad_mixed_norm, second_gain_grad = second_pull(grad_norm_two)
    grad_out = jnp.where(is_valid, cotangent[0], jnp.zeros_like(cotangent[0])).astype(f32)
    grad_mixed = grad_out + grad_mixed_norm
    grad_branch = lax.all_gather(grad_mixed.astype(bf16), "sp", axis=0, tiled=True)

    out_wide = jnp.pad(out_part.reshape(heads, HD, width), ((0, 0), (HD, 0), (0, 0))).reshape(heads * LANES, width)
    grad_wide = contract_cols(grad_branch, out_wide).astype(bf16)
    out_mine = jnp.dot(attended, grad_branch, preferred_element_type=f32).astype(bf16)
    grad_wide, out_mine = lax.optimization_barrier((grad_wide, out_mine))
    out_sum = dp_sum(out_mine)
    gain_cols = jnp.stack([gain_one, second_gain_grad], axis=1)
    grad_wide, gain_cols = lax.optimization_barrier((grad_wide, gain_cols))
    query_grads, pair_grads, turned, query_turned, gates = attend_back(
        ctx_count, base, query_slot, grad_wide, pairs, prob
    )
    turned, out_sum = lax.optimization_barrier((turned, out_sum))
    pair_mine = lax.psum_scatter(pair_grads, "ctx", scatter_dimension=0, tiled=False)
    small = weight_grad(turned, query_turned, gates, score_slot[:, 0], norm_slot, norm_one, all_in, gain_cols)
    late = jnp.concatenate(
        [dp_scatter(small.reshape(dp_count, ctx_count, piece, width)), out_sum.reshape(ctx_count, -1, width)], axis=1
    )
    late_sum = exchange_sum(late, "ctx").astype(bf16)
    gradients = jnp.concatenate([late_sum[:piece], dp_scatter(mlp_ctx), late_sum[piece:]], axis=0)
    pair_mine, gradients, active_late = lax.optimization_barrier((pair_mine, gradients, active))
    gathered = lax.all_gather(gradients, ("sp", "ctx"), axis=0, tiled=False).reshape(seg_count, ctx_count, -1, width)
    proj_piece = hidden // (seg_count * dp_count * ctx_count)

    grad_norm_part = finish(pair_mine, query_grads, key_score, all_in)
    expanded = exchange_sum(
        jnp.dot(active_late, proj_part, preferred_element_type=f32).astype(bf16).reshape(seg_count, rows, width), "sp"
    )
    output = jnp.where(is_valid, mixed + expanded, 0.0).astype(bf16)[None]
    grad_norm_one = exchange_sum(grad_norm_part.reshape(seg_count, rows, width), "sp")
    _, first_pull = jax.vjp(lambda values: layer_norm(values, gain_one), inputs)
    grad_input_norm = first_pull(grad_norm_one)[0]
    input_grad = (grad_mixed + grad_input_norm).astype(bf16)[None]

    qkv_grad, score_grad, fc_grad, proj_grad = unpack(gathered, heads, piece, proj_piece, dp_count, hidden)
    proj_grad = proj_grad.reshape(-1, width)
    out_grad = lax.dynamic_slice_in_dim(
        gathered[:, :, 2 * piece + proj_piece :].reshape(width, width), dp_at * weight_rows, weight_rows, 0
    ).astype(f32)
    gains = jnp.sum(
        gathered[:, :, :piece, head_cols + heads : head_cols + heads + 2].astype(f32), axis=0
    ).reshape(weight_rows, 2)
    return (output, input_grad, gains[:, 0], qkv_grad, score_grad, out_grad, gains[:, 1], fc_grad, proj_grad)


def solution(mesh):
    placed = (
        P("dp", ("sp", "ctx"), None),
        P("dp", ("sp", "ctx"), None),
        P("dp"),
        P("dp", None, "ctx", "sp", None),
        P("dp"),
        P("dp", None),
        P("dp", None),
        P("dp", None),
        P("dp"),
        P("dp", None),
        P("dp", None),
    )
    return jax.shard_map(
        per_device,
        mesh=mesh,
        in_specs=placed,
        out_specs=(
            P("dp", ("sp", "ctx"), None),
            P("dp", ("sp", "ctx"), None),
            P("dp"),
            P("dp", None),
            P("dp", None),
            P("dp", None),
            P("dp"),
            P("dp", None),
            P("dp", None),
        ),
        check_vma=False,
    )
```

```python
import functools

import jax
import jax.numpy as jnp
from jax import lax
from jax.experimental import pallas as pl
from jax.experimental.pallas import tpu as pltpu
from jax.sharding import PartitionSpec as P

H = 12
HD = 64
WIN = 64
LANES = 128
SLOT = 2048


EPSILON = 1e-05


def layer_norm(values, gain):
    mean_value = jnp.mean(values, axis=-1, keepdims=True)
    centred = values - mean_value
    variance = jnp.mean(centred * centred, axis=-1, keepdims=True)
    return centred * lax.rsqrt(variance + EPSILON) * gain


def tanh_gelu(values):
    return jax.nn.gelu(values, approximate=True)


def contract_rows(left, right):
    return lax.dot_general(
        left, right, (((0,), (0,)), ((), ())), preferred_element_type=jnp.float32
    )


def contract_cols(left, right):
    return lax.dot_general(
        left, right, (((1,), (1,)), ((), ())), preferred_element_type=jnp.float32
    )


NT = (((1,), (1,)), ((), ()))


PAD_ROWS = 16
STEP = 128
SUB = 256


def project_kernel(heads, tokens_ref, gain_ref, in_ref, norm_ref, pair_ref, query_ref, score_ref):
    f32, bf16 = jnp.float32, jnp.bfloat16
    keys = heads * 2 * HD
    for start in range(0, tokens_ref.shape[0], SUB):
        rows = slice(start, start + SUB)
        norm = layer_norm(tokens_ref[rows, :].astype(f32), gain_ref[...]).astype(bf16)
        norm_ref[rows, :] = norm
        pair_ref[rows, :] = jnp.dot(norm, in_ref[:, :keys], preferred_element_type=f32).astype(bf16)
        rest = jnp.dot(norm, in_ref[:, keys:], preferred_element_type=f32)
        for head in range(heads):
            query = rest[:, head * HD : (head + 1) * HD]
            query_ref[rows, head * LANES : (head + 1) * LANES] = jnp.concatenate(
                [query, jnp.zeros_like(query)], axis=1
            ).astype(bf16)
        scores = jnp.transpose(rest[:, LANES:])[heads * HD - LANES : heads * HD - LANES + heads, :].astype(bf16)
        for head in range(heads):
            score_ref[head, :, rows] = scores[head : head + 1, :]


def project(heads, tokens, gain, weights):
    slot, width = tokens.shape
    block = 4 * SUB if slot % (4 * SUB) == 0 else SUB
    return pl.pallas_call(
        functools.partial(project_kernel, heads),
        grid=(slot // block,),
        in_specs=[
            pl.BlockSpec((block, width), lambda r: (r, 0)),
            pl.BlockSpec((1, width), lambda r: (0, 0)),
            pl.BlockSpec(weights.shape, lambda r: (0, 0)),
        ],
        out_specs=[
            pl.BlockSpec((block, width), lambda r: (r, 0)),
            pl.BlockSpec((block, heads * LANES), lambda r: (r, 0)),
            pl.BlockSpec((block, heads * LANES), lambda r: (r, 0)),
            pl.BlockSpec((heads, 1, block), lambda r: (0, 0, r)),
        ],
        out_shape=[
            jax.ShapeDtypeStruct((slot, width), jnp.bfloat16),
            jax.ShapeDtypeStruct((slot, heads * LANES), jnp.bfloat16),
            jax.ShapeDtypeStruct((slot, heads * LANES), jnp.bfloat16),
            jax.ShapeDtypeStruct((heads, 1, slot), jnp.bfloat16),
        ],
        name="project",
    )(tokens, gain, weights)


def attend_body(first, tiles, base, idx_ref, q_ref, kv_ref, key_ref, out_ref, prob_ref, score_ref, pair_ref, gate_ref):
    rows = q_ref.shape[0]
    if first:
        gate_ref[...] = jnp.broadcast_to(-jnp.log1p(jnp.exp(-key_ref[0].astype(jnp.float32))), gate_ref.shape)
    span = tiles * LANES
    f32, bf16 = jnp.float32, jnp.bfloat16
    score_ref[:, :span] = (
        lax.dot_general(q_ref[...], kv_ref[:span, :], NT, preferred_element_type=f32) * HD ** (-0.5)
        + gate_ref[0:1, :span]
    )
    kept = idx_ref[0, 0]
    pair_ref[...] = jnp.concatenate([kept, kept], axis=1)
    wide = 8 * HD
    sub = lax.broadcasted_iota(jnp.int32, (8, wide), 0)
    lane = lax.broadcasted_iota(jnp.int32, (8, wide), 1)
    own = (lane // HD) == sub
    subf = sub.astype(f32)
    ahead = lax.broadcasted_iota(jnp.int32, (8, LANES), 0) - lax.broadcasted_iota(jnp.int32, (8, LANES), 1)
    near_from = max(0, tiles - 5)

    def eight(start):
        four = pair_ref[pl.ds(start, 8), :]
        index = jnp.concatenate([four] * 4, axis=1)
        pos = base + start + sub
        high = jnp.where(own & (pos >= WIN), index >> 7, -2).astype(f32)
        low = jnp.sum(jnp.where(own, (index & 127).astype(f32), 0.0), axis=0, keepdims=True) - subf
        high_pair = jnp.concatenate([high, high - 1.0], axis=0).astype(bf16)
        low_pair = jnp.concatenate([low, low - 8.0], axis=0).astype(bf16)
        one, zero = jnp.ones((), bf16), jnp.zeros((), bf16)
        left = jnp.concatenate(
            [jnp.where(high_pair == jnp.array(2 * p, bf16), one, zero) for p in range(tiles // 2)], axis=0
        )
        right = jnp.concatenate(
            [jnp.where(low_pair == jnp.array(16 * p, bf16), one, zero) for p in range(8)], axis=0
        )
        count = lax.dot_general(left, right, NT, preferred_element_type=f32)
        gap = ahead + (base + start)
        masked, counts = [], []
        largest = None
        for tile in range(tiles):
            number = count[8 * tile : 8 * tile + 8, :]
            if tile >= near_from:
                far = gap - tile * LANES
                number = number + jnp.where((far >= 0) & (far < WIN), 1.0, 0.0)
            value = jnp.where(number > 0.0, score_ref[pl.ds(start, 8), tile * LANES : (tile + 1) * LANES], -1e30)
            counts.append(number)
            masked.append(value)
            largest = value if largest is None else jnp.maximum(largest, value)
        top = jnp.max(largest, axis=1, keepdims=True)
        total = None
        expos = []
        for number, value in zip(counts, masked):
            expo = jnp.exp(value - top) * number
            expos.append(expo)
            total = expo if total is None else total + expo
        inverse = 1.0 / jnp.sum(total, axis=1, keepdims=True)
        return [expo * inverse for expo in expos]

    def step(index, carry):
        for at in range(0, STEP, 16):
            start = pl.multiple_of(index * STEP + at, 16)
            near, next_to = eight(start), eight(start + 8)
            for tile in range(tiles):
                prob_ref[0, 0, pl.ds(start, 16), tile * LANES : (tile + 1) * LANES] = jnp.concatenate(
                    [near[tile], next_to[tile]], axis=0
                ).astype(bf16)
        return carry

    if rows == STEP:
        step(0, 0)
    else:
        lax.fori_loop(0, rows // STEP, step, 0)
    both = jnp.dot(prob_ref[0, 0, :, :span], kv_ref[:span, :], preferred_element_type=f32)
    out_ref[0] = jnp.transpose(both)[HD:, :].astype(bf16)


def attend_kernel(parts, chunk, base_ref, *refs):
    part = pl.program_id(1)
    base = base_ref[0] + part * chunk
    for at in range(parts):
        pl.when(part == at)(
            functools.partial(attend_body, at == 0, (at + 1) * chunk // LANES, base, *refs)
        )


def attend(base, kept, query, pairs, key_score):
    heads, parts, block, keep = kept.shape
    slot = pairs.shape[0]
    chunk = slot // parts
    grid_spec = pltpu.PrefetchScalarGridSpec(
        num_scalar_prefetch=1,
        grid=(heads, parts),
        in_specs=[
            pl.BlockSpec((1, 1, block, keep), lambda h, r, b: (h, r, 0, 0)),
            pl.BlockSpec((block, LANES), lambda h, r, b: (r * (chunk // block) + b[1], h)),
            pl.BlockSpec((slot, LANES), lambda h, r, b: (0, h)),
            pl.BlockSpec((1, 1, slot), lambda h, r, b: (h, 0, 0)),
        ],
        out_specs=[
            pl.BlockSpec((1, HD, block), lambda h, r, b: (h, 0, r)),
            pl.BlockSpec((1, 1, block, slot), lambda h, r, b: (h, r, 0, 0)),
        ],
        scratch_shapes=[
            pltpu.VMEM((block, slot), jnp.float32),
            pltpu.VMEM((block, 2 * keep), jnp.int32),
            pltpu.VMEM((8, slot), jnp.float32),
        ],
    )
    return pl.pallas_call(
        functools.partial(attend_kernel, parts, chunk),
        grid_spec=grid_spec,
        out_shape=[
            jax.ShapeDtypeStruct((heads, HD, parts * block), jnp.bfloat16),
            jax.ShapeDtypeStruct((heads, parts, block, slot), jnp.bfloat16),
        ],
        name="attend",
    )(base, kept, query, pairs, key_score)


def attend_back_body(first, last, tiles, chunk, q_ref, grad_ref, kv_ref, prob_ref, dq_ref, out_ref, turned_ref, dq_turned_ref, gates_ref, raw_ref, dkv_ref, gate_ref):
    f32, bf16 = jnp.float32, jnp.bfloat16
    rows = q_ref.shape[0]
    steps = tiles * LANES // chunk
    if first:
        dkv_ref[...] = jnp.zeros_like(dkv_ref)
        gate_ref[...] = jnp.zeros_like(gate_ref)
    dot_sum = None
    for at in range(steps):
        cols = slice(at * chunk, (at + 1) * chunk)
        raw = lax.dot_general(grad_ref[...], kv_ref[cols, :], NT, preferred_element_type=f32)
        raw_ref[:, cols] = raw
        part = jnp.sum(raw * prob_ref[0, 0, :, cols].astype(f32), axis=1, keepdims=True)
        dot_sum = part if dot_sum is None else dot_sum + part
    lane = lax.broadcasted_iota(jnp.int32, (rows, LANES), 1)
    scaled = jnp.where(lane == HD, 1.0, q_ref[...].astype(f32) * HD ** (-0.5))
    query_t = jnp.transpose(scaled)[: HD + 16].astype(bf16)
    grad_t = jnp.transpose(grad_ref[...].astype(f32))[HD:].astype(bf16)
    dq = None
    for at in range(steps):
        cols = slice(at * chunk, (at + 1) * chunk)
        prob = prob_ref[0, 0, :, cols]
        grad_score = (prob.astype(f32) * (raw_ref[:, cols] - dot_sum)).astype(bf16)
        piece = jnp.dot(grad_score, kv_ref[cols, :], preferred_element_type=f32)
        dq = piece if dq is None else dq + piece
        keys = jnp.dot(query_t, grad_score, preferred_element_type=f32)
        dkv_ref[:HD, cols] += keys[:HD]
        gate_ref[:, cols] += keys[HD : HD + 8]
        dkv_ref[HD:, cols] += jnp.dot(grad_t, prob, preferred_element_type=f32)
    dq = dq * HD ** (-0.5)
    dq_ref[...] = dq.astype(dq_ref.dtype)
    dq_turned_ref[0] = jnp.transpose(dq)[:HD, :].astype(bf16)
    if last:
        turned_ref[0] = dkv_ref[...].astype(bf16)
        gates_ref[0] = gate_ref[...]
        count, height, _ = out_ref.shape
        parts = (height - PAD_ROWS) // LANES
        for at in range(count):
            rows_of = []
            for part in range(parts):
                cols = slice((part * count + at) * LANES, (part * count + at + 1) * LANES)
                out_ref[at, part * LANES : (part + 1) * LANES, :] = jnp.transpose(dkv_ref[:, cols]).astype(bf16)
                rows_of.append(gate_ref[0:1, cols])
            rows_of.append(jnp.zeros((PAD_ROWS - parts, LANES), f32))
            out_ref[at, height - PAD_ROWS :, :] = jnp.concatenate(rows_of, axis=0).astype(bf16)


def attend_back_kernel(parts, chunk, base_ref, *refs):
    part = pl.program_id(1)
    for at in range(parts):
        pl.when(part == at)(
            functools.partial(attend_back_body, at == 0, at == parts - 1, (at + 1) * chunk // LANES, chunk, *refs)
        )


def attend_back(count, base, query, grad, pairs, prob):
    heads, parts, block, slot = prob.shape
    width = pairs.shape[1]
    height = slot // count + PAD_ROWS
    chunk = slot // parts
    return pl.pallas_call(
        functools.partial(attend_back_kernel, parts, chunk),
        grid_spec=pltpu.PrefetchScalarGridSpec(
        num_scalar_prefetch=1,
        grid=(heads, parts),
        in_specs=[
            pl.BlockSpec((block, LANES), lambda h, r, b: (r * (chunk // block) + b[1], h)),
            pl.BlockSpec((block, LANES), lambda h, r, b: (r, h)),
            pl.BlockSpec((slot, LANES), lambda h, r, b: (0, h)),
            pl.BlockSpec((1, 1, block, slot), lambda h, r, b: (h, r, 0, 0)),
        ],
        out_specs=[
            pl.BlockSpec((block, LANES), lambda h, r, b: (r, h)),
            pl.BlockSpec((count, height, LANES), lambda h, r, b: (0, 0, h)),
            pl.BlockSpec((1, LANES, slot), lambda h, r, b: (h, 0, 0)),
            pl.BlockSpec((1, HD, block), lambda h, r, b: (h, 0, r)),
            pl.BlockSpec((1, 8, slot), lambda h, r, b: (h, 0, 0)),
        ],
        scratch_shapes=[
            pltpu.VMEM((block, slot), jnp.float32),
            pltpu.VMEM((LANES, slot), jnp.float32),
            pltpu.VMEM((8, slot), jnp.float32),
        ],
        ),
        out_shape=[
            jax.ShapeDtypeStruct((parts * block, heads * LANES), jnp.bfloat16),
            jax.ShapeDtypeStruct((count, height, width), jnp.bfloat16),
            jax.ShapeDtypeStruct((heads, LANES, slot), jnp.bfloat16),
            jax.ShapeDtypeStruct((heads, HD, parts * block), jnp.bfloat16),
            jax.ShapeDtypeStruct((heads, 8, slot), jnp.float32),
        ],
        name="attend_back",
    )(base, query, grad, pairs, prob)


def weight_kernel(turned_ref, dq_ref, gates_ref, score_ref, slot_ref, norm_ref, in_ref, gain_ref, out_ref):
    f32, bf16 = jnp.float32, jnp.bfloat16
    heads, _, slot = turned_ref.shape
    wide = in_ref.shape[1]
    width = slot_ref.shape[1]
    total = jnp.concatenate([gates_ref[head, 0:1, :] for head in range(heads)], axis=0)
    total = total * jax.nn.sigmoid(-score_ref[...].astype(f32))
    total = jnp.concatenate([total, jnp.zeros((PAD_ROWS - heads, slot), f32)], axis=0).astype(bf16)
    turned = [
        jnp.dot(turned_ref[...].reshape(heads * LANES, slot), slot_ref[...], preferred_element_type=f32),
        jnp.dot(dq_ref[...].reshape(heads * HD, -1), norm_ref[...], preferred_element_type=f32),
        jnp.dot(total, slot_ref[...], preferred_element_type=f32),
        jnp.zeros((wide - heads * 3 * HD - PAD_ROWS, width), f32),
    ]
    small = jnp.transpose(jnp.concatenate(turned, axis=0))
    gain_grad = jnp.sum(small * in_ref[...].astype(f32), axis=1, keepdims=True) / gain_ref[:, 0:1]
    lane = lax.broadcasted_iota(jnp.int32, small.shape, 1)
    at = heads * 3 * HD + heads
    small = jnp.where(lane == at, gain_grad, jnp.where(lane == at + 1, gain_ref[:, 1:2], small))
    out_ref[...] = small.astype(bf16)


def weight_grad(turned, dq, gates, score, norm_slot, norm_one, weights, gains):
    width = norm_one.shape[1]
    return pl.pallas_call(
        weight_kernel,
        out_shape=jax.ShapeDtypeStruct((width, weights.shape[1]), jnp.bfloat16),
        name="weight_grad",
    )(turned, dq, gates, score, norm_slot, norm_one, weights, gains)


def finish_kernel(heads, pair_ref, dq_ref, score_ref, in_ref, grad_ref):
    f32, bf16 = jnp.float32, jnp.bfloat16
    group = dq_ref.shape[0]
    parts = group // LANES
    wide = in_ref.shape[1]
    gates = pair_ref[group:, :].astype(f32)
    total = jnp.concatenate(
        [
            jnp.concatenate([gates[at : at + 1, head * LANES : (head + 1) * LANES] for at in range(parts)], axis=1)
            for head in range(heads)
        ],
        axis=0,
    )
    total = total * jax.nn.sigmoid(-score_ref[...].astype(f32))
    scores = jnp.transpose(jnp.concatenate([total, jnp.zeros((LANES - heads, group), f32)], axis=0))
    rest = wide - heads * 3 * HD
    columns = jnp.concatenate(
        [pair_ref[:group, :].astype(f32)]
        + [dq_ref[:, head * LANES : head * LANES + HD].astype(f32) for head in range(heads)]
        + [scores[:, :rest]],
        axis=1,
    ).astype(bf16)
    grad_ref[...] = lax.dot_general(columns, in_ref[...], NT, preferred_element_type=f32).astype(bf16)


def finish(pair, dq, score, weights):
    return pl.pallas_call(
        functools.partial(finish_kernel, score.shape[0]),
        out_shape=jax.ShapeDtypeStruct((dq.shape[0], weights.shape[0]), jnp.bfloat16),
        name="finish",
    )(pair, dq, score, weights)


def unpack_kernel(groups, heads, piece, parts, dp_ref, all_ref, qkv_ref, score_ref, fc_ref, proj_ref, *rest):
    f32 = jnp.float32
    keys = heads * 2 * HD
    part_cols = fc_ref.shape[1] // (groups * parts)
    for out_ref in rest:
        mine = out_ref.shape[0]
        for at in range(mine):
            out_ref[at] = all_ref[dp_ref[0] * mine + at, :, 2 * piece + proj_ref.shape[2] :, :].astype(f32)
    for step in range(all_ref.shape[1]):
        rows = slice(step * piece, (step + 1) * piece)
        for at in range(groups):
            values = all_ref[at, step, :piece, :].astype(f32)
            for head in range(heads):
                start = (at * heads + head) * 3 * HD
                qkv_ref[rows, start : start + HD] = values[:, keys + head * HD : keys + (head + 1) * HD]
                qkv_ref[rows, start + HD : start + 3 * HD] = values[:, head * 2 * HD : (head + 1) * 2 * HD]
            score_ref[rows, at * heads : (at + 1) * heads] = values[:, keys + heads * HD : keys + heads * HD + heads]
            values = all_ref[at, step, piece : 2 * piece, :].astype(f32)
            for part in range(parts):
                start = (part * groups + at) * part_cols
                fc_ref[rows, start : start + part_cols] = values[:, part * part_cols : (part + 1) * part_cols]
            proj_ref[at, step] = all_ref[at, step, 2 * piece : 2 * piece + proj_ref.shape[2], :].astype(f32)


def unpack(at, gathered, heads, piece, proj_piece, parts, hidden):
    groups, count, rows, width = gathered.shape
    step = 1 if piece % 16 == 0 else count
    blocks = [
        ((count * piece, groups * heads * 3 * HD), (step * piece, groups * heads * 3 * HD), lambda c, d: (c, 0)),
        ((count * piece, groups * heads), (step * piece, groups * heads), lambda c, d: (c, 0)),
        ((count * piece, hidden), (step * piece, hidden), lambda c, d: (c, 0)),
        ((groups, count, proj_piece, width), (groups, step, proj_piece, width), lambda c, d: (0, c, 0, 0)),
    ]
    if groups % parts == 0:
        last = rows - 2 * piece - proj_piece
        mine = groups // parts
        blocks.append(((mine, count, last, width), (mine, step, last, width), lambda c, d: (0, c, 0, 0)))
    return pl.pallas_call(
        functools.partial(unpack_kernel, groups, heads, piece, parts),
        grid_spec=pltpu.PrefetchScalarGridSpec(
            num_scalar_prefetch=1,
            grid=(count // step,),
            in_specs=[pl.BlockSpec((groups, step, rows, width), lambda c, d: (0, c, 0, 0))],
            out_specs=[pl.BlockSpec(block, index) for _, block, index in blocks],
        ),
        out_shape=[jax.ShapeDtypeStruct(shape, jnp.float32) for shape, _, _ in blocks],
        name="unpack",
    )(at, gathered)


def arrange_kernel(heads, rows, qkv_ref, score_ref, gains_ref, out_ref):
    f32 = jnp.float32
    values = qkv_ref[...].astype(f32)
    keys = heads * 2 * HD
    width = out_ref.shape[1]
    pieces = [values[:, (3 * head + 1) * HD : (3 * head + 3) * HD] for head in range(heads)]
    pieces += [values[:, 3 * head * HD : (3 * head + 1) * HD] for head in range(heads)]
    pieces += [score_ref[...].astype(f32), jnp.zeros((rows, width - heads * 3 * HD - heads), f32)]
    out_ref[:rows, :] = jnp.concatenate(pieces, axis=1).astype(out_ref.dtype)
    out_ref[rows:, :] = jnp.concatenate(
        [gains_ref[...].astype(f32), jnp.zeros((gains_ref.shape[0], width - rows), f32)], axis=1
    ).astype(out_ref.dtype)


def arrange(qkv, score, gains, width):
    rows, heads = score.shape
    return pl.pallas_call(
        functools.partial(arrange_kernel, heads, rows),
        out_shape=jax.ShapeDtypeStruct((rows + PAD_ROWS, width), qkv.dtype),
        name="arrange",
    )(qkv, score, gains)


def dp_send(mine):
    if lax.axis_size("dp") != 2:
        return lax.all_gather(mine, "dp", axis=0, tiled=True)
    return lax.ppermute(mine, "dp", [(0, 1), (1, 0)])


def dp_join(mine, came):
    if lax.axis_size("dp") != 2:
        return came
    return jnp.where(
        lax.axis_index("dp") == 0, jnp.concatenate([mine, came]), jnp.concatenate([came, mine])
    )


def dp_scatter(parts):
    if lax.axis_size("dp") != 2:
        return lax.psum_scatter(parts, "dp", scatter_dimension=0, tiled=False)
    at = lax.axis_index("dp")
    mine = lax.dynamic_index_in_dim(parts, at, 0, keepdims=False)
    sent = lax.dynamic_index_in_dim(parts, 1 - at, 0, keepdims=False)
    other = lax.ppermute(sent, "dp", [(0, 1), (1, 0)])
    return (mine.astype(jnp.float32) + other.astype(jnp.float32)).astype(parts.dtype)


def group_rows_of(mine, group, count):
    height = mine.shape[0]
    if lax.axis_size("dp") != 2 or height % count != 0:
        whole = lax.all_gather(mine, "dp", axis=0, tiled=True)
        return lax.dynamic_slice_in_dim(whole, group * count, count, 0)
    near = lax.dynamic_slice_in_dim(mine, group * count % height, count, 0)
    far = lax.ppermute(near, "dp", [(0, 1), (1, 0)])
    return jnp.where(lax.axis_index("dp") == group * count // height, near, far)


def ctx_scatter(parts):
    count = lax.axis_size("ctx")
    at = lax.axis_index("ctx")
    total = lax.dynamic_index_in_dim(parts, at, 0, keepdims=False).astype(jnp.float32)
    for step in range(1, count):
        sent = lax.dynamic_index_in_dim(parts, (at + step) % count, 0, keepdims=False)
        came = lax.ppermute(sent, "ctx", [(source, (source + step) % count) for source in range(count)])
        total += came.astype(jnp.float32)
    return total.astype(parts.dtype)


def dp_sum(mine):
    if lax.axis_size("dp") != 2:
        return lax.psum(mine, "dp")
    other = lax.ppermute(mine, "dp", [(0, 1), (1, 0)])
    return (mine.astype(jnp.float32) + other.astype(jnp.float32)).astype(mine.dtype)


def exchange_sum(parts, axis):
    came = lax.all_to_all(parts, axis, split_axis=0, concat_axis=0, tiled=True)
    return jnp.sum(came.astype(jnp.float32), axis=0)


def per_device(
    tokens,
    cotangent,
    lengths,
    kept_keys,
    first_gain,
    qkv_weight,
    score_weight,
    out_weight,
    second_gain,
    fc_weight,
    proj_weight,
):
    f32, bf16 = jnp.float32, jnp.bfloat16
    dp_count = lax.axis_size("dp")
    seg_count = lax.axis_size("sp")
    ctx_count = lax.axis_size("ctx")
    dp_at = lax.axis_index("dp")
    sp_at = lax.axis_index("sp")
    ctx_at = lax.axis_index("ctx")
    rows = tokens.shape[1]
    width = tokens.shape[2]
    group_rows = seg_count * rows
    heads = H // seg_count
    head_cols = heads * 3 * HD
    hidden = fc_weight.shape[1]
    hidden_part = hidden // (dp_count * seg_count)
    piece = width // (dp_count * ctx_count)

    keys = heads * 2 * HD
    wide = -(-(head_cols + heads + 2) // LANES) * LANES
    weight_rows = width // dp_count
    own_in = arrange(
        lax.dynamic_slice_in_dim(qkv_weight, sp_at * head_cols, head_cols, 1),
        lax.dynamic_slice_in_dim(score_weight, sp_at * heads, heads, 1),
        jnp.pad(jnp.stack([first_gain, second_gain]), ((0, PAD_ROWS - 2), (0, 0))),
        wide,
    )
    if dp_count == 2:
        other_in = lax.ppermute(own_in, "dp", [(0, 1), (1, 0)])
        parts_in = [
            jnp.where(dp_at == at, own_in, other_in) for at in range(dp_count)
        ]
    else:
        parts_in = list(lax.all_gather(own_in, "dp", axis=0, tiled=False))
    tokens_slot = lax.all_gather(tokens[0], ("sp", "ctx"), axis=0, tiled=True)
    all_in = jnp.concatenate([part[:weight_rows] for part in parts_in])
    gain_one = jnp.concatenate([part[weight_rows, :weight_rows] for part in parts_in]).astype(f32)
    gain_two = jnp.concatenate([part[weight_rows + 1, :weight_rows] for part in parts_in]).astype(f32)

    fc_own = jnp.concatenate(
        [
            lax.dynamic_slice_in_dim(fc_weight, (at * seg_count + sp_at) * hidden_part, hidden_part, 1)
            for at in range(dp_count)
        ],
        axis=1,
    )
    proj_own = lax.dynamic_slice_in_dim(proj_weight, sp_at * hidden_part, hidden_part, 0)
    all_in, out_own, fc_own, proj_own = lax.optimization_barrier((all_in, out_weight, fc_own, proj_own))
    out_came = dp_send(out_own)
    fc_came = dp_send(fc_own)
    proj_came = dp_send(proj_own)

    cot_own, all_in = lax.optimization_barrier((cotangent[0], all_in))
    cot_group = lax.all_gather(cot_own, "sp", axis=0, tiled=True)
    kept = jnp.transpose(kept_keys[0], (2, 0, 1, 3))
    out_full = dp_join(out_own, out_came)
    fc_part = dp_join(fc_own, fc_came)
    tokens_slot, cot_group, out_full, fc_part, kept = lax.optimization_barrier(
        (tokens_slot, cot_group, out_full, fc_part, kept)
    )

    def group_of(values):
        parts = values.reshape((seg_count, ctx_count, rows) + values.shape[1:])
        return lax.dynamic_index_in_dim(parts, ctx_at, 1, keepdims=False).reshape((group_rows,) + values.shape[1:])

    inputs = tokens[0].astype(f32)
    inputs_group = group_of(tokens_slot).astype(f32)
    norm_slot, pairs, query_slot, score_slot = project(heads, tokens_slot, gain_one[None], all_in)
    key_score = lax.dynamic_index_in_dim(
        score_slot.reshape(heads, seg_count, ctx_count, rows), ctx_at, 2, keepdims=False
    ).reshape(heads, group_rows)
    norm_one = group_of(norm_slot)
    base = jnp.stack([ctx_at * rows, ctx_at]).astype(jnp.int32)
    head_outs, prob = attend(base, kept, query_slot, pairs, score_slot)
    head_outs, proj_came = lax.optimization_barrier((head_outs, proj_came))
    attended = head_outs.reshape(heads * HD, group_rows)
    attended_all = lax.all_gather(attended, "sp", axis=0, tiled=True)
    out_part = lax.dynamic_slice_in_dim(out_full, sp_at * heads * HD, heads * HD, 0)
    proj_part = dp_join(proj_own, proj_came)

    group_at = jnp.arange(group_rows, dtype=jnp.int32)
    group_positions = (group_at // rows) * (ctx_count * rows) + ctx_at * rows + group_at % rows
    grad_out_group = jnp.where((group_positions < lengths[0])[:, None], cot_group, jnp.zeros_like(cot_group))
    positions = (sp_at * ctx_count + ctx_at) * rows + jnp.arange(rows, dtype=jnp.int32)
    is_valid = (positions < lengths[0])[:, None]

    mixed_group = inputs_group + contract_rows(attended_all, out_full)
    norm_two = layer_norm(mixed_group, gain_two).astype(bf16)
    mixed = lax.dynamic_slice_in_dim(mixed_group, sp_at * rows, rows, 0)
    hidden_pre = jnp.dot(norm_two, fc_part, preferred_element_type=f32)
    active = tanh_gelu(hidden_pre).astype(bf16)
    grad_active = contract_cols(grad_out_group, proj_part)
    _, gelu_pull = jax.vjp(tanh_gelu, hidden_pre)
    grad_pre = gelu_pull(grad_active)[0].astype(bf16)
    fc_parts = contract_rows(norm_two, grad_pre).astype(bf16).reshape(dp_count, ctx_count, piece, width)
    proj_parts = contract_rows(active, grad_out_group).astype(bf16).reshape(dp_count, ctx_count, -1, width)
    grad_pre, fc_parts, proj_parts = lax.optimization_barrier((grad_pre, fc_parts, proj_parts))
    mlp_parts = jnp.transpose(jnp.concatenate([fc_parts, proj_parts], axis=2), (1, 0, 2, 3))
    mlp_ctx = lax.psum_scatter(
        mlp_parts.reshape(ctx_count, -1, width), "ctx", scatter_dimension=0, tiled=False
    ).reshape(dp_count, -1, width)
    grad_norm_parts = contract_cols(grad_pre, fc_part).astype(bf16)
    norm_came = lax.all_to_all(
        grad_norm_parts.reshape(seg_count, rows, width), "sp", split_axis=0, concat_axis=0, tiled=True
    )
    score_rows = score_slot[:, 0]
    norm_came, norm_one, score_rows, key_score = lax.optimization_barrier(
        (norm_came, norm_one, score_rows, key_score)
    )
    grad_norm_two = jnp.sum(norm_came.astype(f32), axis=0)
    _, second_pull = jax.vjp(layer_norm, mixed, gain_two)
    grad_mixed_norm, second_gain_grad = second_pull(grad_norm_two)
    grad_out = jnp.where(is_valid, cotangent[0], jnp.zeros_like(cotangent[0])).astype(f32)
    grad_mixed = grad_out + grad_mixed_norm
    grad_branch = lax.all_gather(grad_mixed.astype(bf16), "sp", axis=0, tiled=True)

    out_wide = jnp.pad(out_part.reshape(heads, HD, width), ((0, 0), (HD, 0), (0, 0))).reshape(heads * LANES, width)
    grad_wide = contract_cols(grad_branch, out_wide).astype(bf16)
    out_mine = jnp.dot(attended, grad_branch, preferred_element_type=f32).astype(bf16)
    grad_wide, out_mine = lax.optimization_barrier((grad_wide, out_mine))
    gain_cols = jnp.stack([gain_one, second_gain_grad], axis=1)
    grad_wide, gain_cols = lax.optimization_barrier((grad_wide, gain_cols))
    query_grads, pair_grads, turned, query_turned, gates = attend_back(
        ctx_count, base, query_slot, grad_wide, pairs, prob
    )
    pair_mine = lax.psum_scatter(pair_grads, "ctx", scatter_dimension=0, tiled=False)
    small = weight_grad(turned, query_turned, gates, score_rows, norm_slot, norm_one, all_in, gain_cols)
    small, out_mine = lax.optimization_barrier((small, out_mine))
    small_came = lax.all_to_all(
        small.reshape(dp_count * ctx_count, piece, wide), ("dp", "ctx"), split_axis=0, concat_axis=0, tiled=True
    )
    small_own = jnp.pad(jnp.sum(small_came.astype(f32), axis=0).astype(bf16), ((0, 0), (0, width - wide)))
    out_own = dp_sum(ctx_scatter(out_mine.reshape(ctx_count, -1, width)))
    gradients = jnp.concatenate([small_own, dp_scatter(mlp_ctx), out_own], axis=0)
    pair_mine, gradients, active_late = lax.optimization_barrier((pair_mine, gradients, active))
    gathered = lax.all_gather(gradients, ("sp", "ctx"), axis=0, tiled=False).reshape(seg_count, ctx_count, -1, width)
    proj_piece = hidden // (seg_count * dp_count * ctx_count)

    grad_norm_part = finish(pair_mine, query_grads, key_score, all_in)
    expanded = exchange_sum(
        jnp.dot(active_late, proj_part, preferred_element_type=f32).astype(bf16).reshape(seg_count, rows, width), "sp"
    )
    output = jnp.where(is_valid, mixed + expanded, 0.0).astype(bf16)[None]
    grad_norm_one = exchange_sum(grad_norm_part.reshape(seg_count, rows, width), "sp")
    _, first_pull = jax.vjp(lambda values: layer_norm(values, gain_one), inputs)
    grad_input_norm = first_pull(grad_norm_one)[0]
    input_grad = (grad_mixed + grad_input_norm).astype(bf16)[None]

    qkv_grad, score_grad, fc_grad, proj_grad, *rest = unpack(
        dp_at.astype(jnp.int32)[None], gathered, heads, piece, proj_piece, dp_count, hidden
    )
    proj_grad = proj_grad.reshape(-1, width)
    if rest:
        out_grad = rest[0].reshape(weight_rows, width)
    else:
        out_grad = lax.dynamic_slice_in_dim(
            gathered[:, :, 2 * piece + proj_piece :].reshape(width, width), dp_at * weight_rows, weight_rows, 0
        ).astype(f32)
    gains = jnp.sum(
        gathered[:, :, :piece, head_cols + heads : head_cols + heads + 2].astype(f32), axis=0
    ).reshape(weight_rows, 2)
    return (output, input_grad, gains[:, 0], qkv_grad, score_grad, out_grad, gains[:, 1], fc_grad, proj_grad)


def solution(mesh):
    placed = (
        P("dp", ("sp", "ctx"), None),
        P("dp", ("sp", "ctx"), None),
        P("dp"),
        P("dp", None, "ctx", "sp", None),
        P("dp"),
        P("dp", None),
        P("dp", None),
        P("dp", None),
        P("dp"),
        P("dp", None),
        P("dp", None),
    )
    return jax.shard_map(
        per_device,
        mesh=mesh,
        in_specs=placed,
        out_specs=(
            P("dp", ("sp", "ctx"), None),
            P("dp", ("sp", "ctx"), None),
            P("dp"),
            P("dp", None),
            P("dp", None),
            P("dp", None),
            P("dp"),
            P("dp", None),
            P("dp", None),
        ),
        check_vma=False,
    )
```

```python
import functools

import jax
import jax.numpy as jnp
from jax import lax
from jax.experimental import pallas as pl
from jax.experimental.pallas import tpu as pltpu
from jax.sharding import PartitionSpec as P

H = 12
HD = 64
WIN = 64
LANES = 128
SLOT = 2048


EPSILON = 1e-05


def layer_norm(values, gain):
    mean_value = jnp.mean(values, axis=-1, keepdims=True)
    centred = values - mean_value
    variance = jnp.mean(centred * centred, axis=-1, keepdims=True)
    return centred * lax.rsqrt(variance + EPSILON) * gain


def tanh_gelu(values):
    return jax.nn.gelu(values, approximate=True)


def contract_rows(left, right):
    return lax.dot_general(
        left, right, (((0,), (0,)), ((), ())), preferred_element_type=jnp.float32
    )


def contract_cols(left, right):
    return lax.dot_general(
        left, right, (((1,), (1,)), ((), ())), preferred_element_type=jnp.float32
    )


NT = (((1,), (1,)), ((), ()))


PAD_ROWS = 16
STEP = 128
SUB = 256


def project_kernel(heads, tokens_ref, gain_ref, in_ref, norm_ref, pair_ref, query_ref, score_ref):
    f32, bf16 = jnp.float32, jnp.bfloat16
    keys = heads * 2 * HD
    for start in range(0, tokens_ref.shape[0], SUB):
        rows = slice(start, start + SUB)
        norm = layer_norm(tokens_ref[rows, :].astype(f32), gain_ref[...]).astype(bf16)
        norm_ref[rows, :] = norm
        pair_ref[rows, :] = jnp.dot(norm, in_ref[:, :keys], preferred_element_type=f32).astype(bf16)
        rest = jnp.dot(norm, in_ref[:, keys:], preferred_element_type=f32)
        for head in range(heads):
            query = rest[:, head * HD : (head + 1) * HD]
            query_ref[rows, head * LANES : (head + 1) * LANES] = jnp.concatenate(
                [query, jnp.zeros_like(query)], axis=1
            ).astype(bf16)
        scores = jnp.transpose(rest[:, LANES:])[heads * HD - LANES : heads * HD - LANES + heads, :].astype(bf16)
        for head in range(heads):
            score_ref[head, :, rows] = scores[head : head + 1, :]


def project(heads, tokens, gain, weights):
    slot, width = tokens.shape
    block = 4 * SUB if slot % (4 * SUB) == 0 else SUB
    return pl.pallas_call(
        functools.partial(project_kernel, heads),
        grid=(slot // block,),
        in_specs=[
            pl.BlockSpec((block, width), lambda r: (r, 0)),
            pl.BlockSpec((1, width), lambda r: (0, 0)),
            pl.BlockSpec(weights.shape, lambda r: (0, 0)),
        ],
        out_specs=[
            pl.BlockSpec((block, width), lambda r: (r, 0)),
            pl.BlockSpec((block, heads * LANES), lambda r: (r, 0)),
            pl.BlockSpec((block, heads * LANES), lambda r: (r, 0)),
            pl.BlockSpec((heads, 1, block), lambda r: (0, 0, r)),
        ],
        out_shape=[
            jax.ShapeDtypeStruct((slot, width), jnp.bfloat16),
            jax.ShapeDtypeStruct((slot, heads * LANES), jnp.bfloat16),
            jax.ShapeDtypeStruct((slot, heads * LANES), jnp.bfloat16),
            jax.ShapeDtypeStruct((heads, 1, slot), jnp.bfloat16),
        ],
        name="project",
    )(tokens, gain, weights)


def attend_body(first, tiles, base, idx_ref, q_ref, kv_ref, key_ref, out_ref, prob_ref, score_ref, pair_ref, gate_ref):
    rows = q_ref.shape[0]
    if first:
        gate_ref[...] = jnp.broadcast_to(-jnp.log1p(jnp.exp(-key_ref[0].astype(jnp.float32))), gate_ref.shape)
    span = tiles * LANES
    f32, bf16 = jnp.float32, jnp.bfloat16
    score_ref[:, :span] = (
        lax.dot_general(q_ref[...], kv_ref[:span, :], NT, preferred_element_type=f32) * HD ** (-0.5)
        + gate_ref[0:1, :span]
    )
    kept = idx_ref[0, 0]
    pair_ref[...] = jnp.concatenate([kept, kept], axis=1)
    wide = 8 * HD
    sub = lax.broadcasted_iota(jnp.int32, (8, wide), 0)
    lane = lax.broadcasted_iota(jnp.int32, (8, wide), 1)
    own = (lane // HD) == sub
    subf = sub.astype(f32)
    ahead = lax.broadcasted_iota(jnp.int32, (8, LANES), 0) - lax.broadcasted_iota(jnp.int32, (8, LANES), 1)
    near_from = max(0, tiles - 5)

    def eight(start):
        four = pair_ref[pl.ds(start, 8), :]
        index = jnp.concatenate([four] * 4, axis=1)
        pos = base + start + sub
        high = jnp.where(own & (pos >= WIN), index >> 7, -2).astype(f32)
        low = jnp.sum(jnp.where(own, (index & 127).astype(f32), 0.0), axis=0, keepdims=True) - subf
        high_pair = jnp.concatenate([high, high - 1.0], axis=0).astype(bf16)
        low_pair = jnp.concatenate([low, low - 8.0], axis=0).astype(bf16)
        one, zero = jnp.ones((), bf16), jnp.zeros((), bf16)
        left = jnp.concatenate(
            [jnp.where(high_pair == jnp.array(2 * p, bf16), one, zero) for p in range(tiles // 2)], axis=0
        )
        right = jnp.concatenate(
            [jnp.where(low_pair == jnp.array(16 * p, bf16), one, zero) for p in range(8)], axis=0
        )
        count = lax.dot_general(left, right, NT, preferred_element_type=f32)
        gap = ahead + (base + start)
        masked, counts = [], []
        largest = None
        for tile in range(tiles):
            number = count[8 * tile : 8 * tile + 8, :]
            if tile >= near_from:
                far = gap - tile * LANES
                number = number + jnp.where((far >= 0) & (far < WIN), 1.0, 0.0)
            value = jnp.where(number > 0.0, score_ref[pl.ds(start, 8), tile * LANES : (tile + 1) * LANES], -1e30)
            counts.append(number)
            masked.append(value)
            largest = value if largest is None else jnp.maximum(largest, value)
        top = jnp.max(largest, axis=1, keepdims=True)
        total = None
        expos = []
        for number, value in zip(counts, masked):
            expo = jnp.exp(value - top) * number
            expos.append(expo)
            total = expo if total is None else total + expo
        inverse = 1.0 / jnp.sum(total, axis=1, keepdims=True)
        return [expo * inverse for expo in expos]

    def step(index, carry):
        for at in range(0, STEP, 16):
            start = pl.multiple_of(index * STEP + at, 16)
            near, next_to = eight(start), eight(start + 8)
            for tile in range(tiles):
                prob_ref[0, 0, pl.ds(start, 16), tile * LANES : (tile + 1) * LANES] = jnp.concatenate(
                    [near[tile], next_to[tile]], axis=0
                ).astype(bf16)
        return carry

    if rows == STEP:
        step(0, 0)
    else:
        lax.fori_loop(0, rows // STEP, step, 0)
    both = jnp.dot(prob_ref[0, 0, :, :span], kv_ref[:span, :], preferred_element_type=f32)
    out_ref[0] = jnp.transpose(both)[HD:, :].astype(bf16)


def attend_kernel(parts, chunk, base_ref, *refs):
    part = pl.program_id(1)
    base = base_ref[0] + part * chunk
    for at in range(parts):
        pl.when(part == at)(
            functools.partial(attend_body, at == 0, (at + 1) * chunk // LANES, base, *refs)
        )


def attend(base, kept, query, pairs, key_score):
    heads, parts, block, keep = kept.shape
    slot = pairs.shape[0]
    chunk = slot // parts
    grid_spec = pltpu.PrefetchScalarGridSpec(
        num_scalar_prefetch=1,
        grid=(heads, parts),
        in_specs=[
            pl.BlockSpec((1, 1, block, keep), lambda h, r, b: (h, r, 0, 0)),
            pl.BlockSpec((block, LANES), lambda h, r, b: (r * (chunk // block) + b[1], h)),
            pl.BlockSpec((slot, LANES), lambda h, r, b: (0, h)),
            pl.BlockSpec((1, 1, slot), lambda h, r, b: (h, 0, 0)),
        ],
        out_specs=[
            pl.BlockSpec((1, HD, block), lambda h, r, b: (h, 0, r)),
            pl.BlockSpec((1, 1, block, slot), lambda h, r, b: (h, r, 0, 0)),
        ],
        scratch_shapes=[
            pltpu.VMEM((block, slot), jnp.float32),
            pltpu.VMEM((block, 2 * keep), jnp.int32),
            pltpu.VMEM((8, slot), jnp.float32),
        ],
    )
    return pl.pallas_call(
        functools.partial(attend_kernel, parts, chunk),
        grid_spec=grid_spec,
        out_shape=[
            jax.ShapeDtypeStruct((heads, HD, parts * block), jnp.bfloat16),
            jax.ShapeDtypeStruct((heads, parts, block, slot), jnp.bfloat16),
        ],
        name="attend",
    )(base, kept, query, pairs, key_score)


def attend_back_body(first, last, tiles, chunk, q_ref, grad_ref, kv_ref, prob_ref, dq_ref, out_ref, turned_ref, dq_turned_ref, gates_ref, raw_ref, dkv_ref, gate_ref):
    f32, bf16 = jnp.float32, jnp.bfloat16
    rows = q_ref.shape[0]
    steps = tiles * LANES // chunk
    if first:
        dkv_ref[...] = jnp.zeros_like(dkv_ref)
        gate_ref[...] = jnp.zeros_like(gate_ref)
    dot_sum = None
    for at in range(steps):
        cols = slice(at * chunk, (at + 1) * chunk)
        raw = lax.dot_general(grad_ref[...], kv_ref[cols, :], NT, preferred_element_type=f32)
        raw_ref[:, cols] = raw
        part = jnp.sum(raw * prob_ref[0, 0, :, cols].astype(f32), axis=1, keepdims=True)
        dot_sum = part if dot_sum is None else dot_sum + part
    lane = lax.broadcasted_iota(jnp.int32, (rows, LANES), 1)
    scaled = jnp.where(lane == HD, 1.0, q_ref[...].astype(f32) * HD ** (-0.5))
    query_t = jnp.transpose(scaled)[: HD + 16].astype(bf16)
    grad_t = jnp.transpose(grad_ref[...].astype(f32))[HD:].astype(bf16)
    dq = None
    for at in range(steps):
        cols = slice(at * chunk, (at + 1) * chunk)
        prob = prob_ref[0, 0, :, cols]
        grad_score = (prob.astype(f32) * (raw_ref[:, cols] - dot_sum)).astype(bf16)
        piece = jnp.dot(grad_score, kv_ref[cols, :], preferred_element_type=f32)
        dq = piece if dq is None else dq + piece
        keys = jnp.dot(query_t, grad_score, preferred_element_type=f32)
        dkv_ref[:HD, cols] += keys[:HD]
        gate_ref[:, cols] += keys[HD : HD + 8]
        dkv_ref[HD:, cols] += jnp.dot(grad_t, prob, preferred_element_type=f32)
    dq = dq * HD ** (-0.5)
    dq_ref[...] = dq.astype(dq_ref.dtype)
    dq_turned_ref[0] = jnp.transpose(dq)[:HD, :].astype(bf16)
    if last:
        turned_ref[0] = dkv_ref[...].astype(bf16)
        gates_ref[0] = gate_ref[...]
        count, height, _ = out_ref.shape
        parts = (height - PAD_ROWS) // LANES
        for at in range(count):
            rows_of = []
            for part in range(parts):
                cols = slice((part * count + at) * LANES, (part * count + at + 1) * LANES)
                out_ref[at, part * LANES : (part + 1) * LANES, :] = jnp.transpose(dkv_ref[:, cols]).astype(bf16)
                rows_of.append(gate_ref[0:1, cols])
            rows_of.append(jnp.zeros((PAD_ROWS - parts, LANES), f32))
            out_ref[at, height - PAD_ROWS :, :] = jnp.concatenate(rows_of, axis=0).astype(bf16)


def attend_back_kernel(parts, chunk, base_ref, *refs):
    part = pl.program_id(1)
    for at in range(parts):
        pl.when(part == at)(
            functools.partial(attend_back_body, at == 0, at == parts - 1, (at + 1) * chunk // LANES, chunk, *refs)
        )


def attend_back(count, base, query, grad, pairs, prob):
    heads, parts, block, slot = prob.shape
    width = pairs.shape[1]
    height = slot // count + PAD_ROWS
    chunk = slot // parts
    return pl.pallas_call(
        functools.partial(attend_back_kernel, parts, chunk),
        grid_spec=pltpu.PrefetchScalarGridSpec(
        num_scalar_prefetch=1,
        grid=(heads, parts),
        in_specs=[
            pl.BlockSpec((block, LANES), lambda h, r, b: (r * (chunk // block) + b[1], h)),
            pl.BlockSpec((block, LANES), lambda h, r, b: (r, h)),
            pl.BlockSpec((slot, LANES), lambda h, r, b: (0, h)),
            pl.BlockSpec((1, 1, block, slot), lambda h, r, b: (h, r, 0, 0)),
        ],
        out_specs=[
            pl.BlockSpec((block, LANES), lambda h, r, b: (r, h)),
            pl.BlockSpec((count, height, LANES), lambda h, r, b: (0, 0, h)),
            pl.BlockSpec((1, LANES, slot), lambda h, r, b: (h, 0, 0)),
            pl.BlockSpec((1, HD, block), lambda h, r, b: (h, 0, r)),
            pl.BlockSpec((1, 8, slot), lambda h, r, b: (h, 0, 0)),
        ],
        scratch_shapes=[
            pltpu.VMEM((block, slot), jnp.float32),
            pltpu.VMEM((LANES, slot), jnp.float32),
            pltpu.VMEM((8, slot), jnp.float32),
        ],
        ),
        out_shape=[
            jax.ShapeDtypeStruct((parts * block, heads * LANES), jnp.bfloat16),
            jax.ShapeDtypeStruct((count, height, width), jnp.bfloat16),
            jax.ShapeDtypeStruct((heads, LANES, slot), jnp.bfloat16),
            jax.ShapeDtypeStruct((heads, HD, parts * block), jnp.bfloat16),
            jax.ShapeDtypeStruct((heads, 8, slot), jnp.float32),
        ],
        name="attend_back",
    )(base, query, grad, pairs, prob)


def weight_kernel(turned_ref, dq_ref, gates_ref, score_ref, slot_ref, norm_ref, in_ref, gain_ref, out_ref):
    f32, bf16 = jnp.float32, jnp.bfloat16
    heads, _, slot = turned_ref.shape
    wide = in_ref.shape[1]
    width = slot_ref.shape[1]
    total = jnp.concatenate([gates_ref[head, 0:1, :] for head in range(heads)], axis=0)
    total = total * jax.nn.sigmoid(-score_ref[...].astype(f32))
    total = jnp.concatenate([total, jnp.zeros((PAD_ROWS - heads, slot), f32)], axis=0).astype(bf16)
    turned = [
        jnp.dot(turned_ref[...].reshape(heads * LANES, slot), slot_ref[...], preferred_element_type=f32),
        jnp.dot(dq_ref[...].reshape(heads * HD, -1), norm_ref[...], preferred_element_type=f32),
        jnp.dot(total, slot_ref[...], preferred_element_type=f32),
        jnp.zeros((wide - heads * 3 * HD - PAD_ROWS, width), f32),
    ]
    small = jnp.transpose(jnp.concatenate(turned, axis=0))
    gain_grad = jnp.sum(small * in_ref[...].astype(f32), axis=1, keepdims=True) / gain_ref[:, 0:1]
    lane = lax.broadcasted_iota(jnp.int32, small.shape, 1)
    at = heads * 3 * HD + heads
    small = jnp.where(lane == at, gain_grad, jnp.where(lane == at + 1, gain_ref[:, 1:2], small))
    out_ref[...] = small.astype(bf16)


def weight_grad(turned, dq, gates, score, norm_slot, norm_one, weights, gains):
    width = norm_one.shape[1]
    return pl.pallas_call(
        weight_kernel,
        out_shape=jax.ShapeDtypeStruct((width, weights.shape[1]), jnp.bfloat16),
        name="weight_grad",
    )(turned, dq, gates, score, norm_slot, norm_one, weights, gains)


def finish_kernel(heads, pair_ref, dq_ref, score_ref, in_ref, grad_ref):
    f32, bf16 = jnp.float32, jnp.bfloat16
    group = dq_ref.shape[0]
    parts = group // LANES
    wide = in_ref.shape[1]
    gates = pair_ref[group:, :].astype(f32)
    total = jnp.concatenate(
        [
            jnp.concatenate([gates[at : at + 1, head * LANES : (head + 1) * LANES] for at in range(parts)], axis=1)
            for head in range(heads)
        ],
        axis=0,
    )
    total = total * jax.nn.sigmoid(-score_ref[...].astype(f32))
    scores = jnp.transpose(jnp.concatenate([total, jnp.zeros((LANES - heads, group), f32)], axis=0))
    rest = wide - heads * 3 * HD
    columns = jnp.concatenate(
        [pair_ref[:group, :].astype(f32)]
        + [dq_ref[:, head * LANES : head * LANES + HD].astype(f32) for head in range(heads)]
        + [scores[:, :rest]],
        axis=1,
    ).astype(bf16)
    grad_ref[...] = lax.dot_general(columns, in_ref[...], NT, preferred_element_type=f32).astype(bf16)


def finish(pair, dq, score, weights):
    return pl.pallas_call(
        functools.partial(finish_kernel, score.shape[0]),
        out_shape=jax.ShapeDtypeStruct((dq.shape[0], weights.shape[0]), jnp.bfloat16),
        name="finish",
    )(pair, dq, score, weights)


def unpack_kernel(groups, heads, piece, parts, dp_ref, all_ref, qkv_ref, score_ref, fc_ref, proj_ref, *rest):
    f32 = jnp.float32
    keys = heads * 2 * HD
    part_cols = fc_ref.shape[1] // (groups * parts)
    for out_ref in rest:
        mine = out_ref.shape[0]
        for at in range(mine):
            out_ref[at] = all_ref[dp_ref[0] * mine + at, :, 2 * piece + proj_ref.shape[2] :, :].astype(f32)
    for step in range(all_ref.shape[1]):
        rows = slice(step * piece, (step + 1) * piece)
        scores, gains = [], None
        for at in range(groups):
            values = all_ref[at, step, :piece, :].astype(f32)
            for head in range(heads):
                start = (at * heads + head) * 3 * HD
                qkv_ref[rows, start : start + HD] = values[:, keys + head * HD : keys + (head + 1) * HD]
                qkv_ref[rows, start + HD : start + 3 * HD] = values[:, head * 2 * HD : (head + 1) * 2 * HD]
            scores.append(values[:, keys + heads * HD : keys + heads * HD + heads])
            gain = values[:, keys + heads * HD + heads : keys + heads * HD + heads + 2]
            gains = gain if gains is None else gains + gain
            values = all_ref[at, step, piece : 2 * piece, :].astype(f32)
            for part in range(parts):
                start = (part * groups + at) * part_cols
                fc_ref[rows, start : start + part_cols] = values[:, part * part_cols : (part + 1) * part_cols]
            proj_ref[at, step] = all_ref[at, step, 2 * piece : 2 * piece + proj_ref.shape[2], :].astype(f32)
        narrow = jnp.concatenate(
            scores + [gains, jnp.zeros((piece, LANES - groups * heads - 2), f32)], axis=1
        )
        turned = jnp.transpose(jnp.concatenate([narrow, jnp.zeros((LANES - piece, LANES), f32)], axis=0))

        def store(index):
            score_ref[:, index * piece : (index + 1) * piece] = turned[: score_ref.shape[0], :piece]

        if all_ref.shape[1] > 1:
            store(step)
        else:
            for index in range(score_ref.shape[1] // piece):
                pl.when(pl.program_id(0) == index)(functools.partial(store, index))


def unpack(at, gathered, heads, piece, proj_piece, parts, hidden):
    groups, count, rows, width = gathered.shape
    step = 1 if piece % 16 == 0 else count
    blocks = [
        ((count * piece, groups * heads * 3 * HD), (step * piece, groups * heads * 3 * HD), lambda c, d: (c, 0)),
        ((PAD_ROWS, count * piece), (PAD_ROWS, count * piece), lambda c, d: (0, 0)),
        ((count * piece, hidden), (step * piece, hidden), lambda c, d: (c, 0)),
        ((groups, count, proj_piece, width), (groups, step, proj_piece, width), lambda c, d: (0, c, 0, 0)),
    ]
    if groups % parts == 0:
        last = rows - 2 * piece - proj_piece
        mine = groups // parts
        blocks.append(((mine, count, last, width), (mine, step, last, width), lambda c, d: (0, c, 0, 0)))
    return pl.pallas_call(
        functools.partial(unpack_kernel, groups, heads, piece, parts),
        grid_spec=pltpu.PrefetchScalarGridSpec(
            num_scalar_prefetch=1,
            grid=(count // step,),
            in_specs=[pl.BlockSpec((groups, step, rows, width), lambda c, d: (0, c, 0, 0))],
            out_specs=[pl.BlockSpec(block, index) for _, block, index in blocks],
        ),
        out_shape=[jax.ShapeDtypeStruct(shape, jnp.float32) for shape, _, _ in blocks],
        name="unpack",
    )(at, gathered)


def arrange_kernel(heads, rows, qkv_ref, score_ref, gains_ref, out_ref):
    f32 = jnp.float32
    values = qkv_ref[...].astype(f32)
    keys = heads * 2 * HD
    width = out_ref.shape[1]
    pieces = [values[:, (3 * head + 1) * HD : (3 * head + 3) * HD] for head in range(heads)]
    pieces += [values[:, 3 * head * HD : (3 * head + 1) * HD] for head in range(heads)]
    pieces += [score_ref[...].astype(f32), jnp.zeros((rows, width - heads * 3 * HD - heads), f32)]
    out_ref[:rows, :] = jnp.concatenate(pieces, axis=1).astype(out_ref.dtype)
    out_ref[rows:, :] = jnp.concatenate(
        [gains_ref[...].astype(f32), jnp.zeros((gains_ref.shape[0], width - rows), f32)], axis=1
    ).astype(out_ref.dtype)


def arrange(qkv, score, gains, width):
    rows, heads = score.shape
    return pl.pallas_call(
        functools.partial(arrange_kernel, heads, rows),
        out_shape=jax.ShapeDtypeStruct((rows + PAD_ROWS, width), qkv.dtype),
        name="arrange",
    )(qkv, score, gains)


def dp_send(mine):
    if lax.axis_size("dp") != 2:
        return lax.all_gather(mine, "dp", axis=0, tiled=True)
    return lax.ppermute(mine, "dp", [(0, 1), (1, 0)])


def dp_join(mine, came):
    if lax.axis_size("dp") != 2:
        return came
    return jnp.where(
        lax.axis_index("dp") == 0, jnp.concatenate([mine, came]), jnp.concatenate([came, mine])
    )


def dp_scatter(parts):
    if lax.axis_size("dp") != 2:
        return lax.psum_scatter(parts, "dp", scatter_dimension=0, tiled=False)
    at = lax.axis_index("dp")
    mine = lax.dynamic_index_in_dim(parts, at, 0, keepdims=False)
    sent = lax.dynamic_index_in_dim(parts, 1 - at, 0, keepdims=False)
    other = lax.ppermute(sent, "dp", [(0, 1), (1, 0)])
    return (mine.astype(jnp.float32) + other.astype(jnp.float32)).astype(parts.dtype)


def group_rows_of(mine, group, count):
    height = mine.shape[0]
    if lax.axis_size("dp") != 2 or height % count != 0:
        whole = lax.all_gather(mine, "dp", axis=0, tiled=True)
        return lax.dynamic_slice_in_dim(whole, group * count, count, 0)
    near = lax.dynamic_slice_in_dim(mine, group * count % height, count, 0)
    far = lax.ppermute(near, "dp", [(0, 1), (1, 0)])
    return jnp.where(lax.axis_index("dp") == group * count // height, near, far)


def dp_sum(mine):
    if lax.axis_size("dp") != 2:
        return lax.psum(mine, "dp")
    other = lax.ppermute(mine, "dp", [(0, 1), (1, 0)])
    return (mine.astype(jnp.float32) + other.astype(jnp.float32)).astype(mine.dtype)


def exchange_sum(parts, axis):
    came = lax.all_to_all(parts, axis, split_axis=0, concat_axis=0, tiled=True)
    return jnp.sum(came.astype(jnp.float32), axis=0)


def per_device(
    tokens,
    cotangent,
    lengths,
    kept_keys,
    first_gain,
    qkv_weight,
    score_weight,
    out_weight,
    second_gain,
    fc_weight,
    proj_weight,
):
    f32, bf16 = jnp.float32, jnp.bfloat16
    dp_count = lax.axis_size("dp")
    seg_count = lax.axis_size("sp")
    ctx_count = lax.axis_size("ctx")
    dp_at = lax.axis_index("dp")
    sp_at = lax.axis_index("sp")
    ctx_at = lax.axis_index("ctx")
    rows = tokens.shape[1]
    width = tokens.shape[2]
    group_rows = seg_count * rows
    heads = H // seg_count
    head_cols = heads * 3 * HD
    hidden = fc_weight.shape[1]
    hidden_part = hidden // (dp_count * seg_count)
    piece = width // (dp_count * ctx_count)

    keys = heads * 2 * HD
    wide = -(-(head_cols + heads + 2) // LANES) * LANES
    weight_rows = width // dp_count
    own_in = arrange(
        lax.dynamic_slice_in_dim(qkv_weight, sp_at * head_cols, head_cols, 1),
        lax.dynamic_slice_in_dim(score_weight, sp_at * heads, heads, 1),
        jnp.pad(jnp.stack([first_gain, second_gain]), ((0, PAD_ROWS - 2), (0, 0))),
        wide,
    )
    if dp_count == 2:
        other_in = lax.ppermute(own_in, "dp", [(0, 1), (1, 0)])
        parts_in = [
            jnp.where(dp_at == at, own_in, other_in) for at in range(dp_count)
        ]
    else:
        parts_in = list(lax.all_gather(own_in, "dp", axis=0, tiled=False))
    tokens_slot = lax.all_gather(tokens[0], ("sp", "ctx"), axis=0, tiled=True)
    all_in = jnp.concatenate([part[:weight_rows] for part in parts_in])
    gain_one = jnp.concatenate([part[weight_rows, :weight_rows] for part in parts_in]).astype(f32)
    gain_two = jnp.concatenate([part[weight_rows + 1, :weight_rows] for part in parts_in]).astype(f32)

    fc_own = jnp.concatenate(
        [
            lax.dynamic_slice_in_dim(fc_weight, (at * seg_count + sp_at) * hidden_part, hidden_part, 1)
            for at in range(dp_count)
        ],
        axis=1,
    )
    proj_own = lax.dynamic_slice_in_dim(proj_weight, sp_at * hidden_part, hidden_part, 0)
    all_in, out_own, fc_own, proj_own = lax.optimization_barrier((all_in, out_weight, fc_own, proj_own))
    out_came = dp_send(out_own)
    fc_came = dp_send(fc_own)
    proj_came = dp_send(proj_own)

    cot_own, all_in = lax.optimization_barrier((cotangent[0], all_in))
    cot_group = lax.all_gather(cot_own, "sp", axis=0, tiled=True)
    kept = jnp.transpose(kept_keys[0], (2, 0, 1, 3))
    out_full = dp_join(out_own, out_came)
    fc_part = dp_join(fc_own, fc_came)
    tokens_slot, cot_group, out_full, fc_part, kept = lax.optimization_barrier(
        (tokens_slot, cot_group, out_full, fc_part, kept)
    )

    def group_of(values):
        parts = values.reshape((seg_count, ctx_count, rows) + values.shape[1:])
        return lax.dynamic_index_in_dim(parts, ctx_at, 1, keepdims=False).reshape((group_rows,) + values.shape[1:])

    inputs = tokens[0].astype(f32)
    inputs_group = group_of(tokens_slot).astype(f32)
    norm_slot, pairs, query_slot, score_slot = project(heads, tokens_slot, gain_one[None], all_in)
    key_score = lax.dynamic_index_in_dim(
        score_slot.reshape(heads, seg_count, ctx_count, rows), ctx_at, 2, keepdims=False
    ).reshape(heads, group_rows)
    norm_one = group_of(norm_slot)
    base = jnp.stack([ctx_at * rows, ctx_at]).astype(jnp.int32)
    head_outs, prob = attend(base, kept, query_slot, pairs, score_slot)
    head_outs, proj_came = lax.optimization_barrier((head_outs, proj_came))
    attended = head_outs.reshape(heads * HD, group_rows)
    attended_all = lax.all_gather(attended, "sp", axis=0, tiled=True)
    out_part = lax.dynamic_slice_in_dim(out_full, sp_at * heads * HD, heads * HD, 0)
    proj_part = dp_join(proj_own, proj_came)

    group_at = jnp.arange(group_rows, dtype=jnp.int32)
    group_positions = (group_at // rows) * (ctx_count * rows) + ctx_at * rows + group_at % rows
    grad_out_group = jnp.where((group_positions < lengths[0])[:, None], cot_group, jnp.zeros_like(cot_group))
    positions = (sp_at * ctx_count + ctx_at) * rows + jnp.arange(rows, dtype=jnp.int32)
    is_valid = (positions < lengths[0])[:, None]

    mixed_group = inputs_group + contract_rows(attended_all, out_full)
    norm_two = layer_norm(mixed_group, gain_two).astype(bf16)
    mixed = lax.dynamic_slice_in_dim(mixed_group, sp_at * rows, rows, 0)
    hidden_pre = jnp.dot(norm_two, fc_part, preferred_element_type=f32)
    active = tanh_gelu(hidden_pre).astype(bf16)
    grad_active = contract_cols(grad_out_group, proj_part)
    _, gelu_pull = jax.vjp(tanh_gelu, hidden_pre)
    grad_pre = gelu_pull(grad_active)[0].astype(bf16)
    grad_norm_parts = contract_cols(grad_pre, fc_part).astype(bf16)
    grad_norm_parts, norm_late, active = lax.optimization_barrier((grad_norm_parts, norm_two, active))
    fc_parts = contract_rows(norm_late, grad_pre).astype(bf16).reshape(dp_count, ctx_count, piece, width)
    proj_parts = contract_rows(active, grad_out_group).astype(bf16).reshape(dp_count, ctx_count, -1, width)
    mlp_parts = jnp.transpose(jnp.concatenate([fc_parts, proj_parts], axis=2), (1, 0, 2, 3))
    mlp_ctx = lax.psum_scatter(
        mlp_parts.reshape(ctx_count, -1, width), "ctx", scatter_dimension=0, tiled=False
    ).reshape(dp_count, -1, width)
    norm_came = lax.all_to_all(
        grad_norm_parts.reshape(seg_count, rows, width), "sp", split_axis=0, concat_axis=0, tiled=True
    )
    score_rows = score_slot[:, 0]
    norm_came, norm_one, score_rows, key_score = lax.optimization_barrier(
        (norm_came, norm_one, score_rows, key_score)
    )
    grad_norm_two = jnp.sum(norm_came.astype(f32), axis=0)
    _, second_pull = jax.vjp(layer_norm, mixed, gain_two)
    grad_mixed_norm, second_gain_grad = second_pull(grad_norm_two)
    grad_out = jnp.where(is_valid, cotangent[0], jnp.zeros_like(cotangent[0])).astype(f32)
    grad_mixed = grad_out + grad_mixed_norm
    grad_branch = lax.all_gather(grad_mixed.astype(bf16), "sp", axis=0, tiled=True)

    out_wide = jnp.pad(out_part.reshape(heads, HD, width), ((0, 0), (HD, 0), (0, 0))).reshape(heads * LANES, width)
    grad_wide = contract_cols(grad_branch, out_wide).astype(bf16)
    out_mine = jnp.dot(attended, grad_branch, preferred_element_type=f32).astype(bf16)
    grad_wide, out_mine = lax.optimization_barrier((grad_wide, out_mine))
    out_sum = dp_sum(out_mine)
    gain_cols = jnp.stack([gain_one, second_gain_grad], axis=1)
    grad_wide, gain_cols = lax.optimization_barrier((grad_wide, gain_cols))
    query_grads, pair_grads, turned, query_turned, gates = attend_back(
        ctx_count, base, query_slot, grad_wide, pairs, prob
    )
    pair_mine = lax.psum_scatter(pair_grads, "ctx", scatter_dimension=0, tiled=False)
    small = weight_grad(turned, query_turned, gates, score_rows, norm_slot, norm_one, all_in, gain_cols)
    small_dp = jnp.pad(
        dp_scatter(small.reshape(dp_count, ctx_count, piece, wide)), ((0, 0), (0, 0), (0, width - wide))
    )
    late = jnp.concatenate([small_dp, out_sum.reshape(ctx_count, -1, width)], axis=1)
    late_sum = exchange_sum(late, "ctx").astype(bf16)
    gradients = jnp.concatenate([late_sum[:piece], dp_scatter(mlp_ctx), late_sum[piece:]], axis=0)
    pair_mine, gradients, active_late = lax.optimization_barrier((pair_mine, gradients, active))
    gathered = lax.all_gather(gradients, ("sp", "ctx"), axis=0, tiled=False).reshape(seg_count, ctx_count, -1, width)
    proj_piece = hidden // (seg_count * dp_count * ctx_count)

    grad_norm_part = finish(pair_mine, query_grads, key_score, all_in)
    expanded = exchange_sum(
        jnp.dot(active_late, proj_part, preferred_element_type=f32).astype(bf16).reshape(seg_count, rows, width), "sp"
    )
    output = jnp.where(is_valid, mixed + expanded, 0.0).astype(bf16)[None]
    grad_norm_one = exchange_sum(grad_norm_part.reshape(seg_count, rows, width), "sp")
    _, first_pull = jax.vjp(lambda values: layer_norm(values, gain_one), inputs)
    grad_input_norm = first_pull(grad_norm_one)[0]
    input_grad = (grad_mixed + grad_input_norm).astype(bf16)[None]

    qkv_grad, turned_rows, fc_grad, proj_grad, *rest = unpack(
        dp_at.astype(jnp.int32)[None], gathered, heads, piece, proj_piece, dp_count, hidden
    )
    proj_grad = proj_grad.reshape(-1, width)
    if rest:
        out_grad = rest[0].reshape(weight_rows, width)
    else:
        out_grad = lax.dynamic_slice_in_dim(
            gathered[:, :, 2 * piece + proj_piece :].reshape(width, width), dp_at * weight_rows, weight_rows, 0
        ).astype(f32)
    score_grad = turned_rows[:H].T
    return (output, input_grad, turned_rows[H], qkv_grad, score_grad, out_grad, turned_rows[H + 1], fc_grad, proj_grad)


def solution(mesh):
    placed = (
        P("dp", ("sp", "ctx"), None),
        P("dp", ("sp", "ctx"), None),
        P("dp"),
        P("dp", None, "ctx", "sp", None),
        P("dp"),
        P("dp", None),
        P("dp", None),
        P("dp", None),
        P("dp"),
        P("dp", None),
        P("dp", None),
    )
    return jax.shard_map(
        per_device,
        mesh=mesh,
        in_specs=placed,
        out_specs=(
            P("dp", ("sp", "ctx"), None),
            P("dp", ("sp", "ctx"), None),
            P("dp"),
            P("dp", None),
            P("dp", None),
            P("dp", None),
            P("dp"),
            P("dp", None),
            P("dp", None),
        ),
        check_vma=False,
    )
```

```python
import functools

import jax
import jax.numpy as jnp
from jax import lax
from jax.experimental import pallas as pl
from jax.experimental.pallas import tpu as pltpu
from jax.sharding import PartitionSpec as P

H = 12
HD = 64
WIN = 64
LANES = 128
SLOT = 2048


EPSILON = 1e-05


def layer_norm(values, gain):
    mean_value = jnp.mean(values, axis=-1, keepdims=True)
    centred = values - mean_value
    variance = jnp.mean(centred * centred, axis=-1, keepdims=True)
    return centred * lax.rsqrt(variance + EPSILON) * gain


def tanh_gelu(values):
    return jax.nn.gelu(values, approximate=True)


def contract_rows(left, right):
    return lax.dot_general(
        left, right, (((0,), (0,)), ((), ())), preferred_element_type=jnp.float32
    )


def contract_cols(left, right):
    return lax.dot_general(
        left, right, (((1,), (1,)), ((), ())), preferred_element_type=jnp.float32
    )


NT = (((1,), (1,)), ((), ()))


PAD_ROWS = 16
STEP = 128
SUB = 256


def project_kernel(heads, tokens_ref, gain_ref, in_ref, norm_ref, pair_ref, query_ref, score_ref):
    f32, bf16 = jnp.float32, jnp.bfloat16
    keys = heads * 2 * HD
    for start in range(0, tokens_ref.shape[0], SUB):
        rows = slice(start, start + SUB)
        norm = layer_norm(tokens_ref[rows, :].astype(f32), gain_ref[...]).astype(bf16)
        norm_ref[rows, :] = norm
        pair_ref[rows, :] = jnp.dot(norm, in_ref[:, :keys], preferred_element_type=f32).astype(bf16)
        rest = jnp.dot(norm, in_ref[:, keys:], preferred_element_type=f32)
        for head in range(heads):
            query = rest[:, head * HD : (head + 1) * HD]
            query_ref[rows, head * LANES : (head + 1) * LANES] = jnp.concatenate(
                [query, jnp.zeros_like(query)], axis=1
            ).astype(bf16)
        scores = jnp.transpose(rest[:, LANES:])[heads * HD - LANES : heads * HD - LANES + heads, :].astype(bf16)
        for head in range(heads):
            score_ref[head, :, rows] = scores[head : head + 1, :]


def project(heads, tokens, gain, weights):
    slot, width = tokens.shape
    block = 4 * SUB if slot % (4 * SUB) == 0 else SUB
    return pl.pallas_call(
        functools.partial(project_kernel, heads),
        grid=(slot // block,),
        in_specs=[
            pl.BlockSpec((block, width), lambda r: (r, 0)),
            pl.BlockSpec((1, width), lambda r: (0, 0)),
            pl.BlockSpec(weights.shape, lambda r: (0, 0)),
        ],
        out_specs=[
            pl.BlockSpec((block, width), lambda r: (r, 0)),
            pl.BlockSpec((block, heads * LANES), lambda r: (r, 0)),
            pl.BlockSpec((block, heads * LANES), lambda r: (r, 0)),
            pl.BlockSpec((heads, 1, block), lambda r: (0, 0, r)),
        ],
        out_shape=[
            jax.ShapeDtypeStruct((slot, width), jnp.bfloat16),
            jax.ShapeDtypeStruct((slot, heads * LANES), jnp.bfloat16),
            jax.ShapeDtypeStruct((slot, heads * LANES), jnp.bfloat16),
            jax.ShapeDtypeStruct((heads, 1, slot), jnp.bfloat16),
        ],
        name="project",
    )(tokens, gain, weights)


def attend_body(first, tiles, base, idx_ref, q_ref, kv_ref, key_ref, out_ref, prob_ref, score_ref, pair_ref, gate_ref):
    rows = q_ref.shape[0]
    if first:
        gate_ref[...] = jnp.broadcast_to(-jnp.log1p(jnp.exp(-key_ref[0].astype(jnp.float32))), gate_ref.shape)
    span = tiles * LANES
    f32, bf16 = jnp.float32, jnp.bfloat16
    score_ref[:, :span] = (
        lax.dot_general(q_ref[...], kv_ref[:span, :], NT, preferred_element_type=f32) * HD ** (-0.5)
        + gate_ref[0:1, :span]
    )
    kept = idx_ref[0, 0]
    pair_ref[...] = jnp.concatenate([kept, kept], axis=1)
    wide = 8 * HD
    sub = lax.broadcasted_iota(jnp.int32, (8, wide), 0)
    lane = lax.broadcasted_iota(jnp.int32, (8, wide), 1)
    own = (lane // HD) == sub
    subf = sub.astype(f32)
    ahead = lax.broadcasted_iota(jnp.int32, (8, LANES), 0) - lax.broadcasted_iota(jnp.int32, (8, LANES), 1)
    near_from = max(0, tiles - 5)

    def eight(start):
        four = pair_ref[pl.ds(start, 8), :]
        index = jnp.concatenate([four] * 4, axis=1)
        pos = base + start + sub
        high = jnp.where(own & (pos >= WIN), index >> 7, -2).astype(f32)
        low = jnp.sum(jnp.where(own, (index & 127).astype(f32), 0.0), axis=0, keepdims=True) - subf
        high_pair = jnp.concatenate([high, high - 1.0], axis=0).astype(bf16)
        low_pair = jnp.concatenate([low, low - 8.0], axis=0).astype(bf16)
        one, zero = jnp.ones((), bf16), jnp.zeros((), bf16)
        left = jnp.concatenate(
            [jnp.where(high_pair == jnp.array(2 * p, bf16), one, zero) for p in range(tiles // 2)], axis=0
        )
        right = jnp.concatenate(
            [jnp.where(low_pair == jnp.array(16 * p, bf16), one, zero) for p in range(8)], axis=0
        )
        count = lax.dot_general(left, right, NT, preferred_element_type=f32)
        gap = ahead + (base + start)
        masked, counts = [], []
        largest = None
        for tile in range(tiles):
            number = count[8 * tile : 8 * tile + 8, :]
            if tile >= near_from:
                far = gap - tile * LANES
                number = number + jnp.where((far >= 0) & (far < WIN), 1.0, 0.0)
            value = jnp.where(number > 0.0, score_ref[pl.ds(start, 8), tile * LANES : (tile + 1) * LANES], -1e30)
            counts.append(number)
            masked.append(value)
            largest = value if largest is None else jnp.maximum(largest, value)
        top = jnp.max(largest, axis=1, keepdims=True)
        total = None
        expos = []
        for number, value in zip(counts, masked):
            expo = jnp.exp(value - top) * number
            expos.append(expo)
            total = expo if total is None else total + expo
        inverse = 1.0 / jnp.sum(total, axis=1, keepdims=True)
        return [expo * inverse for expo in expos]

    def step(index, carry):
        for at in range(0, STEP, 16):
            start = pl.multiple_of(index * STEP + at, 16)
            near, next_to = eight(start), eight(start + 8)
            for tile in range(tiles):
                prob_ref[0, 0, pl.ds(start, 16), tile * LANES : (tile + 1) * LANES] = jnp.concatenate(
                    [near[tile], next_to[tile]], axis=0
                ).astype(bf16)
        return carry

    if rows == STEP:
        step(0, 0)
    else:
        lax.fori_loop(0, rows // STEP, step, 0)
    both = jnp.dot(prob_ref[0, 0, :, :span], kv_ref[:span, :], preferred_element_type=f32)
    out_ref[0] = jnp.transpose(both)[HD:, :].astype(bf16)


def attend_kernel(parts, chunk, base_ref, *refs):
    part = pl.program_id(1)
    base = base_ref[0] + part * chunk
    for at in range(parts):
        pl.when(part == at)(
            functools.partial(attend_body, at == 0, (at + 1) * chunk // LANES, base, *refs)
        )


def attend(base, kept, query, pairs, key_score):
    heads, parts, block, keep = kept.shape
    slot = pairs.shape[0]
    chunk = slot // parts
    grid_spec = pltpu.PrefetchScalarGridSpec(
        num_scalar_prefetch=1,
        grid=(heads, parts),
        in_specs=[
            pl.BlockSpec((1, 1, block, keep), lambda h, r, b: (h, r, 0, 0)),
            pl.BlockSpec((block, LANES), lambda h, r, b: (r * (chunk // block) + b[1], h)),
            pl.BlockSpec((slot, LANES), lambda h, r, b: (0, h)),
            pl.BlockSpec((1, 1, slot), lambda h, r, b: (h, 0, 0)),
        ],
        out_specs=[
            pl.BlockSpec((1, HD, block), lambda h, r, b: (h, 0, r)),
            pl.BlockSpec((1, 1, block, slot), lambda h, r, b: (h, r, 0, 0)),
        ],
        scratch_shapes=[
            pltpu.VMEM((block, slot), jnp.float32),
            pltpu.VMEM((block, 2 * keep), jnp.int32),
            pltpu.VMEM((8, slot), jnp.float32),
        ],
    )
    return pl.pallas_call(
        functools.partial(attend_kernel, parts, chunk),
        grid_spec=grid_spec,
        out_shape=[
            jax.ShapeDtypeStruct((heads, HD, parts * block), jnp.bfloat16),
            jax.ShapeDtypeStruct((heads, parts, block, slot), jnp.bfloat16),
        ],
        name="attend",
    )(base, kept, query, pairs, key_score)


def attend_back_body(first, last, tiles, chunk, q_ref, grad_ref, kv_ref, prob_ref, dq_ref, out_ref, turned_ref, dq_turned_ref, gates_ref, raw_ref, dkv_ref, gate_ref):
    f32, bf16 = jnp.float32, jnp.bfloat16
    rows = q_ref.shape[0]
    steps = tiles * LANES // chunk
    if first:
        dkv_ref[...] = jnp.zeros_like(dkv_ref)
        gate_ref[...] = jnp.zeros_like(gate_ref)
    dot_sum = None
    for at in range(steps):
        cols = slice(at * chunk, (at + 1) * chunk)
        raw = lax.dot_general(grad_ref[...], kv_ref[cols, :], NT, preferred_element_type=f32)
        raw_ref[:, cols] = raw
        part = jnp.sum(raw * prob_ref[0, 0, :, cols].astype(f32), axis=1, keepdims=True)
        dot_sum = part if dot_sum is None else dot_sum + part
    lane = lax.broadcasted_iota(jnp.int32, (rows, LANES), 1)
    scaled = jnp.where(lane == HD, 1.0, q_ref[...].astype(f32) * HD ** (-0.5))
    query_t = jnp.transpose(scaled)[: HD + 16].astype(bf16)
    grad_t = jnp.transpose(grad_ref[...].astype(f32))[HD:].astype(bf16)
    dq = None
    for at in range(steps):
        cols = slice(at * chunk, (at + 1) * chunk)
        prob = prob_ref[0, 0, :, cols]
        grad_score = (prob.astype(f32) * (raw_ref[:, cols] - dot_sum)).astype(bf16)
        piece = jnp.dot(grad_score, kv_ref[cols, :], preferred_element_type=f32)
        dq = piece if dq is None else dq + piece
        keys = jnp.dot(query_t, grad_score, preferred_element_type=f32)
        dkv_ref[:HD, cols] += keys[:HD]
        gate_ref[:, cols] += keys[HD : HD + 8]
        dkv_ref[HD:, cols] += jnp.dot(grad_t, prob, preferred_element_type=f32)
    dq = dq * HD ** (-0.5)
    dq_ref[...] = dq.astype(dq_ref.dtype)
    dq_turned_ref[0] = jnp.transpose(dq)[:HD, :].astype(bf16)
    if last:
        turned_ref[0] = dkv_ref[...].astype(bf16)
        gates_ref[0] = gate_ref[...]
        count, height, _ = out_ref.shape
        parts = (height - PAD_ROWS) // LANES
        for at in range(count):
            rows_of = []
            for part in range(parts):
                cols = slice((part * count + at) * LANES, (part * count + at + 1) * LANES)
                out_ref[at, part * LANES : (part + 1) * LANES, :] = jnp.transpose(dkv_ref[:, cols]).astype(bf16)
                rows_of.append(gate_ref[0:1, cols])
            rows_of.append(jnp.zeros((PAD_ROWS - parts, LANES), f32))
            out_ref[at, height - PAD_ROWS :, :] = jnp.concatenate(rows_of, axis=0).astype(bf16)


def attend_back_kernel(parts, chunk, base_ref, *refs):
    part = pl.program_id(1)
    for at in range(parts):
        pl.when(part == at)(
            functools.partial(attend_back_body, at == 0, at == parts - 1, (at + 1) * chunk // LANES, chunk, *refs)
        )


def attend_back(count, base, query, grad, pairs, prob):
    heads, parts, block, slot = prob.shape
    width = pairs.shape[1]
    height = slot // count + PAD_ROWS
    chunk = slot // parts
    return pl.pallas_call(
        functools.partial(attend_back_kernel, parts, chunk),
        grid_spec=pltpu.PrefetchScalarGridSpec(
        num_scalar_prefetch=1,
        grid=(heads, parts),
        in_specs=[
            pl.BlockSpec((block, LANES), lambda h, r, b: (r * (chunk // block) + b[1], h)),
            pl.BlockSpec((block, LANES), lambda h, r, b: (r, h)),
            pl.BlockSpec((slot, LANES), lambda h, r, b: (0, h)),
            pl.BlockSpec((1, 1, block, slot), lambda h, r, b: (h, r, 0, 0)),
        ],
        out_specs=[
            pl.BlockSpec((block, LANES), lambda h, r, b: (r, h)),
            pl.BlockSpec((count, height, LANES), lambda h, r, b: (0, 0, h)),
            pl.BlockSpec((1, LANES, slot), lambda h, r, b: (h, 0, 0)),
            pl.BlockSpec((1, HD, block), lambda h, r, b: (h, 0, r)),
            pl.BlockSpec((1, 8, slot), lambda h, r, b: (h, 0, 0)),
        ],
        scratch_shapes=[
            pltpu.VMEM((block, slot), jnp.float32),
            pltpu.VMEM((LANES, slot), jnp.float32),
            pltpu.VMEM((8, slot), jnp.float32),
        ],
        ),
        out_shape=[
            jax.ShapeDtypeStruct((parts * block, heads * LANES), jnp.bfloat16),
            jax.ShapeDtypeStruct((count, height, width), jnp.bfloat16),
            jax.ShapeDtypeStruct((heads, LANES, slot), jnp.bfloat16),
            jax.ShapeDtypeStruct((heads, HD, parts * block), jnp.bfloat16),
            jax.ShapeDtypeStruct((heads, 8, slot), jnp.float32),
        ],
        name="attend_back",
    )(base, query, grad, pairs, prob)


def weight_kernel(turned_ref, dq_ref, gates_ref, score_ref, slot_ref, norm_ref, in_ref, gain_ref, out_ref):
    f32, bf16 = jnp.float32, jnp.bfloat16
    heads, _, slot = turned_ref.shape
    wide = in_ref.shape[1]
    width = slot_ref.shape[1]
    total = jnp.concatenate([gates_ref[head, 0:1, :] for head in range(heads)], axis=0)
    total = total * jax.nn.sigmoid(-score_ref[...].astype(f32))
    total = jnp.concatenate([total, jnp.zeros((PAD_ROWS - heads, slot), f32)], axis=0).astype(bf16)
    turned = [
        jnp.dot(turned_ref[...].reshape(heads * LANES, slot), slot_ref[...], preferred_element_type=f32),
        jnp.dot(dq_ref[...].reshape(heads * HD, -1), norm_ref[...], preferred_element_type=f32),
        jnp.dot(total, slot_ref[...], preferred_element_type=f32),
        jnp.zeros((wide - heads * 3 * HD - PAD_ROWS, width), f32),
    ]
    small = jnp.transpose(jnp.concatenate(turned, axis=0))
    gain_grad = jnp.sum(small * in_ref[...].astype(f32), axis=1, keepdims=True) / gain_ref[:, 0:1]
    lane = lax.broadcasted_iota(jnp.int32, small.shape, 1)
    at = heads * 3 * HD + heads
    small = jnp.where(lane == at, gain_grad, jnp.where(lane == at + 1, gain_ref[:, 1:2], small))
    out_ref[...] = small.astype(bf16)


def weight_grad(turned, dq, gates, score, norm_slot, norm_one, weights, gains):
    width = norm_one.shape[1]
    return pl.pallas_call(
        weight_kernel,
        out_shape=jax.ShapeDtypeStruct((width, weights.shape[1]), jnp.bfloat16),
        name="weight_grad",
    )(turned, dq, gates, score, norm_slot, norm_one, weights, gains)


def finish_kernel(heads, pair_ref, dq_ref, score_ref, in_ref, grad_ref):
    f32, bf16 = jnp.float32, jnp.bfloat16
    group = dq_ref.shape[0]
    parts = group // LANES
    wide = in_ref.shape[1]
    gates = pair_ref[group:, :].astype(f32)
    total = jnp.concatenate(
        [
            jnp.concatenate([gates[at : at + 1, head * LANES : (head + 1) * LANES] for at in range(parts)], axis=1)
            for head in range(heads)
        ],
        axis=0,
    )
    total = total * jax.nn.sigmoid(-score_ref[...].astype(f32))
    scores = jnp.transpose(jnp.concatenate([total, jnp.zeros((LANES - heads, group), f32)], axis=0))
    rest = wide - heads * 3 * HD
    columns = jnp.concatenate(
        [pair_ref[:group, :].astype(f32)]
        + [dq_ref[:, head * LANES : head * LANES + HD].astype(f32) for head in range(heads)]
        + [scores[:, :rest]],
        axis=1,
    ).astype(bf16)
    grad_ref[...] = lax.dot_general(columns, in_ref[...], NT, preferred_element_type=f32).astype(bf16)


def finish(pair, dq, score, weights):
    return pl.pallas_call(
        functools.partial(finish_kernel, score.shape[0]),
        out_shape=jax.ShapeDtypeStruct((dq.shape[0], weights.shape[0]), jnp.bfloat16),
        name="finish",
    )(pair, dq, score, weights)


def unpack_kernel(groups, heads, piece, parts, dp_ref, all_ref, qkv_ref, score_ref, fc_ref, proj_ref, *rest):
    f32 = jnp.float32
    keys = heads * 2 * HD
    part_cols = fc_ref.shape[1] // (groups * parts)
    for out_ref in rest:
        mine = out_ref.shape[0]
        for at in range(mine):
            out_ref[at] = all_ref[dp_ref[0] * mine + at, :, 2 * piece + proj_ref.shape[2] :, :].astype(f32)
    for step in range(all_ref.shape[1]):
        rows = slice(step * piece, (step + 1) * piece)
        scores, gains = [], None
        for at in range(groups):
            values = all_ref[at, step, :piece, :].astype(f32)
            for head in range(heads):
                start = (at * heads + head) * 3 * HD
                qkv_ref[rows, start : start + HD] = values[:, keys + head * HD : keys + (head + 1) * HD]
                qkv_ref[rows, start + HD : start + 3 * HD] = values[:, head * 2 * HD : (head + 1) * 2 * HD]
            scores.append(values[:, keys + heads * HD : keys + heads * HD + heads])
            gain = values[:, keys + heads * HD + heads : keys + heads * HD + heads + 2]
            gains = gain if gains is None else gains + gain
            values = all_ref[at, step, piece : 2 * piece, :].astype(f32)
            for part in range(parts):
                start = (part * groups + at) * part_cols
                fc_ref[rows, start : start + part_cols] = values[:, part * part_cols : (part + 1) * part_cols]
            proj_ref[at, step] = all_ref[at, step, 2 * piece : 2 * piece + proj_ref.shape[2], :].astype(f32)
        narrow = jnp.concatenate(
            scores + [gains, jnp.zeros((piece, LANES - groups * heads - 2), f32)], axis=1
        )
        turned = jnp.transpose(jnp.concatenate([narrow, jnp.zeros((LANES - piece, LANES), f32)], axis=0))

        def store(index):
            score_ref[:, index * piece : (index + 1) * piece] = turned[: score_ref.shape[0], :piece]

        if all_ref.shape[1] > 1:
            store(step)
        else:
            for index in range(score_ref.shape[1] // piece):
                pl.when(pl.program_id(0) == index)(functools.partial(store, index))


def unpack(at, gathered, heads, piece, proj_piece, parts, hidden):
    groups, count, rows, width = gathered.shape
    step = 1 if piece % 16 == 0 else count
    blocks = [
        ((count * piece, groups * heads * 3 * HD), (step * piece, groups * heads * 3 * HD), lambda c, d: (c, 0)),
        ((PAD_ROWS, count * piece), (PAD_ROWS, count * piece), lambda c, d: (0, 0)),
        ((count * piece, hidden), (step * piece, hidden), lambda c, d: (c, 0)),
        ((groups, count, proj_piece, width), (groups, step, proj_piece, width), lambda c, d: (0, c, 0, 0)),
    ]
    if groups % parts == 0:
        last = rows - 2 * piece - proj_piece
        mine = groups // parts
        blocks.append(((mine, count, last, width), (mine, step, last, width), lambda c, d: (0, c, 0, 0)))
    return pl.pallas_call(
        functools.partial(unpack_kernel, groups, heads, piece, parts),
        grid_spec=pltpu.PrefetchScalarGridSpec(
            num_scalar_prefetch=1,
            grid=(count // step,),
            in_specs=[pl.BlockSpec((groups, step, rows, width), lambda c, d: (0, c, 0, 0))],
            out_specs=[pl.BlockSpec(block, index) for _, block, index in blocks],
        ),
        out_shape=[jax.ShapeDtypeStruct(shape, jnp.float32) for shape, _, _ in blocks],
        name="unpack",
    )(at, gathered)


def arrange_kernel(heads, rows, qkv_ref, score_ref, gains_ref, out_ref):
    f32 = jnp.float32
    values = qkv_ref[...].astype(f32)
    keys = heads * 2 * HD
    width = out_ref.shape[1]
    pieces = [values[:, (3 * head + 1) * HD : (3 * head + 3) * HD] for head in range(heads)]
    pieces += [values[:, 3 * head * HD : (3 * head + 1) * HD] for head in range(heads)]
    pieces += [score_ref[...].astype(f32), jnp.zeros((rows, width - heads * 3 * HD - heads), f32)]
    out_ref[:rows, :] = jnp.concatenate(pieces, axis=1).astype(out_ref.dtype)
    out_ref[rows:, :] = jnp.concatenate(
        [gains_ref[...].astype(f32), jnp.zeros((gains_ref.shape[0], width - rows), f32)], axis=1
    ).astype(out_ref.dtype)


def arrange(qkv, score, gains, width):
    rows, heads = score.shape
    return pl.pallas_call(
        functools.partial(arrange_kernel, heads, rows),
        out_shape=jax.ShapeDtypeStruct((rows + PAD_ROWS, width), qkv.dtype),
        name="arrange",
    )(qkv, score, gains)


def dp_send(mine):
    if lax.axis_size("dp") != 2:
        return lax.all_gather(mine, "dp", axis=0, tiled=True)
    return lax.ppermute(mine, "dp", [(0, 1), (1, 0)])


def dp_join(mine, came):
    if lax.axis_size("dp") != 2:
        return came
    return jnp.where(
        lax.axis_index("dp") == 0, jnp.concatenate([mine, came]), jnp.concatenate([came, mine])
    )


def dp_scatter(parts):
    if lax.axis_size("dp") != 2:
        return lax.psum_scatter(parts, "dp", scatter_dimension=0, tiled=False)
    at = lax.axis_index("dp")
    mine = lax.dynamic_index_in_dim(parts, at, 0, keepdims=False)
    sent = lax.dynamic_index_in_dim(parts, 1 - at, 0, keepdims=False)
    other = lax.ppermute(sent, "dp", [(0, 1), (1, 0)])
    return (mine.astype(jnp.float32) + other.astype(jnp.float32)).astype(parts.dtype)


def group_rows_of(mine, group, count):
    height = mine.shape[0]
    if lax.axis_size("dp") != 2 or height % count != 0:
        whole = lax.all_gather(mine, "dp", axis=0, tiled=True)
        return lax.dynamic_slice_in_dim(whole, group * count, count, 0)
    near = lax.dynamic_slice_in_dim(mine, group * count % height, count, 0)
    far = lax.ppermute(near, "dp", [(0, 1), (1, 0)])
    return jnp.where(lax.axis_index("dp") == group * count // height, near, far)


def dp_sum(mine):
    if lax.axis_size("dp") != 2:
        return lax.psum(mine, "dp")
    other = lax.ppermute(mine, "dp", [(0, 1), (1, 0)])
    return (mine.astype(jnp.float32) + other.astype(jnp.float32)).astype(mine.dtype)


def exchange_sum(parts, axis):
    came = lax.all_to_all(parts, axis, split_axis=0, concat_axis=0, tiled=True)
    return jnp.sum(came.astype(jnp.float32), axis=0)


def per_device(
    tokens,
    cotangent,
    lengths,
    kept_keys,
    first_gain,
    qkv_weight,
    score_weight,
    out_weight,
    second_gain,
    fc_weight,
    proj_weight,
):
    f32, bf16 = jnp.float32, jnp.bfloat16
    dp_count = lax.axis_size("dp")
    seg_count = lax.axis_size("sp")
    ctx_count = lax.axis_size("ctx")
    dp_at = lax.axis_index("dp")
    sp_at = lax.axis_index("sp")
    ctx_at = lax.axis_index("ctx")
    rows = tokens.shape[1]
    width = tokens.shape[2]
    group_rows = seg_count * rows
    heads = H // seg_count
    head_cols = heads * 3 * HD
    hidden = fc_weight.shape[1]
    hidden_part = hidden // (dp_count * seg_count)
    piece = width // (dp_count * ctx_count)

    keys = heads * 2 * HD
    wide = -(-(head_cols + heads + 2) // LANES) * LANES
    weight_rows = width // dp_count
    own_in = arrange(
        lax.dynamic_slice_in_dim(qkv_weight, sp_at * head_cols, head_cols, 1),
        lax.dynamic_slice_in_dim(score_weight, sp_at * heads, heads, 1),
        jnp.pad(jnp.stack([first_gain, second_gain]), ((0, PAD_ROWS - 2), (0, 0))),
        wide,
    )
    if dp_count == 2:
        other_in = lax.ppermute(own_in, "dp", [(0, 1), (1, 0)])
        parts_in = [
            jnp.where(dp_at == at, own_in, other_in) for at in range(dp_count)
        ]
    else:
        parts_in = list(lax.all_gather(own_in, "dp", axis=0, tiled=False))
    tokens_slot = lax.all_gather(tokens[0], ("sp", "ctx"), axis=0, tiled=True)
    all_in = jnp.concatenate([part[:weight_rows] for part in parts_in])
    gain_one = jnp.concatenate([part[weight_rows, :weight_rows] for part in parts_in]).astype(f32)
    gain_two = jnp.concatenate([part[weight_rows + 1, :weight_rows] for part in parts_in]).astype(f32)

    fc_own = jnp.concatenate(
        [
            lax.dynamic_slice_in_dim(fc_weight, (at * seg_count + sp_at) * hidden_part, hidden_part, 1)
            for at in range(dp_count)
        ],
        axis=1,
    )
    proj_own = lax.dynamic_slice_in_dim(proj_weight, sp_at * hidden_part, hidden_part, 0)
    all_in, out_own, fc_own, proj_own = lax.optimization_barrier((all_in, out_weight, fc_own, proj_own))
    out_came = dp_send(out_own)
    fc_came = dp_send(fc_own)
    proj_came = dp_send(proj_own)

    cot_own, all_in = lax.optimization_barrier((cotangent[0], all_in))
    cot_group = lax.all_gather(cot_own, "sp", axis=0, tiled=True)
    kept = jnp.transpose(kept_keys[0], (2, 0, 1, 3))
    out_full = dp_join(out_own, out_came)
    fc_part = dp_join(fc_own, fc_came)
    tokens_slot, cot_group, out_full, fc_part, kept = lax.optimization_barrier(
        (tokens_slot, cot_group, out_full, fc_part, kept)
    )

    def group_of(values):
        parts = values.reshape((seg_count, ctx_count, rows) + values.shape[1:])
        return lax.dynamic_index_in_dim(parts, ctx_at, 1, keepdims=False).reshape((group_rows,) + values.shape[1:])

    inputs = tokens[0].astype(f32)
    inputs_group = group_of(tokens_slot).astype(f32)
    norm_slot, pairs, query_slot, score_slot = project(heads, tokens_slot, gain_one[None], all_in)
    key_score = lax.dynamic_index_in_dim(
        score_slot.reshape(heads, seg_count, ctx_count, rows), ctx_at, 2, keepdims=False
    ).reshape(heads, group_rows)
    norm_one = group_of(norm_slot)
    base = jnp.stack([ctx_at * rows, ctx_at]).astype(jnp.int32)
    head_outs, prob = attend(base, kept, query_slot, pairs, score_slot)
    head_outs, proj_came = lax.optimization_barrier((head_outs, proj_came))
    attended = head_outs.reshape(heads * HD, group_rows)
    attended_all = lax.all_gather(attended, "sp", axis=0, tiled=True)
    out_part = lax.dynamic_slice_in_dim(out_full, sp_at * heads * HD, heads * HD, 0)
    proj_part = dp_join(proj_own, proj_came)

    group_at = jnp.arange(group_rows, dtype=jnp.int32)
    group_positions = (group_at // rows) * (ctx_count * rows) + ctx_at * rows + group_at % rows
    grad_out_group = jnp.where((group_positions < lengths[0])[:, None], cot_group, jnp.zeros_like(cot_group))
    positions = (sp_at * ctx_count + ctx_at) * rows + jnp.arange(rows, dtype=jnp.int32)
    is_valid = (positions < lengths[0])[:, None]

    mixed_group = inputs_group + contract_rows(attended_all, out_full)
    norm_two = layer_norm(mixed_group, gain_two).astype(bf16)
    mixed = lax.dynamic_slice_in_dim(mixed_group, sp_at * rows, rows, 0)
    hidden_pre = jnp.dot(norm_two, fc_part, preferred_element_type=f32)
    active = tanh_gelu(hidden_pre).astype(bf16)
    grad_active = contract_cols(grad_out_group, proj_part)
    _, gelu_pull = jax.vjp(tanh_gelu, hidden_pre)
    grad_pre = gelu_pull(grad_active)[0].astype(bf16)
    grad_norm_parts = contract_cols(grad_pre, fc_part).astype(bf16)
    grad_norm_parts, norm_late, active = lax.optimization_barrier((grad_norm_parts, norm_two, active))
    fc_parts = contract_rows(norm_late, grad_pre).astype(bf16).reshape(dp_count, ctx_count, piece, width)
    proj_parts = contract_rows(active, grad_out_group).astype(bf16).reshape(dp_count, ctx_count, -1, width)
    mlp_parts = jnp.transpose(jnp.concatenate([fc_parts, proj_parts], axis=2), (1, 0, 2, 3))
    mlp_ctx = lax.psum_scatter(
        mlp_parts.reshape(ctx_count, -1, width), "ctx", scatter_dimension=0, tiled=False
    ).reshape(dp_count, -1, width)
    norm_came = lax.all_to_all(
        grad_norm_parts.reshape(seg_count, rows, width), "sp", split_axis=0, concat_axis=0, tiled=True
    )
    score_rows = score_slot[:, 0]
    norm_came, norm_one, score_rows, key_score = lax.optimization_barrier(
        (norm_came, norm_one, score_rows, key_score)
    )
    grad_norm_two = jnp.sum(norm_came.astype(f32), axis=0)
    _, second_pull = jax.vjp(layer_norm, mixed, gain_two)
    grad_mixed_norm, second_gain_grad = second_pull(grad_norm_two)
    grad_out = jnp.where(is_valid, cotangent[0], jnp.zeros_like(cotangent[0])).astype(f32)
    grad_mixed = grad_out + grad_mixed_norm
    grad_branch = lax.all_gather(grad_mixed.astype(bf16), "sp", axis=0, tiled=True)

    out_wide = jnp.pad(out_part.reshape(heads, HD, width), ((0, 0), (HD, 0), (0, 0))).reshape(heads * LANES, width)
    grad_wide = contract_cols(grad_branch, out_wide).astype(bf16)
    out_mine = jnp.dot(attended, grad_branch, preferred_element_type=f32).astype(bf16)
    grad_wide, out_mine = lax.optimization_barrier((grad_wide, out_mine))
    gain_cols = jnp.stack([gain_one, second_gain_grad], axis=1)
    grad_wide, gain_cols = lax.optimization_barrier((grad_wide, gain_cols))
    query_grads, pair_grads, turned, query_turned, gates = attend_back(
        ctx_count, base, query_slot, grad_wide, pairs, prob
    )
    pair_mine = lax.psum_scatter(pair_grads, "ctx", scatter_dimension=0, tiled=False)
    small = weight_grad(turned, query_turned, gates, score_rows, norm_slot, norm_one, all_in, gain_cols)
    small, out_mine = lax.optimization_barrier((small, out_mine))
    out_came = lax.all_to_all(
        out_mine.reshape(ctx_count, -1, width), "ctx", split_axis=0, concat_axis=0, tiled=True
    )
    small_dp, out_came = lax.optimization_barrier(
        (dp_scatter(small.reshape(dp_count, ctx_count, piece, wide)), out_came)
    )
    small_own = jnp.pad(exchange_sum(small_dp, "ctx").astype(bf16), ((0, 0), (0, width - wide)))
    out_own = dp_sum(jnp.sum(out_came.astype(f32), axis=0).astype(bf16))
    gradients = jnp.concatenate([small_own, dp_scatter(mlp_ctx), out_own], axis=0)
    pair_mine, gradients, active_late = lax.optimization_barrier((pair_mine, gradients, active))
    gathered = lax.all_gather(gradients, ("sp", "ctx"), axis=0, tiled=False).reshape(seg_count, ctx_count, -1, width)
    proj_piece = hidden // (seg_count * dp_count * ctx_count)

    grad_norm_part = finish(pair_mine, query_grads, key_score, all_in)
    expanded = exchange_sum(
        jnp.dot(active_late, proj_part, preferred_element_type=f32).astype(bf16).reshape(seg_count, rows, width), "sp"
    )
    output = jnp.where(is_valid, mixed + expanded, 0.0).astype(bf16)[None]
    grad_norm_one = exchange_sum(grad_norm_part.reshape(seg_count, rows, width), "sp")
    _, first_pull = jax.vjp(lambda values: layer_norm(values, gain_one), inputs)
    grad_input_norm = first_pull(grad_norm_one)[0]
    input_grad = (grad_mixed + grad_input_norm).astype(bf16)[None]

    qkv_grad, turned_rows, fc_grad, proj_grad, *rest = unpack(
        dp_at.astype(jnp.int32)[None], gathered, heads, piece, proj_piece, dp_count, hidden
    )
    proj_grad = proj_grad.reshape(-1, width)
    if rest:
        out_grad = rest[0].reshape(weight_rows, width)
    else:
        out_grad = lax.dynamic_slice_in_dim(
            gathered[:, :, 2 * piece + proj_piece :].reshape(width, width), dp_at * weight_rows, weight_rows, 0
        ).astype(f32)
    score_grad = turned_rows[:H].T
    return (output, input_grad, turned_rows[H], qkv_grad, score_grad, out_grad, turned_rows[H + 1], fc_grad, proj_grad)


def solution(mesh):
    placed = (
        P("dp", ("sp", "ctx"), None),
        P("dp", ("sp", "ctx"), None),
        P("dp"),
        P("dp", None, "ctx", "sp", None),
        P("dp"),
        P("dp", None),
        P("dp", None),
        P("dp", None),
        P("dp"),
        P("dp", None),
        P("dp", None),
    )
    return jax.shard_map(
        per_device,
        mesh=mesh,
        in_specs=placed,
        out_specs=(
            P("dp", ("sp", "ctx"), None),
            P("dp", ("sp", "ctx"), None),
            P("dp"),
            P("dp", None),
            P("dp", None),
            P("dp", None),
            P("dp"),
            P("dp", None),
            P("dp", None),
        ),
        check_vma=False,
    )
```

```python
import functools

import jax
import jax.numpy as jnp
from jax import lax
from jax.experimental import pallas as pl
from jax.experimental.pallas import tpu as pltpu
from jax.sharding import PartitionSpec as P

H = 12
HD = 64
WIN = 64
LANES = 128
SLOT = 2048


EPSILON = 1e-05


def layer_norm(values, gain):
    mean_value = jnp.mean(values, axis=-1, keepdims=True)
    centred = values - mean_value
    variance = jnp.mean(centred * centred, axis=-1, keepdims=True)
    return centred * lax.rsqrt(variance + EPSILON) * gain


def tanh_gelu(values):
    return jax.nn.gelu(values, approximate=True)


def contract_rows(left, right):
    return lax.dot_general(
        left, right, (((0,), (0,)), ((), ())), preferred_element_type=jnp.float32
    )


def contract_cols(left, right):
    return lax.dot_general(
        left, right, (((1,), (1,)), ((), ())), preferred_element_type=jnp.float32
    )


NT = (((1,), (1,)), ((), ()))


PAD_ROWS = 16
STEP = 128
SUB = 256


def project_kernel(heads, tokens_ref, gain_ref, in_ref, norm_ref, pair_ref, query_ref, score_ref):
    f32, bf16 = jnp.float32, jnp.bfloat16
    keys = heads * 2 * HD
    for start in range(0, tokens_ref.shape[0], SUB):
        rows = slice(start, start + SUB)
        norm = layer_norm(tokens_ref[rows, :].astype(f32), gain_ref[...]).astype(bf16)
        norm_ref[rows, :] = norm
        pair_ref[rows, :] = jnp.dot(norm, in_ref[:, :keys], preferred_element_type=f32).astype(bf16)
        rest = jnp.dot(norm, in_ref[:, keys:], preferred_element_type=f32)
        for head in range(heads):
            query = rest[:, head * HD : (head + 1) * HD]
            query_ref[rows, head * LANES : (head + 1) * LANES] = jnp.concatenate(
                [query, jnp.zeros_like(query)], axis=1
            ).astype(bf16)
        scores = jnp.transpose(rest[:, LANES:])[heads * HD - LANES : heads * HD - LANES + heads, :].astype(bf16)
        for head in range(heads):
            score_ref[head, :, rows] = scores[head : head + 1, :]


def project(heads, tokens, gain, weights):
    slot, width = tokens.shape
    block = 4 * SUB if slot % (4 * SUB) == 0 else SUB
    return pl.pallas_call(
        functools.partial(project_kernel, heads),
        grid=(slot // block,),
        in_specs=[
            pl.BlockSpec((block, width), lambda r: (r, 0)),
            pl.BlockSpec((1, width), lambda r: (0, 0)),
            pl.BlockSpec(weights.shape, lambda r: (0, 0)),
        ],
        out_specs=[
            pl.BlockSpec((block, width), lambda r: (r, 0)),
            pl.BlockSpec((block, heads * LANES), lambda r: (r, 0)),
            pl.BlockSpec((block, heads * LANES), lambda r: (r, 0)),
            pl.BlockSpec((heads, 1, block), lambda r: (0, 0, r)),
        ],
        out_shape=[
            jax.ShapeDtypeStruct((slot, width), jnp.bfloat16),
            jax.ShapeDtypeStruct((slot, heads * LANES), jnp.bfloat16),
            jax.ShapeDtypeStruct((slot, heads * LANES), jnp.bfloat16),
            jax.ShapeDtypeStruct((heads, 1, slot), jnp.bfloat16),
        ],
        name="project",
    )(tokens, gain, weights)


def attend_body(first, tiles, base, idx_ref, q_ref, kv_ref, key_ref, out_ref, prob_ref, score_ref, pair_ref, gate_ref):
    rows = q_ref.shape[0]
    if first:
        gate_ref[...] = jnp.broadcast_to(-jnp.log1p(jnp.exp(-key_ref[0].astype(jnp.float32))), gate_ref.shape)
    span = tiles * LANES
    f32, bf16 = jnp.float32, jnp.bfloat16
    score_ref[:, :span] = (
        lax.dot_general(q_ref[...], kv_ref[:span, :], NT, preferred_element_type=f32) * HD ** (-0.5)
        + gate_ref[0:1, :span]
    )
    kept = idx_ref[0, 0]
    pair_ref[...] = jnp.concatenate([kept, kept], axis=1)
    wide = 8 * HD
    sub = lax.broadcasted_iota(jnp.int32, (8, wide), 0)
    lane = lax.broadcasted_iota(jnp.int32, (8, wide), 1)
    own = (lane // HD) == sub
    subf = sub.astype(f32)
    ahead = lax.broadcasted_iota(jnp.int32, (8, LANES), 0) - lax.broadcasted_iota(jnp.int32, (8, LANES), 1)
    near_from = max(0, tiles - 5)

    def eight(start):
        four = pair_ref[pl.ds(start, 8), :]
        index = jnp.concatenate([four] * 4, axis=1)
        pos = base + start + sub
        high = jnp.where(own & (pos >= WIN), index >> 7, -2).astype(f32)
        low = jnp.sum(jnp.where(own, (index & 127).astype(f32), 0.0), axis=0, keepdims=True) - subf
        high_pair = jnp.concatenate([high, high - 1.0], axis=0).astype(bf16)
        low_pair = jnp.concatenate([low, low - 8.0], axis=0).astype(bf16)
        one, zero = jnp.ones((), bf16), jnp.zeros((), bf16)
        left = jnp.concatenate(
            [jnp.where(high_pair == jnp.array(2 * p, bf16), one, zero) for p in range(tiles // 2)], axis=0
        )
        right = jnp.concatenate(
            [jnp.where(low_pair == jnp.array(16 * p, bf16), one, zero) for p in range(8)], axis=0
        )
        count = lax.dot_general(left, right, NT, preferred_element_type=f32)
        gap = ahead + (base + start)
        masked, counts = [], []
        largest = None
        for tile in range(tiles):
            number = count[8 * tile : 8 * tile + 8, :]
            if tile >= near_from:
                far = gap - tile * LANES
                number = number + jnp.where((far >= 0) & (far < WIN), 1.0, 0.0)
            value = jnp.where(number > 0.0, score_ref[pl.ds(start, 8), tile * LANES : (tile + 1) * LANES], -1e30)
            counts.append(number)
            masked.append(value)
            largest = value if largest is None else jnp.maximum(largest, value)
        top = jnp.max(largest, axis=1, keepdims=True)
        total = None
        expos = []
        for number, value in zip(counts, masked):
            expo = jnp.exp(value - top) * number
            expos.append(expo)
            total = expo if total is None else total + expo
        inverse = 1.0 / jnp.sum(total, axis=1, keepdims=True)
        return [expo * inverse for expo in expos]

    def step(index, carry):
        for at in range(0, STEP, 16):
            start = pl.multiple_of(index * STEP + at, 16)
            near, next_to = eight(start), eight(start + 8)
            for tile in range(tiles):
                prob_ref[0, 0, pl.ds(start, 16), tile * LANES : (tile + 1) * LANES] = jnp.concatenate(
                    [near[tile], next_to[tile]], axis=0
                ).astype(bf16)
        return carry

    if rows == STEP:
        step(0, 0)
    else:
        lax.fori_loop(0, rows // STEP, step, 0)
    both = jnp.dot(prob_ref[0, 0, :, :span], kv_ref[:span, :], preferred_element_type=f32)
    out_ref[0] = jnp.transpose(both)[HD:, :].astype(bf16)


def attend_kernel(parts, chunk, base_ref, *refs):
    part = pl.program_id(1)
    base = base_ref[0] + part * chunk
    for at in range(parts):
        pl.when(part == at)(
            functools.partial(attend_body, at == 0, (at + 1) * chunk // LANES, base, *refs)
        )


def attend(base, kept, query, pairs, key_score):
    heads, parts, block, keep = kept.shape
    slot = pairs.shape[0]
    chunk = slot // parts
    grid_spec = pltpu.PrefetchScalarGridSpec(
        num_scalar_prefetch=1,
        grid=(heads, parts),
        in_specs=[
            pl.BlockSpec((1, 1, block, keep), lambda h, r, b: (h, r, 0, 0)),
            pl.BlockSpec((block, LANES), lambda h, r, b: (r * (chunk // block) + b[1], h)),
            pl.BlockSpec((slot, LANES), lambda h, r, b: (0, h)),
            pl.BlockSpec((1, 1, slot), lambda h, r, b: (h, 0, 0)),
        ],
        out_specs=[
            pl.BlockSpec((1, HD, block), lambda h, r, b: (h, 0, r)),
            pl.BlockSpec((1, 1, block, slot), lambda h, r, b: (h, r, 0, 0)),
        ],
        scratch_shapes=[
            pltpu.VMEM((block, slot), jnp.float32),
            pltpu.VMEM((block, 2 * keep), jnp.int32),
            pltpu.VMEM((8, slot), jnp.float32),
        ],
    )
    return pl.pallas_call(
        functools.partial(attend_kernel, parts, chunk),
        grid_spec=grid_spec,
        out_shape=[
            jax.ShapeDtypeStruct((heads, HD, parts * block), jnp.bfloat16),
            jax.ShapeDtypeStruct((heads, parts, block, slot), jnp.bfloat16),
        ],
        name="attend",
    )(base, kept, query, pairs, key_score)


def attend_back_kernel(parts, chunk, base_ref, q_ref, grad_ref, kv_ref, prob_ref, dq_ref, out_ref, turned_ref, dq_turned_ref, gates_ref, raw_ref, dkv_ref, gate_ref):
    f32, bf16 = jnp.float32, jnp.bfloat16
    rows = prob_ref.shape[2]
    count, height, _ = out_ref.shape
    lane = lax.broadcasted_iota(jnp.int32, (rows, LANES), 1)
    for part in reversed(range(parts)):
        last = part == parts - 1
        query = q_ref[pl.ds(pl.multiple_of((part * (chunk // rows) + base_ref[1]) * rows, rows), rows), :]
        grad = grad_ref[part * rows : (part + 1) * rows, :]
        dot_sum = None
        for at in range(part + 1):
            cols = slice(at * chunk, (at + 1) * chunk)
            raw = lax.dot_general(grad, kv_ref[cols, :], NT, preferred_element_type=f32)
            raw_ref[part, :, cols] = raw
            piece = jnp.sum(raw * prob_ref[0, part, :, cols].astype(f32), axis=1, keepdims=True)
            dot_sum = piece if dot_sum is None else dot_sum + piece
        scaled = jnp.where(lane == HD, 1.0, query.astype(f32) * HD ** (-0.5))
        query_t = jnp.transpose(scaled)[: HD + 16].astype(bf16)
        grad_t = jnp.transpose(grad.astype(f32))[HD:].astype(bf16)
        dq = None
        for at in range(part + 1):
            cols = slice(at * chunk, (at + 1) * chunk)
            prob = prob_ref[0, part, :, cols]
            grad_score = (prob.astype(f32) * (raw_ref[part, :, cols] - dot_sum)).astype(bf16)
            piece = jnp.dot(grad_score, kv_ref[cols, :], preferred_element_type=f32)
            dq = piece if dq is None else dq + piece
            keys = jnp.dot(query_t, grad_score, preferred_element_type=f32)
            values = jnp.dot(grad_t, prob, preferred_element_type=f32)
            if last:
                dkv_ref[:HD, cols] = keys[:HD]
                gate_ref[:, cols] = keys[HD : HD + 8]
                dkv_ref[HD:, cols] = values
            else:
                dkv_ref[:HD, cols] += keys[:HD]
                gate_ref[:, cols] += keys[HD : HD + 8]
                dkv_ref[HD:, cols] += values
        dq = dq * HD ** (-0.5)
        dq_ref[part * rows : (part + 1) * rows, :] = dq.astype(dq_ref.dtype)
        dq_turned_ref[0, :, part * rows : (part + 1) * rows] = jnp.transpose(dq)[:HD, :].astype(bf16)
    turned_ref[0] = dkv_ref[...].astype(bf16)
    gates_ref[0] = gate_ref[...]
    for at in range(count):
        rows_of = []
        for part in range(parts):
            cols = slice((part * count + at) * LANES, (part * count + at + 1) * LANES)
            out_ref[at, part * LANES : (part + 1) * LANES, :] = jnp.transpose(dkv_ref[:, cols]).astype(bf16)
            rows_of.append(gate_ref[0:1, cols])
        rows_of.append(jnp.zeros((PAD_ROWS - parts, LANES), f32))
        out_ref[at, height - PAD_ROWS :, :] = jnp.concatenate(rows_of, axis=0).astype(bf16)


def attend_back(count, base, query, grad, pairs, prob):
    heads, parts, block, slot = prob.shape
    width = pairs.shape[1]
    height = slot // count + PAD_ROWS
    chunk = slot // parts
    return pl.pallas_call(
        functools.partial(attend_back_kernel, parts, chunk),
        grid_spec=pltpu.PrefetchScalarGridSpec(
            num_scalar_prefetch=1,
            grid=(heads,),
            in_specs=[
                pl.BlockSpec((slot, LANES), lambda h, b: (0, h)),
                pl.BlockSpec((parts * block, LANES), lambda h, b: (0, h)),
                pl.BlockSpec((slot, LANES), lambda h, b: (0, h)),
                pl.BlockSpec((1, parts, block, slot), lambda h, b: (h, 0, 0, 0)),
            ],
            out_specs=[
                pl.BlockSpec((parts * block, LANES), lambda h, b: (0, h)),
                pl.BlockSpec((count, height, LANES), lambda h, b: (0, 0, h)),
                pl.BlockSpec((1, LANES, slot), lambda h, b: (h, 0, 0)),
                pl.BlockSpec((1, HD, parts * block), lambda h, b: (h, 0, 0)),
                pl.BlockSpec((1, 8, slot), lambda h, b: (h, 0, 0)),
            ],
            scratch_shapes=[
                pltpu.VMEM((parts, block, slot), jnp.float32),
                pltpu.VMEM((LANES, slot), jnp.float32),
                pltpu.VMEM((8, slot), jnp.float32),
            ],
        ),
        out_shape=[
            jax.ShapeDtypeStruct((parts * block, heads * LANES), jnp.bfloat16),
            jax.ShapeDtypeStruct((count, height, width), jnp.bfloat16),
            jax.ShapeDtypeStruct((heads, LANES, slot), jnp.bfloat16),
            jax.ShapeDtypeStruct((heads, HD, parts * block), jnp.bfloat16),
            jax.ShapeDtypeStruct((heads, 8, slot), jnp.float32),
        ],
        name="attend_back",
    )(base, query, grad, pairs, prob)


def weight_kernel(turned_ref, dq_ref, gates_ref, score_ref, slot_ref, norm_ref, in_ref, gain_ref, out_ref):
    f32, bf16 = jnp.float32, jnp.bfloat16
    heads, _, slot = turned_ref.shape
    wide = in_ref.shape[1]
    width = slot_ref.shape[1]
    total = jnp.concatenate([gates_ref[head, 0:1, :] for head in range(heads)], axis=0)
    total = total * jax.nn.sigmoid(-score_ref[...].astype(f32))
    total = jnp.concatenate([total, jnp.zeros((PAD_ROWS - heads, slot), f32)], axis=0).astype(bf16)
    turned = [
        jnp.dot(turned_ref[...].reshape(heads * LANES, slot), slot_ref[...], preferred_element_type=f32),
        jnp.dot(dq_ref[...].reshape(heads * HD, -1), norm_ref[...], preferred_element_type=f32),
        jnp.dot(total, slot_ref[...], preferred_element_type=f32),
        jnp.zeros((wide - heads * 3 * HD - PAD_ROWS, width), f32),
    ]
    small = jnp.transpose(jnp.concatenate(turned, axis=0))
    gain_grad = jnp.sum(small * in_ref[...].astype(f32), axis=1, keepdims=True) / gain_ref[:, 0:1]
    lane = lax.broadcasted_iota(jnp.int32, small.shape, 1)
    at = heads * 3 * HD + heads
    small = jnp.where(lane == at, gain_grad, jnp.where(lane == at + 1, gain_ref[:, 1:2], small))
    out_ref[...] = small.astype(bf16)


def weight_grad(turned, dq, gates, score, norm_slot, norm_one, weights, gains):
    width = norm_one.shape[1]
    return pl.pallas_call(
        weight_kernel,
        out_shape=jax.ShapeDtypeStruct((width, weights.shape[1]), jnp.bfloat16),
        name="weight_grad",
    )(turned, dq, gates, score, norm_slot, norm_one, weights, gains)


def finish_kernel(heads, pair_ref, dq_ref, score_ref, in_ref, grad_ref):
    f32, bf16 = jnp.float32, jnp.bfloat16
    group = dq_ref.shape[0]
    parts = group // LANES
    wide = in_ref.shape[1]
    gates = pair_ref[group:, :].astype(f32)
    total = jnp.concatenate(
        [
            jnp.concatenate([gates[at : at + 1, head * LANES : (head + 1) * LANES] for at in range(parts)], axis=1)
            for head in range(heads)
        ],
        axis=0,
    )
    total = total * jax.nn.sigmoid(-score_ref[...].astype(f32))
    scores = jnp.transpose(jnp.concatenate([total, jnp.zeros((LANES - heads, group), f32)], axis=0))
    rest = wide - heads * 3 * HD
    columns = jnp.concatenate(
        [pair_ref[:group, :].astype(f32)]
        + [dq_ref[:, head * LANES : head * LANES + HD].astype(f32) for head in range(heads)]
        + [scores[:, :rest]],
        axis=1,
    ).astype(bf16)
    grad_ref[...] = lax.dot_general(columns, in_ref[...], NT, preferred_element_type=f32).astype(bf16)


def finish(pair, dq, score, weights):
    return pl.pallas_call(
        functools.partial(finish_kernel, score.shape[0]),
        out_shape=jax.ShapeDtypeStruct((dq.shape[0], weights.shape[0]), jnp.bfloat16),
        name="finish",
    )(pair, dq, score, weights)


def unpack_kernel(groups, heads, piece, parts, dp_ref, all_ref, qkv_ref, score_ref, gain_ref, fc_ref, proj_ref, *rest):
    f32 = jnp.float32
    keys = heads * 2 * HD
    part_cols = fc_ref.shape[1] // (groups * parts)
    for out_ref in rest:
        mine = out_ref.shape[0]
        for at in range(mine):
            out_ref[at] = all_ref[dp_ref[0] * mine + at, :, 2 * piece + proj_ref.shape[2] :, :].astype(f32)
    for step in range(all_ref.shape[1]):
        rows = slice(step * piece, (step + 1) * piece)
        scores, gains = [], None
        for at in range(groups):
            values = all_ref[at, step, :piece, :].astype(f32)
            for head in range(heads):
                start = (at * heads + head) * 3 * HD
                qkv_ref[rows, start : start + HD] = values[:, keys + head * HD : keys + (head + 1) * HD]
                qkv_ref[rows, start + HD : start + 3 * HD] = values[:, head * 2 * HD : (head + 1) * 2 * HD]
            scores.append(values[:, keys + heads * HD : keys + heads * HD + heads])
            gain = values[:, keys + heads * HD + heads : keys + heads * HD + heads + 2]
            gains = gain if gains is None else gains + gain
            values = all_ref[at, step, piece : 2 * piece, :].astype(f32)
            for part in range(parts):
                start = (part * groups + at) * part_cols
                fc_ref[rows, start : start + part_cols] = values[:, part * part_cols : (part + 1) * part_cols]
            proj_ref[at, step] = all_ref[at, step, 2 * piece : 2 * piece + proj_ref.shape[2], :].astype(f32)
        narrow = jnp.concatenate(
            scores + [gains, jnp.zeros((piece, LANES - groups * heads - 2), f32)], axis=1
        )
        turned = jnp.transpose(jnp.concatenate([narrow, jnp.zeros((LANES - piece, LANES), f32)], axis=0))

        def store(index):
            gain_ref[:, index * piece : (index + 1) * piece] = turned[groups * heads : groups * heads + 8, :piece]
            score_ref[:, index * piece : (index + 1) * piece] = turned[: groups * heads, :piece]

        if all_ref.shape[1] > 1:
            store(step)
        else:
            for index in range(score_ref.shape[1] // piece):
                pl.when(pl.program_id(0) == index)(functools.partial(store, index))


def unpack(at, gathered, heads, piece, proj_piece, parts, hidden):
    groups, count, rows, width = gathered.shape
    step = 1 if piece % 16 == 0 else count
    blocks = [
        ((count * piece, groups * heads * 3 * HD), (step * piece, groups * heads * 3 * HD), lambda c, d: (c, 0)),
        ((groups * heads, count * piece), (groups * heads, count * piece), lambda c, d: (0, 0)),
        ((8, count * piece), (8, count * piece), lambda c, d: (0, 0)),
        ((count * piece, hidden), (step * piece, hidden), lambda c, d: (c, 0)),
        ((groups, count, proj_piece, width), (groups, step, proj_piece, width), lambda c, d: (0, c, 0, 0)),
    ]
    if groups % parts == 0:
        last = rows - 2 * piece - proj_piece
        mine = groups // parts
        blocks.append(((mine, count, last, width), (mine, step, last, width), lambda c, d: (0, c, 0, 0)))
    return pl.pallas_call(
        functools.partial(unpack_kernel, groups, heads, piece, parts),
        grid_spec=pltpu.PrefetchScalarGridSpec(
            num_scalar_prefetch=1,
            grid=(count // step,),
            in_specs=[pl.BlockSpec((groups, step, rows, width), lambda c, d: (0, c, 0, 0))],
            out_specs=[pl.BlockSpec(block, index) for _, block, index in blocks],
        ),
        out_shape=[jax.ShapeDtypeStruct(shape, jnp.float32) for shape, _, _ in blocks],
        name="unpack",
    )(at, gathered)


def arrange_kernel(heads, rows, qkv_ref, score_ref, gains_ref, out_ref):
    f32 = jnp.float32
    values = qkv_ref[...].astype(f32)
    keys = heads * 2 * HD
    width = out_ref.shape[1]
    pieces = [values[:, (3 * head + 1) * HD : (3 * head + 3) * HD] for head in range(heads)]
    pieces += [values[:, 3 * head * HD : (3 * head + 1) * HD] for head in range(heads)]
    pieces += [score_ref[...].astype(f32), jnp.zeros((rows, width - heads * 3 * HD - heads), f32)]
    out_ref[:rows, :] = jnp.concatenate(pieces, axis=1).astype(out_ref.dtype)
    out_ref[rows:, :] = jnp.concatenate(
        [gains_ref[...].astype(f32), jnp.zeros((gains_ref.shape[0], width - rows), f32)], axis=1
    ).astype(out_ref.dtype)


def arrange(qkv, score, gains, width):
    rows, heads = score.shape
    return pl.pallas_call(
        functools.partial(arrange_kernel, heads, rows),
        out_shape=jax.ShapeDtypeStruct((rows + PAD_ROWS, width), qkv.dtype),
        name="arrange",
    )(qkv, score, gains)


def dp_send(mine):
    if lax.axis_size("dp") != 2:
        return lax.all_gather(mine, "dp", axis=0, tiled=True)
    return lax.ppermute(mine, "dp", [(0, 1), (1, 0)])


def dp_join(mine, came):
    if lax.axis_size("dp") != 2:
        return came
    return jnp.where(
        lax.axis_index("dp") == 0, jnp.concatenate([mine, came]), jnp.concatenate([came, mine])
    )


def dp_scatter(parts):
    if lax.axis_size("dp") != 2:
        return lax.psum_scatter(parts, "dp", scatter_dimension=0, tiled=False)
    at = lax.axis_index("dp")
    mine = lax.dynamic_index_in_dim(parts, at, 0, keepdims=False)
    sent = lax.dynamic_index_in_dim(parts, 1 - at, 0, keepdims=False)
    other = lax.ppermute(sent, "dp", [(0, 1), (1, 0)])
    return (mine.astype(jnp.float32) + other.astype(jnp.float32)).astype(parts.dtype)


def group_rows_of(mine, group, count):
    height = mine.shape[0]
    if lax.axis_size("dp") != 2 or height % count != 0:
        whole = lax.all_gather(mine, "dp", axis=0, tiled=True)
        return lax.dynamic_slice_in_dim(whole, group * count, count, 0)
    near = lax.dynamic_slice_in_dim(mine, group * count % height, count, 0)
    far = lax.ppermute(near, "dp", [(0, 1), (1, 0)])
    return jnp.where(lax.axis_index("dp") == group * count // height, near, far)


def dp_sum(mine):
    if lax.axis_size("dp") != 2:
        return lax.psum(mine, "dp")
    other = lax.ppermute(mine, "dp", [(0, 1), (1, 0)])
    return (mine.astype(jnp.float32) + other.astype(jnp.float32)).astype(mine.dtype)


def exchange_sum(parts, axis):
    came = lax.all_to_all(parts, axis, split_axis=0, concat_axis=0, tiled=True)
    return jnp.sum(came.astype(jnp.float32), axis=0)


def per_device(
    tokens,
    cotangent,
    lengths,
    kept_keys,
    first_gain,
    qkv_weight,
    score_weight,
    out_weight,
    second_gain,
    fc_weight,
    proj_weight,
):
    f32, bf16 = jnp.float32, jnp.bfloat16
    dp_count = lax.axis_size("dp")
    seg_count = lax.axis_size("sp")
    ctx_count = lax.axis_size("ctx")
    dp_at = lax.axis_index("dp")
    sp_at = lax.axis_index("sp")
    ctx_at = lax.axis_index("ctx")
    rows = tokens.shape[1]
    width = tokens.shape[2]
    group_rows = seg_count * rows
    heads = H // seg_count
    head_cols = heads * 3 * HD
    hidden = fc_weight.shape[1]
    hidden_part = hidden // (dp_count * seg_count)
    piece = width // (dp_count * ctx_count)

    keys = heads * 2 * HD
    wide = -(-(head_cols + heads + 2) // LANES) * LANES
    weight_rows = width // dp_count
    own_in = arrange(
        lax.dynamic_slice_in_dim(qkv_weight, sp_at * head_cols, head_cols, 1),
        lax.dynamic_slice_in_dim(score_weight, sp_at * heads, heads, 1),
        jnp.pad(jnp.stack([first_gain, second_gain]), ((0, PAD_ROWS - 2), (0, 0))),
        wide,
    )
    if dp_count == 2:
        other_in = lax.ppermute(own_in, "dp", [(0, 1), (1, 0)])
        parts_in = [
            jnp.where(dp_at == at, own_in, other_in) for at in range(dp_count)
        ]
    else:
        parts_in = list(lax.all_gather(own_in, "dp", axis=0, tiled=False))
    tokens_slot = lax.all_gather(tokens[0], ("sp", "ctx"), axis=0, tiled=True)
    all_in = jnp.concatenate([part[:weight_rows] for part in parts_in])
    gain_one = jnp.concatenate([part[weight_rows, :weight_rows] for part in parts_in]).astype(f32)
    gain_two = jnp.concatenate([part[weight_rows + 1, :weight_rows] for part in parts_in]).astype(f32)

    fc_own = jnp.concatenate(
        [
            lax.dynamic_slice_in_dim(fc_weight, (at * seg_count + sp_at) * hidden_part, hidden_part, 1)
            for at in range(dp_count)
        ],
        axis=1,
    )
    proj_own = lax.dynamic_slice_in_dim(proj_weight, sp_at * hidden_part, hidden_part, 0)
    all_in, out_own, fc_own, proj_own = lax.optimization_barrier((all_in, out_weight, fc_own, proj_own))
    out_came = dp_send(out_own)
    fc_came = dp_send(fc_own)
    proj_came = dp_send(proj_own)

    cot_own, all_in = lax.optimization_barrier((cotangent[0], all_in))
    cot_group = lax.all_gather(cot_own, "sp", axis=0, tiled=True)
    kept = jnp.transpose(kept_keys[0], (2, 0, 1, 3))
    out_full = dp_join(out_own, out_came)
    fc_part = dp_join(fc_own, fc_came)
    tokens_slot, cot_group, out_full, fc_part, kept = lax.optimization_barrier(
        (tokens_slot, cot_group, out_full, fc_part, kept)
    )

    def group_of(values):
        parts = values.reshape((seg_count, ctx_count, rows) + values.shape[1:])
        return lax.dynamic_index_in_dim(parts, ctx_at, 1, keepdims=False).reshape((group_rows,) + values.shape[1:])

    inputs = tokens[0].astype(f32)
    inputs_group = group_of(tokens_slot).astype(f32)
    norm_slot, pairs, query_slot, score_slot = project(heads, tokens_slot, gain_one[None], all_in)
    key_score = lax.dynamic_index_in_dim(
        score_slot.reshape(heads, seg_count, ctx_count, rows), ctx_at, 2, keepdims=False
    ).reshape(heads, group_rows)
    norm_one = group_of(norm_slot)
    base = jnp.stack([ctx_at * rows, ctx_at]).astype(jnp.int32)
    head_outs, prob = attend(base, kept, query_slot, pairs, score_slot)
    head_outs, proj_came = lax.optimization_barrier((head_outs, proj_came))
    attended = head_outs.reshape(heads * HD, group_rows)
    attended_all = lax.all_gather(attended, "sp", axis=0, tiled=True)
    out_part = lax.dynamic_slice_in_dim(out_full, sp_at * heads * HD, heads * HD, 0)
    proj_part = dp_join(proj_own, proj_came)

    group_at = jnp.arange(group_rows, dtype=jnp.int32)
    group_positions = (group_at // rows) * (ctx_count * rows) + ctx_at * rows + group_at % rows
    grad_out_group = jnp.where((group_positions < lengths[0])[:, None], cot_group, jnp.zeros_like(cot_group))
    positions = (sp_at * ctx_count + ctx_at) * rows + jnp.arange(rows, dtype=jnp.int32)
    is_valid = (positions < lengths[0])[:, None]

    mixed_group = inputs_group + contract_rows(attended_all, out_full)
    norm_two = layer_norm(mixed_group, gain_two).astype(bf16)
    mixed = lax.dynamic_slice_in_dim(mixed_group, sp_at * rows, rows, 0)
    hidden_pre = jnp.dot(norm_two, fc_part, preferred_element_type=f32)
    active = tanh_gelu(hidden_pre).astype(bf16)
    grad_active = contract_cols(grad_out_group, proj_part)
    _, gelu_pull = jax.vjp(tanh_gelu, hidden_pre)
    grad_pre = gelu_pull(grad_active)[0].astype(bf16)
    grad_norm_parts = contract_cols(grad_pre, fc_part).astype(bf16)
    grad_norm_parts, norm_late, active = lax.optimization_barrier((grad_norm_parts, norm_two, active))
    fc_parts = contract_rows(norm_late, grad_pre).astype(bf16).reshape(dp_count, ctx_count, piece, width)
    proj_parts = contract_rows(active, grad_out_group).astype(bf16).reshape(dp_count, ctx_count, -1, width)
    mlp_parts = jnp.transpose(jnp.concatenate([fc_parts, proj_parts], axis=2), (1, 0, 2, 3))
    mlp_ctx = lax.psum_scatter(
        mlp_parts.reshape(ctx_count, -1, width), "ctx", scatter_dimension=0, tiled=False
    ).reshape(dp_count, -1, width)
    norm_came = lax.all_to_all(
        grad_norm_parts.reshape(seg_count, rows, width), "sp", split_axis=0, concat_axis=0, tiled=True
    )
    score_rows = score_slot[:, 0]
    norm_came, norm_one, score_rows, key_score = lax.optimization_barrier(
        (norm_came, norm_one, score_rows, key_score)
    )
    grad_norm_two = jnp.sum(norm_came.astype(f32), axis=0)
    _, second_pull = jax.vjp(layer_norm, mixed, gain_two)
    grad_mixed_norm, second_gain_grad = second_pull(grad_norm_two)
    grad_out = jnp.where(is_valid, cotangent[0], jnp.zeros_like(cotangent[0])).astype(f32)
    grad_mixed = grad_out + grad_mixed_norm
    grad_branch = lax.all_gather(grad_mixed.astype(bf16), "sp", axis=0, tiled=True)

    out_wide = jnp.pad(out_part.reshape(heads, HD, width), ((0, 0), (HD, 0), (0, 0))).reshape(heads * LANES, width)
    grad_wide = contract_cols(grad_branch, out_wide).astype(bf16)
    out_mine = jnp.dot(attended, grad_branch, preferred_element_type=f32).astype(bf16)
    grad_wide, out_mine = lax.optimization_barrier((grad_wide, out_mine))
    gain_cols = jnp.stack([gain_one, second_gain_grad], axis=1)
    grad_wide, gain_cols = lax.optimization_barrier((grad_wide, gain_cols))
    query_grads, pair_grads, turned, query_turned, gates = attend_back(
        ctx_count, base, query_slot, grad_wide, pairs, prob
    )
    pair_mine = lax.psum_scatter(pair_grads, "ctx", scatter_dimension=0, tiled=False)
    small = weight_grad(turned, query_turned, gates, score_rows, norm_slot, norm_one, all_in, gain_cols)
    small, out_mine = lax.optimization_barrier((small, out_mine))
    out_came = lax.all_to_all(
        out_mine.reshape(ctx_count, -1, width), "ctx", split_axis=0, concat_axis=0, tiled=True
    )
    small_dp, out_came = lax.optimization_barrier(
        (dp_scatter(small.reshape(dp_count, ctx_count, piece, wide)), out_came)
    )
    small_own = jnp.pad(exchange_sum(small_dp, "ctx").astype(bf16), ((0, 0), (0, width - wide)))
    out_own = dp_sum(jnp.sum(out_came.astype(f32), axis=0).astype(bf16))
    gradients = jnp.concatenate([small_own, dp_scatter(mlp_ctx), out_own], axis=0)
    pair_mine, gradients, active_late = lax.optimization_barrier((pair_mine, gradients, active))
    gathered = lax.all_gather(gradients, ("sp", "ctx"), axis=0, tiled=False).reshape(seg_count, ctx_count, -1, width)
    proj_piece = hidden // (seg_count * dp_count * ctx_count)

    grad_norm_part = finish(pair_mine, query_grads, key_score, all_in)
    expanded = exchange_sum(
        jnp.dot(active_late, proj_part, preferred_element_type=f32).astype(bf16).reshape(seg_count, rows, width), "sp"
    )
    output = jnp.where(is_valid, mixed + expanded, 0.0).astype(bf16)[None]
    grad_norm_one = exchange_sum(grad_norm_part.reshape(seg_count, rows, width), "sp")
    _, first_pull = jax.vjp(lambda values: layer_norm(values, gain_one), inputs)
    grad_input_norm = first_pull(grad_norm_one)[0]
    input_grad = (grad_mixed + grad_input_norm).astype(bf16)[None]

    qkv_grad, turned_scores, gains, fc_grad, proj_grad, *rest = unpack(
        dp_at.astype(jnp.int32)[None], gathered, heads, piece, proj_piece, dp_count, hidden
    )
    proj_grad = proj_grad.reshape(-1, width)
    if rest:
        out_grad = rest[0].reshape(weight_rows, width)
    else:
        out_grad = lax.dynamic_slice_in_dim(
            gathered[:, :, 2 * piece + proj_piece :].reshape(width, width), dp_at * weight_rows, weight_rows, 0
        ).astype(f32)
    score_grad = turned_scores.T
    return (output, input_grad, gains[0], qkv_grad, score_grad, out_grad, gains[1], fc_grad, proj_grad)


def solution(mesh):
    placed = (
        P("dp", ("sp", "ctx"), None),
        P("dp", ("sp", "ctx"), None),
        P("dp"),
        P("dp", None, "ctx", "sp", None),
        P("dp"),
        P("dp", None),
        P("dp", None),
        P("dp", None),
        P("dp"),
        P("dp", None),
        P("dp", None),
    )
    return jax.shard_map(
        per_device,
        mesh=mesh,
        in_specs=placed,
        out_specs=(
            P("dp", ("sp", "ctx"), None),
            P("dp", ("sp", "ctx"), None),
            P("dp"),
            P("dp", None),
            P("dp", None),
            P("dp", None),
            P("dp"),
            P("dp", None),
            P("dp", None),
        ),
        check_vma=False,
    )
```

```python
import functools

import jax
import jax.numpy as jnp
from jax import lax
from jax.experimental import pallas as pl
from jax.experimental.pallas import tpu as pltpu
from jax.sharding import PartitionSpec as P

H = 12
HD = 64
WIN = 64
LANES = 128
SLOT = 2048


EPSILON = 1e-05


def layer_norm(values, gain):
    mean_value = jnp.mean(values, axis=-1, keepdims=True)
    centred = values - mean_value
    variance = jnp.mean(centred * centred, axis=-1, keepdims=True)
    return centred * lax.rsqrt(variance + EPSILON) * gain


def tanh_gelu(values):
    return jax.nn.gelu(values, approximate=True)


def contract_rows(left, right):
    return lax.dot_general(
        left, right, (((0,), (0,)), ((), ())), preferred_element_type=jnp.float32
    )


def contract_cols(left, right):
    return lax.dot_general(
        left, right, (((1,), (1,)), ((), ())), preferred_element_type=jnp.float32
    )


NT = (((1,), (1,)), ((), ()))


PAD_ROWS = 16
STEP = 128
SUB = 256


def project_kernel(heads, tokens_ref, gain_ref, in_ref, norm_ref, pair_ref, query_ref, score_ref):
    f32, bf16 = jnp.float32, jnp.bfloat16
    keys = heads * 2 * HD
    for start in range(0, tokens_ref.shape[0], SUB):
        rows = slice(start, start + SUB)
        norm = layer_norm(tokens_ref[rows, :].astype(f32), gain_ref[...]).astype(bf16)
        norm_ref[rows, :] = norm
        pair_ref[rows, :] = jnp.dot(norm, in_ref[:, :keys], preferred_element_type=f32).astype(bf16)
        rest = jnp.dot(norm, in_ref[:, keys:], preferred_element_type=f32)
        for head in range(heads):
            query = rest[:, head * HD : (head + 1) * HD]
            query_ref[rows, head * LANES : (head + 1) * LANES] = jnp.concatenate(
                [query, jnp.zeros_like(query)], axis=1
            ).astype(bf16)
        scores = jnp.transpose(rest[:, LANES:])[heads * HD - LANES : heads * HD - LANES + heads, :].astype(bf16)
        for head in range(heads):
            score_ref[head, :, rows] = scores[head : head + 1, :]


def project(heads, tokens, gain, weights):
    slot, width = tokens.shape
    block = 4 * SUB if slot % (4 * SUB) == 0 else SUB
    return pl.pallas_call(
        functools.partial(project_kernel, heads),
        grid=(slot // block,),
        in_specs=[
            pl.BlockSpec((block, width), lambda r: (r, 0)),
            pl.BlockSpec((1, width), lambda r: (0, 0)),
            pl.BlockSpec(weights.shape, lambda r: (0, 0)),
        ],
        out_specs=[
            pl.BlockSpec((block, width), lambda r: (r, 0)),
            pl.BlockSpec((block, heads * LANES), lambda r: (r, 0)),
            pl.BlockSpec((block, heads * LANES), lambda r: (r, 0)),
            pl.BlockSpec((heads, 1, block), lambda r: (0, 0, r)),
        ],
        out_shape=[
            jax.ShapeDtypeStruct((slot, width), jnp.bfloat16),
            jax.ShapeDtypeStruct((slot, heads * LANES), jnp.bfloat16),
            jax.ShapeDtypeStruct((slot, heads * LANES), jnp.bfloat16),
            jax.ShapeDtypeStruct((heads, 1, slot), jnp.bfloat16),
        ],
        name="project",
    )(tokens, gain, weights)


def attend_body(first, tiles, base, idx_ref, q_ref, kv_ref, key_ref, out_ref, prob_ref, score_ref, pair_ref, gate_ref):
    rows = q_ref.shape[0]
    if first:
        gate_ref[...] = jnp.broadcast_to(-jnp.log1p(jnp.exp(-key_ref[0].astype(jnp.float32))), gate_ref.shape)
    span = tiles * LANES
    f32, bf16 = jnp.float32, jnp.bfloat16
    score_ref[:, :span] = (
        lax.dot_general(q_ref[...], kv_ref[:span, :], NT, preferred_element_type=f32) * HD ** (-0.5)
        + gate_ref[0:1, :span]
    )
    kept = idx_ref[0, 0]
    pair_ref[...] = jnp.concatenate([kept, kept], axis=1)
    wide = 8 * HD
    sub = lax.broadcasted_iota(jnp.int32, (8, wide), 0)
    lane = lax.broadcasted_iota(jnp.int32, (8, wide), 1)
    own = (lane // HD) == sub
    subf = sub.astype(f32)
    ahead = lax.broadcasted_iota(jnp.int32, (8, LANES), 0) - lax.broadcasted_iota(jnp.int32, (8, LANES), 1)
    near_from = max(0, tiles - 5)

    def eight(start):
        four = pair_ref[pl.ds(start, 8), :]
        index = jnp.concatenate([four] * 4, axis=1)
        pos = base + start + sub
        high = jnp.where(own & (pos >= WIN), index >> 7, -2).astype(f32)
        low = jnp.sum(jnp.where(own, (index & 127).astype(f32), 0.0), axis=0, keepdims=True) - subf
        high_pair = jnp.concatenate([high, high - 1.0], axis=0).astype(bf16)
        low_pair = jnp.concatenate([low, low - 8.0], axis=0).astype(bf16)
        one, zero = jnp.ones((), bf16), jnp.zeros((), bf16)
        left = jnp.concatenate(
            [jnp.where(high_pair == jnp.array(2 * p, bf16), one, zero) for p in range(tiles // 2)], axis=0
        )
        right = jnp.concatenate(
            [jnp.where(low_pair == jnp.array(16 * p, bf16), one, zero) for p in range(8)], axis=0
        )
        count = lax.dot_general(left, right, NT, preferred_element_type=f32)
        gap = ahead + (base + start)
        masked, counts = [], []
        largest = None
        for tile in range(tiles):
            number = count[8 * tile : 8 * tile + 8, :]
            if tile >= near_from:
                far = gap - tile * LANES
                number = number + jnp.where((far >= 0) & (far < WIN), 1.0, 0.0)
            value = jnp.where(number > 0.0, score_ref[pl.ds(start, 8), tile * LANES : (tile + 1) * LANES], -1e30)
            counts.append(number)
            masked.append(value)
            largest = value if largest is None else jnp.maximum(largest, value)
        top = jnp.max(largest, axis=1, keepdims=True)
        total = None
        expos = []
        for number, value in zip(counts, masked):
            expo = jnp.exp(value - top) * number
            expos.append(expo)
            total = expo if total is None else total + expo
        inverse = 1.0 / jnp.sum(total, axis=1, keepdims=True)
        return [expo * inverse for expo in expos]

    def step(index, carry):
        for at in range(0, STEP, 16):
            start = pl.multiple_of(index * STEP + at, 16)
            near, next_to = eight(start), eight(start + 8)
            for tile in range(tiles):
                prob_ref[0, 0, pl.ds(start, 16), tile * LANES : (tile + 1) * LANES] = jnp.concatenate(
                    [near[tile], next_to[tile]], axis=0
                ).astype(bf16)
        return carry

    if rows == STEP:
        step(0, 0)
    else:
        lax.fori_loop(0, rows // STEP, step, 0)
    both = jnp.dot(prob_ref[0, 0, :, :span], kv_ref[:span, :], preferred_element_type=f32)
    out_ref[0] = jnp.transpose(both)[HD:, :].astype(bf16)


def attend_kernel(parts, chunk, base_ref, *refs):
    part = pl.program_id(1)
    base = base_ref[0] + part * chunk
    for at in range(parts):
        pl.when(part == at)(
            functools.partial(attend_body, at == 0, (at + 1) * chunk // LANES, base, *refs)
        )


def attend(base, kept, query, pairs, key_score):
    heads, parts, block, keep = kept.shape
    slot = pairs.shape[0]
    chunk = slot // parts
    grid_spec = pltpu.PrefetchScalarGridSpec(
        num_scalar_prefetch=1,
        grid=(heads, parts),
        in_specs=[
            pl.BlockSpec((1, 1, block, keep), lambda h, r, b: (h, r, 0, 0)),
            pl.BlockSpec((block, LANES), lambda h, r, b: (r * (chunk // block) + b[1], h)),
            pl.BlockSpec((slot, LANES), lambda h, r, b: (0, h)),
            pl.BlockSpec((1, 1, slot), lambda h, r, b: (h, 0, 0)),
        ],
        out_specs=[
            pl.BlockSpec((1, HD, block), lambda h, r, b: (h, 0, r)),
            pl.BlockSpec((1, 1, block, slot), lambda h, r, b: (h, r, 0, 0)),
        ],
        scratch_shapes=[
            pltpu.VMEM((block, slot), jnp.float32),
            pltpu.VMEM((block, 2 * keep), jnp.int32),
            pltpu.VMEM((8, slot), jnp.float32),
        ],
    )
    return pl.pallas_call(
        functools.partial(attend_kernel, parts, chunk),
        grid_spec=grid_spec,
        out_shape=[
            jax.ShapeDtypeStruct((heads, HD, parts * block), jnp.bfloat16),
            jax.ShapeDtypeStruct((heads, parts, block, slot), jnp.bfloat16),
        ],
        name="attend",
    )(base, kept, query, pairs, key_score)


def attend_back_kernel(parts, chunk, base_ref, q_ref, grad_ref, kv_ref, prob_ref, dq_ref, out_ref, turned_ref, dq_turned_ref, gates_ref, raw_ref, dkv_ref, gate_ref):
    f32, bf16 = jnp.float32, jnp.bfloat16
    rows = prob_ref.shape[2]
    count, height, _ = out_ref.shape
    lane = lax.broadcasted_iota(jnp.int32, (rows, LANES), 1)
    for part in reversed(range(parts)):
        last = part == parts - 1
        query = q_ref[pl.ds(pl.multiple_of((part * (chunk // rows) + base_ref[1]) * rows, rows), rows), :]
        grad = grad_ref[part * rows : (part + 1) * rows, :]
        dot_sum = None
        for at in range(part + 1):
            cols = slice(at * chunk, (at + 1) * chunk)
            raw = lax.dot_general(grad, kv_ref[cols, :], NT, preferred_element_type=f32)
            raw_ref[part, :, cols] = raw
            piece = jnp.sum(raw * prob_ref[0, part, :, cols].astype(f32), axis=1, keepdims=True)
            dot_sum = piece if dot_sum is None else dot_sum + piece
        scaled = jnp.where(lane == HD, 1.0, query.astype(f32) * HD ** (-0.5))
        query_t = jnp.transpose(scaled)[: HD + 16].astype(bf16)
        grad_t = jnp.transpose(grad.astype(f32))[HD:].astype(bf16)
        dq = None
        for at in range(part + 1):
            cols = slice(at * chunk, (at + 1) * chunk)
            prob = prob_ref[0, part, :, cols]
            grad_score = (prob.astype(f32) * (raw_ref[part, :, cols] - dot_sum)).astype(bf16)
            piece = jnp.dot(grad_score, kv_ref[cols, :], preferred_element_type=f32)
            dq = piece if dq is None else dq + piece
            keys = jnp.dot(query_t, grad_score, preferred_element_type=f32)
            values = jnp.dot(grad_t, prob, preferred_element_type=f32)
            if last:
                dkv_ref[:HD, cols] = keys[:HD]
                gate_ref[:, cols] = keys[HD : HD + 8]
                dkv_ref[HD:, cols] = values
            else:
                dkv_ref[:HD, cols] += keys[:HD]
                gate_ref[:, cols] += keys[HD : HD + 8]
                dkv_ref[HD:, cols] += values
        dq = dq * HD ** (-0.5)
        dq_ref[part * rows : (part + 1) * rows, :] = dq.astype(dq_ref.dtype)
        dq_turned_ref[0, :, part * rows : (part + 1) * rows] = jnp.transpose(dq)[:HD, :].astype(bf16)
    turned_ref[0] = dkv_ref[...].astype(bf16)
    gates_ref[0] = gate_ref[...]
    for at in range(count):
        rows_of = []
        for part in range(parts):
            cols = slice((part * count + at) * LANES, (part * count + at + 1) * LANES)
            out_ref[at, part * LANES : (part + 1) * LANES, :] = jnp.transpose(dkv_ref[:, cols]).astype(bf16)
            rows_of.append(gate_ref[0:1, cols])
        rows_of.append(jnp.zeros((PAD_ROWS - parts, LANES), f32))
        out_ref[at, height - PAD_ROWS :, :] = jnp.concatenate(rows_of, axis=0).astype(bf16)


def attend_back(count, base, query, grad, pairs, prob):
    heads, parts, block, slot = prob.shape
    width = pairs.shape[1]
    height = slot // count + PAD_ROWS
    chunk = slot // parts
    return pl.pallas_call(
        functools.partial(attend_back_kernel, parts, chunk),
        grid_spec=pltpu.PrefetchScalarGridSpec(
            num_scalar_prefetch=1,
            grid=(heads,),
            in_specs=[
                pl.BlockSpec((slot, LANES), lambda h, b: (0, h)),
                pl.BlockSpec((parts * block, LANES), lambda h, b: (0, h)),
                pl.BlockSpec((slot, LANES), lambda h, b: (0, h)),
                pl.BlockSpec((1, parts, block, slot), lambda h, b: (h, 0, 0, 0)),
            ],
            out_specs=[
                pl.BlockSpec((parts * block, LANES), lambda h, b: (0, h)),
                pl.BlockSpec((count, height, LANES), lambda h, b: (0, 0, h)),
                pl.BlockSpec((1, LANES, slot), lambda h, b: (h, 0, 0)),
                pl.BlockSpec((1, HD, parts * block), lambda h, b: (h, 0, 0)),
                pl.BlockSpec((1, 8, slot), lambda h, b: (h, 0, 0)),
            ],
            scratch_shapes=[
                pltpu.VMEM((parts, block, slot), jnp.float32),
                pltpu.VMEM((LANES, slot), jnp.float32),
                pltpu.VMEM((8, slot), jnp.float32),
            ],
        ),
        out_shape=[
            jax.ShapeDtypeStruct((parts * block, heads * LANES), jnp.bfloat16),
            jax.ShapeDtypeStruct((count, height, width), jnp.bfloat16),
            jax.ShapeDtypeStruct((heads, LANES, slot), jnp.bfloat16),
            jax.ShapeDtypeStruct((heads, HD, parts * block), jnp.bfloat16),
            jax.ShapeDtypeStruct((heads, 8, slot), jnp.float32),
        ],
        name="attend_back",
    )(base, query, grad, pairs, prob)


def weight_kernel(turned_ref, dq_ref, gates_ref, score_ref, slot_ref, norm_ref, in_ref, gain_ref, out_ref):
    f32, bf16 = jnp.float32, jnp.bfloat16
    heads, _, slot = turned_ref.shape
    wide = in_ref.shape[1]
    width = slot_ref.shape[1]
    total = jnp.concatenate([gates_ref[head, 0:1, :] for head in range(heads)], axis=0)
    total = total * jax.nn.sigmoid(-score_ref[...].astype(f32))
    total = jnp.concatenate([total, jnp.zeros((PAD_ROWS - heads, slot), f32)], axis=0).astype(bf16)
    turned = [
        jnp.dot(turned_ref[...].reshape(heads * LANES, slot), slot_ref[...], preferred_element_type=f32),
        jnp.dot(dq_ref[...].reshape(heads * HD, -1), norm_ref[...], preferred_element_type=f32),
        jnp.dot(total, slot_ref[...], preferred_element_type=f32),
        jnp.zeros((wide - heads * 3 * HD - PAD_ROWS, width), f32),
    ]
    small = jnp.transpose(jnp.concatenate(turned, axis=0))
    gain_grad = jnp.sum(small * in_ref[...].astype(f32), axis=1, keepdims=True) / gain_ref[:, 0:1]
    lane = lax.broadcasted_iota(jnp.int32, small.shape, 1)
    at = heads * 3 * HD + heads
    small = jnp.where(lane == at, gain_grad, jnp.where(lane == at + 1, gain_ref[:, 1:2], small))
    out_ref[...] = small.astype(bf16)


def weight_grad(turned, dq, gates, score, norm_slot, norm_one, weights, gains):
    width = norm_one.shape[1]
    return pl.pallas_call(
        weight_kernel,
        out_shape=jax.ShapeDtypeStruct((width, weights.shape[1]), jnp.bfloat16),
        name="weight_grad",
    )(turned, dq, gates, score, norm_slot, norm_one, weights, gains)


def finish_kernel(heads, pair_ref, dq_ref, score_ref, in_ref, grad_ref):
    f32, bf16 = jnp.float32, jnp.bfloat16
    group = dq_ref.shape[0]
    parts = group // LANES
    wide = in_ref.shape[1]
    gates = pair_ref[group:, :].astype(f32)
    total = jnp.concatenate(
        [
            jnp.concatenate([gates[at : at + 1, head * LANES : (head + 1) * LANES] for at in range(parts)], axis=1)
            for head in range(heads)
        ],
        axis=0,
    )
    total = total * jax.nn.sigmoid(-score_ref[...].astype(f32))
    scores = jnp.transpose(jnp.concatenate([total, jnp.zeros((LANES - heads, group), f32)], axis=0))
    rest = wide - heads * 3 * HD
    columns = jnp.concatenate(
        [pair_ref[:group, :].astype(f32)]
        + [dq_ref[:, head * LANES : head * LANES + HD].astype(f32) for head in range(heads)]
        + [scores[:, :rest]],
        axis=1,
    ).astype(bf16)
    grad_ref[...] = lax.dot_general(columns, in_ref[...], NT, preferred_element_type=f32).astype(bf16)


def finish(pair, dq, score, weights):
    return pl.pallas_call(
        functools.partial(finish_kernel, score.shape[0]),
        out_shape=jax.ShapeDtypeStruct((dq.shape[0], weights.shape[0]), jnp.bfloat16),
        name="finish",
    )(pair, dq, score, weights)


def unpack_kernel(groups, heads, piece, parts, dp_ref, all_ref, qkv_ref, score_ref, gain_ref, fc_ref, proj_ref, *rest):
    f32 = jnp.float32
    keys = heads * 2 * HD
    part_cols = fc_ref.shape[1] // (groups * parts)
    for out_ref in rest:
        mine = out_ref.shape[0]
        for at in range(mine):
            out_ref[at] = all_ref[dp_ref[0] * mine + at, :, 2 * piece + proj_ref.shape[2] :, :].astype(f32)
    for step in range(all_ref.shape[1]):
        rows = slice(step * piece, (step + 1) * piece)
        scores, gains = [], None
        for at in range(groups):
            values = all_ref[at, step, :piece, :].astype(f32)
            for head in range(heads):
                start = (at * heads + head) * 3 * HD
                qkv_ref[rows, start : start + HD] = values[:, keys + head * HD : keys + (head + 1) * HD]
                qkv_ref[rows, start + HD : start + 3 * HD] = values[:, head * 2 * HD : (head + 1) * 2 * HD]
            scores.append(values[:, keys + heads * HD : keys + heads * HD + heads])
            gain = values[:, keys + heads * HD + heads : keys + heads * HD + heads + 2]
            gains = gain if gains is None else gains + gain
            values = all_ref[at, step, piece : 2 * piece, :].astype(f32)
            for part in range(parts):
                start = (part * groups + at) * part_cols
                fc_ref[rows, start : start + part_cols] = values[:, part * part_cols : (part + 1) * part_cols]
            proj_ref[at, step] = all_ref[at, step, 2 * piece : 2 * piece + proj_ref.shape[2], :].astype(f32)
        narrow = jnp.concatenate(
            scores + [gains, jnp.zeros((piece, LANES - groups * heads - 2), f32)], axis=1
        )
        turned = jnp.transpose(jnp.concatenate([narrow, jnp.zeros((LANES - piece, LANES), f32)], axis=0))

        def store(index):
            gain_ref[:, index * piece : (index + 1) * piece] = turned[groups * heads : groups * heads + 8, :piece]
            score_ref[:, index * piece : (index + 1) * piece] = turned[: groups * heads, :piece]

        if all_ref.shape[1] > 1:
            store(step)
        else:
            for index in range(score_ref.shape[1] // piece):
                pl.when(pl.program_id(0) == index)(functools.partial(store, index))


def unpack(at, gathered, heads, piece, proj_piece, parts, hidden):
    groups, count, rows, width = gathered.shape
    step = 1 if piece % 16 == 0 else count
    blocks = [
        ((count * piece, groups * heads * 3 * HD), (step * piece, groups * heads * 3 * HD), lambda c, d: (c, 0)),
        ((groups * heads, count * piece), (groups * heads, count * piece), lambda c, d: (0, 0)),
        ((8, count * piece), (8, count * piece), lambda c, d: (0, 0)),
        ((count * piece, hidden), (step * piece, hidden), lambda c, d: (c, 0)),
        ((groups, count, proj_piece, width), (groups, step, proj_piece, width), lambda c, d: (0, c, 0, 0)),
    ]
    if groups % parts == 0:
        last = rows - 2 * piece - proj_piece
        mine = groups // parts
        blocks.append(((mine, count, last, width), (mine, step, last, width), lambda c, d: (0, c, 0, 0)))
    return pl.pallas_call(
        functools.partial(unpack_kernel, groups, heads, piece, parts),
        grid_spec=pltpu.PrefetchScalarGridSpec(
            num_scalar_prefetch=1,
            grid=(count // step,),
            in_specs=[pl.BlockSpec((groups, step, rows, width), lambda c, d: (0, c, 0, 0))],
            out_specs=[pl.BlockSpec(block, index) for _, block, index in blocks],
        ),
        out_shape=[jax.ShapeDtypeStruct(shape, jnp.float32) for shape, _, _ in blocks],
        name="unpack",
    )(at, gathered)


def arrange_kernel(heads, rows, qkv_ref, score_ref, gains_ref, out_ref):
    f32 = jnp.float32
    values = qkv_ref[...].astype(f32)
    keys = heads * 2 * HD
    width = out_ref.shape[1]
    pieces = [values[:, (3 * head + 1) * HD : (3 * head + 3) * HD] for head in range(heads)]
    pieces += [values[:, 3 * head * HD : (3 * head + 1) * HD] for head in range(heads)]
    pieces += [score_ref[...].astype(f32), jnp.zeros((rows, width - heads * 3 * HD - heads), f32)]
    out_ref[:rows, :] = jnp.concatenate(pieces, axis=1).astype(out_ref.dtype)
    out_ref[rows:, :] = jnp.concatenate(
        [gains_ref[...].astype(f32), jnp.zeros((gains_ref.shape[0], width - rows), f32)], axis=1
    ).astype(out_ref.dtype)


def arrange(qkv, score, gains, width):
    rows, heads = score.shape
    return pl.pallas_call(
        functools.partial(arrange_kernel, heads, rows),
        out_shape=jax.ShapeDtypeStruct((rows + PAD_ROWS, width), qkv.dtype),
        name="arrange",
    )(qkv, score, gains)


def dp_send(mine):
    if lax.axis_size("dp") != 2:
        return lax.all_gather(mine, "dp", axis=0, tiled=True)
    return lax.ppermute(mine, "dp", [(0, 1), (1, 0)])


def dp_join(mine, came):
    if lax.axis_size("dp") != 2:
        return came
    return jnp.where(
        lax.axis_index("dp") == 0, jnp.concatenate([mine, came]), jnp.concatenate([came, mine])
    )


def dp_scatter(parts):
    if lax.axis_size("dp") != 2:
        return lax.psum_scatter(parts, "dp", scatter_dimension=0, tiled=False)
    at = lax.axis_index("dp")
    mine = lax.dynamic_index_in_dim(parts, at, 0, keepdims=False)
    sent = lax.dynamic_index_in_dim(parts, 1 - at, 0, keepdims=False)
    other = lax.ppermute(sent, "dp", [(0, 1), (1, 0)])
    return (mine.astype(jnp.float32) + other.astype(jnp.float32)).astype(parts.dtype)


def group_rows_of(mine, group, count):
    height = mine.shape[0]
    if lax.axis_size("dp") != 2 or height % count != 0:
        whole = lax.all_gather(mine, "dp", axis=0, tiled=True)
        return lax.dynamic_slice_in_dim(whole, group * count, count, 0)
    near = lax.dynamic_slice_in_dim(mine, group * count % height, count, 0)
    far = lax.ppermute(near, "dp", [(0, 1), (1, 0)])
    return jnp.where(lax.axis_index("dp") == group * count // height, near, far)


def dp_sum(mine):
    if lax.axis_size("dp") != 2:
        return lax.psum(mine, "dp")
    other = lax.ppermute(mine, "dp", [(0, 1), (1, 0)])
    return (mine.astype(jnp.float32) + other.astype(jnp.float32)).astype(mine.dtype)


def exchange_sum(parts, axis):
    came = lax.all_to_all(parts, axis, split_axis=0, concat_axis=0, tiled=True)
    return jnp.sum(came.astype(jnp.float32), axis=0)


def per_device(
    tokens,
    cotangent,
    lengths,
    kept_keys,
    first_gain,
    qkv_weight,
    score_weight,
    out_weight,
    second_gain,
    fc_weight,
    proj_weight,
):
    f32, bf16 = jnp.float32, jnp.bfloat16
    dp_count = lax.axis_size("dp")
    seg_count = lax.axis_size("sp")
    ctx_count = lax.axis_size("ctx")
    dp_at = lax.axis_index("dp")
    sp_at = lax.axis_index("sp")
    ctx_at = lax.axis_index("ctx")
    rows = tokens.shape[1]
    width = tokens.shape[2]
    group_rows = seg_count * rows
    heads = H // seg_count
    head_cols = heads * 3 * HD
    hidden = fc_weight.shape[1]
    hidden_part = hidden // (dp_count * seg_count)
    piece = width // (dp_count * ctx_count)

    keys = heads * 2 * HD
    wide = -(-(head_cols + heads + 2) // LANES) * LANES
    weight_rows = width // dp_count
    own_in = arrange(
        lax.dynamic_slice_in_dim(qkv_weight, sp_at * head_cols, head_cols, 1),
        lax.dynamic_slice_in_dim(score_weight, sp_at * heads, heads, 1),
        jnp.pad(jnp.stack([first_gain, second_gain]), ((0, PAD_ROWS - 2), (0, 0))),
        wide,
    )
    if dp_count == 2:
        other_in = lax.ppermute(own_in, "dp", [(0, 1), (1, 0)])
        parts_in = [
            jnp.where(dp_at == at, own_in, other_in) for at in range(dp_count)
        ]
    else:
        parts_in = list(lax.all_gather(own_in, "dp", axis=0, tiled=False))
    tokens_slot = lax.all_gather(tokens[0], ("sp", "ctx"), axis=0, tiled=True)
    all_in = jnp.concatenate([part[:weight_rows] for part in parts_in])
    gain_one = jnp.concatenate([part[weight_rows, :weight_rows] for part in parts_in]).astype(f32)
    gain_two = jnp.concatenate([part[weight_rows + 1, :weight_rows] for part in parts_in]).astype(f32)

    fc_own = jnp.concatenate(
        [
            lax.dynamic_slice_in_dim(fc_weight, (at * seg_count + sp_at) * hidden_part, hidden_part, 1)
            for at in range(dp_count)
        ],
        axis=1,
    )
    proj_own = lax.dynamic_slice_in_dim(proj_weight, sp_at * hidden_part, hidden_part, 0)
    all_in, out_own, fc_own, proj_own = lax.optimization_barrier((all_in, out_weight, fc_own, proj_own))
    out_came = dp_send(out_own)
    fc_came = dp_send(fc_own)
    proj_came = dp_send(proj_own)

    cot_own, all_in = lax.optimization_barrier((cotangent[0], all_in))
    cot_group = lax.all_gather(cot_own, "sp", axis=0, tiled=True)
    kept = jnp.transpose(kept_keys[0], (2, 0, 1, 3))
    out_full = dp_join(out_own, out_came)
    fc_part = dp_join(fc_own, fc_came)
    tokens_slot, cot_group, out_full, fc_part, kept = lax.optimization_barrier(
        (tokens_slot, cot_group, out_full, fc_part, kept)
    )

    def group_of(values):
        parts = values.reshape((seg_count, ctx_count, rows) + values.shape[1:])
        return lax.dynamic_index_in_dim(parts, ctx_at, 1, keepdims=False).reshape((group_rows,) + values.shape[1:])

    inputs = tokens[0].astype(f32)
    inputs_group = group_of(tokens_slot).astype(f32)
    norm_slot, pairs, query_slot, score_slot = project(heads, tokens_slot, gain_one[None], all_in)
    key_score = lax.dynamic_index_in_dim(
        score_slot.reshape(heads, seg_count, ctx_count, rows), ctx_at, 2, keepdims=False
    ).reshape(heads, group_rows)
    norm_one = group_of(norm_slot)
    base = jnp.stack([ctx_at * rows, ctx_at]).astype(jnp.int32)
    head_outs, prob = attend(base, kept, query_slot, pairs, score_slot)
    head_outs, proj_came = lax.optimization_barrier((head_outs, proj_came))
    attended = head_outs.reshape(heads * HD, group_rows)
    attended_all = lax.all_gather(attended, "sp", axis=0, tiled=True)
    out_part = lax.dynamic_slice_in_dim(out_full, sp_at * heads * HD, heads * HD, 0)
    proj_part = dp_join(proj_own, proj_came)

    group_at = jnp.arange(group_rows, dtype=jnp.int32)
    group_positions = (group_at // rows) * (ctx_count * rows) + ctx_at * rows + group_at % rows
    grad_out_group = jnp.where((group_positions < lengths[0])[:, None], cot_group, jnp.zeros_like(cot_group))
    positions = (sp_at * ctx_count + ctx_at) * rows + jnp.arange(rows, dtype=jnp.int32)
    is_valid = (positions < lengths[0])[:, None]

    mixed_group = inputs_group + contract_rows(attended_all, out_full)
    norm_two = layer_norm(mixed_group, gain_two).astype(bf16)
    mixed = lax.dynamic_slice_in_dim(mixed_group, sp_at * rows, rows, 0)
    hidden_pre = jnp.dot(norm_two, fc_part, preferred_element_type=f32)
    active = tanh_gelu(hidden_pre).astype(bf16)
    grad_active = contract_cols(grad_out_group, proj_part)
    _, gelu_pull = jax.vjp(tanh_gelu, hidden_pre)
    grad_pre = gelu_pull(grad_active)[0].astype(bf16)
    grad_norm_parts = contract_cols(grad_pre, fc_part).astype(bf16)
    grad_norm_parts, norm_late, active = lax.optimization_barrier((grad_norm_parts, norm_two, active))
    fc_parts = contract_rows(norm_late, grad_pre).astype(bf16).reshape(dp_count, ctx_count, piece, width)
    proj_parts = contract_rows(active, grad_out_group).astype(bf16).reshape(dp_count, ctx_count, -1, width)
    mlp_parts = jnp.transpose(jnp.concatenate([fc_parts, proj_parts], axis=2), (1, 0, 2, 3))
    mlp_ctx = lax.psum_scatter(
        mlp_parts.reshape(ctx_count, -1, width), "ctx", scatter_dimension=0, tiled=False
    ).reshape(dp_count, -1, width)
    norm_came = lax.all_to_all(
        grad_norm_parts.reshape(seg_count, rows, width), "sp", split_axis=0, concat_axis=0, tiled=True
    )
    score_rows = score_slot[:, 0]
    norm_came, norm_one, score_rows, key_score = lax.optimization_barrier(
        (norm_came, norm_one, score_rows, key_score)
    )
    grad_norm_two = jnp.sum(norm_came.astype(f32), axis=0)
    _, second_pull = jax.vjp(layer_norm, mixed, gain_two)
    grad_mixed_norm, second_gain_grad = second_pull(grad_norm_two)
    grad_out = jnp.where(is_valid, cotangent[0], jnp.zeros_like(cotangent[0])).astype(f32)
    grad_mixed = grad_out + grad_mixed_norm
    grad_branch = lax.all_gather(grad_mixed.astype(bf16), "sp", axis=0, tiled=True)

    out_wide = jnp.pad(out_part.reshape(heads, HD, width), ((0, 0), (HD, 0), (0, 0))).reshape(heads * LANES, width)
    grad_wide = contract_cols(grad_branch, out_wide).astype(bf16)
    out_mine = jnp.dot(attended, grad_branch, preferred_element_type=f32).astype(bf16)
    grad_wide, out_mine = lax.optimization_barrier((grad_wide, out_mine))
    gain_cols = jnp.stack([gain_one, second_gain_grad], axis=1)
    grad_wide, gain_cols = lax.optimization_barrier((grad_wide, gain_cols))
    query_grads, pair_grads, turned, query_turned, gates = attend_back(
        ctx_count, base, query_slot, grad_wide, pairs, prob
    )
    small = weight_grad(turned, query_turned, gates, score_rows, norm_slot, norm_one, all_in, gain_cols)
    small, out_mine = lax.optimization_barrier((small, out_mine))
    out_came = lax.all_to_all(
        out_mine.reshape(ctx_count, -1, width), "ctx", split_axis=0, concat_axis=0, tiled=True
    )
    small_dp, out_came = lax.optimization_barrier(
        (dp_scatter(small.reshape(dp_count, ctx_count, piece, wide)), out_came)
    )
    small_own = jnp.pad(exchange_sum(small_dp, "ctx").astype(bf16), ((0, 0), (0, width - wide)))
    out_own = dp_sum(jnp.sum(out_came.astype(f32), axis=0).astype(bf16))
    gradients = jnp.concatenate([small_own, dp_scatter(mlp_ctx), out_own], axis=0)
    pair_grads, gradients, active_late = lax.optimization_barrier((pair_grads, gradients, active))
    pair_mine = exchange_sum(pair_grads, "ctx").astype(bf16)
    pair_mine, active_late = lax.optimization_barrier((pair_mine, active_late))
    gathered = lax.all_gather(gradients, ("sp", "ctx"), axis=0, tiled=False).reshape(seg_count, ctx_count, -1, width)
    proj_piece = hidden // (seg_count * dp_count * ctx_count)

    grad_norm_part = finish(pair_mine, query_grads, key_score, all_in)
    expanded = exchange_sum(
        jnp.dot(active_late, proj_part, preferred_element_type=f32).astype(bf16).reshape(seg_count, rows, width), "sp"
    )
    output = jnp.where(is_valid, mixed + expanded, 0.0).astype(bf16)[None]
    grad_norm_one = exchange_sum(grad_norm_part.reshape(seg_count, rows, width), "sp")
    _, first_pull = jax.vjp(lambda values: layer_norm(values, gain_one), inputs)
    grad_input_norm = first_pull(grad_norm_one)[0]
    input_grad = (grad_mixed + grad_input_norm).astype(bf16)[None]

    qkv_grad, turned_scores, gains, fc_grad, proj_grad, *rest = unpack(
        dp_at.astype(jnp.int32)[None], gathered, heads, piece, proj_piece, dp_count, hidden
    )
    proj_grad = proj_grad.reshape(-1, width)
    if rest:
        out_grad = rest[0].reshape(weight_rows, width)
    else:
        out_grad = lax.dynamic_slice_in_dim(
            gathered[:, :, 2 * piece + proj_piece :].reshape(width, width), dp_at * weight_rows, weight_rows, 0
        ).astype(f32)
    score_grad = turned_scores.T
    return (output, input_grad, gains[0], qkv_grad, score_grad, out_grad, gains[1], fc_grad, proj_grad)


def solution(mesh):
    placed = (
        P("dp", ("sp", "ctx"), None),
        P("dp", ("sp", "ctx"), None),
        P("dp"),
        P("dp", None, "ctx", "sp", None),
        P("dp"),
        P("dp", None),
        P("dp", None),
        P("dp", None),
        P("dp"),
        P("dp", None),
        P("dp", None),
    )
    return jax.shard_map(
        per_device,
        mesh=mesh,
        in_specs=placed,
        out_specs=(
            P("dp", ("sp", "ctx"), None),
            P("dp", ("sp", "ctx"), None),
            P("dp"),
            P("dp", None),
            P("dp", None),
            P("dp", None),
            P("dp"),
            P("dp", None),
            P("dp", None),
        ),
        check_vma=False,
    )
```
